32 devices in a mesh: dp: 8 (over z, y), shard: 4 (over x, core).
Axes of the slice: x: 2, y: 2, z: 4, core: 2. Of those that a mesh axis runs over, the one named last changes fastest.
Arguments:
- tokens: bfloat16 [32768, 768], P(('dp', 'shard')), may hold values from -6 to 6
- teacher_tokens: bfloat16 [32768, 768], P(('dp', 'shard')), may hold values from -6 to 6
- cotangent: bfloat16 [32768, 768], P(('dp', 'shard')), may hold values from -6 to 6
- lengths: int32 [32], replicated, may hold values from 512 to 1024, as said below
- clip_scales: float32 [4], replicated, may hold values from 0.15 to 0.4
- attn_latent: float32 [4, 768, 768], P(None, ('dp', 'shard')), may hold values from -1 to 1
- up_latent: float32 [3072, 768], P(('dp', 'shard')), may hold values from -0.21875 to 0.21875
- down_latent: float32 [768, 3072], P(('dp', 'shard')), may hold values from -0.109375 to 0.109375
- biases: bfloat16 [5, 768], P(None, ('dp', 'shard')), may hold values from -1.1953125 to 1.1953125
- up_bias: bfloat16 [3072], P(('dp', 'shard')), may hold values from -1.1953125 to 1.1953125
- norm_gains: bfloat16 [2, 768], P(None, ('dp', 'shard')), may hold values from 0.5 to 1.5
- norm_shifts: bfloat16 [2, 768], P(None, ('dp', 'shard')), may hold values from -1.1953125 to 1.1953125
- teacher_attn: bfloat16 [4, 768, 768], P(None, ('dp', 'shard')), may hold values from -1 to 1
- teacher_up: bfloat16 [3072, 768], P(('dp', 'shard')), may hold values from -0.21875 to 0.21875
- teacher_down: bfloat16 [768, 3072], P(('dp', 'shard')), may hold values from -0.109375 to 0.109375
- teacher_biases: bfloat16 [5, 768], P(None, ('dp', 'shard')), may hold values from -1.1953125 to 1.1953125
- teacher_up_bias: bfloat16 [3072], P(('dp', 'shard')), may hold values from -1.1953125 to 1.1953125
- teacher_gains: bfloat16 [2, 768], P(None, ('dp', 'shard')), may hold values from 0.5 to 1.5
- teacher_shifts: bfloat16 [2, 768], P(None, ('dp', 'shard')), may hold values from -1.1953125 to 1.1953125
Outputs:
- output: bfloat16 [32768, 768], P(('dp', 'shard'))
- loss: float32 [], replicated
- input_grad: bfloat16 [32768, 768], P(('dp', 'shard'))
- attn_grad: float32 [4, 768, 768], P(None, ('dp', 'shard'))
- up_grad: float32 [3072, 768], P(('dp', 'shard'))
- down_grad: float32 [768, 3072], P(('dp', 'shard'))
- bias_grad: float32 [5, 768], P(None, ('dp', 'shard'))
- up_bias_grad: float32 [3072], P(('dp', 'shard'))
- gain_grad: float32 [2, 768], P(None, ('dp', 'shard'))
- shift_grad: float32 [2, 768], P(None, ('dp', 'shard'))
The draws below stay inside these ranges and needn't reach their ends.
Inputs may be any that keep to these rules, and one draw needn't show every extreme that they name: The first lengths[s] positions of sequence s are tokens and the rest padding; some sequence has exactly 1024 and another exactly 512.
All inputs are finite; a program needn't handle non-finite values. Where the reference program divides by a largest or mean magnitude, that divisor is 1e-20 or more.
Results may differ from the reference program's by a relative error of at most 0.012.
The reference program's roundings to bfloat16 on the way count: a program that leaves them out, or rounds other values in their place, can miss the bound.
Values may be sent and summed in bfloat16 or wider, within the bound.
A program may use at most 256 MiB of HBM per device.

```python
import math
import jax
import jax.numpy as jnp
from jax import lax

D = 768
FF = 3072
HEADS = 12
HEAD_DIM = 64
SEQ_LEN = 1024
SEQS = 32
TOKENS = 32768


def draw_lengths(key, part):
    first_key, second_key, third_key = jax.random.split(key, 3)
    drawn = jax.random.randint(first_key, (SEQS,), SEQ_LEN // 2, SEQ_LEN + 1, dtype=jnp.int32)
    longest = jax.random.randint(second_key, (), 0, SEQS, dtype=jnp.int32)
    shortest = (longest + 1 + jax.random.randint(third_key, (), 0, SEQS - 1, dtype=jnp.int32)) % SEQS
    places = jnp.arange(SEQS, dtype=jnp.int32)
    drawn = jnp.where(places == longest, SEQ_LEN, drawn)
    return jnp.where(places == shortest, SEQ_LEN // 2, drawn).astype(jnp.int32)


def attention_draw(key):
    factors = jnp.array([(D // 4) ** (-0.5), (D // 4) ** (-0.5), D ** (-0.5), (D // 8) ** (-0.5)], jnp.float32)
    normal = jnp.clip(jax.random.normal(key, (4, D, D), jnp.float32), -6.0, 6.0)
    return normal * factors[:, None, None]


def draw_attn_latent(key, part):
    return attention_draw(jax.random.fold_in(key, 11))


def draw_teacher_attn(key, part):
    return attention_draw(jax.random.fold_in(key, 23)).astype(jnp.bfloat16)


def block_levels(key, extent, shards, smallest, largest):
    def one(axis_at, parts):
        heights = jax.random.uniform(jax.random.fold_in(jax.random.fold_in(key, 6), axis_at), (parts,), jnp.float32, smallest / len(shards), largest / len(shards))
        return jnp.repeat(jnp.exp(heights), extent[axis_at] // parts).reshape((-1,) + (1,) * (len(extent) - axis_at - 1))

    factor_of = one(*shards[0])
    for cut in shards[1:]:
        factor_of = factor_of * one(*cut)
    return factor_of


def noise(key, dims, deviation, reach, pieces=(), held_as=jnp.bfloat16):
    loudness = block_levels(key, dims, pieces, -0.22, 0.18) if pieces else 1.0
    values = jax.random.normal(key, dims, jnp.float32) * deviation * loudness
    return jnp.minimum(jnp.maximum(values, -reach), reach).astype(held_as)


def setup_inputs(seed: int = 0) -> dict:
    streams_of = jax.random.split(jax.random.key(seed), 20)
    return {
        "tokens": noise(streams_of[0], (TOKENS, D), 1.0, 6.0, ((0, 32),)),
        "teacher_tokens": noise(streams_of[1], (TOKENS, D), 1.0, 6.0, ((0, 32),)),
        "cotangent": noise(streams_of[2], (TOKENS, D), 1.0, 6.0, ((0, 32),)),
        "lengths": draw_lengths(jax.random.fold_in(streams_of[19], 71), 0),
        "clip_scales": jnp.clip(jnp.exp(jax.random.uniform(streams_of[4], (4,), jnp.float32, math.log(0.15), math.log(0.4))), 0.15, 0.4),
        "attn_latent": draw_attn_latent(jax.random.fold_in(streams_of[19], 71), 0),
        "up_latent": noise(streams_of[6], (FF, D), D ** -0.5, 0.21875, ((0, 32),), jnp.float32),
        "down_latent": noise(streams_of[7], (D, FF), FF ** -0.5, 0.109375, ((0, 32),), jnp.float32),
        "biases": noise(streams_of[8], (5, D), 0.2, 1.1953125, ((1, 32),)),
        "up_bias": noise(streams_of[9], (FF,), 0.2, 1.1953125, ((0, 32),)),
        "norm_gains": jnp.clip(1.0 + 0.1 * jax.random.normal(streams_of[10], (2, D), jnp.float32), 0.5, 1.5).astype(jnp.bfloat16),
        "norm_shifts": noise(streams_of[11], (2, D), 0.2, 1.1953125, ((1, 32),)),
        "teacher_attn": draw_teacher_attn(jax.random.fold_in(streams_of[19], 71), 0),
        "teacher_up": noise(streams_of[13], (FF, D), D ** -0.5, 0.21875, ((0, 32),)),
        "teacher_down": noise(streams_of[14], (D, FF), FF ** -0.5, 0.109375, ((0, 32),)),
        "teacher_biases": noise(streams_of[15], (5, D), 0.2, 1.1953125, ((1, 32),)),
        "teacher_up_bias": noise(streams_of[16], (FF,), 0.2, 1.1953125, ((0, 32),)),
        "teacher_gains": jnp.clip(1.0 + 0.1 * jax.random.normal(streams_of[17], (2, D), jnp.float32), 0.5, 1.5).astype(jnp.bfloat16),
        "teacher_shifts": noise(streams_of[18], (2, D), 0.2, 1.1953125, ((1, 32),)),
    }


@jax.custom_vjp
def low(v):
    return lax.optimization_barrier(v.astype(jnp.bfloat16)).astype(jnp.float32)

@jax.custom_vjp
def low_back(v):
    return v

def low_keep(v):
    return (low(v), None)

def low_pass(kept, grad):
    return (grad,)

def back_keep(v):
    return (v, None)

def back_low(kept, grad):
    return (low(grad),)
low.defvjp(low_keep, low_pass)
low_back.defvjp(back_keep, back_low)
highest = lax.Precision.HIGHEST
epsilon = 1e-05
masked_score = -1e+30
hidden_weight = 0.25
saturation = 7.5

def dense(inputs, weight, bias):
    return jnp.dot(inputs, weight.T, precision=highest) + bias

def layer_norm(values, gain, shift):
    center = values - lax.optimization_barrier(jnp.mean(values, axis=-1, keepdims=True))
    spread = lax.optimization_barrier(jnp.mean(center * center, axis=-1, keepdims=True))
    return center * lax.rsqrt(spread + epsilon) * gain + shift

def clamp_act(values, scale):
    return saturation * scale * jnp.tanh(values / (saturation * scale))

def binarize(latent):
    scale = lax.optimization_barrier(jnp.mean(jnp.abs(latent), axis=-1, keepdims=True))
    return low(scale * jnp.sign(latent))

def surrogate(latent):
    return lax.optimization_barrier(jnp.mean(jnp.abs(latent), axis=-1, keepdims=True)) * latent

def latent_grad(latent, grad):
    _, pull = jax.vjp(surrogate, latent)
    return pull(grad)[0]

def teacher_forward(teach_in, teach, length):
    attn_w, up_w, down_w, bias_w, up_b, gain_w, shift_w = teach
    queries = low(dense(teach_in, attn_w[0], bias_w[0]))
    keys_all = low(dense(teach_in, attn_w[1], bias_w[1]))
    values_all = low(dense(teach_in, attn_w[2], bias_w[2]))
    block_rows = min(512, SEQ_LEN)
    key_heads = keys_all.reshape(SEQ_LEN, HEADS, HEAD_DIM)
    value_heads = values_all.reshape(SEQ_LEN, HEADS, HEAD_DIM)
    key_live = jnp.arange(SEQ_LEN, dtype=jnp.int32) < length

    def one_block(start):
        query_block = lax.dynamic_slice_in_dim(queries, start, block_rows, 0).reshape(block_rows, HEADS, HEAD_DIM)
        scores = jnp.einsum('qhe,khe->hqk', query_block, key_heads, precision=highest) * HEAD_DIM ** (-0.5)
        masked = jnp.where(key_live[None, None, :], scores, masked_score)
        probs = low(jax.nn.softmax(masked, axis=-1))
        context = jnp.einsum('hqk,khe->qhe', probs, value_heads, precision=highest)
        return context.reshape(block_rows, D)
    starts = jnp.arange(SEQ_LEN // block_rows, dtype=jnp.int32) * block_rows
    context = low(lax.map(one_block, starts).reshape(SEQ_LEN, D))
    hidden = layer_norm(teach_in + dense(context, attn_w[3], bias_w[3]), gain_w[0], shift_w[0])
    upper = dense(low(hidden), up_w, up_b)
    lower = dense(low(jax.nn.gelu(upper, approximate=False)), down_w, bias_w[4])
    return (layer_norm(hidden + lower, gain_w[1], shift_w[1]), queries, keys_all)

def student_forward(params, tokens_seq, teacher_q, teacher_k, teacher_out, length, clip_scales, pair_norm):
    attn_w, up_w, down_w, bias_w, up_b, gain_w, shift_w = params
    x_low = low(clamp_act(tokens_seq, clip_scales[0]))
    queries = low(low_back(dense(x_low, attn_w[0], bias_w[0])))
    keys_all = low(low_back(dense(x_low, attn_w[1], bias_w[1])))
    values_all = low(low_back(dense(x_low, attn_w[2], bias_w[2])))
    block_rows = min(512, SEQ_LEN)
    key_heads = keys_all.reshape(SEQ_LEN, HEADS, HEAD_DIM)
    value_heads = values_all.reshape(SEQ_LEN, HEADS, HEAD_DIM)
    teacher_keys = teacher_k.reshape(SEQ_LEN, HEADS, HEAD_DIM)
    key_live = jnp.arange(SEQ_LEN, dtype=jnp.int32) < length

    def one_block(start):
        query_block = lax.dynamic_slice_in_dim(queries, start, block_rows, 0).reshape(block_rows, HEADS, HEAD_DIM)
        teacher_block = lax.dynamic_slice_in_dim(teacher_q, start, block_rows, 0).reshape(block_rows, HEADS, HEAD_DIM)
        row_live = start + jnp.arange(block_rows, dtype=jnp.int32) < length
        scores = low_back(jnp.einsum('qhe,khe->hqk', query_block, key_heads, precision=highest) * HEAD_DIM ** (-0.5))
        teacher_scores = jnp.einsum('qhe,khe->hqk', teacher_block, teacher_keys, precision=highest) * HEAD_DIM ** (-0.5)
        pair_live = row_live[None, :, None] & key_live[None, None, :]
        differ = jnp.where(pair_live, scores - teacher_scores, 0.0)
        masked = jnp.where(key_live[None, None, :], scores, masked_score)
        probs = low(jax.nn.softmax(masked, axis=-1))
        context = jnp.einsum('hqk,khe->qhe', probs, value_heads, precision=highest)
        return (context.reshape(block_rows, D), jnp.sum(differ * differ))
    starts = jnp.arange(SEQ_LEN // block_rows, dtype=jnp.int32) * block_rows
    contexts, squares = lax.map(jax.checkpoint(one_block), starts)
    context = low_back(contexts.reshape(SEQ_LEN, D))
    ctx_low = low(clamp_act(context, clip_scales[1]))
    attn_out = low_back(dense(ctx_low, attn_w[3], bias_w[3]))
    hidden = layer_norm(tokens_seq + attn_out, gain_w[0], shift_w[0])
    upper = low_back(dense(low(clamp_act(hidden, clip_scales[2])), up_w, up_b))
    lower = low_back(dense(low(clamp_act(jax.nn.gelu(upper, approximate=False), clip_scales[3])), down_w, bias_w[4]))
    result = layer_norm(hidden + lower, gain_w[1], shift_w[1])
    row_live = jnp.arange(SEQ_LEN, dtype=jnp.int32) < length
    gap = jnp.where(row_live[:, None], result - teacher_out, 0.0)
    return (result, jnp.sum(gap * gap), jnp.sum(squares) / pair_norm)

def reference(tokens, teacher_tokens, cotangent, lengths, clip_scales, attn_latent, up_latent, down_latent, biases, up_bias, norm_gains, norm_shifts, teacher_attn, teacher_up, teacher_down, teacher_biases, teacher_up_bias, teacher_gains, teacher_shifts):
    live_float = lengths.astype(jnp.float32)
    token_norm = jnp.sum(live_float)
    pair_norm = HEADS * jnp.sum(live_float * live_float)
    params = (binarize(attn_latent), binarize(up_latent), binarize(down_latent), biases.astype(jnp.float32), up_bias.astype(jnp.float32), norm_gains.astype(jnp.float32), norm_shifts.astype(jnp.float32))
    teach = tuple((item.astype(jnp.float32) for item in (teacher_attn, teacher_up, teacher_down, teacher_biases, teacher_up_bias, teacher_gains, teacher_shifts)))
    inputs = (tokens.astype(jnp.float32).reshape(SEQS, SEQ_LEN, D), teacher_tokens.astype(jnp.float32).reshape(SEQS, SEQ_LEN, D), cotangent.astype(jnp.float32).reshape(SEQS, SEQ_LEN, D), lengths)

    def one_sequence(carry, items):
        grad_total, loss_total = carry
        tokens_seq, teach_seq, cot_seq, length = items
        teacher_out, teacher_q, teacher_k = teacher_forward(teach_seq, teach, length)

        def forward(weights, inputs_seq):
            return student_forward(weights, inputs_seq, teacher_q, teacher_k, teacher_out, length, clip_scales, pair_norm)
        (result, hidden_sq, score_term), pull = jax.vjp(forward, params, tokens_seq)
        weight_grads, input_grad = pull((cot_seq, jnp.full_like(hidden_sq, hidden_weight), jnp.ones_like(score_term)))
        grad_total = jax.tree.map(jnp.add, grad_total, weight_grads)
        loss = hidden_sq / (D * token_norm) + score_term
        return ((grad_total, loss_total + loss), (result.astype(jnp.bfloat16), input_grad.astype(jnp.bfloat16)))
    start = (jax.tree.map(jnp.zeros_like, params), jnp.zeros((), jnp.float32))
    (grads, loss), (results, input_grads) = lax.scan(one_sequence, start, inputs)
    return (results.reshape(TOKENS, D), loss, input_grads.reshape(TOKENS, D), latent_grad(attn_latent, grads[0]), latent_grad(up_latent, grads[1]), latent_grad(down_latent, grads[2]), grads[3], grads[4], grads[5], grads[6])
```

```python
import math

import jax
import jax.numpy as jnp
from jax import lax
from jax.sharding import PartitionSpec as P

D = 768
HEADS = 12
HEAD_DIM = 64
SEQ_LEN = 1024


epsilon = 1e-05
masked_score = -1e30
hidden_weight = 0.25
saturation = 7.5


def project(inputs, weight):
    return lax.dot_general(
        inputs, weight, (((1,), (1,)), ((), ())), preferred_element_type=jnp.float32
    )


def outer_rows(left, right):
    return lax.dot_general(
        left, right, (((0,), (0,)), ((), ())), preferred_element_type=jnp.float32
    )


def binarize(latent):
    scale = jnp.mean(jnp.abs(latent), axis=-1, keepdims=True)
    return (scale * jnp.sign(latent)).astype(jnp.bfloat16)


def surrogate(latent):
    return jnp.mean(jnp.abs(latent), axis=-1, keepdims=True) * latent


def latent_grad(latent, grad):
    _, pull = jax.vjp(surrogate, latent)
    return pull(grad)[0]


def normalize(values):
    center = values - jnp.mean(values, axis=-1, keepdims=True)
    inverse = lax.rsqrt(jnp.mean(center * center, axis=-1, keepdims=True) + epsilon)
    return (center * inverse, inverse)


def norm_back(grad_norm, normed, inverse):
    return inverse * (
        grad_norm
        - jnp.mean(grad_norm, axis=-1, keepdims=True)
        - normed * jnp.mean(grad_norm * normed, axis=-1, keepdims=True)
    )


def clamp_act(values, scale):
    return saturation * scale * jnp.tanh(values / (saturation * scale))


def clamp_slope(values, scale):
    bent = jnp.tanh(values / (saturation * scale))
    return 1.0 - bent * bent


def live_softmax(scores, key_live):
    masked = jnp.where(key_live[None, None, :], scores, masked_score)
    top = jnp.max(masked, axis=-1, keepdims=True)
    expo = jnp.exp(masked - top)
    total = jnp.sum(expo, axis=-1, keepdims=True)
    return (expo / total, top[..., 0] + jnp.log(total[..., 0]))


def teacher_attend(query_seq, key_seq, value_seq, length):
    block_rows = min(512, SEQ_LEN)
    key_heads = key_seq.reshape(SEQ_LEN, HEADS, HEAD_DIM)
    value_heads = value_seq.reshape(SEQ_LEN, HEADS, HEAD_DIM)
    key_live = jnp.arange(SEQ_LEN, dtype=jnp.int32) < length

    def teacher_one_block(start):
        query_block = lax.dynamic_slice_in_dim(query_seq, start, block_rows, 0).reshape(
            block_rows, HEADS, HEAD_DIM
        )
        scores = jnp.einsum(
            "qhe,khe->hqk", query_block, key_heads, preferred_element_type=jnp.float32
        ) * HEAD_DIM ** (-0.5)
        probs, _ = live_softmax(scores, key_live)
        context = jnp.einsum(
            "hqk,khe->qhe",
            probs.astype(jnp.bfloat16),
            value_heads,
            preferred_element_type=jnp.float32,
        )
        return context.reshape(block_rows, D)

    starts = jnp.arange(SEQ_LEN // block_rows, dtype=jnp.int32) * block_rows
    return lax.map(teacher_one_block, starts).reshape(SEQ_LEN, D)


def student_attend(query_seq, key_seq, value_seq, tq_seq, tk_seq, length):
    block_rows = min(512, SEQ_LEN)
    key_heads = key_seq.reshape(SEQ_LEN, HEADS, HEAD_DIM)
    value_heads = value_seq.reshape(SEQ_LEN, HEADS, HEAD_DIM)
    teacher_keys = tk_seq.reshape(SEQ_LEN, HEADS, HEAD_DIM)
    key_live = jnp.arange(SEQ_LEN, dtype=jnp.int32) < length

    def student_one_block(start):
        query_block = lax.dynamic_slice_in_dim(query_seq, start, block_rows, 0).reshape(
            block_rows, HEADS, HEAD_DIM
        )
        teacher_block = lax.dynamic_slice_in_dim(tq_seq, start, block_rows, 0).reshape(
            block_rows, HEADS, HEAD_DIM
        )
        row_live = start + jnp.arange(block_rows, dtype=jnp.int32) < length
        scores = jnp.einsum(
            "qhe,khe->hqk", query_block, key_heads, preferred_element_type=jnp.float32
        ) * HEAD_DIM ** (-0.5)
        teacher_scores = jnp.einsum(
            "qhe,khe->hqk", teacher_block, teacher_keys, preferred_element_type=jnp.float32
        ) * HEAD_DIM ** (-0.5)
        pair_live = row_live[None, :, None] & key_live[None, None, :]
        differ = jnp.where(pair_live, scores - teacher_scores, 0.0)
        probs, logsum = live_softmax(scores, key_live)
        context = jnp.einsum(
            "hqk,khe->qhe",
            probs.astype(jnp.bfloat16),
            value_heads,
            preferred_element_type=jnp.float32,
        )
        return (context.reshape(block_rows, D), logsum, jnp.sum(differ * differ))

    starts = jnp.arange(SEQ_LEN // block_rows, dtype=jnp.int32) * block_rows
    contexts, logsums, squares = lax.map(student_one_block, starts)
    return (contexts.reshape(SEQ_LEN, D), logsums, jnp.sum(squares))


def attend_back(
    query_seq, key_seq, value_seq, tq_seq, tk_seq, dctx_seq, logsums, length, pair_norm
):
    block_rows = min(512, SEQ_LEN)
    key_heads = key_seq.reshape(SEQ_LEN, HEADS, HEAD_DIM)
    value_heads = value_seq.reshape(SEQ_LEN, HEADS, HEAD_DIM)
    teacher_keys = tk_seq.reshape(SEQ_LEN, HEADS, HEAD_DIM)
    key_live = jnp.arange(SEQ_LEN, dtype=jnp.int32) < length
    scaling = HEAD_DIM ** (-0.5)

    def attend_one_block(carry, items):
        key_acc, value_acc = carry
        start, logsum = items
        query_block = lax.dynamic_slice_in_dim(query_seq, start, block_rows, 0).reshape(
            block_rows, HEADS, HEAD_DIM
        )
        teacher_block = lax.dynamic_slice_in_dim(tq_seq, start, block_rows, 0).reshape(
            block_rows, HEADS, HEAD_DIM
        )
        grad_block = lax.dynamic_slice_in_dim(dctx_seq, start, block_rows, 0).reshape(
            block_rows, HEADS, HEAD_DIM
        )
        row_live = start + jnp.arange(block_rows, dtype=jnp.int32) < length
        scores = (
            jnp.einsum("qhe,khe->hqk", query_block, key_heads, preferred_element_type=jnp.float32)
            * scaling
        )
        teacher_scores = (
            jnp.einsum(
                "qhe,khe->hqk", teacher_block, teacher_keys, preferred_element_type=jnp.float32
            )
            * scaling
        )
        masked = jnp.where(key_live[None, None, :], scores, masked_score)
        probs = jnp.exp(masked - logsum[..., None])
        grad_probs = jnp.einsum(
            "qhe,khe->hqk", grad_block, value_heads, preferred_element_type=jnp.float32
        )
        weighted = jnp.sum(probs * grad_probs, axis=-1, keepdims=True)
        pair_live = row_live[None, :, None] & key_live[None, None, :]
        distill = jnp.where(pair_live, 2.0 * (scores - teacher_scores) / pair_norm, 0.0)
        grad_scores = (probs * (grad_probs - weighted) + distill).astype(jnp.bfloat16)
        grad_query = (
            jnp.einsum("hqk,khe->qhe", grad_scores, key_heads, preferred_element_type=jnp.float32)
            * scaling
        )
        key_acc = (
            key_acc
            + jnp.einsum(
                "hqk,qhe->khe", grad_scores, query_block, preferred_element_type=jnp.float32
            )
            * scaling
        )
        value_acc = value_acc + jnp.einsum(
            "hqk,qhe->khe",
            probs.astype(jnp.bfloat16),
            grad_block,
            preferred_element_type=jnp.float32,
        )
        return ((key_acc, value_acc), grad_query.reshape(block_rows, D))

    starts = jnp.arange(SEQ_LEN // block_rows, dtype=jnp.int32) * block_rows
    zeros = jnp.zeros((SEQ_LEN, HEADS, HEAD_DIM), jnp.float32)
    (key_acc, value_acc), grad_queries = lax.scan(
        attend_one_block, (zeros, zeros), (starts, logsums)
    )
    return (
        grad_queries.reshape(SEQ_LEN, D),
        key_acc.reshape(SEQ_LEN, D),
        value_acc.reshape(SEQ_LEN, D),
    )


def device_count():
    return lax.axis_size(("dp", "shard"))


def by_owner(rows):
    return rows.reshape(rows.shape[0], device_count(), -1).transpose(1, 0, 2).reshape(device_count(), -1)


def gather_layer(attn, up, down, bias, up_bias, gain, shift):
    count, narrow, wide = device_count(), bias.shape[1], up.shape[0]
    small = jnp.concatenate([bias.reshape(-1), up_bias, gain.reshape(-1), shift.reshape(-1)])
    small = jnp.pad(small, (0, 8 * D - small.shape[0])).reshape(8, D)
    block = jnp.concatenate([attn.reshape(-1, D), up, down.reshape(-1, D), small], axis=0)
    every = lax.all_gather(block, ("dp", "shard"), axis=0, tiled=False)
    at = 4 * narrow
    attn_all = every[:, :at].reshape(count, 4, narrow, D).transpose(1, 0, 2, 3).reshape(4, D, D)
    up_all = every[:, at : at + wide].reshape(-1, D)
    down_all = every[:, at + wide : at + 2 * wide].reshape(D, -1)
    flat = every[:, at + 2 * wide :].reshape(count, -1)

    def spread(start, rows, width):
        part = flat[:, start : start + rows * width].reshape(count, rows, width)
        return part.transpose(1, 0, 2).reshape(rows, count * width)

    start = 5 * narrow
    bias_all = spread(0, 5, narrow)
    up_bias_all = spread(start, 1, wide)[0]
    gain_all = spread(start + wide, 2, narrow)
    shift_all = spread(start + wide + 2 * narrow, 2, narrow)
    return attn_all, up_all, down_all, bias_all, up_bias_all, gain_all, shift_all


def by_sequence(array):
    return array.reshape(array.shape[0] // SEQ_LEN, SEQ_LEN, array.shape[1])


def on_device(
    tokens,
    teacher_tokens,
    cotangent,
    lengths,
    clip_scales,
    attn_latent,
    up_latent,
    down_latent,
    biases,
    up_bias,
    norm_gains,
    norm_shifts,
    teacher_attn,
    teacher_up,
    teacher_down,
    teacher_biases,
    teacher_up_bias,
    teacher_gains,
    teacher_shifts,
):
    rows = tokens.shape[0]
    seq_count = rows // SEQ_LEN
    own_lengths = lax.dynamic_slice_in_dim(
        lengths, lax.axis_index(("dp", "shard")) * seq_count, seq_count
    )
    live_float = lengths.astype(jnp.float32)
    token_norm = jnp.sum(live_float)
    pair_norm = HEADS * jnp.sum(live_float * live_float)
    positions = jnp.arange(SEQ_LEN, dtype=jnp.int32)
    row_live = (positions[None, :] < own_lengths[:, None]).reshape(rows)
    student = gather_layer(
        binarize(attn_latent), binarize(up_latent), binarize(down_latent),
        biases, up_bias, norm_gains, norm_shifts,
    )
    attn_w, up_w, down_w, bias_w, up_b, gain_w, shift_w = student
    bias_float = bias_w.astype(jnp.float32)
    gain_float = gain_w.astype(jnp.float32)
    shift_float = shift_w.astype(jnp.float32)
    teacher = gather_layer(
        teacher_attn, teacher_up, teacher_down,
        teacher_biases, teacher_up_bias, teacher_gains, teacher_shifts,
    )
    teach_attn, teach_up, teach_down, teach_bias, teach_up_bias, teach_gain, teach_shift = teacher
    teach_bias_float = teach_bias.astype(jnp.float32)
    teach_qkv = (
        project(teacher_tokens, teach_attn[:3].reshape(3 * D, D))
        + teach_bias_float[:3].reshape(3 * D)
    ).astype(jnp.bfloat16)
    teach_query, teach_key, teach_value = (
        teach_qkv[:, :D],
        teach_qkv[:, D : 2 * D],
        teach_qkv[:, 2 * D :],
    )
    teach_context = (
        lax.map(
            lambda items: teacher_attend(*items),
            (
                by_sequence(teach_query),
                by_sequence(teach_key),
                by_sequence(teach_value),
                own_lengths,
            ),
        )
        .reshape(rows, D)
        .astype(jnp.bfloat16)
    )
    teach_normed, _ = normalize(
        teacher_tokens.astype(jnp.float32)
        + project(teach_context, teach_attn[3])
        + teach_bias_float[3]
    )
    teach_hidden = teach_normed * teach_gain[0].astype(jnp.float32) + teach_shift[0].astype(
        jnp.float32
    )
    teach_upper = project(teach_hidden.astype(jnp.bfloat16), teach_up) + teach_up_bias.astype(
        jnp.float32
    )
    teach_lower = (
        project(jax.nn.gelu(teach_upper, approximate=False).astype(jnp.bfloat16), teach_down)
        + teach_bias_float[4]
    )
    teach_final, _ = normalize(teach_hidden + teach_lower)
    teach_out = teach_final * teach_gain[1].astype(jnp.float32) + teach_shift[1].astype(jnp.float32)
    x_float = tokens.astype(jnp.float32)
    x_low = clamp_act(x_float, clip_scales[0]).astype(jnp.bfloat16)
    qkv_low = (project(x_low, attn_w[:3].reshape(3 * D, D)) + bias_float[:3].reshape(3 * D)).astype(
        jnp.bfloat16
    )
    queries, keys_all, values_all = (qkv_low[:, :D], qkv_low[:, D : 2 * D], qkv_low[:, 2 * D :])
    contexts, logsums, squares = lax.map(
        lambda items: student_attend(*items),
        (
            by_sequence(queries),
            by_sequence(keys_all),
            by_sequence(values_all),
            by_sequence(teach_query),
            by_sequence(teach_key),
            own_lengths,
        ),
    )
    context = contexts.reshape(rows, D)
    ctx_low = clamp_act(context, clip_scales[1]).astype(jnp.bfloat16)
    first_normed, first_inverse = normalize(x_float + project(ctx_low, attn_w[3]) + bias_float[3])
    hidden = first_normed * gain_float[0] + shift_float[0]
    hidden_low = clamp_act(hidden, clip_scales[2]).astype(jnp.bfloat16)
    upper = project(hidden_low, up_w) + up_b.astype(jnp.float32)
    gelu_out = jax.nn.gelu(upper, approximate=False)
    gelu_low = clamp_act(gelu_out, clip_scales[3]).astype(jnp.bfloat16)
    lower = project(gelu_low, down_w) + bias_float[4]
    second_normed, second_inverse = normalize(hidden + lower)
    result = second_normed * gain_float[1] + shift_float[1]
    gap = jnp.where(row_live[:, None], result - teach_out, 0.0)
    local_loss = jnp.sum(gap * gap) / (D * token_norm) + jnp.sum(squares) / pair_norm
    back_attn, back_up, back_down = attn_w, up_w, down_w
    grad_out = cotangent.astype(jnp.float32) + gap * (2.0 * hidden_weight)
    gain_two = jnp.sum(grad_out * second_normed, axis=0)
    shift_two = jnp.sum(grad_out, axis=0)
    grad_second = norm_back(grad_out * gain_float[1], second_normed, second_inverse)
    grad_lower = grad_second.astype(jnp.bfloat16)
    down_bias_grad = jnp.sum(grad_lower.astype(jnp.float32), axis=0)
    down_weight_grad = outer_rows(grad_lower, gelu_low)
    grad_gelu = jnp.dot(grad_lower, back_down, preferred_element_type=jnp.float32) * clamp_slope(
        gelu_out, clip_scales[3]
    )
    slope = 0.5 * (1.0 + lax.erf(upper * (1.0 / math.sqrt(2.0)))) + upper * jnp.exp(
        -0.5 * upper * upper
    ) * (1.0 / math.sqrt(2.0 * math.pi))
    grad_upper = (grad_gelu * slope).astype(jnp.bfloat16)
    up_bias_grad = jnp.sum(grad_upper.astype(jnp.float32), axis=0)
    up_weight_grad = outer_rows(grad_upper, hidden_low)
    grad_hidden = grad_second + jnp.dot(
        grad_upper, back_up, preferred_element_type=jnp.float32
    ) * clamp_slope(hidden, clip_scales[2])
    gain_one = jnp.sum(grad_hidden * first_normed, axis=0)
    shift_one = jnp.sum(grad_hidden, axis=0)
    grad_first = norm_back(grad_hidden * gain_float[0], first_normed, first_inverse)
    grad_attn_out = grad_first.astype(jnp.bfloat16)
    out_bias_grad = jnp.sum(grad_attn_out.astype(jnp.float32), axis=0)
    out_weight_grad = outer_rows(grad_attn_out, ctx_low)
    grad_context = (
        jnp.dot(grad_attn_out, back_attn[3], preferred_element_type=jnp.float32)
        * clamp_slope(context, clip_scales[1])
    ).astype(jnp.bfloat16)
    grad_queries, grad_keys, grad_values = lax.map(
        lambda items: attend_back(*items, pair_norm),
        (
            by_sequence(queries),
            by_sequence(keys_all),
            by_sequence(values_all),
            by_sequence(teach_query),
            by_sequence(teach_key),
            by_sequence(grad_context),
            logsums,
            own_lengths,
        ),
    )
    grad_qkv = jnp.concatenate(
        [grad_queries.reshape(rows, D), grad_keys.reshape(rows, D), grad_values.reshape(rows, D)],
        axis=1,
    ).astype(jnp.bfloat16)
    qkv_bias_grad = jnp.sum(grad_qkv.astype(jnp.float32), axis=0).reshape(3, D)
    qkv_weight_grad = outer_rows(grad_qkv, x_low).reshape(3, D, D)
    grad_input = jnp.dot(
        grad_qkv, back_attn[:3].reshape(3 * D, D), preferred_element_type=jnp.float32
    )
    input_grad = (grad_first + grad_input * clamp_slope(x_float, clip_scales[0])).astype(
        jnp.bfloat16
    )
    attn_weight_grad = jnp.concatenate([qkv_weight_grad, out_weight_grad[None]], axis=0)
    bias_terms = jnp.concatenate([qkv_bias_grad, out_bias_grad[None], down_bias_grad[None]], axis=0)
    gain_terms = jnp.stack([gain_one, gain_two])
    shift_terms = jnp.stack([shift_one, shift_two])
    small = jnp.concatenate(
        [
            by_owner(bias_terms), by_owner(up_bias_grad[None]),
            by_owner(gain_terms), by_owner(shift_terms),
            jnp.full((device_count(), 1), local_loss, jnp.float32),
        ],
        axis=1,
    )
    small = jnp.pad(small, ((0, 0), (0, 8 * D - small.shape[1]))).reshape(-1, 8, D)
    packed = jnp.concatenate(
        [
            attn_weight_grad.reshape(4, device_count(), -1, D).transpose(1, 0, 2, 3).reshape(device_count(), -1, D),
            up_weight_grad.reshape(device_count(), -1, D),
            small,
        ],
        axis=1,
    )
    total = lax.psum_scatter(packed, ("dp", "shard"), scatter_dimension=0, tiled=True)[0]
    down_total = lax.psum_scatter(down_weight_grad, ("dp", "shard"), scatter_dimension=0, tiled=True)
    attn_rows, up_rows = attn_latent.shape[0] * attn_latent.shape[1], up_latent.shape[0]
    attn_total = total[:attn_rows].reshape(attn_latent.shape)
    up_total = total[attn_rows : attn_rows + up_rows]
    flat = total[attn_rows + up_rows :].reshape(-1)
    narrow = biases.shape[1]
    bias_total, flat = flat[: 5 * narrow].reshape(5, narrow), flat[5 * narrow :]
    up_bias_total, flat = flat[:up_rows], flat[up_rows:]
    gain_total, flat = flat[: 2 * narrow].reshape(2, narrow), flat[2 * narrow :]
    shift_total, flat = flat[: 2 * narrow].reshape(2, narrow), flat[2 * narrow :]
    loss = flat[0]
    return (
        result.astype(jnp.bfloat16),
        loss,
        input_grad,
        latent_grad(attn_latent, attn_total),
        latent_grad(up_latent, up_total),
        latent_grad(down_latent, down_total),
        bias_total,
        up_bias_total,
        gain_total,
        shift_total,
    )


def solution(mesh):
    in_specs = (
        P(("dp", "shard"), None),
        P(("dp", "shard"), None),
        P(("dp", "shard"), None),
        P(),
        P(),
        P(None, ("dp", "shard"), None),
        P(("dp", "shard"), None),
        P(("dp", "shard"), None),
        P(None, ("dp", "shard")),
        P(("dp", "shard")),
        P(None, ("dp", "shard")),
        P(None, ("dp", "shard")),
        P(None, ("dp", "shard"), None),
        P(("dp", "shard"), None),
        P(("dp", "shard"), None),
        P(None, ("dp", "shard")),
        P(("dp", "shard")),
        P(None, ("dp", "shard")),
        P(None, ("dp", "shard")),
    )
    out_specs = (
        P(("dp", "shard"), None),
        P(),
        P(("dp", "shard"), None),
        P(None, ("dp", "shard"), None),
        P(("dp", "shard"), None),
        P(("dp", "shard"), None),
        P(None, ("dp", "shard")),
        P(("dp", "shard")),
        P(None, ("dp", "shard")),
        P(None, ("dp", "shard")),
    )
    return jax.shard_map(
        on_device, mesh=mesh, in_specs=in_specs, out_specs=out_specs, check_vma=False
    )
```

```python
import functools
import math

import jax
import jax.numpy as jnp
from jax import lax
from jax.experimental import pallas as pl
from jax.experimental.pallas import tpu as pltpu
from jax.sharding import PartitionSpec as P

D = 768
HEADS = 12
HEAD_DIM = 64
SEQ_LEN = 1024
AXES = ("dp", "shard")
MESH = pl.DeviceIdType.MESH
F32 = jnp.float32
BF16 = jnp.bfloat16

epsilon = 1e-05
masked_score = -1e30
hidden_weight = 0.25
saturation = 7.5
LANES = 128
log2e = math.log2(math.e)
scaling = HEAD_DIM ** (-0.5)
exponent = scaling * log2e
vmem_bytes = 60 * 1024 * 1024


def dot(left, right, left_dim, right_dim):
    return lax.dot_general(
        left, right, (((left_dim,), (right_dim,)), ((), ())), preferred_element_type=F32
    )


def outer_rows(left, right):
    return dot(left, right, 0, 0)


def binarize(latent):
    scale = jnp.mean(jnp.abs(latent), axis=-1, keepdims=True)
    return (scale * jnp.sign(latent)).astype(BF16)


def surrogate(latent):
    return jnp.mean(jnp.abs(latent), axis=-1, keepdims=True) * latent


def latent_grad(latent, grad):
    _, pull = jax.vjp(surrogate, latent)
    return pull(grad)[0]


def normalize(values):
    center = values - jnp.mean(values, axis=-1, keepdims=True)
    inverse = lax.rsqrt(jnp.mean(center * center, axis=-1, keepdims=True) + epsilon)
    return (center * inverse, inverse)


def norm_back(grad_norm, normed, inverse):
    return inverse * (
        grad_norm
        - jnp.mean(grad_norm, axis=-1, keepdims=True)
        - normed * jnp.mean(grad_norm * normed, axis=-1, keepdims=True)
    )


def whole(memory=pltpu.VMEM):
    return pl.BlockSpec(memory_space=memory)


def fixed(shape):
    return pl.BlockSpec(shape, lambda *_: (0,) * len(shape), pipeline_mode=pl.Buffered(1))


def columns(shape):
    return pl.BlockSpec(shape, lambda i: (0,) * (len(shape) - 1) + (i,))


def row_blocks(shape):
    return pl.BlockSpec(shape, lambda i: (i,) + (0,) * (len(shape) - 1))


def gather_kernel(count, shapes, chunks, depth, *refs):
    ins, outs = refs[:count], refs[count : 2 * count]
    line_send, line_recv, pair_send, pair_recv, own_sem = refs[2 * count :]
    dp, shard = lax.axis_index("dp"), lax.axis_index("shard")
    z, y = dp // 2, lax.rem(dp, 2)
    x, core = shard // 2, lax.rem(shard, 2)

    def device(z_at, y_at, x_at, core_at):
        return (z_at * 2 + y_at, x_at * 2 + core_at)

    above = device(jnp.minimum(z + 1, depth - 1), y, x, core)
    below = device(jnp.maximum(z - 1, 0), y, x, core)
    y_one, x_one = lax.rem(y + 1 - core, 2), lax.rem(x + core, 2)
    y_two, x_two = lax.rem(y + core, 2), lax.rem(x + 1 - core, 2)
    first, second = device(z, y_one, x_one, core), device(z, y_two, x_two, core)
    sibling = device(z, y, x, 1 - core)
    barrier = pltpu.get_barrier_semaphore()
    for partner in (first, second, sibling):
        pl.semaphore_signal(barrier, inc=1, device_id=partner, device_id_type=MESH)

    @pl.when(z < depth - 1)
    def _():
        pl.semaphore_signal(barrier, inc=1, device_id=above, device_id_type=MESH)

    @pl.when(z > 0)
    def _():
        pl.semaphore_signal(barrier, inc=1, device_id=below, device_id_type=MESH)

    pl.semaphore_wait(barrier, 3 + jnp.minimum(z, 1) + jnp.minimum(depth - 1 - z, 1))

    def slot(item, *index):
        return outs[item].at[((slice(None),) if shapes[item][0] > 1 else ()) + index]

    def line_copy(chunk, at, item, turn, upward):
        if upward:
            owner, target = jnp.maximum(z - (turn - 1), 0), above
        else:
            owner, target = jnp.minimum(z + (turn - 1), depth - 1), below
        block = slot(item, owner, y, x, core)
        return pltpu.make_async_remote_copy(
            src_ref=block,
            dst_ref=block,
            send_sem=line_send.at[chunk, at, turn - 1, int(upward)],
            recv_sem=line_recv.at[chunk, at, turn - 1, int(upward)],
            device_id=target,
            device_id_type=MESH,
        )

    def sends(turn, upward):
        if upward:
            return (z - (turn - 1) >= 0) & (z < depth - 1)
        return (z + (turn - 1) <= depth - 1) & (z > 0)

    def receives(turn, upward):
        return (z - turn >= 0) if upward else (z + turn <= depth - 1)

    def own_copy(chunk, at, item):
        return pltpu.make_async_copy(
            ins[item], slot(item, z, y, x, core), own_sem.at[chunk, at]
        )

    plans = (
        ((y, x), first),
        ((y, x), second),
        ((y_one, x_one), second),
        ((y, x), sibling),
        ((y_one, x_one), sibling),
        ((y_two, x_two), sibling),
        ((1 - y, 1 - x), sibling),
    )

    def pair_copy(chunk, at, item, plan):
        (y_at, x_at), target = plans[plan]
        block = slot(item, slice(None), y_at, x_at, core)
        return pltpu.make_async_remote_copy(
            src_ref=block,
            dst_ref=block,
            send_sem=pair_send.at[chunk, at, plan],
            recv_sem=pair_recv.at[chunk, at, plan],
            device_id=target,
            device_id_type=MESH,
        )

    def each(chunk, action):
        for at, item in enumerate(chunks[chunk]):
            action(at, item)

    def line_start(chunk, turn):
        for upward in (True, False):

            @pl.when(sends(turn, upward))
            def _():
                each(chunk, lambda at, item: line_copy(chunk, at, item, turn, upward).start())

    def line_received(chunk, turn):
        for upward in (True, False):

            @pl.when(receives(turn, upward))
            def _():
                each(chunk, lambda at, item: line_copy(chunk, at, item, turn, upward).wait_recv())

    def line_sent(chunk, turn):
        for upward in (True, False):

            @pl.when(sends(turn, upward))
            def _():
                each(chunk, lambda at, item: line_copy(chunk, at, item, turn, upward).wait_send())

    def start(chunk, *plan_list):
        for plan in plan_list:
            each(chunk, lambda at, item: pair_copy(chunk, at, item, plan).start())

    def received(chunk, *plan_list):
        for plan in plan_list:
            each(chunk, lambda at, item: pair_copy(chunk, at, item, plan).wait_recv())

    def stage(chunk, number):
        if number == 0:
            each(chunk, lambda at, item: own_copy(chunk, at, item).wait())
            line_start(chunk, 1)
        elif number < depth:
            line_received(chunk, number)
            if number < depth - 1:
                line_start(chunk, number + 1)
            else:
                start(chunk, 0, 1, 3)
        elif number == depth:
            received(chunk, 0)
            start(chunk, 2, 4)
        elif number == depth + 1:
            received(chunk, 1)
            start(chunk, 5)
        elif number == depth + 2:
            received(chunk, 2)
            start(chunk, 6)
        else:
            received(chunk, 3, 4, 5, 6)
            for turn in range(1, depth):
                line_sent(chunk, turn)
            for plan in range(7):
                each(chunk, lambda at, item: pair_copy(chunk, at, item, plan).wait_send())

    for chunk in range(len(chunks)):
        each(chunk, lambda at, item: own_copy(chunk, at, item).start())
    order = sorted(
        (number + 2 * chunk, chunk, number)
        for chunk in range(len(chunks))
        for number in range(depth + 4)
    )
    for _, chunk, number in order:
        stage(chunk, number)


def gather(arrays, chunks, collective_id):
    dp, shard = lax.axis_size("dp"), lax.axis_size("shard")
    narrow = min(array.shape[-2] for array in arrays)
    if (dp, shard) != (8, 4) or narrow % 8:
        return [
            lax.all_gather(array, AXES, axis=array.ndim - 2, tiled=True) for array in arrays
        ]
    depth = dp // 2
    shapes = [((1,) + array.shape)[-3:] for array in arrays]
    sizes = (len(chunks), max(len(chunk) for chunk in chunks))
    dma = pltpu.SemaphoreType.DMA
    results = pl.pallas_call(
        functools.partial(gather_kernel, len(arrays), shapes, chunks, depth),
        out_shape=[
            jax.ShapeDtypeStruct(
                ((lead,) if lead > 1 else ()) + (depth, 2, 2, 2, rows, cols), BF16
            )
            for lead, rows, cols in shapes
        ],
        in_specs=[whole(pl.ANY)] * len(arrays),
        out_specs=[whole(pl.ANY)] * len(arrays),
        scratch_shapes=[
            dma(sizes + (depth - 1, 2)),
            dma(sizes + (depth - 1, 2)),
            dma(sizes + (7,)),
            dma(sizes + (7,)),
            dma(sizes),
        ],
        compiler_params=pltpu.CompilerParams(
            collective_id=collective_id, has_side_effects=True, vmem_limit_bytes=1 << 20
        ),
        name="gather_weights",
    )(*arrays)
    return [
        result.reshape(((lead,) if lead > 1 else ()) + (dp * shard * rows, cols))
        for result, (lead, rows, cols) in zip(results, shapes)
    ]


def lane_index(rows):
    return lax.broadcasted_iota(jnp.int32, (rows, LANES), 1)


def halves(lane, odd):
    own = (lane >= HEAD_DIM) if odd else (lane < HEAD_DIM)
    other = lane if odd else lane - HEAD_DIM
    return own, other


def three_parts(values):
    high = values.astype(BF16).astype(F32)
    rest = values - high
    middle = rest.astype(BF16).astype(F32)
    return high, middle, rest - middle


def with_terms(own, other, values, terms):
    result = jnp.zeros_like(values)
    for at, term in enumerate(terms):
        result = jnp.where(other == at, term, result)
    return jnp.where(own, values, result)


def attend_kernel(student, lengths, *refs):
    if student:
        clip, x_ref, w_ref, b_ref, q_ref, k_ref, v_ref, ctx_ref, low_ref = refs

        @pl.when(pl.program_id(0) == 0)
        def _():
            width = saturation * clip[0]
            low_ref[...] = (width * jnp.tanh(x_ref[...].astype(F32) / width)).astype(BF16)

        inputs = low_ref[...]
    else:
        x_ref, w_ref, b_ref, q_ref, k_ref, ctx_ref = refs
        inputs = x_ref[...]
    rows = inputs.shape[0]
    lane = lane_index(rows)
    position = lax.broadcasted_iota(jnp.int32, (rows, LANES), 0)
    hidden_key = jnp.where(position < lengths[0], 0.0, masked_score)
    queries, keys, values = (
        (dot(inputs, w_ref[slot], 1, 1) + b_ref[slot]).astype(BF16) for slot in range(3)
    )
    if not student:
        q_ref[...] = queries
        k_ref[...] = keys
    block = 512
    for pair in range(2):
        lanes = slice(pair * LANES, (pair + 1) * LANES)
        query, key, value = (
            array[:, lanes].astype(F32) for array in (queries, keys, values)
        )
        parts = []
        for odd in range(2):
            own, other = halves(lane, odd)
            place = slice((pair * 2 + odd) * LANES, (pair * 2 + odd + 1) * LANES)
            query_full = with_terms(own, other, query, (0.0, 0.0, 0.0, 1.0)).astype(BF16)
            key_full = with_terms(own, other, key, (1.0, 1.0, 1.0, hidden_key)).astype(BF16)
            value_full = with_terms(own, other, value, (1.0, 1.0, 1.0)).astype(BF16)
            if student:
                k_ref[:, place] = key_full
                v_ref[:, place] = value_full
            found = []
            for start in range(0, rows, block):
                take = slice(start, start + block)
                scores = dot(query_full[take], key_full, 1, 1)
                top = jnp.max(scores, axis=1, keepdims=True)
                expo = jnp.exp2((scores - top) * exponent).astype(BF16)
                mixed = dot(expo, value_full, 1, 0)
                at = 0 if odd else HEAD_DIM
                total = mixed[:, at : at + 1]
                found.append(mixed / total)
                if student:
                    logsum = top + jnp.log(total) / scaling
                    q_ref[take, place] = with_terms(
                        own[take],
                        other[take],
                        query[take],
                        tuple(-part for part in three_parts(logsum)) + (1.0,),
                    ).astype(BF16)
            parts.append(jnp.concatenate(found, axis=0))
        context = jnp.where(lane < HEAD_DIM, parts[0], parts[1])
        ctx_ref[:, lanes] = context.astype(ctx_ref.dtype)


def attend(student, own_length, clip_scales, inputs, weights, bias):
    rows = inputs.shape[0]
    wide = 4 * LANES
    narrow = 2 * LANES
    scalar = whole(pltpu.SMEM)
    in_specs = [scalar] + ([scalar] if student else [])
    in_specs += [
        fixed((rows, D)),
        pl.BlockSpec((3, narrow, D), lambda i: (0, i, 0)),
        columns((3, 1, narrow)),
    ]
    if student:
        out_shape = [jax.ShapeDtypeStruct((rows, 2 * D), BF16)] * 3 + [
            jax.ShapeDtypeStruct((rows, D), F32),
            jax.ShapeDtypeStruct((rows, D), BF16),
        ]
        out_specs = [columns((rows, wide))] * 3 + [columns((rows, narrow)), fixed((rows, D))]
        args = (own_length, clip_scales, inputs, weights, bias)
    else:
        out_shape = [jax.ShapeDtypeStruct((rows, D), BF16)] * 3
        out_specs = [columns((rows, narrow))] * 3
        args = (own_length, inputs, weights, bias)
    return pl.pallas_call(
        functools.partial(attend_kernel, student),
        grid=(D // narrow,),
        in_specs=in_specs,
        out_specs=out_specs,
        out_shape=out_shape,
        compiler_params=pltpu.CompilerParams(vmem_limit_bytes=vmem_bytes),
        name="student_attention" if student else "teacher_attention",
    )(*args)


def split_dot(left, right):
    high = right.astype(BF16)
    low = (right - high.astype(F32)).astype(BF16)
    return dot(left, high, 1, 0) + dot(left, low, 1, 0)


def attend_back_kernel(
    lengths, inverse_pairs, q_ref, k_ref, v_ref, ctx_ref, dctx_ref, tq_ref, tk_ref, grad_ref, sum_ref
):
    rows = ctx_ref.shape[0]
    lane = lane_index(rows)
    position = lax.broadcasted_iota(jnp.int32, (rows, LANES), 0)
    live = position < lengths[0]
    low_half = lane < HEAD_DIM
    grad_context = dctx_ref[...].astype(F32)
    product = grad_context * ctx_ref[...]
    block = 512
    pieces = []
    for odd in range(2):
        own, other = halves(lane, odd)
        place = slice(odd * LANES, (odd + 1) * LANES)
        query, key, value = q_ref[:, place], k_ref[:, place], v_ref[:, place]
        weighted = jnp.sum(jnp.where(own, product, 0.0), axis=1, keepdims=True)
        grad_full = with_terms(
            own, other, grad_context, tuple(-part for part in three_parts(weighted))
        ).astype(BF16)
        grad_query = None
        key_parts, value_parts = [], []
        for start in range(0, rows, block):
            take = slice(start, start + block)
            probs = jnp.exp2(dot(key[take], query, 1, 1) * exponent)
            grad_scores = (probs * dot(value[take], grad_full, 1, 1)).astype(BF16)
            value_parts.append(dot(probs.astype(BF16), grad_full, 1, 0))
            key_parts.append(dot(grad_scores, query, 1, 0))
            part = dot(grad_scores, key[take], 0, 0)
            grad_query = part if grad_query is None else grad_query + part
        pieces.append(
            (grad_query, jnp.concatenate(key_parts, axis=0), jnp.concatenate(value_parts, axis=0))
        )
    query_live, key_live = (
        jnp.where(live, jnp.where(low_half, ref[:, :LANES], ref[:, LANES:]), 0.0).astype(BF16)
        for ref in (q_ref, k_ref)
    )
    teach_query, teach_key = (
        jnp.where(live, ref[...], 0.0).astype(BF16) for ref in (tq_ref, tk_ref)
    )
    row = lax.broadcasted_iota(jnp.int32, (LANES, LANES), 0)
    col = lax.broadcasted_iota(jnp.int32, (LANES, LANES), 1)
    same = (row < HEAD_DIM) == (col < HEAD_DIM)

    def gram(left, right):
        return jnp.where(same, outer_rows(left, right), 0.0)

    key_key, teach_key_key = gram(key_live, key_live), gram(teach_key, key_live)
    query_query, teach_query_query = gram(query_live, query_live), gram(teach_query, query_live)
    squares = (
        query_query * key_key
        - 2.0 * teach_query_query * teach_key_key
        + gram(teach_query, teach_query) * gram(teach_key, teach_key)
    )
    squares = jnp.sum(squares.reshape(LANES // 8, 8, LANES), axis=0)

    @pl.when(pl.program_id(0) == 0)
    def _():
        sum_ref[...] = jnp.zeros_like(sum_ref)

    sum_ref[...] += squares * (scaling * scaling * inverse_pairs[0])
    factor = 2.0 * scaling * scaling * inverse_pairs[0]
    query_term = split_dot(
        jnp.concatenate([query_live, teach_query], axis=1),
        jnp.concatenate([key_key, -teach_key_key], axis=0),
    )
    key_term = split_dot(
        jnp.concatenate([key_live, teach_key], axis=1),
        jnp.concatenate([query_query, -teach_query_query], axis=0),
    )
    (even_q, even_k, even_v), (odd_q, odd_k, odd_v) = pieces
    grad_ref[0] = (jnp.where(low_half, even_q, odd_q) * scaling + factor * query_term).astype(BF16)
    grad_ref[1] = (jnp.where(low_half, even_k, odd_k) * scaling + factor * key_term).astype(BF16)
    grad_ref[2] = jnp.where(low_half, even_v, odd_v).astype(BF16)


def attend_back(own_length, inverse_pairs, query, key, value, context, grad_context, tq, tk):
    rows = context.shape[0]
    scalar = whole(pltpu.SMEM)
    return pl.pallas_call(
        attend_back_kernel,
        grid=(D // LANES,),
        in_specs=[scalar, scalar]
        + [columns((rows, 2 * LANES))] * 3
        + [columns((rows, LANES))] * 4,
        out_specs=[columns((3, rows, LANES)), fixed((8, LANES))],
        out_shape=[
            jax.ShapeDtypeStruct((3, rows, D), BF16),
            jax.ShapeDtypeStruct((8, LANES), F32),
        ],
        compiler_params=pltpu.CompilerParams(vmem_limit_bytes=vmem_bytes),
        name="attention_backward",
    )(own_length, inverse_pairs, query, key, value, context, grad_context, tq, tk)


def gelu_parts(upper):
    cumulative = 0.5 * (1.0 + lax.erf(upper * (1.0 / math.sqrt(2.0))))
    return cumulative, upper * cumulative


ff_part = 1024


def teacher_kernel(tok_ref, ctx_ref, wo_ref, w1_ref, w2_ref, vec_ref, ub_ref, out_ref):
    vec = vec_ref[...]
    normed, _ = normalize(
        tok_ref[...].astype(F32) + dot(ctx_ref[...], wo_ref[...], 1, 1) + vec[3:4]
    )
    hidden = normed * vec[5:6] + vec[7:8]
    low = hidden.astype(BF16)
    lower = None
    for start in range(0, w1_ref.shape[0], ff_part):
        take = slice(start, start + ff_part)
        _, bent = gelu_parts(dot(low, w1_ref[take], 1, 1) + ub_ref[:, take])
        part = dot(bent.astype(BF16), w2_ref[:, take], 1, 1)
        lower = part if lower is None else lower + part
    final, _ = normalize(hidden + lower + vec[4:5])
    out_ref[...] = final * vec[6:7] + vec[8:9]


def teacher_tail(tokens, context, wo, w1, w2, vectors, up_bias):
    rows, wide = tokens.shape[0], w1.shape[0]
    block = 256
    return pl.pallas_call(
        teacher_kernel,
        grid=(rows // block,),
        in_specs=[
            row_blocks((block, D)),
            row_blocks((block, D)),
            fixed((D, D)),
            fixed((wide, D)),
            fixed((D, wide)),
            fixed(vectors.shape),
            fixed((1, wide)),
        ],
        out_specs=row_blocks((block, D)),
        out_shape=jax.ShapeDtypeStruct((rows, D), F32),
        compiler_params=pltpu.CompilerParams(vmem_limit_bytes=vmem_bytes),
        name="teacher_feed_forward",
    )(tokens, context, wo, w1, w2, vectors, up_bias)


def student_kernel(
    lengths,
    clip,
    tok_ref,
    cot_ref,
    teach_ref,
    ctx_ref,
    wo_ref,
    w1_ref,
    w2_ref,
    vec_ref,
    ub_ref,
    out_ref,
    dctx_ref,
    dao_ref,
    cb_ref,
    du_ref,
    hb_ref,
    df_ref,
    fb_ref,
    res_ref,
    sums_ref,
    upsum_ref,
    slope_ref,
):
    step = pl.program_id(0)
    vec = vec_ref[...]
    wide = w1_ref.shape[0]
    ctx_width, hid_width, act_width = (saturation * clip[at] for at in (1, 2, 3))
    ctx_bent = jnp.tanh(ctx_ref[...] / ctx_width)
    ctx_low = (ctx_width * ctx_bent).astype(BF16)
    cb_ref[...] = ctx_low
    first, first_inverse = normalize(
        tok_ref[...].astype(F32) + dot(ctx_low, wo_ref[...], 1, 1) + vec[3:4]
    )
    hidden = first * vec[5:6] + vec[7:8]
    hid_bent = jnp.tanh(hidden / hid_width)
    hid_low = (hid_width * hid_bent).astype(BF16)
    hb_ref[...] = hid_low
    lower = None
    for start in range(0, wide, ff_part):
        take = slice(start, start + ff_part)
        upper = dot(hid_low, w1_ref[take], 1, 1) + ub_ref[:, take]
        cumulative, bent = gelu_parts(upper)
        act = jnp.tanh(bent / act_width)
        density = jnp.exp(-0.5 * upper * upper) * (1.0 / math.sqrt(2.0 * math.pi))
        slope_ref[:, take] = (1.0 - act * act) * (cumulative + upper * density)
        act_low = (act_width * act).astype(BF16)
        fb_ref[:, take] = act_low
        part = dot(act_low, w2_ref[:, take], 1, 1)
        lower = part if lower is None else lower + part
    second, second_inverse = normalize(hidden + lower + vec[4:5])
    result = second * vec[6:7] + vec[8:9]
    out_ref[...] = result.astype(BF16)
    rows = result.shape[0]
    position = lax.broadcasted_iota(jnp.int32, (rows, D), 0) + step * rows
    gap = jnp.where(position < lengths[0], result - teach_ref[...], 0.0)
    grad_out = cot_ref[...].astype(F32) + gap * (2.0 * hidden_weight)
    grad_second = norm_back(grad_out * vec[6:7], second, second_inverse)
    grad_lower = grad_second.astype(BF16)
    df_ref[...] = grad_lower
    grad_hidden = None
    up_sums = []
    for start in range(0, wide, ff_part):
        take = slice(start, start + ff_part)
        grad_upper = (dot(grad_lower, w2_ref[:, take], 1, 0) * slope_ref[:, take]).astype(BF16)
        du_ref[:, take] = grad_upper
        up_sums.append(jnp.sum(grad_upper.astype(F32), axis=0, keepdims=True))
        part = dot(grad_upper, w1_ref[take], 1, 0)
        grad_hidden = part if grad_hidden is None else grad_hidden + part
    grad_hidden = grad_second + grad_hidden * (1.0 - hid_bent * hid_bent)
    grad_first = norm_back(grad_hidden * vec[5:6], first, first_inverse)
    res_ref[...] = grad_first
    grad_attn = grad_first.astype(BF16)
    dao_ref[...] = grad_attn
    dctx_ref[...] = (
        dot(grad_attn, wo_ref[...], 1, 0) * (1.0 - ctx_bent * ctx_bent)
    ).astype(BF16)

    @pl.when(step == 0)
    def _():
        sums_ref[...] = jnp.zeros_like(sums_ref)
        upsum_ref[...] = jnp.zeros_like(upsum_ref)

    for at, term in enumerate(
        (
            grad_attn.astype(F32),
            grad_lower.astype(F32),
            grad_hidden * first,
            grad_out * second,
            grad_hidden,
            grad_out,
            gap * gap,
        )
    ):
        sums_ref[at : at + 1] += jnp.sum(term, axis=0, keepdims=True)
    upsum_ref[...] += jnp.concatenate(up_sums, axis=1)


def student_middle(
    own_length, clip_scales, tokens, cotangent, teach_out, context, wo, w1, w2, vectors, up_bias
):
    rows, wide = tokens.shape[0], w1.shape[0]
    block = 256
    scalar = whole(pltpu.SMEM)
    narrow_spec, wide_spec = row_blocks((block, D)), row_blocks((block, wide))
    narrow, broad = jax.ShapeDtypeStruct((rows, D), BF16), jax.ShapeDtypeStruct((rows, wide), BF16)
    return pl.pallas_call(
        student_kernel,
        grid=(rows // block,),
        in_specs=[scalar, scalar]
        + [narrow_spec] * 4
        + [
            fixed((D, D)),
            fixed((wide, D)),
            fixed((D, wide)),
            fixed(vectors.shape),
            fixed((1, wide)),
        ],
        out_specs=[narrow_spec] * 4
        + [wide_spec, narrow_spec, narrow_spec, wide_spec, narrow_spec, fixed((8, D)), fixed((1, wide))],
        out_shape=[narrow] * 4
        + [
            broad,
            narrow,
            narrow,
            broad,
            jax.ShapeDtypeStruct((rows, D), F32),
            jax.ShapeDtypeStruct((8, D), F32),
            jax.ShapeDtypeStruct((1, wide), F32),
        ],
        scratch_shapes=[pltpu.VMEM((block, wide), F32)],
        compiler_params=pltpu.CompilerParams(vmem_limit_bytes=vmem_bytes),
        name="student_feed_forward",
    )(own_length, clip_scales, tokens, cotangent, teach_out, context, wo, w1, w2, vectors, up_bias)


def input_kernel(clip, grad_ref, w_ref, low_ref, tok_ref, res_ref, out_ref, dw_ref, sum_ref, acc_ref):
    slot = pl.program_id(0)
    grad = grad_ref[0]
    part = dot(grad, w_ref[0], 1, 0)
    dw_ref[0] = outer_rows(grad, low_ref[...]).astype(dw_ref.dtype)
    sum_ref[0] = jnp.sum(grad.astype(F32), axis=0, keepdims=True)

    @pl.when(slot == 0)
    def _():
        acc_ref[...] = part

    @pl.when(slot > 0)
    def _():
        acc_ref[...] += part

    @pl.when(slot == pl.num_programs(0) - 1)
    def _():
        bent = jnp.tanh(tok_ref[...].astype(F32) / (saturation * clip[0]))
        out_ref[...] = (res_ref[...] + acc_ref[...] * (1.0 - bent * bent)).astype(BF16)


def input_grads(clip_scales, grads, weights, low, tokens, residual):
    rows = tokens.shape[0]
    slotted = lambda *shape: pl.BlockSpec((1,) + shape, lambda i: (i, 0, 0))
    return pl.pallas_call(
        input_kernel,
        grid=(3,),
        in_specs=[
            whole(pltpu.SMEM),
            slotted(rows, D),
            slotted(D, D),
            fixed((rows, D)),
            fixed((rows, D)),
            fixed((rows, D)),
        ],
        out_specs=[fixed((rows, D)), slotted(D, D), slotted(1, D)],
        out_shape=[
            jax.ShapeDtypeStruct((rows, D), BF16),
            jax.ShapeDtypeStruct((3, D, D), F32),
            jax.ShapeDtypeStruct((3, 1, D), F32),
        ],
        scratch_shapes=[pltpu.VMEM((rows, D), F32)],
        compiler_params=pltpu.CompilerParams(vmem_limit_bytes=vmem_bytes),
        name="input_gradient",
    )(clip_scales, grads, weights, low, tokens, residual)


def on_device(
    tokens,
    teacher_tokens,
    cotangent,
    lengths,
    clip_scales,
    attn_latent,
    up_latent,
    down_latent,
    biases,
    up_bias,
    norm_gains,
    norm_shifts,
    teacher_attn,
    teacher_up,
    teacher_down,
    teacher_biases,
    teacher_up_bias,
    teacher_gains,
    teacher_shifts,
):
    count = lax.axis_size(AXES)
    narrow, wide = biases.shape[1], up_bias.shape[0]
    own_length = lax.dynamic_slice_in_dim(lengths, lax.axis_index(AXES), 1)
    live_float = lengths.astype(F32)
    token_norm = jnp.sum(live_float)
    pair_norm = HEADS * jnp.sum(live_float * live_float)
    inverse_pairs = (1.0 / pair_norm).reshape(1)
    vectors = jnp.concatenate(
        [teacher_biases, teacher_gains, teacher_shifts, biases, norm_gains, norm_shifts], axis=0
    )
    small = jnp.concatenate([vectors.reshape(-1), teacher_up_bias, up_bias])
    small = jnp.pad(small, (0, 8 * D - small.shape[0])).reshape(8, D)
    (
        small_all,
        teach_qkv,
        attn_w,
        teach_wo,
        teach_up,
        teach_down,
        up_w,
        down_w,
    ) = gather(
        [
            small,
            teacher_attn[:3],
            binarize(attn_latent),
            teacher_attn[3],
            teacher_up,
            teacher_down,
            binarize(up_latent),
            binarize(down_latent),
        ],
        ((0, 1), (2, 3), (4,), (5,), (6,), (7,)),
        0,
    )
    small_all = small_all.reshape(count, -1)
    lines = vectors.shape[0]
    vec = (
        small_all[:, : lines * narrow]
        .reshape(count, lines, narrow)
        .transpose(1, 0, 2)
        .reshape(lines, D)
        .astype(F32)
    )
    teach_vec, student_vec = vec[: lines // 2], vec[lines // 2 :]
    at = lines * narrow
    teach_up_bias = small_all[:, at : at + wide].reshape(1, -1).astype(F32)
    student_up_bias = small_all[:, at + wide : at + 2 * wide].reshape(1, -1).astype(F32)
    tq, tk, teach_context = attend(
        False, own_length, clip_scales, teacher_tokens, teach_qkv, teach_vec[:3].reshape(3, 1, D)
    )
    query, key, value, context, x_low = attend(
        True, own_length, clip_scales, tokens, attn_w[:3], student_vec[:3].reshape(3, 1, D)
    )
    teach_out = teacher_tail(
        teacher_tokens, teach_context, teach_wo, teach_up, teach_down, teach_vec, teach_up_bias
    )
    (
        result,
        grad_context,
        grad_attn,
        ctx_low,
        grad_upper,
        hid_low,
        grad_lower,
        act_low,
        residual,
        sums,
        up_sums,
    ) = student_middle(
        own_length,
        clip_scales,
        tokens,
        cotangent,
        teach_out,
        context,
        attn_w[3],
        up_w,
        down_w,
        student_vec,
        student_up_bias,
    )
    down_weight_grad = outer_rows(grad_lower, act_low)
    up_weight_grad = outer_rows(grad_upper, hid_low)
    out_weight_grad = outer_rows(grad_attn, ctx_low)
    grads, squares = attend_back(
        own_length, inverse_pairs, query, key, value, context, grad_context, tq, tk
    )
    input_grad, qkv_weight_grad, qkv_sums = input_grads(
        clip_scales, grads, attn_w[:3], x_low, tokens, residual
    )
    local_loss = jnp.sum(sums[6]) / (D * token_norm) + jnp.sum(squares)
    attn_weight_grad = jnp.concatenate([qkv_weight_grad, out_weight_grad[None]], axis=0)
    bias_terms = jnp.concatenate([qkv_sums[:, 0], sums[:2]], axis=0)
    lines = jnp.concatenate([bias_terms, sums[2:6]], axis=0)
    own_sums = jnp.concatenate(
        [
            lines.reshape(9, count, narrow).transpose(1, 0, 2).reshape(count, -1),
            up_sums.reshape(count, wide),
            jnp.broadcast_to(local_loss, (count, 1)),
        ],
        axis=1,
    )
    own_sums = jnp.pad(own_sums, ((0, 0), (0, D - own_sums.shape[1])))
    attn_total = lax.psum_scatter(attn_weight_grad, AXES, scatter_dimension=1, tiled=True)
    up_total = lax.psum_scatter(up_weight_grad, AXES, scatter_dimension=0, tiled=True)
    down_total = lax.psum_scatter(down_weight_grad, AXES, scatter_dimension=0, tiled=True)
    sum_total = lax.psum_scatter(own_sums, AXES, scatter_dimension=0, tiled=True)[0]
    line_total = sum_total[: 9 * narrow].reshape(9, narrow)
    up_bias_total = sum_total[9 * narrow : 9 * narrow + wide]
    loss = sum_total[9 * narrow + wide]
    return (
        result,
        loss,
        input_grad,
        latent_grad(attn_latent, attn_total),
        latent_grad(up_latent, up_total),
        latent_grad(down_latent, down_total),
        line_total[:5],
        up_bias_total,
        line_total[5:7],
        line_total[7:9],
    )
def solution(mesh):
    in_specs = (
        P(("dp", "shard"), None),
        P(("dp", "shard"), None),
        P(("dp", "shard"), None),
        P(),
        P(),
        P(None, ("dp", "shard"), None),
        P(("dp", "shard"), None),
        P(("dp", "shard"), None),
        P(None, ("dp", "shard")),
        P(("dp", "shard")),
        P(None, ("dp", "shard")),
        P(None, ("dp", "shard")),
        P(None, ("dp", "shard"), None),
        P(("dp", "shard"), None),
        P(("dp", "shard"), None),
        P(None, ("dp", "shard")),
        P(("dp", "shard")),
        P(None, ("dp", "shard")),
        P(None, ("dp", "shard")),
    )
    out_specs = (
        P(("dp", "shard"), None),
        P(),
        P(("dp", "shard"), None),
        P(None, ("dp", "shard"), None),
        P(("dp", "shard"), None),
        P(("dp", "shard"), None),
        P(None, ("dp", "shard")),
        P(("dp", "shard")),
        P(None, ("dp", "shard")),
        P(None, ("dp", "shard")),
    )
    return jax.shard_map(
        on_device, mesh=mesh, in_specs=in_specs, out_specs=out_specs, check_vma=False
    )
```

```python
import functools
import math

import jax
import jax.numpy as jnp
from jax import lax
from jax.experimental import pallas as pl
from jax.experimental.pallas import tpu as pltpu
from jax.sharding import PartitionSpec as P

D = 768
HEADS = 12
HEAD_DIM = 64
SEQ_LEN = 1024
AXES = ("dp", "shard")
MESH = pl.DeviceIdType.MESH
F32 = jnp.float32
BF16 = jnp.bfloat16

epsilon = 1e-05
masked_score = -1e30
hidden_weight = 0.25
saturation = 7.5
LANES = 128
log2e = math.log2(math.e)
scaling = HEAD_DIM ** (-0.5)
exponent = scaling * log2e
vmem_bytes = 60 * 1024 * 1024


def dot(left, right, left_dim, right_dim):
    return lax.dot_general(
        left, right, (((left_dim,), (right_dim,)), ((), ())), preferred_element_type=F32
    )


def outer_rows(left, right):
    return dot(left, right, 0, 0)


def binarize(latent):
    scale = jnp.mean(jnp.abs(latent), axis=-1, keepdims=True)
    return (scale * jnp.sign(latent)).astype(BF16)


def surrogate(latent):
    return jnp.mean(jnp.abs(latent), axis=-1, keepdims=True) * latent


def latent_grad(latent, grad):
    _, pull = jax.vjp(surrogate, latent)
    return pull(grad)[0]


def normalize(values):
    center = values - jnp.mean(values, axis=-1, keepdims=True)
    inverse = lax.rsqrt(jnp.mean(center * center, axis=-1, keepdims=True) + epsilon)
    return (center * inverse, inverse)


def norm_back(grad_norm, normed, inverse):
    return inverse * (
        grad_norm
        - jnp.mean(grad_norm, axis=-1, keepdims=True)
        - normed * jnp.mean(grad_norm * normed, axis=-1, keepdims=True)
    )


def whole(memory=pltpu.VMEM):
    return pl.BlockSpec(memory_space=memory)


def fixed(shape):
    return pl.BlockSpec(shape, lambda *_: (0,) * len(shape), pipeline_mode=pl.Buffered(1))


def columns(shape):
    return pl.BlockSpec(shape, lambda i: (0,) * (len(shape) - 1) + (i,))


def row_blocks(shape):
    return pl.BlockSpec(shape, lambda i: (i,) + (0,) * (len(shape) - 1))


class Place:
    def __init__(self, depth):
        self.depth = depth
        dp, shard = lax.axis_index("dp"), lax.axis_index("shard")
        z, y = dp // 2, lax.rem(dp, 2)
        x, core = shard // 2, lax.rem(shard, 2)
        self.z, self.y, self.x, self.core = z, y, x, core

        def device(z_at, y_at, x_at, core_at):
            return (z_at * 2 + y_at, x_at * 2 + core_at)

        self.above = device(jnp.minimum(z + 1, depth - 1), y, x, core)
        self.below = device(jnp.maximum(z - 1, 0), y, x, core)
        one = (lax.rem(y + 1 - core, 2), lax.rem(x + core, 2))
        two = (lax.rem(y + core, 2), lax.rem(x + 1 - core, 2))
        self.pieces = ((y, x), one, two, (1 - y, 1 - x))
        self.first, self.second = device(z, *one, core), device(z, *two, core)
        self.sibling = device(z, y, x, 1 - core)

    def barrier(self):
        semaphore = pltpu.get_barrier_semaphore()
        for partner in (self.first, self.second, self.sibling):
            pl.semaphore_signal(semaphore, inc=1, device_id=partner, device_id_type=MESH)

        @pl.when(self.z < self.depth - 1)
        def _():
            pl.semaphore_signal(semaphore, inc=1, device_id=self.above, device_id_type=MESH)

        @pl.when(self.z > 0)
        def _():
            pl.semaphore_signal(semaphore, inc=1, device_id=self.below, device_id_type=MESH)

        pl.semaphore_wait(
            semaphore, 3 + jnp.minimum(self.z, 1) + jnp.minimum(self.depth - 1 - self.z, 1)
        )


def remote(source, target, send_sem, recv_sem, device):
    return pltpu.make_async_remote_copy(
        src_ref=source,
        dst_ref=target,
        send_sem=send_sem,
        recv_sem=recv_sem,
        device_id=device,
        device_id_type=MESH,
    )


def tiled_over(mesh_sizes, rows):
    return mesh_sizes == (8, 4) and rows % 8 == 0


def in_order(counts, apart):
    return [
        (chunk, number)
        for _, chunk, number in sorted(
            (number + apart * chunk, chunk, number)
            for chunk, count in enumerate(counts)
            for number in range(count)
        )
    ]


def gather_scratch(chunks, depth):
    dma = pltpu.SemaphoreType.DMA
    sizes = (len(chunks), max(len(chunk) for chunk in chunks))
    return [
        dma(sizes + (depth - 1, 2)),
        dma(sizes + (depth - 1, 2)),
        dma(sizes + (7,)),
        dma(sizes + (7,)),
        dma(sizes),
    ]


def gather_stages(place, ins, outs, leads, chunks, sems, apart=2):
    line_send, line_recv, pair_send, pair_recv, own_sem = sems
    depth, z, y, x, core = place.depth, place.z, place.y, place.x, place.core

    def slot(item, *index):
        return outs[item].at[((slice(None),) if leads[item] > 1 else ()) + index]

    def line_copy(chunk, at, item, turn, upward):
        if upward:
            owner, target = jnp.maximum(z - (turn - 1), 0), place.above
        else:
            owner, target = jnp.minimum(z + (turn - 1), depth - 1), place.below
        block = slot(item, owner, y, x, core)
        where = (chunk, at, turn - 1, int(upward))
        return remote(block, block, line_send.at[where], line_recv.at[where], target)

    def sends(turn, upward):
        if upward:
            return (z - (turn - 1) >= 0) & (z < depth - 1)
        return (z + (turn - 1) <= depth - 1) & (z > 0)

    def receives(turn, upward):
        return (z - turn >= 0) if upward else (z + turn <= depth - 1)

    def own_copy(chunk, at, item):
        return pltpu.make_async_copy(
            ins[item], slot(item, z, y, x, core), own_sem.at[chunk, at]
        )

    plans = (
        (0, place.first),
        (0, place.second),
        (1, place.second),
        (0, place.sibling),
        (1, place.sibling),
        (2, place.sibling),
        (3, place.sibling),
    )

    def pair_copy(chunk, at, item, plan):
        piece, target = plans[plan]
        block = slot(item, slice(None), *place.pieces[piece], core)
        where = (chunk, at, plan)
        return remote(block, block, pair_send.at[where], pair_recv.at[where], target)

    def each(chunk, action):
        for at, item in enumerate(chunks[chunk]):
            action(at, item)

    def line_start(chunk, turn):
        for upward in (True, False):

            @pl.when(sends(turn, upward))
            def _():
                each(chunk, lambda at, item: line_copy(chunk, at, item, turn, upward).start())

    def line_received(chunk, turn):
        for upward in (True, False):

            @pl.when(receives(turn, upward))
            def _():
                each(chunk, lambda at, item: line_copy(chunk, at, item, turn, upward).wait_recv())

    def line_sent(chunk, turn):
        for upward in (True, False):

            @pl.when(sends(turn, upward))
            def _():
                each(chunk, lambda at, item: line_copy(chunk, at, item, turn, upward).wait_send())

    def start(chunk, *plan_list):
        for plan in plan_list:
            each(chunk, lambda at, item: pair_copy(chunk, at, item, plan).start())

    def received(chunk, *plan_list):
        for plan in plan_list:
            each(chunk, lambda at, item: pair_copy(chunk, at, item, plan).wait_recv())

    def stage(chunk, number):
        if number == 0:
            each(chunk, lambda at, item: own_copy(chunk, at, item).wait())
            line_start(chunk, 1)
        elif number < depth:
            line_received(chunk, number)
            if number < depth - 1:
                line_start(chunk, number + 1)
            else:
                start(chunk, 0, 1, 3)
        elif number == depth:
            received(chunk, 0)
            start(chunk, 2, 4)
        elif number == depth + 1:
            received(chunk, 1)
            start(chunk, 5)
        elif number == depth + 2:
            received(chunk, 2)
            start(chunk, 6)
        else:
            received(chunk, 3, 4, 5, 6)
            for turn in range(1, depth):
                line_sent(chunk, turn)
            for plan in range(7):
                each(chunk, lambda at, item: pair_copy(chunk, at, item, plan).wait_send())

    def begin():
        for chunk in range(len(chunks)):
            each(chunk, lambda at, item: own_copy(chunk, at, item).start())

    return [begin] + [
        functools.partial(stage, chunk, number)
        for chunk, number in in_order([depth + 4] * len(chunks), apart)
    ]


def gather_shapes(arrays, depth):
    shapes = [((1,) + array.shape)[-3:] for array in arrays]
    leads = [shape[0] for shape in shapes]
    results = [
        jax.ShapeDtypeStruct(((lead,) if lead > 1 else ()) + (depth, 2, 2, 2, rows, cols), BF16)
        for lead, rows, cols in shapes
    ]
    return leads, results


def gathered(results):
    return [
        result.reshape(result.shape[:-6] + (-1, result.shape[-1])) for result in results
    ]


def gather_kernel(leads, chunks, depth, *refs):
    count = len(leads)
    place = Place(depth)
    place.barrier()
    for stage in gather_stages(
        place, refs[:count], refs[count : 2 * count], leads, chunks, refs[2 * count :]
    ):
        stage()


def gather(arrays, chunks, collective_id):
    dp, shard = lax.axis_size("dp"), lax.axis_size("shard")
    if not tiled_over((dp, shard), min(array.shape[-2] for array in arrays)):
        return [
            lax.all_gather(array, AXES, axis=array.ndim - 2, tiled=True) for array in arrays
        ]
    depth = dp // 2
    leads, results = gather_shapes(arrays, depth)
    results = pl.pallas_call(
        functools.partial(gather_kernel, leads, chunks, depth),
        out_shape=results,
        in_specs=[whole(pl.ANY)] * len(arrays),
        out_specs=[whole(pl.ANY)] * len(arrays),
        scratch_shapes=gather_scratch(chunks, depth),
        compiler_params=pltpu.CompilerParams(
            collective_id=collective_id, has_side_effects=True, vmem_limit_bytes=1 << 20
        ),
        name="gather_weights",
    )(*arrays)
    return gathered(results)


def scatter_scratch(shapes, dtypes, depth):
    dma = pltpu.SemaphoreType.DMA
    scratch = []
    for shape, dtype in zip(shapes, dtypes):
        lead, rows, cols = shape
        block = (depth, lead, rows, cols)
        scratch += [
            pltpu.VMEM((4,) + block, dtype),
            pltpu.VMEM((4,) + block, dtype),
            pltpu.VMEM((3,) + block, dtype),
            pltpu.VMEM((2,) + block, dtype),
        ]
    count = len(shapes)
    return scratch + [
        dma((count, 4)),
        dma((count, 7)),
        dma((count, 7)),
        dma((count, depth, 2)),
        dma((count, depth, 2)),
    ]


def scatter_stages(place, ins, outs, scratch, count, apart=2):
    depth, z, core = place.depth, place.z, place.core
    own_sem, pair_send, pair_recv, line_send, line_recv = scratch[4 * count :]

    def buffers(item):
        return scratch[4 * item : 4 * item + 4]

    def source(item, piece, lead, side):
        index = (slice(None),) + place.pieces[piece] + (side,)
        ref = ins[item]
        return ref.at[((lead,) if ref.shape[:-6] else ()) + index]

    def leads(item):
        return range(buffers(item)[0].shape[2])

    def own_copy(item, piece, lead):
        held = buffers(item)[0]
        return pltpu.make_async_copy(
            source(item, piece, lead, core), held.at[piece, :, lead], own_sem.at[item, piece]
        )

    names = (0, 2, 1, 3)

    def core_copy(item, piece, lead):
        arrived = buffers(item)[1]
        name = names[piece]
        return remote(
            source(item, piece, lead, 1 - core),
            arrived.at[name, :, lead],
            pair_send.at[item, piece],
            pair_recv.at[item, name],
            place.sibling,
        )

    def core_wait(item, piece):
        arrived = buffers(item)[1]
        block = arrived.at[piece]
        remote(
            block, block, pair_send.at[item, piece], pair_recv.at[item, piece], place.sibling
        ).wait_recv()

    def chip_copy(item, plan):
        held, _, arrived, _ = buffers(item)
        piece, target = ((2, place.second), (3, place.second), (1, place.first))[plan]
        return remote(
            held.at[piece],
            arrived.at[plan],
            pair_send.at[item, 4 + plan],
            pair_recv.at[item, 4 + plan],
            target,
        )

    def line_copy(item, owner, upward, fresh):
        held, _, _, arrived = buffers(item)
        block = arrived.at[int(upward), owner]
        where = (item, owner, int(upward))
        return remote(
            held.at[0, owner] if fresh else block,
            block,
            line_send.at[where],
            line_recv.at[where],
            place.above if upward else place.below,
        )

    def add(target, *others):
        def one(at):
            total = target[at].astype(F32)
            for other in others:
                total = total + other[at].astype(F32)
            target[at] = total.astype(target.dtype)

        for first in range(target.shape[0]):
            for second in range(target.shape[1]):
                one((first, second))

    def add_block(target, other):
        for lead in range(target.shape[0]):
            target[lead] = (target[lead].astype(F32) + other[lead].astype(F32)).astype(
                target.dtype
            )

    def merge(item, piece):
        held, arrived, _, _ = buffers(item)
        block = held.at[piece]
        pltpu.make_async_copy(block, block, own_sem.at[item, piece]).wait()
        core_wait(item, piece)
        add(block, arrived.at[piece])

    def line_turn(item, turn, upward):
        held, _, _, arrived = buffers(item)
        at = turn if upward else depth - 1 - turn
        beyond = range(at + 1, depth) if upward else range(at)

        @pl.when(z == at)
        def _():
            for owner in sorted(beyond, key=lambda owner: -abs(owner - at)):
                if turn:
                    line_copy(item, owner, upward, False).wait_recv()
                    add_block(arrived.at[int(upward), owner], held.at[0, owner])
                line_copy(item, owner, upward, not turn).start()
            if turn:
                line_copy(item, at, upward, False).wait_recv()

    def stage(item, number):
        held, _, arrived, line = buffers(item)
        if number == 0:
            for piece in (3, 1, 2, 0):
                for lead in leads(item):
                    core_copy(item, piece, lead).start()
            for piece in (2, 3, 1, 0):
                for lead in leads(item):
                    own_copy(item, piece, lead).start()
        elif number == 1:
            for piece, plan in ((3, 1), (2, 0)):
                merge(item, piece)
                chip_copy(item, plan).start()
        elif number == 2:
            merge(item, 1)
            merge(item, 0)
        elif number == 3:
            chip_copy(item, 1).wait_recv()
            add(held.at[1], arrived.at[1])
            chip_copy(item, 2).start()
        elif number == 4:
            chip_copy(item, 0).wait_recv()
            chip_copy(item, 2).wait_recv()
            add(held.at[0], arrived.at[0], arrived.at[2])
            for upward in (True, False):
                line_turn(item, 0, upward)
        elif number < 4 + depth:
            for upward in (True, False):
                line_turn(item, number - 4, upward)
        else:
            for lead in leads(item):
                outs[item][lead] = held[0, z, lead].astype(F32)

            for upward, other in ((1, z > 0), (0, z < depth - 1)):

                @pl.when(other)
                def _():
                    for lead in leads(item):
                        outs[item][lead] += line[upward, z, lead].astype(F32)

            for piece in range(4):
                block = buffers(item)[1].at[piece]
                remote(
                    block, block, pair_send.at[item, piece], pair_recv.at[item, piece], place.sibling
                ).wait_send()
            for plan in range(3):
                chip_copy(item, plan).wait_send()
            for upward in (True, False):
                for owner in range(depth):

                    @pl.when((z < owner) if upward else (z > owner))
                    def _():
                        line_copy(item, owner, upward, False).wait_send()

    return [
        functools.partial(stage, item, number)
        for item, number in in_order([5 + depth] * count, apart)
    ]


def scatter_kernel(count, depth, *refs):
    place = Place(depth)
    place.barrier()
    for stage in scatter_stages(
        place, refs[:count], refs[count : 2 * count], refs[2 * count :], count
    ):
        stage()


def split_rows(array, depth):
    return array.reshape(array.shape[:-2] + (depth, 2, 2, 2, -1, array.shape[-1]))


def scatter(arrays, collective_id):
    dp, shard = lax.axis_size("dp"), lax.axis_size("shard")
    owned = min(array.shape[-2] for array in arrays) // (dp * shard)
    if not tiled_over((dp, shard), owned):
        return [
            lax.psum_scatter(
                array.astype(F32), AXES, scatter_dimension=array.ndim - 2, tiled=True
            )
            for array in arrays
        ]
    depth = dp // 2
    arrays = [split_rows(array, depth) for array in arrays]
    shapes = [(math.prod(array.shape[:-6]),) + array.shape[-2:] for array in arrays]
    results = pl.pallas_call(
        functools.partial(scatter_kernel, len(arrays), depth),
        out_shape=[jax.ShapeDtypeStruct(shape, F32) for shape in shapes],
        in_specs=[whole(pl.ANY)] * len(arrays),
        out_specs=[whole()] * len(arrays),
        scratch_shapes=scatter_scratch(shapes, [array.dtype for array in arrays], depth),
        compiler_params=pltpu.CompilerParams(
            collective_id=collective_id, has_side_effects=True, vmem_limit_bytes=vmem_bytes
        ),
        name="scatter_gradients",
    )(*arrays)
    return [
        result.reshape(array.shape[:-6] + result.shape[1:])
        for result, array in zip(results, arrays)
    ]


def lane_index(rows):
    return lax.broadcasted_iota(jnp.int32, (rows, LANES), 1)


def halves(lane, odd):
    own = (lane >= HEAD_DIM) if odd else (lane < HEAD_DIM)
    other = lane if odd else lane - HEAD_DIM
    return own, other


def three_parts(values):
    high = values.astype(BF16).astype(F32)
    rest = values - high
    middle = rest.astype(BF16).astype(F32)
    return high, middle, rest - middle


def with_terms(own, other, values, terms):
    result = jnp.zeros_like(values)
    for at, term in enumerate(terms):
        result = jnp.where(other == at, term, result)
    return jnp.where(own, values, result)


def attend_kernel(student, lengths, *refs):
    if student:
        clip, x_ref, w_ref, b_ref, q_ref, k_ref, v_ref, ctx_ref, low_ref = refs

        @pl.when(pl.program_id(0) == 0)
        def _():
            width = saturation * clip[0]
            low_ref[...] = (width * jnp.tanh(x_ref[...].astype(F32) / width)).astype(BF16)

        inputs = low_ref[...]
    else:
        x_ref, w_ref, b_ref, q_ref, k_ref, ctx_ref = refs
        inputs = x_ref[...]
    rows = inputs.shape[0]
    lane = lane_index(rows)
    position = lax.broadcasted_iota(jnp.int32, (rows, LANES), 0)
    hidden_key = jnp.where(position < lengths[0], 0.0, masked_score)
    queries, keys, values = (
        (dot(inputs, w_ref[slot], 1, 1) + b_ref[slot]).astype(BF16) for slot in range(3)
    )
    if not student:
        q_ref[...] = queries
        k_ref[...] = keys
    block = 512
    for pair in range(2):
        lanes = slice(pair * LANES, (pair + 1) * LANES)
        query, key, value = (
            array[:, lanes].astype(F32) for array in (queries, keys, values)
        )
        parts = []
        for odd in range(2):
            own, other = halves(lane, odd)
            place = slice((pair * 2 + odd) * LANES, (pair * 2 + odd + 1) * LANES)
            query_full = with_terms(own, other, query, (0.0, 0.0, 0.0, 1.0)).astype(BF16)
            key_full = with_terms(own, other, key, (1.0, 1.0, 1.0, hidden_key)).astype(BF16)
            value_full = with_terms(own, other, value, (1.0, 1.0, 1.0)).astype(BF16)
            if student:
                k_ref[:, place] = key_full
                v_ref[:, place] = value_full
            found = []
            for start in range(0, rows, block):
                take = slice(start, start + block)
                scores = dot(query_full[take], key_full, 1, 1)
                top = jnp.max(scores, axis=1, keepdims=True)
                expo = jnp.exp2((scores - top) * exponent).astype(BF16)
                mixed = dot(expo, value_full, 1, 0)
                at = 0 if odd else HEAD_DIM
                total = mixed[:, at : at + 1]
                found.append(mixed / total)
                if student:
                    logsum = top + jnp.log(total) / scaling
                    q_ref[take, place] = with_terms(
                        own[take],
                        other[take],
                        query[take],
                        tuple(-part for part in three_parts(logsum)) + (1.0,),
                    ).astype(BF16)
            parts.append(jnp.concatenate(found, axis=0))
        context = jnp.where(lane < HEAD_DIM, parts[0], parts[1])
        ctx_ref[:, lanes] = context.astype(ctx_ref.dtype)


def attend(student, own_length, clip_scales, inputs, weights, bias):
    rows = inputs.shape[0]
    wide = 4 * LANES
    narrow = 2 * LANES
    scalar = whole(pltpu.SMEM)
    in_specs = [scalar] + ([scalar] if student else [])
    in_specs += [
        fixed((rows, D)),
        pl.BlockSpec((3, narrow, D), lambda i: (0, i, 0)),
        columns((3, 1, narrow)),
    ]
    if student:
        out_shape = [jax.ShapeDtypeStruct((rows, 2 * D), BF16)] * 3 + [
            jax.ShapeDtypeStruct((rows, D), F32),
            jax.ShapeDtypeStruct((rows, D), BF16),
        ]
        out_specs = [columns((rows, wide))] * 3 + [columns((rows, narrow)), fixed((rows, D))]
        args = (own_length, clip_scales, inputs, weights, bias)
    else:
        out_shape = [jax.ShapeDtypeStruct((rows, D), BF16)] * 3
        out_specs = [columns((rows, narrow))] * 3
        args = (own_length, inputs, weights, bias)
    return pl.pallas_call(
        functools.partial(attend_kernel, student),
        grid=(D // narrow,),
        in_specs=in_specs,
        out_specs=out_specs,
        out_shape=out_shape,
        compiler_params=pltpu.CompilerParams(vmem_limit_bytes=vmem_bytes),
        name="student_attention" if student else "teacher_attention",
    )(*args)


def split_dot(left, right):
    high = right.astype(BF16)
    low = (right - high.astype(F32)).astype(BF16)
    return dot(left, high, 1, 0) + dot(left, low, 1, 0)


def attend_back_kernel(
    lengths, inverse_pairs, q_ref, k_ref, v_ref, ctx_ref, dctx_ref, tq_ref, tk_ref, grad_ref, sum_ref
):
    rows = ctx_ref.shape[0]
    lane = lane_index(rows)
    position = lax.broadcasted_iota(jnp.int32, (rows, LANES), 0)
    live = position < lengths[0]
    low_half = lane < HEAD_DIM
    grad_context = dctx_ref[...].astype(F32)
    product = grad_context * ctx_ref[...]
    block = 512
    pieces = []
    for odd in range(2):
        own, other = halves(lane, odd)
        place = slice(odd * LANES, (odd + 1) * LANES)
        query, key, value = q_ref[:, place], k_ref[:, place], v_ref[:, place]
        weighted = jnp.sum(jnp.where(own, product, 0.0), axis=1, keepdims=True)
        grad_full = with_terms(
            own, other, grad_context, tuple(-part for part in three_parts(weighted))
        ).astype(BF16)
        grad_query = None
        key_parts, value_parts = [], []
        for start in range(0, rows, block):
            take = slice(start, start + block)
            probs = jnp.exp2(dot(key[take], query, 1, 1) * exponent)
            grad_scores = (probs * dot(value[take], grad_full, 1, 1)).astype(BF16)
            value_parts.append(dot(probs.astype(BF16), grad_full, 1, 0))
            key_parts.append(dot(grad_scores, query, 1, 0))
            part = dot(grad_scores, key[take], 0, 0)
            grad_query = part if grad_query is None else grad_query + part
        pieces.append(
            (grad_query, jnp.concatenate(key_parts, axis=0), jnp.concatenate(value_parts, axis=0))
        )
    query_live, key_live = (
        jnp.where(live, jnp.where(low_half, ref[:, :LANES], ref[:, LANES:]), 0.0).astype(BF16)
        for ref in (q_ref, k_ref)
    )
    teach_query, teach_key = (
        jnp.where(live, ref[...], 0.0).astype(BF16) for ref in (tq_ref, tk_ref)
    )
    row = lax.broadcasted_iota(jnp.int32, (LANES, LANES), 0)
    col = lax.broadcasted_iota(jnp.int32, (LANES, LANES), 1)
    same = (row < HEAD_DIM) == (col < HEAD_DIM)

    def gram(left, right):
        return jnp.where(same, outer_rows(left, right), 0.0)

    key_key, teach_key_key = gram(key_live, key_live), gram(teach_key, key_live)
    query_query, teach_query_query = gram(query_live, query_live), gram(teach_query, query_live)
    squares = (
        query_query * key_key
        - 2.0 * teach_query_query * teach_key_key
        + gram(teach_query, teach_query) * gram(teach_key, teach_key)
    )
    squares = jnp.sum(squares.reshape(LANES // 8, 8, LANES), axis=0)

    @pl.when(pl.program_id(0) == 0)
    def _():
        sum_ref[...] = jnp.zeros_like(sum_ref)

    sum_ref[...] += squares * (scaling * scaling * inverse_pairs[0])
    factor = 2.0 * scaling * scaling * inverse_pairs[0]
    query_term = split_dot(
        jnp.concatenate([query_live, teach_query], axis=1),
        jnp.concatenate([key_key, -teach_key_key], axis=0),
    )
    key_term = split_dot(
        jnp.concatenate([key_live, teach_key], axis=1),
        jnp.concatenate([query_query, -teach_query_query], axis=0),
    )
    (even_q, even_k, even_v), (odd_q, odd_k, odd_v) = pieces
    grad_ref[0] = (jnp.where(low_half, even_q, odd_q) * scaling + factor * query_term).astype(BF16)
    grad_ref[1] = (jnp.where(low_half, even_k, odd_k) * scaling + factor * key_term).astype(BF16)
    grad_ref[2] = jnp.where(low_half, even_v, odd_v).astype(BF16)


def attend_back(own_length, inverse_pairs, query, key, value, context, grad_context, tq, tk):
    rows = context.shape[0]
    scalar = whole(pltpu.SMEM)
    return pl.pallas_call(
        attend_back_kernel,
        grid=(D // LANES,),
        in_specs=[scalar, scalar]
        + [columns((rows, 2 * LANES))] * 3
        + [columns((rows, LANES))] * 4,
        out_specs=[columns((3, rows, LANES)), fixed((8, LANES))],
        out_shape=[
            jax.ShapeDtypeStruct((3, rows, D), BF16),
            jax.ShapeDtypeStruct((8, LANES), F32),
        ],
        compiler_params=pltpu.CompilerParams(vmem_limit_bytes=vmem_bytes),
        name="attention_backward",
    )(own_length, inverse_pairs, query, key, value, context, grad_context, tq, tk)


def gelu_parts(upper):
    cumulative = 0.5 * (1.0 + lax.erf(upper * (1.0 / math.sqrt(2.0))))
    return cumulative, upper * cumulative


ff_part = 1024


def teacher_kernel(tok_ref, ctx_ref, wo_ref, w1_ref, w2_ref, vec_ref, ub_ref, out_ref):
    vec = vec_ref[...]
    normed, _ = normalize(
        tok_ref[...].astype(F32) + dot(ctx_ref[...], wo_ref[...], 1, 1) + vec[3:4]
    )
    hidden = normed * vec[5:6] + vec[7:8]
    low = hidden.astype(BF16)
    lower = None
    for start in range(0, w1_ref.shape[0], ff_part):
        take = slice(start, start + ff_part)
        _, bent = gelu_parts(dot(low, w1_ref[take], 1, 1) + ub_ref[:, take])
        part = dot(bent.astype(BF16), w2_ref[:, take], 1, 1)
        lower = part if lower is None else lower + part
    final, _ = normalize(hidden + lower + vec[4:5])
    out_ref[...] = final * vec[6:7] + vec[8:9]


def teacher_tail(tokens, context, wo, w1, w2, vectors, up_bias):
    rows, wide = tokens.shape[0], w1.shape[0]
    block = 256
    return pl.pallas_call(
        teacher_kernel,
        grid=(rows // block,),
        in_specs=[
            row_blocks((block, D)),
            row_blocks((block, D)),
            fixed((D, D)),
            fixed((wide, D)),
            fixed((D, wide)),
            fixed(vectors.shape),
            fixed((1, wide)),
        ],
        out_specs=row_blocks((block, D)),
        out_shape=jax.ShapeDtypeStruct((rows, D), F32),
        compiler_params=pltpu.CompilerParams(vmem_limit_bytes=vmem_bytes),
        name="teacher_feed_forward",
    )(tokens, context, wo, w1, w2, vectors, up_bias)


def student_kernel(
    lengths,
    clip,
    tok_ref,
    cot_ref,
    teach_ref,
    ctx_ref,
    wo_ref,
    w1_ref,
    w2_ref,
    vec_ref,
    ub_ref,
    out_ref,
    dctx_ref,
    dao_ref,
    cb_ref,
    du_ref,
    hb_ref,
    df_ref,
    fb_ref,
    res_ref,
    sums_ref,
    upsum_ref,
    slope_ref,
):
    step = pl.program_id(0)
    vec = vec_ref[...]
    wide = w1_ref.shape[0]
    ctx_width, hid_width, act_width = (saturation * clip[at] for at in (1, 2, 3))
    ctx_bent = jnp.tanh(ctx_ref[...] / ctx_width)
    ctx_low = (ctx_width * ctx_bent).astype(BF16)
    cb_ref[...] = ctx_low
    first, first_inverse = normalize(
        tok_ref[...].astype(F32) + dot(ctx_low, wo_ref[...], 1, 1) + vec[3:4]
    )
    hidden = first * vec[5:6] + vec[7:8]
    hid_bent = jnp.tanh(hidden / hid_width)
    hid_low = (hid_width * hid_bent).astype(BF16)
    hb_ref[...] = hid_low
    lower = None
    for start in range(0, wide, ff_part):
        take = slice(start, start + ff_part)
        upper = dot(hid_low, w1_ref[take], 1, 1) + ub_ref[:, take]
        cumulative, bent = gelu_parts(upper)
        act = jnp.tanh(bent / act_width)
        density = jnp.exp(-0.5 * upper * upper) * (1.0 / math.sqrt(2.0 * math.pi))
        slope_ref[:, take] = (1.0 - act * act) * (cumulative + upper * density)
        act_low = (act_width * act).astype(BF16)
        fb_ref[:, take] = act_low
        part = dot(act_low, w2_ref[:, take], 1, 1)
        lower = part if lower is None else lower + part
    second, second_inverse = normalize(hidden + lower + vec[4:5])
    result = second * vec[6:7] + vec[8:9]
    out_ref[...] = result.astype(BF16)
    rows = result.shape[0]
    position = lax.broadcasted_iota(jnp.int32, (rows, D), 0) + step * rows
    gap = jnp.where(position < lengths[0], result - teach_ref[...], 0.0)
    grad_out = cot_ref[...].astype(F32) + gap * (2.0 * hidden_weight)
    grad_second = norm_back(grad_out * vec[6:7], second, second_inverse)
    grad_lower = grad_second.astype(BF16)
    df_ref[...] = grad_lower
    grad_hidden = None
    up_sums = []
    for start in range(0, wide, ff_part):
        take = slice(start, start + ff_part)
        grad_upper = (dot(grad_lower, w2_ref[:, take], 1, 0) * slope_ref[:, take]).astype(BF16)
        du_ref[:, take] = grad_upper
        up_sums.append(jnp.sum(grad_upper.astype(F32), axis=0, keepdims=True))
        part = dot(grad_upper, w1_ref[take], 1, 0)
        grad_hidden = part if grad_hidden is None else grad_hidden + part
    grad_hidden = grad_second + grad_hidden * (1.0 - hid_bent * hid_bent)
    grad_first = norm_back(grad_hidden * vec[5:6], first, first_inverse)
    res_ref[...] = grad_first
    grad_attn = grad_first.astype(BF16)
    dao_ref[...] = grad_attn
    dctx_ref[...] = (
        dot(grad_attn, wo_ref[...], 1, 0) * (1.0 - ctx_bent * ctx_bent)
    ).astype(BF16)

    @pl.when(step == 0)
    def _():
        sums_ref[...] = jnp.zeros_like(sums_ref)
        upsum_ref[...] = jnp.zeros_like(upsum_ref)

    for at, term in enumerate(
        (
            grad_attn.astype(F32),
            grad_lower.astype(F32),
            grad_hidden * first,
            grad_out * second,
            grad_hidden,
            grad_out,
            gap * gap,
        )
    ):
        sums_ref[at : at + 1] += jnp.sum(term, axis=0, keepdims=True)
    upsum_ref[...] += jnp.concatenate(up_sums, axis=1)


def student_middle(
    own_length, clip_scales, tokens, cotangent, teach_out, context, wo, w1, w2, vectors, up_bias
):
    rows, wide = tokens.shape[0], w1.shape[0]
    block = 256
    scalar = whole(pltpu.SMEM)
    narrow_spec, wide_spec = row_blocks((block, D)), row_blocks((block, wide))
    narrow, broad = jax.ShapeDtypeStruct((rows, D), BF16), jax.ShapeDtypeStruct((rows, wide), BF16)
    return pl.pallas_call(
        student_kernel,
        grid=(rows // block,),
        in_specs=[scalar, scalar]
        + [narrow_spec] * 4
        + [
            fixed((D, D)),
            fixed((wide, D)),
            fixed((D, wide)),
            fixed(vectors.shape),
            fixed((1, wide)),
        ],
        out_specs=[narrow_spec] * 4
        + [wide_spec, narrow_spec, narrow_spec, wide_spec, narrow_spec, fixed((8, D)), fixed((1, wide))],
        out_shape=[narrow] * 4
        + [
            broad,
            narrow,
            narrow,
            broad,
            jax.ShapeDtypeStruct((rows, D), F32),
            jax.ShapeDtypeStruct((8, D), F32),
            jax.ShapeDtypeStruct((1, wide), F32),
        ],
        scratch_shapes=[pltpu.VMEM((block, wide), F32)],
        compiler_params=pltpu.CompilerParams(vmem_limit_bytes=vmem_bytes),
        name="student_feed_forward",
    )(own_length, clip_scales, tokens, cotangent, teach_out, context, wo, w1, w2, vectors, up_bias)


def input_kernel(clip, grad_ref, w_ref, low_ref, tok_ref, res_ref, out_ref, dw_ref, sum_ref, acc_ref):
    slot = pl.program_id(0)
    grad = grad_ref[0]
    part = dot(grad, w_ref[0], 1, 0)
    dw_ref[0] = outer_rows(grad, low_ref[...]).astype(dw_ref.dtype)
    sum_ref[0] = jnp.sum(grad.astype(F32), axis=0, keepdims=True)

    @pl.when(slot == 0)
    def _():
        acc_ref[...] = part

    @pl.when(slot > 0)
    def _():
        acc_ref[...] += part

    @pl.when(slot == pl.num_programs(0) - 1)
    def _():
        bent = jnp.tanh(tok_ref[...].astype(F32) / (saturation * clip[0]))
        out_ref[...] = (res_ref[...] + acc_ref[...] * (1.0 - bent * bent)).astype(BF16)


def input_grads(clip_scales, grads, weights, low, tokens, residual):
    rows = tokens.shape[0]
    slotted = lambda *shape: pl.BlockSpec((1,) + shape, lambda i: (i, 0, 0))
    return pl.pallas_call(
        input_kernel,
        grid=(3,),
        in_specs=[
            whole(pltpu.SMEM),
            slotted(rows, D),
            slotted(D, D),
            fixed((rows, D)),
            fixed((rows, D)),
            fixed((rows, D)),
        ],
        out_specs=[fixed((rows, D)), slotted(D, D), slotted(1, D)],
        out_shape=[
            jax.ShapeDtypeStruct((rows, D), BF16),
            jax.ShapeDtypeStruct((3, D, D), BF16),
            jax.ShapeDtypeStruct((3, 1, D), F32),
        ],
        scratch_shapes=[pltpu.VMEM((rows, D), F32)],
        compiler_params=pltpu.CompilerParams(vmem_limit_bytes=vmem_bytes),
        name="input_gradient",
    )(clip_scales, grads, weights, low, tokens, residual)


def on_device(
    tokens,
    teacher_tokens,
    cotangent,
    lengths,
    clip_scales,
    attn_latent,
    up_latent,
    down_latent,
    biases,
    up_bias,
    norm_gains,
    norm_shifts,
    teacher_attn,
    teacher_up,
    teacher_down,
    teacher_biases,
    teacher_up_bias,
    teacher_gains,
    teacher_shifts,
):
    count = lax.axis_size(AXES)
    narrow, wide = biases.shape[1], up_bias.shape[0]
    own_length = lax.dynamic_slice_in_dim(lengths, lax.axis_index(AXES), 1)
    live_float = lengths.astype(F32)
    token_norm = jnp.sum(live_float)
    pair_norm = HEADS * jnp.sum(live_float * live_float)
    inverse_pairs = (1.0 / pair_norm).reshape(1)
    vectors = jnp.concatenate(
        [teacher_biases, teacher_gains, teacher_shifts, biases, norm_gains, norm_shifts], axis=0
    )
    small = jnp.concatenate([vectors.reshape(-1), teacher_up_bias, up_bias])
    small = jnp.pad(small, (0, 8 * D - small.shape[0])).reshape(8, D)
    (
        small_all,
        teach_qkv,
        attn_w,
        teach_wo,
        teach_up,
        teach_down,
        up_w,
        down_w,
    ) = gather(
        [
            small,
            teacher_attn[:3],
            binarize(attn_latent),
            teacher_attn[3],
            teacher_up,
            teacher_down,
            binarize(up_latent),
            binarize(down_latent),
        ],
        ((0, 1), (2, 3), (4,), (5,), (6,), (7,)),
        0,
    )
    small_all = small_all.reshape(count, -1)
    lines = vectors.shape[0]
    vec = (
        small_all[:, : lines * narrow]
        .reshape(count, lines, narrow)
        .transpose(1, 0, 2)
        .reshape(lines, D)
        .astype(F32)
    )
    teach_vec, student_vec = vec[: lines // 2], vec[lines // 2 :]
    at = lines * narrow
    teach_up_bias = small_all[:, at : at + wide].reshape(1, -1).astype(F32)
    student_up_bias = small_all[:, at + wide : at + 2 * wide].reshape(1, -1).astype(F32)
    tq, tk, teach_context = attend(
        False, own_length, clip_scales, teacher_tokens, teach_qkv, teach_vec[:3].reshape(3, 1, D)
    )
    query, key, value, context, x_low = attend(
        True, own_length, clip_scales, tokens, attn_w[:3], student_vec[:3].reshape(3, 1, D)
    )
    teach_out = teacher_tail(
        teacher_tokens, teach_context, teach_wo, teach_up, teach_down, teach_vec, teach_up_bias
    )
    (
        result,
        grad_context,
        grad_attn,
        ctx_low,
        grad_upper,
        hid_low,
        grad_lower,
        act_low,
        residual,
        sums,
        up_sums,
    ) = student_middle(
        own_length,
        clip_scales,
        tokens,
        cotangent,
        teach_out,
        context,
        attn_w[3],
        up_w,
        down_w,
        student_vec,
        student_up_bias,
    )
    down_weight_grad = outer_rows(grad_lower, act_low)
    up_weight_grad = outer_rows(grad_upper, hid_low)
    out_weight_grad = outer_rows(grad_attn, ctx_low)
    grads, squares = attend_back(
        own_length, inverse_pairs, query, key, value, context, grad_context, tq, tk
    )
    input_grad, qkv_weight_grad, qkv_sums = input_grads(
        clip_scales, grads, attn_w[:3], x_low, tokens, residual
    )
    local_loss = jnp.sum(sums[6]) / (D * token_norm) + jnp.sum(squares)
    bias_terms = jnp.concatenate([qkv_sums[:, 0], sums[:2]], axis=0)
    lines = jnp.concatenate([bias_terms, sums[2:6]], axis=0)
    own_sums = jnp.concatenate(
        [
            lines.reshape(9, count, narrow).transpose(1, 0, 2).reshape(count, -1),
            up_sums.reshape(count, wide),
            jnp.broadcast_to(local_loss, (count, 1)),
        ],
        axis=1,
    )
    own_sums = jnp.pad(own_sums, ((0, 0), (0, 8 * LANES - own_sums.shape[1])))
    down_total, up_total, out_total, qkv_total, sum_total = scatter(
        [
            down_weight_grad.astype(BF16),
            up_weight_grad.astype(BF16),
            out_weight_grad.astype(BF16),
            qkv_weight_grad,
            own_sums.reshape(count * 8, LANES),
        ],
        1,
    )
    attn_total = jnp.concatenate([qkv_total, out_total[None]], axis=0)
    sum_total = sum_total.reshape(-1)
    line_total = sum_total[: 9 * narrow].reshape(9, narrow)
    up_bias_total = sum_total[9 * narrow : 9 * narrow + wide]
    loss = sum_total[9 * narrow + wide]
    return (
        result,
        loss,
        input_grad,
        latent_grad(attn_latent, attn_total),
        latent_grad(up_latent, up_total),
        latent_grad(down_latent, down_total),
        line_total[:5],
        up_bias_total,
        line_total[5:7],
        line_total[7:9],
    )
def solution(mesh):
    in_specs = (
        P(("dp", "shard"), None),
        P(("dp", "shard"), None),
        P(("dp", "shard"), None),
        P(),
        P(),
        P(None, ("dp", "shard"), None),
        P(("dp", "shard"), None),
        P(("dp", "shard"), None),
        P(None, ("dp", "shard")),
        P(("dp", "shard")),
        P(None, ("dp", "shard")),
        P(None, ("dp", "shard")),
        P(None, ("dp", "shard"), None),
        P(("dp", "shard"), None),
        P(("dp", "shard"), None),
        P(None, ("dp", "shard")),
        P(("dp", "shard")),
        P(None, ("dp", "shard")),
        P(None, ("dp", "shard")),
    )
    out_specs = (
        P(("dp", "shard"), None),
        P(),
        P(("dp", "shard"), None),
        P(None, ("dp", "shard"), None),
        P(("dp", "shard"), None),
        P(("dp", "shard"), None),
        P(None, ("dp", "shard")),
        P(("dp", "shard")),
        P(None, ("dp", "shard")),
        P(None, ("dp", "shard")),
    )
    return jax.shard_map(
        on_device, mesh=mesh, in_specs=in_specs, out_specs=out_specs, check_vma=False
    )
```

```python
import functools
import math

import jax
import jax.numpy as jnp
from jax import lax
from jax.experimental import pallas as pl
from jax.experimental.pallas import tpu as pltpu
from jax.sharding import PartitionSpec as P

D = 768
HEADS = 12
HEAD_DIM = 64
SEQ_LEN = 1024
AXES = ("dp", "shard")
MESH = pl.DeviceIdType.MESH
F32 = jnp.float32
BF16 = jnp.bfloat16

epsilon = 1e-05
masked_score = -1e30
hidden_weight = 0.25
saturation = 7.5
LANES = 128
log2e = math.log2(math.e)
scaling = HEAD_DIM ** (-0.5)
exponent = scaling * log2e
vmem_bytes = 60 * 1024 * 1024
line_rows = 16


def dot(left, right, left_dim, right_dim):
    return lax.dot_general(
        left, right, (((left_dim,), (right_dim,)), ((), ())), preferred_element_type=F32
    )


def outer_rows(left, right):
    return dot(left, right, 0, 0)


def binarize(latent):
    scale = jnp.mean(jnp.abs(latent), axis=-1, keepdims=True)
    return (scale * jnp.sign(latent)).astype(BF16)


def surrogate(latent):
    return jnp.mean(jnp.abs(latent), axis=-1, keepdims=True) * latent


def latent_grad(latent, grad):
    _, pull = jax.vjp(surrogate, latent)
    return pull(grad)[0]


def normalize(values):
    center = values - jnp.mean(values, axis=-1, keepdims=True)
    inverse = lax.rsqrt(jnp.mean(center * center, axis=-1, keepdims=True) + epsilon)
    return (center * inverse, inverse)


def norm_back(grad_norm, normed, inverse):
    return inverse * (
        grad_norm
        - jnp.mean(grad_norm, axis=-1, keepdims=True)
        - normed * jnp.mean(grad_norm * normed, axis=-1, keepdims=True)
    )


def whole(memory=pltpu.VMEM):
    return pl.BlockSpec(memory_space=memory)


def fixed(shape):
    return pl.BlockSpec(shape, lambda *_: (0,) * len(shape), pipeline_mode=pl.Buffered(1))


def columns(shape):
    return pl.BlockSpec(shape, lambda i: (0,) * (len(shape) - 1) + (i,))


def row_blocks(shape):
    return pl.BlockSpec(shape, lambda i: (i,) + (0,) * (len(shape) - 1))


class Place:
    def __init__(self, depth):
        self.depth = depth
        dp, shard = lax.axis_index("dp"), lax.axis_index("shard")
        z, y = dp // 2, lax.rem(dp, 2)
        x, core = shard // 2, lax.rem(shard, 2)
        self.z, self.y, self.x, self.core = z, y, x, core

        def device(z_at, y_at, x_at, core_at):
            return (z_at * 2 + y_at, x_at * 2 + core_at)

        self.above = device(jnp.minimum(z + 1, depth - 1), y, x, core)
        self.below = device(jnp.maximum(z - 1, 0), y, x, core)
        one = (lax.rem(y + 1 - core, 2), lax.rem(x + core, 2))
        two = (lax.rem(y + core, 2), lax.rem(x + 1 - core, 2))
        self.pieces = ((y, x), one, two, (1 - y, 1 - x))
        self.first, self.second = device(z, *one, core), device(z, *two, core)
        self.sibling = device(z, y, x, 1 - core)

    def barrier(self):
        semaphore = pltpu.get_barrier_semaphore()
        for partner in (self.first, self.second, self.sibling):
            pl.semaphore_signal(semaphore, inc=1, device_id=partner, device_id_type=MESH)

        @pl.when(self.z < self.depth - 1)
        def _():
            pl.semaphore_signal(semaphore, inc=1, device_id=self.above, device_id_type=MESH)

        @pl.when(self.z > 0)
        def _():
            pl.semaphore_signal(semaphore, inc=1, device_id=self.below, device_id_type=MESH)

        pl.semaphore_wait(
            semaphore, 3 + jnp.minimum(self.z, 1) + jnp.minimum(self.depth - 1 - self.z, 1)
        )


def remote(source, target, send_sem, recv_sem, device):
    return pltpu.make_async_remote_copy(
        src_ref=source,
        dst_ref=target,
        send_sem=send_sem,
        recv_sem=recv_sem,
        device_id=device,
        device_id_type=MESH,
    )


def tiled_over(mesh_sizes, rows):
    return mesh_sizes == (8, 4) and rows % 8 == 0


def in_order(counts, apart):
    return [
        (chunk, number)
        for _, chunk, number in sorted(
            (number + apart * chunk, chunk, number)
            for chunk, count in enumerate(counts)
            for number in range(count)
        )
    ]


def gather_scratch(chunks, depth):
    dma = pltpu.SemaphoreType.DMA
    sizes = (len(chunks), max(len(chunk) for chunk in chunks))
    return [
        dma(sizes + (depth - 1, 2)),
        dma(sizes + (depth - 1, 2)),
        dma(sizes + (7,)),
        dma(sizes + (7,)),
        dma(sizes),
    ]


def gather_stages(place, ins, outs, leads, chunks, sems, apart=2):
    line_send, line_recv, pair_send, pair_recv, own_sem = sems
    depth, z, y, x, core = place.depth, place.z, place.y, place.x, place.core

    def slot(item, *index):
        return outs[item].at[((slice(None),) if leads[item] > 1 else ()) + index]

    def line_copy(chunk, at, item, turn, upward):
        if upward:
            owner, target = jnp.maximum(z - (turn - 1), 0), place.above
        else:
            owner, target = jnp.minimum(z + (turn - 1), depth - 1), place.below
        block = slot(item, owner, y, x, core)
        where = (chunk, at, turn - 1, int(upward))
        return remote(block, block, line_send.at[where], line_recv.at[where], target)

    def sends(turn, upward):
        if upward:
            return (z - (turn - 1) >= 0) & (z < depth - 1)
        return (z + (turn - 1) <= depth - 1) & (z > 0)

    def receives(turn, upward):
        return (z - turn >= 0) if upward else (z + turn <= depth - 1)

    def own_copy(chunk, at, item):
        return pltpu.make_async_copy(
            ins[item], slot(item, z, y, x, core), own_sem.at[chunk, at]
        )

    plans = (
        (0, place.first),
        (0, place.second),
        (1, place.second),
        (0, place.sibling),
        (1, place.sibling),
        (2, place.sibling),
        (3, place.sibling),
    )

    def pair_copy(chunk, at, item, plan):
        piece, target = plans[plan]
        block = slot(item, slice(None), *place.pieces[piece], core)
        where = (chunk, at, plan)
        return remote(block, block, pair_send.at[where], pair_recv.at[where], target)

    def each(chunk, action):
        for at, item in enumerate(chunks[chunk]):
            action(at, item)

    def line_start(chunk, turn):
        for upward in (True, False):

            @pl.when(sends(turn, upward))
            def _():
                each(chunk, lambda at, item: line_copy(chunk, at, item, turn, upward).start())

    def line_received(chunk, turn):
        for upward in (True, False):

            @pl.when(receives(turn, upward))
            def _():
                each(chunk, lambda at, item: line_copy(chunk, at, item, turn, upward).wait_recv())

    def line_sent(chunk, turn):
        for upward in (True, False):

            @pl.when(sends(turn, upward))
            def _():
                each(chunk, lambda at, item: line_copy(chunk, at, item, turn, upward).wait_send())

    def start(chunk, *plan_list):
        for plan in plan_list:
            each(chunk, lambda at, item: pair_copy(chunk, at, item, plan).start())

    def received(chunk, *plan_list):
        for plan in plan_list:
            each(chunk, lambda at, item: pair_copy(chunk, at, item, plan).wait_recv())

    def stage(chunk, number):
        if number == 0:
            each(chunk, lambda at, item: own_copy(chunk, at, item).wait())
            line_start(chunk, 1)
        elif number < depth:
            line_received(chunk, number)
            if number < depth - 1:
                line_start(chunk, number + 1)
            else:
                start(chunk, 0, 1, 3)
        elif number == depth:
            received(chunk, 0)
            start(chunk, 2, 4)
        elif number == depth + 1:
            received(chunk, 1)
            start(chunk, 5)
        elif number == depth + 2:
            received(chunk, 2)
            start(chunk, 6)
        else:
            received(chunk, 3, 4, 5, 6)
            for turn in range(1, depth):
                line_sent(chunk, turn)
            for plan in range(7):
                each(chunk, lambda at, item: pair_copy(chunk, at, item, plan).wait_send())

    def begin():
        for chunk in range(len(chunks)):
            each(chunk, lambda at, item: own_copy(chunk, at, item).start())

    return [begin] + [
        functools.partial(stage, chunk, number)
        for chunk, number in in_order([depth + 4] * len(chunks), apart)
    ]


def gather_shapes(arrays, depth):
    shapes = [((1,) + array.shape)[-3:] for array in arrays]
    leads = [shape[0] for shape in shapes]
    results = [
        jax.ShapeDtypeStruct(((lead,) if lead > 1 else ()) + (depth, 2, 2, 2, rows, cols), BF16)
        for lead, rows, cols in shapes
    ]
    return leads, results


def gathered(results):
    return [
        result.reshape(result.shape[:-6] + (-1, result.shape[-1])) for result in results
    ]


def gather_kernel(leads, chunks, depth, *refs):
    count = len(leads)
    place = Place(depth)
    place.barrier()
    for stage in gather_stages(
        place, refs[:count], refs[count : 2 * count], leads, chunks, refs[2 * count :]
    ):
        stage()


def gather(arrays, chunks, collective_id):
    dp, shard = lax.axis_size("dp"), lax.axis_size("shard")
    if not tiled_over((dp, shard), min(array.shape[-2] for array in arrays)):
        return [
            lax.all_gather(array, AXES, axis=array.ndim - 2, tiled=True) for array in arrays
        ]
    depth = dp // 2
    leads, results = gather_shapes(arrays, depth)
    results = pl.pallas_call(
        functools.partial(gather_kernel, leads, chunks, depth),
        out_shape=results,
        in_specs=[whole(pl.ANY)] * len(arrays),
        out_specs=[whole(pl.ANY)] * len(arrays),
        scratch_shapes=gather_scratch(chunks, depth),
        compiler_params=pltpu.CompilerParams(
            collective_id=collective_id, has_side_effects=True, vmem_limit_bytes=1 << 20
        ),
        name="gather_weights",
    )(*arrays)
    return gathered(results)


def scatter_scratch(shapes, dtypes, depth):
    dma = pltpu.SemaphoreType.DMA
    scratch = []
    for shape, dtype in zip(shapes, dtypes):
        lead, rows, cols = shape
        block = (depth, lead, rows, cols)
        scratch += [
            pltpu.VMEM((4,) + block, dtype),
            pltpu.VMEM((4,) + block, dtype),
            pltpu.VMEM((3,) + block, dtype),
            pltpu.VMEM((2,) + block, dtype),
        ]
    count = len(shapes)
    return scratch + [
        dma((count, 4)),
        dma((count, 7)),
        dma((count, 7)),
        dma((count, depth, 2)),
        dma((count, depth, 2)),
    ]


def scatter_stage(place, ins, finish, scratch, count):
    depth, z, core = place.depth, place.z, place.core
    own_sem, pair_send, pair_recv, line_send, line_recv = scratch[4 * count :]

    def buffers(item):
        return scratch[4 * item : 4 * item + 4]

    def source(item, piece, lead, side):
        index = (slice(None),) + place.pieces[piece] + (side,)
        ref = ins[item]
        return ref.at[((lead,) if ref.shape[:-6] else ()) + index]

    def leads(item):
        return range(buffers(item)[0].shape[2])

    def own_copy(item, piece, lead):
        held = buffers(item)[0]
        return pltpu.make_async_copy(
            source(item, piece, lead, core), held.at[piece, :, lead], own_sem.at[item, piece]
        )

    names = (0, 2, 1, 3)

    def core_copy(item, piece, lead):
        arrived = buffers(item)[1]
        name = names[piece]
        return remote(
            source(item, piece, lead, 1 - core),
            arrived.at[name, :, lead],
            pair_send.at[item, piece],
            pair_recv.at[item, name],
            place.sibling,
        )

    def core_wait(item, piece):
        arrived = buffers(item)[1]
        block = arrived.at[piece]
        remote(
            block, block, pair_send.at[item, piece], pair_recv.at[item, piece], place.sibling
        ).wait_recv()

    def chip_copy(item, plan):
        held, _, arrived, _ = buffers(item)
        piece, target = ((2, place.second), (3, place.second), (1, place.first))[plan]
        return remote(
            held.at[piece],
            arrived.at[plan],
            pair_send.at[item, 4 + plan],
            pair_recv.at[item, 4 + plan],
            target,
        )

    def line_copy(item, owner, upward, fresh):
        held, _, _, arrived = buffers(item)
        block = arrived.at[int(upward), owner]
        where = (item, owner, int(upward))
        return remote(
            held.at[0, owner] if fresh else block,
            block,
            line_send.at[where],
            line_recv.at[where],
            place.above if upward else place.below,
        )

    def add(target, *others):
        def one(at):
            total = target[at].astype(F32)
            for other in others:
                total = total + other[at].astype(F32)
            target[at] = total.astype(target.dtype)

        for first in range(target.shape[0]):
            for second in range(target.shape[1]):
                one((first, second))

    def add_block(target, other):
        for lead in range(target.shape[0]):
            target[lead] = (target[lead].astype(F32) + other[lead].astype(F32)).astype(
                target.dtype
            )

    def merge(item, piece):
        held, arrived, _, _ = buffers(item)
        block = held.at[piece]
        pltpu.make_async_copy(block, block, own_sem.at[item, piece]).wait()
        core_wait(item, piece)
        add(block, arrived.at[piece])

    def line_turn(item, turn, upward):
        held, _, _, arrived = buffers(item)
        at = turn if upward else depth - 1 - turn
        beyond = range(at + 1, depth) if upward else range(at)

        @pl.when(z == at)
        def _():
            for owner in sorted(beyond, key=lambda owner: -abs(owner - at)):
                if turn:
                    line_copy(item, owner, upward, False).wait_recv()
                    add_block(arrived.at[int(upward), owner], held.at[0, owner])
                line_copy(item, owner, upward, not turn).start()
            if turn:
                line_copy(item, at, upward, False).wait_recv()

    def stage(item, number):
        held, _, arrived, line = buffers(item)
        if number == 0:
            for piece in (3, 1, 2, 0):
                for lead in leads(item):
                    core_copy(item, piece, lead).start()
            for piece in (2, 3, 1, 0):
                for lead in leads(item):
                    own_copy(item, piece, lead).start()
        elif number == 1:
            for piece, plan in ((3, 1), (2, 0)):
                merge(item, piece)
                chip_copy(item, plan).start()
        elif number == 2:
            merge(item, 1)
            merge(item, 0)
        elif number == 3:
            chip_copy(item, 1).wait_recv()
            add(held.at[1], arrived.at[1])
            chip_copy(item, 2).start()
        elif number == 4:
            chip_copy(item, 0).wait_recv()
            chip_copy(item, 2).wait_recv()
            add(held.at[0], arrived.at[0], arrived.at[2])
            for upward in (True, False):
                line_turn(item, 0, upward)
        elif number < 4 + depth:
            for upward in (True, False):
                line_turn(item, number - 4, upward)
        else:
            for lead in leads(item):
                total = held[0, z, lead].astype(F32)
                for upward, near in ((1, z > 0), (0, z < depth - 1)):
                    total = jnp.where(near, total + line[upward, z, lead].astype(F32), total)
                finish(item, lead, total)

            for piece in range(4):
                block = buffers(item)[1].at[piece]
                remote(
                    block, block, pair_send.at[item, piece], pair_recv.at[item, piece], place.sibling
                ).wait_send()
            for plan in range(3):
                chip_copy(item, plan).wait_send()
            for upward in (True, False):
                for owner in range(depth):

                    @pl.when((z < owner) if upward else (z > owner))
                    def _():
                        line_copy(item, owner, upward, False).wait_send()

    return stage


def split_rows(array, depth):
    return array.reshape(array.shape[:-2] + (depth, 2, 2, 2, -1, array.shape[-1]))


def shared_scratch(depth):
    dma = pltpu.SemaphoreType.DMA
    return [
        pltpu.VMEM((4, line_rows, D), F32),
        pltpu.VMEM((5, line_rows, D), F32),
        pltpu.VMEM((2, line_rows, D), F32),
        dma((5,)),
        dma((5,)),
    ]


def shared_stage(place, finish, scratch):
    held, arrived, line, send_sem, recv_sem = scratch
    depth, z = place.depth, place.z
    partners = (place.sibling, place.second, place.first)

    def pair_copy(at):
        return remote(
            held.at[at], arrived.at[at], send_sem.at[at], recv_sem.at[at], partners[at]
        )

    def line_copy(upward, fresh):
        at = 3 + int(upward)
        return remote(
            held.at[3] if fresh else line.at[int(upward)],
            arrived.at[at],
            send_sem.at[at],
            recv_sem.at[at],
            place.above if upward else place.below,
        )

    def line_turn(turn, upward):
        at = turn if upward else depth - 1 - turn

        @pl.when(z == at)
        def _():
            if turn:
                line_copy(upward, False).wait_recv()
            if turn < depth - 1:
                if turn:
                    line[int(upward)] = held[3] + arrived[3 + int(upward)]
                line_copy(upward, not turn).start()

    def stage(number):
        if number == 0:
            pair_copy(0).start()
        elif number < 4:
            pair_copy(number - 1).wait_recv()
            held[number] = held[number - 1] + arrived[number - 1]
            if number < 3:
                pair_copy(number).start()
            else:
                for upward in (True, False):
                    line_turn(0, upward)
        elif number < 3 + depth:
            for upward in (True, False):
                line_turn(number - 3, upward)
        else:
            total = held[3]
            total = jnp.where(z > 0, total + arrived[4], total)
            finish(jnp.where(z < depth - 1, total + arrived[3], total))
            for at in range(3):
                pair_copy(at).wait_send()
            for upward in (True, False):

                @pl.when((z < depth - 1) if upward else (z > 0))
                def _():
                    line_copy(upward, False).wait_send()

    return stage


def scatter(arrays):
    return [
        lax.psum_scatter(array.astype(F32), AXES, scatter_dimension=array.ndim - 2, tiled=True)
        for array in arrays
    ]


def lane_index(rows):
    return lax.broadcasted_iota(jnp.int32, (rows, LANES), 1)


def halves(lane, odd):
    own = (lane >= HEAD_DIM) if odd else (lane < HEAD_DIM)
    other = lane if odd else lane - HEAD_DIM
    return own, other


def three_parts(values):
    high = values.astype(BF16).astype(F32)
    rest = values - high
    middle = rest.astype(BF16).astype(F32)
    return high, middle, rest - middle


def with_terms(own, other, values, terms):
    result = jnp.zeros_like(values)
    for at, term in enumerate(terms):
        result = jnp.where(other == at, term, result)
    return jnp.where(own, values, result)


def attend_kernel(student, lengths, *refs):
    if student:
        clip, x_ref, w_ref, b_ref, q_ref, k_ref, v_ref, ctx_ref, low_ref = refs

        @pl.when(pl.program_id(0) == 0)
        def _():
            width = saturation * clip[0]
            low_ref[...] = (width * jnp.tanh(x_ref[...].astype(F32) / width)).astype(BF16)

        inputs = low_ref[...]
    else:
        x_ref, w_ref, b_ref, q_ref, k_ref, ctx_ref = refs
        inputs = x_ref[...]
    rows = inputs.shape[0]
    lane = lane_index(rows)
    position = lax.broadcasted_iota(jnp.int32, (rows, LANES), 0)
    hidden_key = jnp.where(position < lengths[0], 0.0, masked_score)
    queries, keys, values = (
        (dot(inputs, w_ref[slot], 1, 1) + b_ref[slot]).astype(BF16) for slot in range(3)
    )
    if not student:
        q_ref[...] = queries
        k_ref[...] = keys
    block = 512
    for pair in range(2):
        lanes = slice(pair * LANES, (pair + 1) * LANES)
        query, key, value = (
            array[:, lanes].astype(F32) for array in (queries, keys, values)
        )
        parts = []
        for odd in range(2):
            own, other = halves(lane, odd)
            place = slice((pair * 2 + odd) * LANES, (pair * 2 + odd + 1) * LANES)
            query_full = with_terms(own, other, query, (0.0, 0.0, 0.0, 1.0)).astype(BF16)
            key_full = with_terms(own, other, key, (1.0, 1.0, 1.0, hidden_key)).astype(BF16)
            value_full = with_terms(own, other, value, (1.0, 1.0, 1.0)).astype(BF16)
            if student:
                k_ref[:, place] = key_full
                v_ref[:, place] = value_full
            found = []
            for start in range(0, rows, block):
                take = slice(start, start + block)
                scores = dot(query_full[take], key_full, 1, 1)
                top = jnp.max(scores, axis=1, keepdims=True)
                expo = jnp.exp2((scores - top) * exponent).astype(BF16)
                mixed = dot(expo, value_full, 1, 0)
                at = 0 if odd else HEAD_DIM
                total = mixed[:, at : at + 1]
                found.append(mixed / total)
                if student:
                    logsum = top + jnp.log(total) / scaling
                    q_ref[take, place] = with_terms(
                        own[take],
                        other[take],
                        query[take],
                        tuple(-part for part in three_parts(logsum)) + (1.0,),
                    ).astype(BF16)
            parts.append(jnp.concatenate(found, axis=0))
        context = jnp.where(lane < HEAD_DIM, parts[0], parts[1])
        ctx_ref[:, lanes] = context.astype(ctx_ref.dtype)


def attend(student, own_length, clip_scales, inputs, weights, bias):
    rows = inputs.shape[0]
    wide = 4 * LANES
    narrow = 2 * LANES
    scalar = whole(pltpu.SMEM)
    in_specs = [scalar] + ([scalar] if student else [])
    in_specs += [
        fixed((rows, D)),
        pl.BlockSpec((3, narrow, D), lambda i: (0, i, 0)),
        columns((3, 1, narrow)),
    ]
    if student:
        out_shape = [jax.ShapeDtypeStruct((rows, 2 * D), BF16)] * 3 + [
            jax.ShapeDtypeStruct((rows, D), F32),
            jax.ShapeDtypeStruct((rows, D), BF16),
        ]
        out_specs = [columns((rows, wide))] * 3 + [columns((rows, narrow)), fixed((rows, D))]
        args = (own_length, clip_scales, inputs, weights, bias)
    else:
        out_shape = [jax.ShapeDtypeStruct((rows, D), BF16)] * 3
        out_specs = [columns((rows, narrow))] * 3
        args = (own_length, inputs, weights, bias)
    return pl.pallas_call(
        functools.partial(attend_kernel, student),
        grid=(D // narrow,),
        in_specs=in_specs,
        out_specs=out_specs,
        out_shape=out_shape,
        compiler_params=pltpu.CompilerParams(vmem_limit_bytes=vmem_bytes),
        name="student_attention" if student else "teacher_attention",
    )(*args)


def split_dot(left, right):
    high = right.astype(BF16)
    low = (right - high.astype(F32)).astype(BF16)
    return dot(left, high, 1, 0) + dot(left, low, 1, 0)


def attend_back_pair(length, inverse_pairs, q_ref, k_ref, v_ref, ctx_ref, dctx_ref, tq_ref, tk_ref, between):
    rows = ctx_ref.shape[0]
    lane = lane_index(rows)
    position = lax.broadcasted_iota(jnp.int32, (rows, LANES), 0)
    live = position < length
    low_half = lane < HEAD_DIM
    grad_context = dctx_ref[...].astype(F32)
    product = grad_context * ctx_ref[...]
    block = 512
    pieces = []
    for odd in range(2):
        own, other = halves(lane, odd)
        place = slice(odd * LANES, (odd + 1) * LANES)
        query, key, value = q_ref[:, place], k_ref[:, place], v_ref[:, place]
        weighted = jnp.sum(jnp.where(own, product, 0.0), axis=1, keepdims=True)
        grad_full = with_terms(
            own, other, grad_context, tuple(-part for part in three_parts(weighted))
        ).astype(BF16)
        grad_query = None
        key_parts, value_parts = [], []
        for start in range(0, rows, block):
            take = slice(start, start + block)
            probs = jnp.exp2(dot(key[take], query, 1, 1) * exponent)
            grad_scores = (probs * dot(value[take], grad_full, 1, 1)).astype(BF16)
            value_parts.append(dot(probs.astype(BF16), grad_full, 1, 0))
            key_parts.append(dot(grad_scores, query, 1, 0))
            part = dot(grad_scores, key[take], 0, 0)
            grad_query = part if grad_query is None else grad_query + part
        pieces.append(
            (grad_query, jnp.concatenate(key_parts, axis=0), jnp.concatenate(value_parts, axis=0))
        )
        between(odd)
    query_live, key_live = (
        jnp.where(live, jnp.where(low_half, ref[:, :LANES], ref[:, LANES:]), 0.0).astype(BF16)
        for ref in (q_ref, k_ref)
    )
    teach_query, teach_key = (
        jnp.where(live, ref[...], 0.0).astype(BF16) for ref in (tq_ref, tk_ref)
    )
    row = lax.broadcasted_iota(jnp.int32, (LANES, LANES), 0)
    col = lax.broadcasted_iota(jnp.int32, (LANES, LANES), 1)
    same = (row < HEAD_DIM) == (col < HEAD_DIM)

    def gram(left, right):
        return jnp.where(same, outer_rows(left, right), 0.0)

    key_key, teach_key_key = gram(key_live, key_live), gram(teach_key, key_live)
    query_query, teach_query_query = gram(query_live, query_live), gram(teach_query, query_live)
    squares = (
        query_query * key_key
        - 2.0 * teach_query_query * teach_key_key
        + gram(teach_query, teach_query) * gram(teach_key, teach_key)
    )
    squares = jnp.sum(squares.reshape(LANES // 8, 8, LANES), axis=0)

    squares = squares * (scaling * scaling * inverse_pairs)
    factor = 2.0 * scaling * scaling * inverse_pairs
    query_term = split_dot(
        jnp.concatenate([query_live, teach_query], axis=1),
        jnp.concatenate([key_key, -teach_key_key], axis=0),
    )
    key_term = split_dot(
        jnp.concatenate([key_live, teach_key], axis=1),
        jnp.concatenate([query_query, -teach_query_query], axis=0),
    )
    (even_q, even_k, even_v), (odd_q, odd_k, odd_v) = pieces
    return (
        (jnp.where(low_half, even_q, odd_q) * scaling + factor * query_term).astype(BF16),
        (jnp.where(low_half, even_k, odd_k) * scaling + factor * key_term).astype(BF16),
        jnp.where(low_half, even_v, odd_v).astype(BF16),
    ), squares


def attend_back_kernel(
    lengths, inverse_pairs, q_ref, k_ref, v_ref, ctx_ref, dctx_ref, tq_ref, tk_ref, grad_ref, sum_ref
):
    refs = (q_ref, k_ref, v_ref, ctx_ref, dctx_ref, tq_ref, tk_ref)
    grads, squares = attend_back_pair(lengths[0], inverse_pairs[0], *refs, lambda odd: None)

    @pl.when(pl.program_id(0) == 0)
    def _():
        sum_ref[...] = jnp.zeros_like(sum_ref)

    sum_ref[...] += squares
    for slot in range(3):
        grad_ref[slot] = grads[slot]


def attend_back(own_length, inverse_pairs, query, key, value, context, grad_context, tq, tk):
    rows = context.shape[0]
    scalar = whole(pltpu.SMEM)
    return pl.pallas_call(
        attend_back_kernel,
        grid=(D // LANES,),
        in_specs=[scalar, scalar]
        + [columns((rows, 2 * LANES))] * 3
        + [columns((rows, LANES))] * 4,
        out_specs=[columns((3, rows, LANES)), fixed((8, LANES))],
        out_shape=[
            jax.ShapeDtypeStruct((3, rows, D), BF16),
            jax.ShapeDtypeStruct((8, LANES), F32),
        ],
        compiler_params=pltpu.CompilerParams(vmem_limit_bytes=vmem_bytes),
        name="attention_backward",
    )(own_length, inverse_pairs, query, key, value, context, grad_context, tq, tk)


def gelu_parts(upper):
    cumulative = 0.5 * (1.0 + lax.erf(upper * (1.0 / math.sqrt(2.0))))
    return cumulative, upper * cumulative


ff_part = 1024


def teacher_kernel(tok_ref, ctx_ref, wo_ref, w1_ref, w2_ref, vec_ref, ub_ref, out_ref):
    vec = vec_ref[...]
    normed, _ = normalize(
        tok_ref[...].astype(F32) + dot(ctx_ref[...], wo_ref[...], 1, 1) + vec[3:4]
    )
    hidden = normed * vec[5:6] + vec[7:8]
    low = hidden.astype(BF16)
    lower = None
    for start in range(0, w1_ref.shape[0], ff_part):
        take = slice(start, start + ff_part)
        _, bent = gelu_parts(dot(low, w1_ref[take], 1, 1) + ub_ref[:, take])
        part = dot(bent.astype(BF16), w2_ref[:, take], 1, 1)
        lower = part if lower is None else lower + part
    final, _ = normalize(hidden + lower + vec[4:5])
    out_ref[...] = final * vec[6:7] + vec[8:9]


def teacher_tail(tokens, context, wo, w1, w2, vectors, up_bias):
    rows, wide = tokens.shape[0], w1.shape[0]
    block = 256
    return pl.pallas_call(
        teacher_kernel,
        grid=(rows // block,),
        in_specs=[
            row_blocks((block, D)),
            row_blocks((block, D)),
            fixed((D, D)),
            fixed((wide, D)),
            fixed((D, wide)),
            fixed(vectors.shape),
            fixed((1, wide)),
        ],
        out_specs=row_blocks((block, D)),
        out_shape=jax.ShapeDtypeStruct((rows, D), F32),
        compiler_params=pltpu.CompilerParams(vmem_limit_bytes=vmem_bytes),
        name="teacher_feed_forward",
    )(tokens, context, wo, w1, w2, vectors, up_bias)


def student_kernel(
    lengths,
    clip,
    tok_ref,
    cot_ref,
    teach_ref,
    ctx_ref,
    wo_ref,
    w1_ref,
    w2_ref,
    vec_ref,
    ub_ref,
    out_ref,
    dctx_ref,
    dao_ref,
    cb_ref,
    du_ref,
    hb_ref,
    df_ref,
    fb_ref,
    res_ref,
    sums_ref,
    upsum_ref,
    slope_ref,
):
    step = pl.program_id(0)
    vec = vec_ref[...]
    wide = w1_ref.shape[0]
    ctx_width, hid_width, act_width = (saturation * clip[at] for at in (1, 2, 3))
    ctx_bent = jnp.tanh(ctx_ref[...] / ctx_width)
    ctx_low = (ctx_width * ctx_bent).astype(BF16)
    cb_ref[...] = ctx_low
    first, first_inverse = normalize(
        tok_ref[...].astype(F32) + dot(ctx_low, wo_ref[...], 1, 1) + vec[3:4]
    )
    hidden = first * vec[5:6] + vec[7:8]
    hid_bent = jnp.tanh(hidden / hid_width)
    hid_low = (hid_width * hid_bent).astype(BF16)
    hb_ref[...] = hid_low
    lower = None
    for start in range(0, wide, ff_part):
        take = slice(start, start + ff_part)
        upper = dot(hid_low, w1_ref[take], 1, 1) + ub_ref[:, take]
        cumulative, bent = gelu_parts(upper)
        act = jnp.tanh(bent / act_width)
        density = jnp.exp(-0.5 * upper * upper) * (1.0 / math.sqrt(2.0 * math.pi))
        slope_ref[:, take] = (1.0 - act * act) * (cumulative + upper * density)
        act_low = (act_width * act).astype(BF16)
        fb_ref[:, take] = act_low
        part = dot(act_low, w2_ref[:, take], 1, 1)
        lower = part if lower is None else lower + part
    second, second_inverse = normalize(hidden + lower + vec[4:5])
    result = second * vec[6:7] + vec[8:9]
    out_ref[...] = result.astype(BF16)
    rows = result.shape[0]
    position = lax.broadcasted_iota(jnp.int32, (rows, D), 0) + step * rows
    gap = jnp.where(position < lengths[0], result - teach_ref[...], 0.0)
    grad_out = cot_ref[...].astype(F32) + gap * (2.0 * hidden_weight)
    grad_second = norm_back(grad_out * vec[6:7], second, second_inverse)
    grad_lower = grad_second.astype(BF16)
    df_ref[...] = grad_lower
    grad_hidden = None
    up_sums = []
    for start in range(0, wide, ff_part):
        take = slice(start, start + ff_part)
        grad_upper = (dot(grad_lower, w2_ref[:, take], 1, 0) * slope_ref[:, take]).astype(BF16)
        du_ref[:, take] = grad_upper
        up_sums.append(jnp.sum(grad_upper.astype(F32), axis=0, keepdims=True))
        part = dot(grad_upper, w1_ref[take], 1, 0)
        grad_hidden = part if grad_hidden is None else grad_hidden + part
    grad_hidden = grad_second + grad_hidden * (1.0 - hid_bent * hid_bent)
    grad_first = norm_back(grad_hidden * vec[5:6], first, first_inverse)
    res_ref[...] = grad_first
    grad_attn = grad_first.astype(BF16)
    dao_ref[...] = grad_attn
    dctx_ref[...] = (
        dot(grad_attn, wo_ref[...], 1, 0) * (1.0 - ctx_bent * ctx_bent)
    ).astype(BF16)

    @pl.when(step == 0)
    def _():
        sums_ref[...] = jnp.zeros_like(sums_ref)
        upsum_ref[...] = jnp.zeros_like(upsum_ref)

    for at, term in enumerate(
        (
            grad_attn.astype(F32),
            grad_lower.astype(F32),
            grad_hidden * first,
            grad_out * second,
            grad_hidden,
            grad_out,
            gap * gap,
        )
    ):
        sums_ref[at : at + 1] += jnp.sum(term, axis=0, keepdims=True)
    upsum_ref[...] += jnp.concatenate(up_sums, axis=1)


def student_middle(
    own_length, clip_scales, tokens, cotangent, teach_out, context, wo, w1, w2, vectors, up_bias
):
    rows, wide = tokens.shape[0], w1.shape[0]
    block = 256
    scalar = whole(pltpu.SMEM)
    narrow_spec, wide_spec = row_blocks((block, D)), row_blocks((block, wide))
    narrow, broad = jax.ShapeDtypeStruct((rows, D), BF16), jax.ShapeDtypeStruct((rows, wide), BF16)
    return pl.pallas_call(
        student_kernel,
        grid=(rows // block,),
        in_specs=[scalar, scalar]
        + [narrow_spec] * 4
        + [
            fixed((D, D)),
            fixed((wide, D)),
            fixed((D, wide)),
            fixed(vectors.shape),
            fixed((1, wide)),
        ],
        out_specs=[narrow_spec] * 4
        + [wide_spec, narrow_spec, narrow_spec, wide_spec, narrow_spec, fixed((8, D)), fixed((1, wide))],
        out_shape=[narrow] * 4
        + [
            broad,
            narrow,
            narrow,
            broad,
            jax.ShapeDtypeStruct((rows, D), F32),
            jax.ShapeDtypeStruct((8, D), F32),
            jax.ShapeDtypeStruct((1, wide), F32),
        ],
        scratch_shapes=[pltpu.VMEM((block, wide), F32)],
        compiler_params=pltpu.CompilerParams(vmem_limit_bytes=vmem_bytes),
        name="student_feed_forward",
    )(own_length, clip_scales, tokens, cotangent, teach_out, context, wo, w1, w2, vectors, up_bias)


def input_kernel(clip, grad_ref, w_ref, low_ref, tok_ref, res_ref, out_ref, dw_ref, sum_ref, acc_ref):
    slot = pl.program_id(0)
    grad = grad_ref[0]
    part = dot(grad, w_ref[0], 1, 0)
    dw_ref[0] = outer_rows(grad, low_ref[...]).astype(dw_ref.dtype)
    sum_ref[0] = jnp.sum(grad.astype(F32), axis=0, keepdims=True)

    @pl.when(slot == 0)
    def _():
        acc_ref[...] = part

    @pl.when(slot > 0)
    def _():
        acc_ref[...] += part

    @pl.when(slot == pl.num_programs(0) - 1)
    def _():
        bent = jnp.tanh(tok_ref[...].astype(F32) / (saturation * clip[0]))
        out_ref[...] = (res_ref[...] + acc_ref[...] * (1.0 - bent * bent)).astype(BF16)


def input_grads(clip_scales, grads, weights, low, tokens, residual):
    rows = tokens.shape[0]
    slotted = lambda *shape: pl.BlockSpec((1,) + shape, lambda i: (i, 0, 0))
    return pl.pallas_call(
        input_kernel,
        grid=(3,),
        in_specs=[
            whole(pltpu.SMEM),
            slotted(rows, D),
            slotted(D, D),
            fixed((rows, D)),
            fixed((rows, D)),
            fixed((rows, D)),
        ],
        out_specs=[fixed((rows, D)), slotted(D, D), slotted(1, D)],
        out_shape=[
            jax.ShapeDtypeStruct((rows, D), BF16),
            jax.ShapeDtypeStruct((3, D, D), BF16),
            jax.ShapeDtypeStruct((3, 1, D), F32),
        ],
        scratch_shapes=[pltpu.VMEM((rows, D), F32)],
        compiler_params=pltpu.CompilerParams(vmem_limit_bytes=vmem_bytes),
        name="input_gradient",
    )(clip_scales, grads, weights, low, tokens, residual)


between_stages = {
    0: ((0, 1),),
    1: ((0, 2), (1, 1), (1, 2)),
    2: ((2, 1), (2, 2)),
    4: ((0, 3),),
    6: ((1, 3),),
    7: ((0, 4), (2, 3)),
    8: ((0, 5),),
    9: ((1, 4), (0, 6)),
    10: ((0, 7), (2, 4), (1, 5)),
    11: ((0, 8), (1, 6), (2, 5)),
}
after_query = ((1, 7), (2, 6))
after_key = ((3, 1), (1, 8), (2, 7))
after_value = ((4, 1), (3, 2), (2, 8))


def latent_rows(latent, grad):
    size = latent.shape[-1]
    scale = jnp.mean(jnp.abs(latent), axis=-1, keepdims=True)
    sign = jnp.where(latent > 0, 1.0, jnp.where(latent < 0, -1.0, 0.0))
    return scale * grad + sign * (jnp.sum(grad * latent, axis=-1, keepdims=True) / size)


def finish_kernel(depth, lengths, scalars, clip, *refs):
    pair_refs, refs = refs[:7], refs[7:]
    dw_refs, refs = refs[:3], refs[3:]
    (w_ref, low_ref, tok_ref, res_ref, sums_ref, upsum_ref, attn_ref, up_ref, down_ref), refs = (
        refs[:9],
        refs[9:],
    )
    (input_ref, attn_grad, up_grad, down_grad, line_grad), refs = refs[:5], refs[5:]
    (grad_ref, square_ref, dwq_ref, dwk_ref, dwv_ref), refs = refs[:5], refs[5:]
    shared, scratch = refs[:5], refs[5:]
    place = Place(depth)
    step = pl.program_id(0)
    last = pl.num_programs(0) - 1
    pairs = D // LANES

    def finish(item, lead, total):
        if item == 0:
            down_grad[...] = latent_rows(down_ref[...], total)
        elif item == 1:
            up_grad[...] = latent_rows(up_ref[...], total)
        else:
            slot = 3 if item == 2 else item - 3
            attn_grad[slot] = latent_rows(attn_ref[slot], total)

    def finish_lines(total):
        line_grad[...] = total

    own = (dwq_ref, dwk_ref, dwv_ref)
    stage = scatter_stage(place, tuple(dw_refs) + own, finish, scratch, 6)
    line_stage = shared_stage(place, finish_lines, shared)

    @pl.when(step == 0)
    def _():
        place.barrier()
        for item in range(3):
            stage(item, 0)
        square_ref[...] = jnp.zeros_like(square_ref)

    @pl.when(step < pairs)
    def _():
        def between(odd):
            for at, stages in between_stages.items():
                if at % 2 == odd:

                    @pl.when(step == at // 2)
                    def _():
                        for item, number in stages:
                            stage(item, number)

        grads, squares = attend_back_pair(lengths[0], scalars[0], *pair_refs, between)
        square_ref[...] += squares
        lanes = pl.ds(pl.multiple_of(step * LANES, LANES), LANES)
        for slot in range(3):
            grad_ref[slot, :, lanes] = grads[slot]

    def weight_grad(slot):
        total = outer_rows(grad_ref[slot], low_ref[...]).astype(BF16)
        rows = dwq_ref.shape[-2]
        for owner in range(D // rows):
            where = (owner // 8, owner // 4 % 2, owner // 2 % 2, owner % 2)
            own[slot][where] = total[owner * rows : (owner + 1) * rows]
        stage(3 + slot, 0)

    def run(stages):
        for item, number in stages:
            stage(item, number)

    @pl.when(step == pairs)
    def _():
        weight_grad(0)
        run(after_query)
        weight_grad(1)
        run(after_key)

    @pl.when(step == last)
    def _():
        weight_grad(2)
        held = shared[0]
        held[0] = jnp.zeros_like(held[0])
        for slot in range(3):
            held[0, slot : slot + 1] = jnp.sum(
                grad_ref[slot].astype(F32), axis=0, keepdims=True
            )
        held[0, 3:9] = sums_ref[0:6]
        held[0, 9:13] = upsum_ref[...]
        held[0, 13:14] = sums_ref[6:7] * scalars[1]
        held[0, 13:14, :LANES] += jnp.sum(square_ref[...], axis=0, keepdims=True)
        line_stage(0)
        run(after_value)
        total = dot(grad_ref[0], w_ref[0], 1, 0)
        line_stage(1)
        run(((3, 3), (5, 1), (4, 2)))
        total += dot(grad_ref[1], w_ref[1], 1, 0)
        line_stage(2)
        run(((3, 4), (5, 2), (4, 3)))
        total += dot(grad_ref[2], w_ref[2], 1, 0)
        bent = jnp.tanh(tok_ref[...].astype(F32) / (saturation * clip[0]))
        input_ref[...] = (res_ref[...] + total * (1.0 - bent * bent)).astype(BF16)
        line_stage(3)
        run(((4, 4), (3, 5), (5, 3)))
        line_stage(4)
        run(((3, 6), (4, 5), (5, 4)))
        line_stage(5)
        run(((3, 7), (4, 6), (5, 5)))
        line_stage(6)
        run(((3, 8), (4, 7), (5, 6), (4, 8), (5, 7), (5, 8)))
        line_stage(7)


def finish_backward(
    own_length,
    inverse_pairs,
    inverse_hidden,
    clip_scales,
    pair_arrays,
    weight_grads,
    attn_w,
    low,
    tokens,
    residual,
    sums,
    up_sums,
    latents,
    narrow,
    wide,
):
    dp, shard = lax.axis_size("dp"), lax.axis_size("shard")
    attn_latent, up_latent, down_latent = latents
    if not tiled_over((dp, shard), narrow):
        grads, squares = attend_back(own_length, inverse_pairs, *pair_arrays)
        input_grad, qkv_weight_grad, qkv_sums = input_grads(
            clip_scales, grads, attn_w[:3], low, tokens, residual
        )
        local_loss = sums[6:7] * inverse_hidden
        local_loss = local_loss + jnp.pad(
            jnp.sum(squares, axis=0, keepdims=True), ((0, 0), (0, D - LANES))
        )
        lines = jnp.concatenate(
            [qkv_sums[:, 0], sums[:6], up_sums.reshape(-1, D), local_loss], axis=0
        )
        lines = lax.psum(lines, AXES)
        down_total, up_total, attn_total = scatter(
            weight_grads[:2]
            + [jnp.concatenate([qkv_weight_grad, weight_grads[2][None].astype(BF16)], axis=0)]
        )
        attn_grad = latent_grad(attn_latent, attn_total)
        up_grad = latent_grad(up_latent, up_total)
        down_grad = latent_grad(down_latent, down_total)
    else:
        depth = dp // 2
        rows = tokens.shape[0]
        dw = [split_rows(grad, depth) for grad in weight_grads]
        own_shape = (depth, 2, 2, 2, narrow, D)
        shapes = [(1,) + grad.shape[-2:] for grad in dw] + [(1, narrow, D)] * 3
        scalar = whole(pltpu.SMEM)
        pairs = D // LANES

        def pair_columns(width):
            return pl.BlockSpec((rows, width), lambda i: (0, jnp.minimum(i, pairs - 1)))

        input_grad, attn_grad, up_grad, down_grad, lines = pl.pallas_call(
            functools.partial(finish_kernel, depth),
            grid=(pairs + 2,),
            in_specs=[scalar] * 3
            + [pair_columns(2 * LANES)] * 3
            + [pair_columns(LANES)] * 4
            + [whole(pl.ANY)] * 3
            + [
                fixed(array_shape)
                for array_shape in (
                    (3, D, D),
                    (rows, D),
                    (rows, D),
                    (rows, D),
                    sums.shape,
                    (up_sums.size // D, D),
                    attn_latent.shape,
                    up_latent.shape,
                    down_latent.shape,
                )
            ],
            out_specs=[
                fixed(array_shape)
                for array_shape in (
                    (rows, D),
                    attn_latent.shape,
                    up_latent.shape,
                    down_latent.shape,
                    (line_rows, D),
                )
            ],
            out_shape=[
                jax.ShapeDtypeStruct((rows, D), BF16),
                jax.ShapeDtypeStruct(attn_latent.shape, F32),
                jax.ShapeDtypeStruct(up_latent.shape, F32),
                jax.ShapeDtypeStruct(down_latent.shape, F32),
                jax.ShapeDtypeStruct((line_rows, D), F32),
            ],
            scratch_shapes=[
                pltpu.VMEM((3, rows, D), BF16),
                pltpu.VMEM((8, LANES), F32),
                pltpu.VMEM(own_shape, BF16),
                pltpu.VMEM(own_shape, BF16),
                pltpu.VMEM(own_shape, BF16),
            ]
            + shared_scratch(depth)
            + scatter_scratch(shapes, [BF16] * 6, depth),
            compiler_params=pltpu.CompilerParams(
                collective_id=1, has_side_effects=True, vmem_limit_bytes=vmem_bytes
            ),
            name="attention_backward_and_sums",
        )(
            own_length,
            jnp.stack([inverse_pairs[0], inverse_hidden]),
            clip_scales,
            *pair_arrays,
            *dw,
            attn_w[:3],
            low,
            tokens,
            residual,
            sums,
            up_sums.reshape(-1, D),
            attn_latent,
            up_latent,
            down_latent,
        )
    at = lax.axis_index(AXES)
    line_total = lax.dynamic_slice_in_dim(lines[:9], at * narrow, narrow, axis=1)
    up_bias_total = lax.dynamic_slice_in_dim(lines[9:13].reshape(-1), at * wide, wide)
    return (
        jnp.sum(lines[13]),
        input_grad,
        attn_grad,
        up_grad,
        down_grad,
        line_total[:5],
        up_bias_total,
        line_total[5:7],
        line_total[7:9],
    )


def on_device(
    tokens,
    teacher_tokens,
    cotangent,
    lengths,
    clip_scales,
    attn_latent,
    up_latent,
    down_latent,
    biases,
    up_bias,
    norm_gains,
    norm_shifts,
    teacher_attn,
    teacher_up,
    teacher_down,
    teacher_biases,
    teacher_up_bias,
    teacher_gains,
    teacher_shifts,
):
    count = lax.axis_size(AXES)
    narrow, wide = biases.shape[1], up_bias.shape[0]
    own_length = lax.dynamic_slice_in_dim(lengths, lax.axis_index(AXES), 1)
    live_float = lengths.astype(F32)
    token_norm = jnp.sum(live_float)
    pair_norm = HEADS * jnp.sum(live_float * live_float)
    inverse_pairs = (1.0 / pair_norm).reshape(1)
    vectors = jnp.concatenate(
        [teacher_biases, teacher_gains, teacher_shifts, biases, norm_gains, norm_shifts], axis=0
    )
    small = jnp.concatenate([vectors.reshape(-1), teacher_up_bias, up_bias])
    small = jnp.pad(small, (0, 8 * D - small.shape[0])).reshape(8, D)
    (
        small_all,
        teach_qkv,
        attn_w,
        teach_wo,
        teach_up,
        teach_down,
        up_w,
        down_w,
    ) = gather(
        [
            small,
            teacher_attn[:3],
            binarize(attn_latent),
            teacher_attn[3],
            teacher_up,
            teacher_down,
            binarize(up_latent),
            binarize(down_latent),
        ],
        ((0, 1), (2, 3), (4,), (5,), (6,), (7,)),
        0,
    )
    small_all = small_all.reshape(count, -1)
    lines = vectors.shape[0]
    vec = (
        small_all[:, : lines * narrow]
        .reshape(count, lines, narrow)
        .transpose(1, 0, 2)
        .reshape(lines, D)
        .astype(F32)
    )
    teach_vec, student_vec = vec[: lines // 2], vec[lines // 2 :]
    at = lines * narrow
    teach_up_bias = small_all[:, at : at + wide].reshape(1, -1).astype(F32)
    student_up_bias = small_all[:, at + wide : at + 2 * wide].reshape(1, -1).astype(F32)
    tq, tk, teach_context = attend(
        False, own_length, clip_scales, teacher_tokens, teach_qkv, teach_vec[:3].reshape(3, 1, D)
    )
    query, key, value, context, x_low = attend(
        True, own_length, clip_scales, tokens, attn_w[:3], student_vec[:3].reshape(3, 1, D)
    )
    teach_out = teacher_tail(
        teacher_tokens, teach_context, teach_wo, teach_up, teach_down, teach_vec, teach_up_bias
    )
    (
        result,
        grad_context,
        grad_attn,
        ctx_low,
        grad_upper,
        hid_low,
        grad_lower,
        act_low,
        residual,
        sums,
        up_sums,
    ) = student_middle(
        own_length,
        clip_scales,
        tokens,
        cotangent,
        teach_out,
        context,
        attn_w[3],
        up_w,
        down_w,
        student_vec,
        student_up_bias,
    )
    down_weight_grad = outer_rows(grad_lower, act_low)
    up_weight_grad = outer_rows(grad_upper, hid_low)
    out_weight_grad = outer_rows(grad_attn, ctx_low)
    weight_grads = [
        grad.astype(BF16) for grad in (down_weight_grad, up_weight_grad, out_weight_grad)
    ]
    return (result,) + finish_backward(
        own_length,
        inverse_pairs,
        1.0 / (D * token_norm),
        clip_scales,
        (query, key, value, context, grad_context, tq, tk),
        weight_grads,
        attn_w,
        x_low,
        tokens,
        residual,
        sums,
        up_sums,
        (attn_latent, up_latent, down_latent),
        narrow,
        wide,
    )


def solution(mesh):
    in_specs = (
        P(("dp", "shard"), None),
        P(("dp", "shard"), None),
        P(("dp", "shard"), None),
        P(),
        P(),
        P(None, ("dp", "shard"), None),
        P(("dp", "shard"), None),
        P(("dp", "shard"), None),
        P(None, ("dp", "shard")),
        P(("dp", "shard")),
        P(None, ("dp", "shard")),
        P(None, ("dp", "shard")),
        P(None, ("dp", "shard"), None),
        P(("dp", "shard"), None),
        P(("dp", "shard"), None),
        P(None, ("dp", "shard")),
        P(("dp", "shard")),
        P(None, ("dp", "shard")),
        P(None, ("dp", "shard")),
    )
    out_specs = (
        P(("dp", "shard"), None),
        P(),
        P(("dp", "shard"), None),
        P(None, ("dp", "shard"), None),
        P(("dp", "shard"), None),
        P(("dp", "shard"), None),
        P(None, ("dp", "shard")),
        P(("dp", "shard")),
        P(None, ("dp", "shard")),
        P(None, ("dp", "shard")),
    )
    return jax.shard_map(
        on_device, mesh=mesh, in_specs=in_specs, out_specs=out_specs, check_vma=False
    )
```

```python
import functools
import math

import jax
import jax.numpy as jnp
from jax import lax
from jax.experimental import pallas as pl
from jax.experimental.pallas import tpu as pltpu
from jax.sharding import PartitionSpec as P

D = 768
HEADS = 12
HEAD_DIM = 64
SEQ_LEN = 1024
AXES = ("dp", "shard")
MESH = pl.DeviceIdType.MESH
F32 = jnp.float32
BF16 = jnp.bfloat16

epsilon = 1e-05
masked_score = -1e30
hidden_weight = 0.25
saturation = 7.5
LANES = 128
log2e = math.log2(math.e)
scaling = HEAD_DIM ** (-0.5)
exponent = scaling * log2e
vmem_bytes = 60 * 1024 * 1024
line_rows = 16


def dot(left, right, left_dim, right_dim):
    return lax.dot_general(
        left, right, (((left_dim,), (right_dim,)), ((), ())), preferred_element_type=F32
    )


def outer_rows(left, right):
    return dot(left, right, 0, 0)


def binarize(latent):
    scale = jnp.mean(jnp.abs(latent), axis=-1, keepdims=True)
    return (scale * jnp.sign(latent)).astype(BF16)


def surrogate(latent):
    return jnp.mean(jnp.abs(latent), axis=-1, keepdims=True) * latent


def latent_grad(latent, grad):
    _, pull = jax.vjp(surrogate, latent)
    return pull(grad)[0]


def normalize(values):
    center = values - jnp.mean(values, axis=-1, keepdims=True)
    inverse = lax.rsqrt(jnp.mean(center * center, axis=-1, keepdims=True) + epsilon)
    return (center * inverse, inverse)


def norm_back(grad_norm, normed, inverse):
    return inverse * (
        grad_norm
        - jnp.mean(grad_norm, axis=-1, keepdims=True)
        - normed * jnp.mean(grad_norm * normed, axis=-1, keepdims=True)
    )


def whole(memory=pltpu.VMEM):
    return pl.BlockSpec(memory_space=memory)


def fixed(shape):
    return pl.BlockSpec(shape, lambda *_: (0,) * len(shape), pipeline_mode=pl.Buffered(1))


def columns(shape):
    return pl.BlockSpec(shape, lambda i: (0,) * (len(shape) - 1) + (i,))


def row_blocks(shape):
    return pl.BlockSpec(shape, lambda i: (i,) + (0,) * (len(shape) - 1))


class Place:
    def __init__(self, depth):
        self.depth = depth
        dp, shard = lax.axis_index("dp"), lax.axis_index("shard")
        z, y = dp // 2, lax.rem(dp, 2)
        x, core = shard // 2, lax.rem(shard, 2)
        self.z, self.y, self.x, self.core = z, y, x, core

        def device(z_at, y_at, x_at, core_at):
            return (z_at * 2 + y_at, x_at * 2 + core_at)

        self.above = device(jnp.minimum(z + 1, depth - 1), y, x, core)
        self.below = device(jnp.maximum(z - 1, 0), y, x, core)
        one = (lax.rem(y + 1 - core, 2), lax.rem(x + core, 2))
        two = (lax.rem(y + core, 2), lax.rem(x + 1 - core, 2))
        self.pieces = ((y, x), one, two, (1 - y, 1 - x))
        self.first, self.second = device(z, *one, core), device(z, *two, core)
        self.sibling = device(z, y, x, 1 - core)

    def barrier(self):
        semaphore = pltpu.get_barrier_semaphore()
        for partner in (self.first, self.second, self.sibling):
            pl.semaphore_signal(semaphore, inc=1, device_id=partner, device_id_type=MESH)

        @pl.when(self.z < self.depth - 1)
        def _():
            pl.semaphore_signal(semaphore, inc=1, device_id=self.above, device_id_type=MESH)

        @pl.when(self.z > 0)
        def _():
            pl.semaphore_signal(semaphore, inc=1, device_id=self.below, device_id_type=MESH)

        pl.semaphore_wait(
            semaphore, 3 + jnp.minimum(self.z, 1) + jnp.minimum(self.depth - 1 - self.z, 1)
        )


def remote(source, target, send_sem, recv_sem, device):
    return pltpu.make_async_remote_copy(
        src_ref=source,
        dst_ref=target,
        send_sem=send_sem,
        recv_sem=recv_sem,
        device_id=device,
        device_id_type=MESH,
    )


def tiled_over(mesh_sizes, rows):
    return mesh_sizes == (8, 4) and rows % 8 == 0


def gather_scratch(chunks, depth):
    dma = pltpu.SemaphoreType.DMA
    sizes = (len(chunks), max(len(chunk) for chunk in chunks))
    return [
        dma(sizes + (depth - 1, 2)),
        dma(sizes + (depth - 1, 2)),
        dma(sizes + (3 + max(depth, 4),)),
        dma(sizes + (3 + max(depth, 4),)),
        dma(sizes),
    ]


def gather_stage(place, ins, outs, leads, chunks, late, sems):
    line_send, line_recv, pair_send, pair_recv, own_sem = sems
    depth, z, y, x, core = place.depth, place.z, place.y, place.x, place.core

    def slot(item, *index):
        return outs[item].at[((slice(None),) if leads[item] > 1 else ()) + index]

    def group(chunk, item, z_at):
        if chunk in late:
            return slot(item, z_at, slice(None), slice(None), core)
        return slot(item, z_at, y, x, core)

    def line_copy(chunk, at, item, turn, upward):
        if upward:
            owner, target = jnp.maximum(z - (turn - 1), 0), place.above
        else:
            owner, target = jnp.minimum(z + (turn - 1), depth - 1), place.below
        block = group(chunk, item, owner)
        where = (chunk, at, turn - 1, int(upward))
        return remote(block, block, line_send.at[where], line_recv.at[where], target)

    def sends(turn, upward):
        if upward:
            return (z - (turn - 1) >= 0) & (z < depth - 1)
        return (z + (turn - 1) <= depth - 1) & (z > 0)

    def receives(turn, upward):
        return (z - turn >= 0) if upward else (z + turn <= depth - 1)

    def own_copy(chunk, at, item):
        return pltpu.make_async_copy(
            ins[item], slot(item, z, y, x, core), own_sem.at[chunk, at]
        )

    plans = (
        (0, place.first),
        (0, place.second),
        (1, place.second),
        (0, place.sibling),
        (1, place.sibling),
        (2, place.sibling),
        (3, place.sibling),
    )

    def pair_copy(chunk, at, item, plan):
        piece, target = plans[plan]
        z_at = z if chunk in late else slice(None)
        block = slot(item, z_at, *place.pieces[piece], core)
        where = (chunk, at, plan)
        return remote(block, block, pair_send.at[where], pair_recv.at[where], target)

    def each(chunk, action):
        for at, item in enumerate(chunks[chunk]):
            action(at, item)

    def line_start(chunk, turn):
        for upward in (True, False):

            @pl.when(sends(turn, upward))
            def _():
                each(chunk, lambda at, item: line_copy(chunk, at, item, turn, upward).start())

    def line_received(chunk, turn):
        for upward in (True, False):

            @pl.when(receives(turn, upward))
            def _():
                each(chunk, lambda at, item: line_copy(chunk, at, item, turn, upward).wait_recv())

    def line_sent(chunk, turn):
        for upward in (True, False):

            @pl.when(sends(turn, upward))
            def _():
                each(chunk, lambda at, item: line_copy(chunk, at, item, turn, upward).wait_send())

    def start(chunk, *plan_list):
        for plan in plan_list:
            each(chunk, lambda at, item: pair_copy(chunk, at, item, plan).start())

    def received(chunk, *plan_list):
        for plan in plan_list:
            each(chunk, lambda at, item: pair_copy(chunk, at, item, plan).wait_recv())

    def plane_copy(chunk, at, item, z_at):
        block = group(chunk, item, z_at)
        where = (chunk, at, 3 + z_at)
        return remote(block, block, pair_send.at[where], pair_recv.at[where], place.sibling)

    def late_stage(chunk, number):
        if number == 0:
            each(chunk, lambda at, item: own_copy(chunk, at, item).wait())
            start(chunk, 0, 1)
        elif number == 1:
            received(chunk, 0)
            start(chunk, 2)
        elif number == 2:
            received(chunk, 1, 2)
            line_start(chunk, 1)
            each(chunk, lambda at, item: plane_copy(chunk, at, item, z).start())
        elif number < depth + 2:
            turn = number - 2
            line_received(chunk, turn)
            if turn < depth - 1:
                line_start(chunk, turn + 1)
            for upward in (True, False):
                owner = jnp.maximum(z - turn, 0) if upward else jnp.minimum(z + turn, depth - 1)

                @pl.when(receives(turn, upward))
                def _():
                    each(chunk, lambda at, item: plane_copy(chunk, at, item, owner).start())
        elif number == depth + 2:
            for z_at in range(depth):
                each(chunk, lambda at, item: plane_copy(chunk, at, item, z_at).wait_recv())

    def stage(chunk, number):
        if chunk in late:
            late_stage(chunk, number)
        elif number == 0:
            each(chunk, lambda at, item: own_copy(chunk, at, item).wait())
            line_start(chunk, 1)
        elif number < depth:
            line_received(chunk, number)
            if number < depth - 1:
                line_start(chunk, number + 1)
            else:
                start(chunk, 0, 1, 3)
        elif number == depth:
            received(chunk, 0)
            start(chunk, 2, 4)
        elif number == depth + 1:
            received(chunk, 1)
            start(chunk, 5)
        elif number == depth + 2:
            received(chunk, 2)
            start(chunk, 6)
        else:
            received(chunk, 3, 4, 5, 6)

    def sent(chunk):
        for turn in range(1, depth):
            line_sent(chunk, turn)
        for plan in range(3 if chunk in late else 7):
            each(chunk, lambda at, item: pair_copy(chunk, at, item, plan).wait_send())
        if chunk in late:
            for z_at in range(depth):
                each(chunk, lambda at, item: plane_copy(chunk, at, item, z_at).wait_send())

    def begin(begun):
        for chunk in begun:
            each(chunk, lambda at, item: own_copy(chunk, at, item).start())

    return begin, stage, sent


def gathered(results):
    return [
        result.reshape(result.shape[:-6] + (-1, result.shape[-1])) for result in results
    ]


def gather(arrays):
    return [lax.all_gather(array, AXES, axis=array.ndim - 2, tiled=True) for array in arrays]


def scatter_scratch(shapes, dtypes, depth):
    dma = pltpu.SemaphoreType.DMA
    scratch = []
    for shape, dtype in zip(shapes, dtypes):
        lead, rows, cols = shape
        block = (depth, lead, rows, cols)
        scratch += [
            pltpu.VMEM((4,) + block, dtype),
            pltpu.VMEM((4,) + block, dtype),
            pltpu.VMEM((3,) + block, dtype),
            pltpu.VMEM((2,) + block, dtype),
        ]
    count = len(shapes)
    return scratch + [
        dma((count, 4)),
        dma((count, 7)),
        dma((count, 7)),
        dma((count, depth, 2)),
        dma((count, depth, 2)),
    ]


def scatter_stage(place, ins, finish, scratch, count):
    depth, z, core = place.depth, place.z, place.core
    own_sem, pair_send, pair_recv, line_send, line_recv = scratch[4 * count :]

    def buffers(item):
        return scratch[4 * item : 4 * item + 4]

    def source(item, piece, lead, side):
        index = (slice(None),) + place.pieces[piece] + (side,)
        ref = ins[item]
        return ref.at[((lead,) if ref.shape[:-6] else ()) + index]

    def leads(item):
        return range(buffers(item)[0].shape[2])

    def own_copy(item, piece, lead):
        held = buffers(item)[0]
        return pltpu.make_async_copy(
            source(item, piece, lead, core), held.at[piece, :, lead], own_sem.at[item, piece]
        )

    names = (0, 2, 1, 3)

    def core_copy(item, piece, lead):
        arrived = buffers(item)[1]
        name = names[piece]
        return remote(
            source(item, piece, lead, 1 - core),
            arrived.at[name, :, lead],
            pair_send.at[item, piece],
            pair_recv.at[item, name],
            place.sibling,
        )

    def core_wait(item, piece):
        arrived = buffers(item)[1]
        block = arrived.at[piece]
        remote(
            block, block, pair_send.at[item, piece], pair_recv.at[item, piece], place.sibling
        ).wait_recv()

    def chip_copy(item, plan):
        held, _, arrived, _ = buffers(item)
        piece, target = ((2, place.second), (3, place.second), (1, place.first))[plan]
        return remote(
            held.at[piece],
            arrived.at[plan],
            pair_send.at[item, 4 + plan],
            pair_recv.at[item, 4 + plan],
            target,
        )

    def line_copy(item, owner, upward, fresh):
        held, _, _, arrived = buffers(item)
        block = arrived.at[int(upward), owner]
        where = (item, owner, int(upward))
        return remote(
            held.at[0, owner] if fresh else block,
            block,
            line_send.at[where],
            line_recv.at[where],
            place.above if upward else place.below,
        )

    def add(target, *others):
        def one(at):
            total = target[at].astype(F32)
            for other in others:
                total = total + other[at].astype(F32)
            target[at] = total.astype(target.dtype)

        for first in range(target.shape[0]):
            for second in range(target.shape[1]):
                one((first, second))

    def add_block(target, other):
        for lead in range(target.shape[0]):
            target[lead] = (target[lead].astype(F32) + other[lead].astype(F32)).astype(
                target.dtype
            )

    def merge(item, piece):
        held, arrived, _, _ = buffers(item)
        block = held.at[piece]
        pltpu.make_async_copy(block, block, own_sem.at[item, piece]).wait()
        core_wait(item, piece)
        add(block, arrived.at[piece])

    def line_turn(item, turn, upward):
        held, _, _, arrived = buffers(item)
        at = turn if upward else depth - 1 - turn
        beyond = range(at + 1, depth) if upward else range(at)

        @pl.when(z == at)
        def _():
            for owner in sorted(beyond, key=lambda owner: -abs(owner - at)):
                if turn:
                    line_copy(item, owner, upward, False).wait_recv()
                    add_block(arrived.at[int(upward), owner], held.at[0, owner])
                line_copy(item, owner, upward, not turn).start()
            if turn:
                line_copy(item, at, upward, False).wait_recv()

    def stage(item, number):
        held, _, arrived, line = buffers(item)
        if number == 0:
            for piece in (3, 1, 2, 0):
                for lead in leads(item):
                    core_copy(item, piece, lead).start()
            for piece in (2, 3, 1, 0):
                for lead in leads(item):
                    own_copy(item, piece, lead).start()
        elif number == 1:
            for piece, plan in ((3, 1), (2, 0)):
                merge(item, piece)
                chip_copy(item, plan).start()
        elif number == 2:
            merge(item, 1)
            merge(item, 0)
        elif number == 3:
            chip_copy(item, 1).wait_recv()
            add(held.at[1], arrived.at[1])
            chip_copy(item, 2).start()
        elif number == 4:
            chip_copy(item, 0).wait_recv()
            chip_copy(item, 2).wait_recv()
            add(held.at[0], arrived.at[0], arrived.at[2])
            for upward in (True, False):
                line_turn(item, 0, upward)
        elif number < 4 + depth:
            for upward in (True, False):
                line_turn(item, number - 4, upward)
        else:
            for lead in leads(item):
                total = held[0, z, lead].astype(F32)
                for upward, near in ((1, z > 0), (0, z < depth - 1)):
                    total = jnp.where(near, total + line[upward, z, lead].astype(F32), total)
                finish(item, lead, total)

            for piece in range(4):
                block = buffers(item)[1].at[piece]
                remote(
                    block, block, pair_send.at[item, piece], pair_recv.at[item, piece], place.sibling
                ).wait_send()
            for plan in range(3):
                chip_copy(item, plan).wait_send()
            for upward in (True, False):
                for owner in range(depth):

                    @pl.when((z < owner) if upward else (z > owner))
                    def _():
                        line_copy(item, owner, upward, False).wait_send()

    return stage


def split_rows(array, depth):
    return array.reshape(array.shape[:-2] + (depth, 2, 2, 2, -1, array.shape[-1]))


def shared_scratch(depth, rows, dtype):
    dma = pltpu.SemaphoreType.DMA
    return [
        pltpu.VMEM((4, rows, D), dtype),
        pltpu.VMEM((5, rows, D), dtype),
        pltpu.VMEM((2, rows, D), dtype),
        dma((5,)),
        dma((5,)),
    ]


def shared_stage(place, finish, scratch):
    held, arrived, line, send_sem, recv_sem = scratch
    depth, z = place.depth, place.z
    partners = (place.sibling, place.second, place.first)

    def pair_copy(at):
        return remote(
            held.at[at], arrived.at[at], send_sem.at[at], recv_sem.at[at], partners[at]
        )

    def line_copy(upward, fresh):
        at = 3 + int(upward)
        return remote(
            held.at[3] if fresh else line.at[int(upward)],
            arrived.at[at],
            send_sem.at[at],
            recv_sem.at[at],
            place.above if upward else place.below,
        )

    def line_turn(turn, upward):
        at = turn if upward else depth - 1 - turn

        @pl.when(z == at)
        def _():
            if turn:
                line_copy(upward, False).wait_recv()
            if turn < depth - 1:
                if turn:
                    line[int(upward)] = held[3] + arrived[3 + int(upward)]
                line_copy(upward, not turn).start()

    def stage(number):
        if number == 0:
            pair_copy(0).start()
        elif number < 4:
            pair_copy(number - 1).wait_recv()
            held[number] = held[number - 1] + arrived[number - 1]
            if number < 3:
                pair_copy(number).start()
            else:
                for upward in (True, False):
                    line_turn(0, upward)
        elif number < 3 + depth:
            for upward in (True, False):
                line_turn(number - 3, upward)
        else:
            total = held[3]
            total = jnp.where(z > 0, total + arrived[4], total)
            finish(jnp.where(z < depth - 1, total + arrived[3], total))
            for at in range(3):
                pair_copy(at).wait_send()
            for upward in (True, False):

                @pl.when((z < depth - 1) if upward else (z > 0))
                def _():
                    line_copy(upward, False).wait_send()

    return stage


def scatter(arrays):
    return [
        lax.psum_scatter(array.astype(F32), AXES, scatter_dimension=array.ndim - 2, tiled=True)
        for array in arrays
    ]


def lane_index(rows):
    return lax.broadcasted_iota(jnp.int32, (rows, LANES), 1)


def halves(lane, odd):
    own = (lane >= HEAD_DIM) if odd else (lane < HEAD_DIM)
    other = lane if odd else lane - HEAD_DIM
    return own, other


def three_parts(values):
    high = values.astype(BF16).astype(F32)
    rest = values - high
    middle = rest.astype(BF16).astype(F32)
    return high, middle, rest - middle


def with_terms(own, other, values, terms):
    result = jnp.zeros_like(values)
    for at, term in enumerate(terms):
        result = jnp.where(other == at, term, result)
    return jnp.where(own, values, result)


def attend_quad(student, length, inputs, weights, biases, targets, between):
    q_ref, k_ref, v_ref, ctx_ref = targets
    rows = inputs.shape[0]
    lane = lane_index(rows)
    position = lax.broadcasted_iota(jnp.int32, (rows, LANES), 0)
    hidden_key = jnp.where(position < length, 0.0, masked_score)
    queries, keys, values = (
        (dot(inputs, weight, 1, 1) + bias).astype(BF16) for weight, bias in zip(weights, biases)
    )
    if not student:
        q_ref[...] = queries
        k_ref[...] = keys
    block = 512
    for pair in range(2):
        lanes = slice(pair * LANES, (pair + 1) * LANES)
        query, key, value = (
            array[:, lanes].astype(F32) for array in (queries, keys, values)
        )
        parts = []
        for odd in range(2):
            own, other = halves(lane, odd)
            place = slice((pair * 2 + odd) * LANES, (pair * 2 + odd + 1) * LANES)
            query_full = with_terms(own, other, query, (0.0, 0.0, 0.0, 1.0)).astype(BF16)
            key_full = with_terms(own, other, key, (1.0, 1.0, 1.0, hidden_key)).astype(BF16)
            value_full = with_terms(own, other, value, (1.0, 1.0, 1.0)).astype(BF16)
            if student:
                k_ref[:, place] = key_full
                v_ref[:, place] = value_full
            found = []
            for start in range(0, rows, block):
                take = slice(start, start + block)
                scores = dot(query_full[take], key_full, 1, 1)
                top = jnp.max(scores, axis=1, keepdims=True)
                expo = jnp.exp2((scores - top) * exponent).astype(BF16)
                mixed = dot(expo, value_full, 1, 0)
                at = 0 if odd else HEAD_DIM
                total = mixed[:, at : at + 1]
                found.append(mixed / total)
                if student:
                    logsum = top + jnp.log(total) / scaling
                    q_ref[take, place] = with_terms(
                        own[take],
                        other[take],
                        query[take],
                        tuple(-part for part in three_parts(logsum)) + (1.0,),
                    ).astype(BF16)
            parts.append(jnp.concatenate(found, axis=0))
            between(pair * 2 + odd)
        context = jnp.where(lane < HEAD_DIM, parts[0], parts[1])
        ctx_ref[:, lanes] = context.astype(ctx_ref.dtype)


def attend_kernel(student, lengths, *refs):
    if student:
        clip, x_ref, w_ref, b_ref, q_ref, k_ref, v_ref, ctx_ref, low_ref = refs

        @pl.when(pl.program_id(0) == 0)
        def _():
            width = saturation * clip[0]
            low_ref[...] = (width * jnp.tanh(x_ref[...].astype(F32) / width)).astype(BF16)

        x_ref = low_ref
        targets = (q_ref, k_ref, v_ref, ctx_ref)
    else:
        x_ref, w_ref, b_ref, q_ref, k_ref, ctx_ref = refs
        targets = (q_ref, k_ref, None, ctx_ref)
    attend_quad(
        student,
        lengths[0],
        x_ref[...],
        [w_ref[slot] for slot in range(3)],
        [b_ref[slot] for slot in range(3)],
        targets,
        lambda head: None,
    )


def attend(student, own_length, clip_scales, inputs, weights, bias):
    rows = inputs.shape[0]
    wide = 4 * LANES
    narrow = 2 * LANES
    scalar = whole(pltpu.SMEM)
    in_specs = [scalar] + ([scalar] if student else [])
    in_specs += [
        fixed((rows, D)),
        pl.BlockSpec((3, narrow, D), lambda i: (0, i, 0)),
        columns((3, 1, narrow)),
    ]
    if student:
        out_shape = [jax.ShapeDtypeStruct((rows, 2 * D), BF16)] * 3 + [
            jax.ShapeDtypeStruct((rows, D), F32),
            jax.ShapeDtypeStruct((rows, D), BF16),
        ]
        out_specs = [columns((rows, wide))] * 3 + [columns((rows, narrow)), fixed((rows, D))]
        args = (own_length, clip_scales, inputs, weights, bias)
    else:
        out_shape = [jax.ShapeDtypeStruct((rows, D), BF16)] * 3
        out_specs = [columns((rows, narrow))] * 3
        args = (own_length, inputs, weights, bias)
    return pl.pallas_call(
        functools.partial(attend_kernel, student),
        grid=(D // narrow,),
        in_specs=in_specs,
        out_specs=out_specs,
        out_shape=out_shape,
        compiler_params=pltpu.CompilerParams(vmem_limit_bytes=vmem_bytes),
        name="student_attention" if student else "teacher_attention",
    )(*args)


def split_dot(left, right):
    high = right.astype(BF16)
    low = (right - high.astype(F32)).astype(BF16)
    return dot(left, high, 1, 0) + dot(left, low, 1, 0)


def attend_back_pair(length, inverse_pairs, q_ref, k_ref, v_ref, ctx_ref, dctx_ref, tq_ref, tk_ref, between):
    rows = ctx_ref.shape[0]
    lane = lane_index(rows)
    position = lax.broadcasted_iota(jnp.int32, (rows, LANES), 0)
    live = position < length
    low_half = lane < HEAD_DIM
    grad_context = dctx_ref[...].astype(F32)
    product = grad_context * ctx_ref[...]
    block = 512
    pieces = []
    for odd in range(2):
        own, other = halves(lane, odd)
        place = slice(odd * LANES, (odd + 1) * LANES)
        query, key, value = q_ref[:, place], k_ref[:, place], v_ref[:, place]
        weighted = jnp.sum(jnp.where(own, product, 0.0), axis=1, keepdims=True)
        grad_full = with_terms(
            own, other, grad_context, tuple(-part for part in three_parts(weighted))
        ).astype(BF16)
        grad_query = None
        key_parts, value_parts = [], []
        for start in range(0, rows, block):
            take = slice(start, start + block)
            probs = jnp.exp2(dot(key[take], query, 1, 1) * exponent)
            grad_scores = (probs * dot(value[take], grad_full, 1, 1)).astype(BF16)
            value_parts.append(dot(probs.astype(BF16), grad_full, 1, 0))
            key_parts.append(dot(grad_scores, query, 1, 0))
            part = dot(grad_scores, key[take], 0, 0)
            grad_query = part if grad_query is None else grad_query + part
        pieces.append(
            (grad_query, jnp.concatenate(key_parts, axis=0), jnp.concatenate(value_parts, axis=0))
        )
        between(odd)
    query_live, key_live = (
        jnp.where(live, jnp.where(low_half, ref[:, :LANES], ref[:, LANES:]), 0.0).astype(BF16)
        for ref in (q_ref, k_ref)
    )
    teach_query, teach_key = (
        jnp.where(live, ref[...], 0.0).astype(BF16) for ref in (tq_ref, tk_ref)
    )
    row = lax.broadcasted_iota(jnp.int32, (LANES, LANES), 0)
    col = lax.broadcasted_iota(jnp.int32, (LANES, LANES), 1)
    same = (row < HEAD_DIM) == (col < HEAD_DIM)

    def gram(left, right):
        return jnp.where(same, outer_rows(left, right), 0.0)

    key_key, teach_key_key = gram(key_live, key_live), gram(teach_key, key_live)
    query_query, teach_query_query = gram(query_live, query_live), gram(teach_query, query_live)
    squares = (
        query_query * key_key
        - 2.0 * teach_query_query * teach_key_key
        + gram(teach_query, teach_query) * gram(teach_key, teach_key)
    )
    squares = jnp.sum(squares.reshape(LANES // 8, 8, LANES), axis=0)

    squares = squares * (scaling * scaling * inverse_pairs)
    factor = 2.0 * scaling * scaling * inverse_pairs
    query_term = split_dot(
        jnp.concatenate([query_live, teach_query], axis=1),
        jnp.concatenate([key_key, -teach_key_key], axis=0),
    )
    key_term = split_dot(
        jnp.concatenate([key_live, teach_key], axis=1),
        jnp.concatenate([query_query, -teach_query_query], axis=0),
    )
    (even_q, even_k, even_v), (odd_q, odd_k, odd_v) = pieces
    return (
        (jnp.where(low_half, even_q, odd_q) * scaling + factor * query_term).astype(BF16),
        (jnp.where(low_half, even_k, odd_k) * scaling + factor * key_term).astype(BF16),
        jnp.where(low_half, even_v, odd_v).astype(BF16),
    ), squares


def attend_back_kernel(
    lengths, inverse_pairs, q_ref, k_ref, v_ref, ctx_ref, dctx_ref, tq_ref, tk_ref, grad_ref, sum_ref
):
    refs = (q_ref, k_ref, v_ref, ctx_ref, dctx_ref, tq_ref, tk_ref)
    grads, squares = attend_back_pair(lengths[0], inverse_pairs[0], *refs, lambda odd: None)

    @pl.when(pl.program_id(0) == 0)
    def _():
        sum_ref[...] = jnp.zeros_like(sum_ref)

    sum_ref[...] += squares
    for slot in range(3):
        grad_ref[slot] = grads[slot]


def attend_back(own_length, inverse_pairs, query, key, value, context, grad_context, tq, tk):
    rows = context.shape[0]
    scalar = whole(pltpu.SMEM)
    return pl.pallas_call(
        attend_back_kernel,
        grid=(D // LANES,),
        in_specs=[scalar, scalar]
        + [columns((rows, 2 * LANES))] * 3
        + [columns((rows, LANES))] * 4,
        out_specs=[columns((3, rows, LANES)), fixed((8, LANES))],
        out_shape=[
            jax.ShapeDtypeStruct((3, rows, D), BF16),
            jax.ShapeDtypeStruct((8, LANES), F32),
        ],
        compiler_params=pltpu.CompilerParams(vmem_limit_bytes=vmem_bytes),
        name="attention_backward",
    )(own_length, inverse_pairs, query, key, value, context, grad_context, tq, tk)


def gelu_parts(upper):
    cumulative = 0.5 * (1.0 + lax.erf(upper * (1.0 / math.sqrt(2.0))))
    return cumulative, upper * cumulative


ff_part = D


def teacher_rows(tokens, context, wo_ref, up_part, w2_ref, vec, up_bias, out_ref, between):
    normed, _ = normalize(tokens.astype(F32) + dot(context, wo_ref[...], 1, 1) + vec[3:4])
    hidden = normed * vec[5:6] + vec[7:8]
    low = hidden.astype(BF16)
    lower = None
    for at in range(w2_ref.shape[1] // ff_part):
        take = slice(at * ff_part, (at + 1) * ff_part)
        _, bent = gelu_parts(dot(low, up_part(at), 1, 1) + up_bias[at : at + 1])
        part = dot(bent.astype(BF16), w2_ref[:, take], 1, 1)
        lower = part if lower is None else lower + part
        between(at)
    final, _ = normalize(hidden + lower + vec[4:5])
    out_ref[...] = final * vec[6:7] + vec[8:9]


def teacher_kernel(tok_ref, ctx_ref, wo_ref, w1_ref, w2_ref, vec_ref, ub_ref, out_ref):
    teacher_rows(
        tok_ref[...],
        ctx_ref[...],
        wo_ref,
        lambda at: w1_ref[at * ff_part : (at + 1) * ff_part],
        w2_ref,
        vec_ref[...],
        ub_ref[...],
        out_ref,
        lambda at: None,
    )


def teacher_tail(tokens, context, wo, w1, w2, vectors, up_bias):
    rows, wide = tokens.shape[0], w1.shape[0]
    block = 256
    return pl.pallas_call(
        teacher_kernel,
        grid=(rows // block,),
        in_specs=[
            row_blocks((block, D)),
            row_blocks((block, D)),
            fixed((D, D)),
            fixed((wide, D)),
            fixed((D, wide)),
            fixed(vectors.shape),
            fixed(up_bias.shape),
        ],
        out_specs=row_blocks((block, D)),
        out_shape=jax.ShapeDtypeStruct((rows, D), F32),
        compiler_params=pltpu.CompilerParams(vmem_limit_bytes=vmem_bytes),
        name="teacher_feed_forward",
    )(tokens, context, wo, w1, w2, vectors, up_bias)


def student_kernel(
    row_steps,
    lengths,
    clip,
    tok_ref,
    cot_ref,
    teach_ref,
    ctx_ref,
    wo_ref,
    w1_ref,
    w2_ref,
    vec_ref,
    out_ref,
    dctx_ref,
    res_ref,
    sums_ref,
    upsum_ref,
    dw2_ref,
    dw1_ref,
    dwo_ref,
    df_all,
    fb_all,
    du_all,
    hb_all,
    dao_all,
    cb_all,
    slope_ref,
):
    step = pl.program_id(0)
    down_steps, up_steps = D // dw2_ref.shape[0], w1_ref.shape[0] // dw1_ref.shape[0]

    @pl.when(step < row_steps)
    def _():
        rows = out_ref.shape[0]
        here = pl.ds(pl.multiple_of(step * rows, rows), rows)
        student_rows(
            step,
            lengths,
            clip,
            tok_ref,
            cot_ref,
            teach_ref,
            ctx_ref,
            wo_ref,
            w1_ref,
            w2_ref,
            vec_ref[9:18],
            vec_ref[22:26],
            out_ref,
            dctx_ref,
            *(ref.at[here] for ref in (dao_all, cb_all, du_all, hb_all, df_all, fb_all)),
            res_ref,
            sums_ref,
            upsum_ref,
            slope_ref,
        )

    def weight_grad(target, left, right, at):
        width = target.shape[0]
        lanes = pl.ds(pl.multiple_of(at * width, width), width)
        target[...] = outer_rows(left[:, lanes], right[...]).astype(BF16)

    @pl.when((step >= row_steps) & (step < row_steps + down_steps))
    def _():
        weight_grad(dw2_ref, df_all, fb_all, step - row_steps)

    @pl.when((step >= row_steps + down_steps) & (step < row_steps + down_steps + up_steps))
    def _():
        weight_grad(dw1_ref, du_all, hb_all, step - row_steps - down_steps)

    @pl.when(step == row_steps + down_steps + up_steps)
    def _():
        dwo_ref[...] = outer_rows(dao_all[...], cb_all[...]).astype(BF16)


def student_rows(
    step,
    lengths,
    clip,
    tok_ref,
    cot_ref,
    teach_ref,
    ctx_ref,
    wo_ref,
    w1_ref,
    w2_ref,
    vec,
    up_bias,
    out_ref,
    dctx_ref,
    dao_ref,
    cb_ref,
    du_ref,
    hb_ref,
    df_ref,
    fb_ref,
    res_ref,
    sums_ref,
    upsum_ref,
    slope_ref,
):
    wide = w1_ref.shape[0]
    ctx_width, hid_width, act_width = (saturation * clip[at] for at in (1, 2, 3))
    ctx_bent = jnp.tanh(ctx_ref[...] / ctx_width)
    ctx_low = (ctx_width * ctx_bent).astype(BF16)
    cb_ref[...] = ctx_low
    first, first_inverse = normalize(
        tok_ref[...].astype(F32) + dot(ctx_low, wo_ref[...], 1, 1) + vec[3:4]
    )
    hidden = first * vec[5:6] + vec[7:8]
    hid_bent = jnp.tanh(hidden / hid_width)
    hid_low = (hid_width * hid_bent).astype(BF16)
    hb_ref[...] = hid_low
    lower = None
    for at in range(wide // ff_part):
        take = slice(at * ff_part, (at + 1) * ff_part)
        upper = dot(hid_low, w1_ref[take], 1, 1) + up_bias[at : at + 1]
        cumulative, bent = gelu_parts(upper)
        act = jnp.tanh(bent / act_width)
        density = jnp.exp(-0.5 * upper * upper) * (1.0 / math.sqrt(2.0 * math.pi))
        slope_ref[:, take] = (1.0 - act * act) * (cumulative + upper * density)
        act_low = (act_width * act).astype(BF16)
        fb_ref[:, take] = act_low
        part = dot(act_low, w2_ref[:, take], 1, 1)
        lower = part if lower is None else lower + part
    second, second_inverse = normalize(hidden + lower + vec[4:5])
    result = second * vec[6:7] + vec[8:9]
    out_ref[...] = result.astype(BF16)
    rows = result.shape[0]
    position = lax.broadcasted_iota(jnp.int32, (rows, D), 0) + step * rows
    gap = jnp.where(position < lengths[0], result - teach_ref[...], 0.0)
    grad_out = cot_ref[...].astype(F32) + gap * (2.0 * hidden_weight)
    grad_second = norm_back(grad_out * vec[6:7], second, second_inverse)
    grad_lower = grad_second.astype(BF16)
    df_ref[...] = grad_lower
    grad_hidden = None
    up_sums = []
    for at in range(wide // ff_part):
        take = slice(at * ff_part, (at + 1) * ff_part)
        grad_upper = (dot(grad_lower, w2_ref[:, take], 1, 0) * slope_ref[:, take]).astype(BF16)
        du_ref[:, take] = grad_upper
        up_sums.append(jnp.sum(grad_upper.astype(F32), axis=0, keepdims=True))
        part = dot(grad_upper, w1_ref[take], 1, 0)
        grad_hidden = part if grad_hidden is None else grad_hidden + part
    grad_hidden = grad_second + grad_hidden * (1.0 - hid_bent * hid_bent)
    grad_first = norm_back(grad_hidden * vec[5:6], first, first_inverse)
    res_ref[...] = grad_first
    grad_attn = grad_first.astype(BF16)
    dao_ref[...] = grad_attn
    dctx_ref[...] = (
        dot(grad_attn, wo_ref[...], 1, 0) * (1.0 - ctx_bent * ctx_bent)
    ).astype(BF16)

    @pl.when(step == 0)
    def _():
        sums_ref[...] = jnp.zeros_like(sums_ref)
        upsum_ref[...] = jnp.zeros_like(upsum_ref)

    for at, term in enumerate(
        (
            grad_attn.astype(F32),
            grad_lower.astype(F32),
            grad_hidden * first,
            grad_out * second,
            grad_hidden,
            grad_out,
            gap * gap,
        )
    ):
        sums_ref[at : at + 1] += jnp.sum(term, axis=0, keepdims=True)
    upsum_ref[...] += jnp.concatenate(up_sums, axis=1)


def student_middle(
    own_length, clip_scales, tokens, cotangent, teach_out, context, wo, w1, w2, vectors
):
    rows, wide = tokens.shape[0], w1.shape[0]
    block, down_block, up_block = 256, 256, D
    row_steps, down_steps, up_steps = rows // block, D // down_block, wide // up_block
    scalar = whole(pltpu.SMEM)

    def window(first, count, shape):
        return pl.BlockSpec(shape, lambda i: (jnp.clip(i - first, 0, count - 1), 0))

    row_spec = window(0, row_steps, (block, D))
    narrow, broad = pltpu.VMEM((rows, D), BF16), pltpu.VMEM((rows, wide), BF16)
    return pl.pallas_call(
        functools.partial(student_kernel, row_steps),
        grid=(row_steps + down_steps + up_steps + 1,),
        in_specs=[scalar, scalar]
        + [row_spec] * 4
        + [fixed((D, D)), fixed((wide, D)), fixed((D, wide)), fixed(vectors.shape)],
        out_specs=[row_spec] * 3
        + [
            fixed((8, D)),
            fixed((1, wide)),
            window(row_steps, down_steps, (down_block, wide)),
            window(row_steps + down_steps, up_steps, (up_block, D)),
            fixed((D, D)),
        ],
        out_shape=[
            jax.ShapeDtypeStruct((rows, D), BF16),
            jax.ShapeDtypeStruct((rows, D), BF16),
            jax.ShapeDtypeStruct((rows, D), F32),
            jax.ShapeDtypeStruct((8, D), F32),
            jax.ShapeDtypeStruct((1, wide), F32),
            jax.ShapeDtypeStruct((D, wide), BF16),
            jax.ShapeDtypeStruct((wide, D), BF16),
            jax.ShapeDtypeStruct((D, D), BF16),
        ],
        scratch_shapes=[narrow, broad, broad, narrow, narrow, narrow]
        + [pltpu.VMEM((block, wide), F32)],
        compiler_params=pltpu.CompilerParams(vmem_limit_bytes=vmem_bytes),
        name="student_feed_forward",
    )(own_length, clip_scales, tokens, cotangent, teach_out, context, wo, w1, w2, vectors)


def input_kernel(clip, grad_ref, w_ref, low_ref, tok_ref, res_ref, out_ref, dw_ref, sum_ref, acc_ref):
    slot = pl.program_id(0)
    grad = grad_ref[0]
    part = dot(grad, w_ref[0], 1, 0)
    dw_ref[0] = outer_rows(grad, low_ref[...]).astype(dw_ref.dtype)
    sum_ref[0] = jnp.sum(grad.astype(F32), axis=0, keepdims=True)

    @pl.when(slot == 0)
    def _():
        acc_ref[...] = part

    @pl.when(slot > 0)
    def _():
        acc_ref[...] += part

    @pl.when(slot == pl.num_programs(0) - 1)
    def _():
        bent = jnp.tanh(tok_ref[...].astype(F32) / (saturation * clip[0]))
        out_ref[...] = (res_ref[...] + acc_ref[...] * (1.0 - bent * bent)).astype(BF16)


def input_grads(clip_scales, grads, weights, low, tokens, residual):
    rows = tokens.shape[0]
    slotted = lambda *shape: pl.BlockSpec((1,) + shape, lambda i: (i, 0, 0))
    return pl.pallas_call(
        input_kernel,
        grid=(3,),
        in_specs=[
            whole(pltpu.SMEM),
            slotted(rows, D),
            slotted(D, D),
            fixed((rows, D)),
            fixed((rows, D)),
            fixed((rows, D)),
        ],
        out_specs=[fixed((rows, D)), slotted(D, D), slotted(1, D)],
        out_shape=[
            jax.ShapeDtypeStruct((rows, D), BF16),
            jax.ShapeDtypeStruct((3, D, D), BF16),
            jax.ShapeDtypeStruct((3, 1, D), F32),
        ],
        scratch_shapes=[pltpu.VMEM((rows, D), F32)],
        compiler_params=pltpu.CompilerParams(vmem_limit_bytes=vmem_bytes),
        name="input_gradient",
    )(clip_scales, grads, weights, low, tokens, residual)


gather_chunks = ((0,), (1,), (2,), (3,), (4, 5), (6,), (7, 8), (9,))
gather_leads = (1, 1, 1, 3, 1, 1, 1, 1, 1, 1)
late_chunks = (7,)
ahead_stages = ((0, 0), (1, 0), (2, 0), (0, 1), (1, 1), (2, 1), (0, 2), (3, 0), (1, 2), (2, 2), (0, 3), (3, 1), (1, 3), (0, 4), (2, 3), (0, 5), (3, 2), (1, 4), (1, 5), (5, 0), (4, 0), (0, 6), (3, 3), (2, 4), (0, 7), (2, 5), (5, 1), (1, 6), (1, 7), (4, 1), (7, 0), (3, 4), (5, 2), (3, 5), (4, 2), (2, 6), (7, 1), (2, 7))
opening_stages = {3: (), 6: ((4, 7),)}
gather_between = {(0, 0): ((5, 3),), (0, 1): ((4, 3),), (0, 2): ((3, 6), (6, 0)), (0, 3): ((7, 2),), (1, 0): ((3, 7),), (1, 1): ((6, 1),), (1, 2): ((5, 4),), (2, 1): ((5, 5),), (2, 3): ((7, 3),), (3, 1): ((4, 4), (6, 2)), (4, 0): ((4, 5),), (4, 3): ((7, 4), (5, 6)), (5, 0): ((6, 3),), (5, 1): ((5, 7),), (5, 2): ((4, 6),), (6, 3): ((7, 5), (6, 4)), (7, 1): ((7, 6),), (8, 0): ((6, 5),), (9, 2): ((6, 6),)}
closing_stages = ((6, 7),)


def lay_flat(flat, owners):
    rows = owners.shape[-2]
    for owner in range(flat.shape[0] // rows):
        flat[owner * rows : (owner + 1) * rows] = owners[
            owner // 8, owner // 4 % 2, owner // 2 % 2, owner % 2
        ]


def forward_kernel(depth, tail_steps, lengths, clip, *refs):
    (teach_attn, teach_up, teach_down, vec_in, attn_ref, up_ref, down_ref, teach_tok, tok), refs = (
        refs[:9],
        refs[9:],
    )
    (tq_ref, tk_ref, q_ref, k_ref, v_ref, ctx_ref, low_ref, out_ref, vec_ref), refs = (
        refs[:9],
        refs[9:],
    )
    (qkv_out, wo_out, up_out, down_out), refs = refs[:4], refs[4:]
    (teach_qkv, own_qkv, teach_wo, teach_w1, teach_w2, attn_low, up_low, down_low, teach_ctx), refs = (
        refs[:9],
        refs[9:],
    )
    (qkv_flat, wo_flat, w2_flat), refs = refs[:3], refs[3:]
    qkv_sem, shared, sems = refs[0], refs[1:6], refs[6:]
    place = Place(depth)
    step = pl.program_id(0)
    narrow = 2 * LANES
    attend_steps = D // narrow
    last = pl.num_programs(0) - 1

    ins = [teach_attn.at[slot] for slot in range(3)] + [
        attn_low.at[pl.ds(0, 3)],
        teach_attn.at[3],
        teach_up,
        teach_down,
        attn_low.at[3],
        up_low,
        down_low,
    ]
    outs = [teach_qkv.at[slot] for slot in range(3)] + [
        own_qkv,
        teach_wo,
        teach_w1,
        teach_w2,
        wo_out,
        up_out,
        down_out,
    ]
    begin, stage, sent = gather_stage(place, ins, outs, gather_leads, gather_chunks, late_chunks, sems)

    def run(stages):
        for chunk, number in stages:
            stage(chunk, number)

    def finish_lines(total):
        vec_ref[...] = total.astype(F32)

    line_stage = shared_stage(place, finish_lines, shared)
    line_count = depth + 4

    @pl.when(step == 0)
    def _():
        shared[0][0] = vec_in[...]
        place.barrier()
        begin((0, 1, 2))
        lines = iter(range(line_count))
        for at, (chunk, number) in enumerate(ahead_stages):
            if at == 2:
                for latent, low in ((attn_ref, attn_low), (up_ref, up_low), (down_ref, down_low)):
                    values = latent[...]
                    scale = jnp.mean(jnp.abs(values), axis=-1, keepdims=True)
                    sign = jnp.where(values > 0, 1.0, jnp.where(values < 0, -1.0, 0.0))
                    low[...] = (scale * sign).astype(BF16)
                begin((4, 5, 3, 6, 7))
            stage(chunk, number)
            if at % 2 == 0:
                for line in lines:
                    line_stage(line)
                    break
        for line in lines:
            line_stage(line)

    def slots(first, steps, at):
        for local in range(steps):
            stages = gather_between.get((first + local, at))
            if stages:

                @pl.when(step == first + local)
                def _():
                    run(stages)

    def opening(first):
        if opening_stages[first]:

            @pl.when(step == first)
            def _():
                run(opening_stages[first])

    def qkv_copy():
        return pltpu.make_async_copy(own_qkv, qkv_out, qkv_sem)

    def attend_step(student, first, inputs, weights, line, targets):
        local = step - first
        @pl.when(local == 0)
        def _():
            for slot in range(3):
                lay_flat(qkv_flat.at[slot], weights.at[slot])

        rows = pl.ds(pl.multiple_of(local * narrow, narrow), narrow)
        attend_quad(
            student,
            lengths[0],
            inputs[...],
            [qkv_flat[slot, rows, :] for slot in range(3)],
            [vec_ref[line + slot : line + slot + 1, rows] for slot in range(3)],
            targets,
            lambda head: slots(first, attend_steps, head),
        )

    @pl.when(step < attend_steps)
    def _():
        lanes = pl.ds(pl.multiple_of(step * narrow, narrow), narrow)
        attend_step(
            False, 0, teach_tok, teach_qkv, 0, (tq_ref, tk_ref, None, teach_ctx.at[:, lanes])
        )

    @pl.when((step >= attend_steps) & (step < 2 * attend_steps))
    def _():
        opening(attend_steps)

        @pl.when(step == attend_steps)
        def _():
            qkv_copy().start()
            width = saturation * clip[0]
            low_ref[...] = (width * jnp.tanh(tok[...].astype(F32) / width)).astype(BF16)

        attend_step(True, attend_steps, low_ref, own_qkv, 9, (q_ref, k_ref, v_ref, ctx_ref))

    @pl.when(step >= 2 * attend_steps)
    def _():
        first = 2 * attend_steps
        opening(first)

        @pl.when(step == first)
        def _():
            lay_flat(wo_flat, teach_wo)
            lay_flat(w2_flat, teach_w2)

        block = out_ref.shape[0]
        rows = pl.ds(pl.multiple_of((step - first) * block, block), block)
        teacher_rows(
            teach_tok[rows, :],
            teach_ctx[rows, :],
            wo_flat,
            lambda at: teach_w1[at].reshape(D, D),
            w2_flat,
            vec_ref[0:9],
            vec_ref[18:22],
            out_ref,
            lambda at: slots(first, tail_steps, at),
        )

    @pl.when(step == last)
    def _():
        run(closing_stages)
        qkv_copy().wait()
        for chunk in range(len(gather_chunks)):
            sent(chunk)


def forward(
    own_length,
    clip_scales,
    teacher_attn,
    teacher_up,
    teacher_down,
    vectors,
    latents,
    teacher_tokens,
    tokens,
):
    rows = tokens.shape[0]
    depth = lax.axis_size("dp") // 2
    attn_latent, up_latent, down_latent = latents
    narrow, wide = attn_latent.shape[1], up_latent.shape[0]
    lanes, quad, block = 2 * LANES, 4 * LANES, 256
    attend_steps, tail_steps = D // lanes, rows // block
    dma = pltpu.SemaphoreType.DMA
    owners = (depth, 2, 2, 2)
    qkv_shape, wo_shape = (3,) + owners + (narrow, D), owners + (narrow, D)
    up_shape, down_shape = owners + (wide, D), owners + (narrow, down_latent.shape[1])
    scalar = whole(pltpu.SMEM)

    def window(first, count, shape, along):
        def index(i):
            at = jnp.clip(i - first, 0, count - 1)
            return (at, 0) if along == 0 else (0, at)

        return pl.BlockSpec(shape, index)

    def student_columns(width):
        return window(attend_steps, attend_steps, (rows, width), 1)

    results = pl.pallas_call(
        functools.partial(forward_kernel, depth, tail_steps),
        grid=(2 * attend_steps + tail_steps,),
        in_specs=[scalar] * 2
        + [whole(pl.ANY)] * 3
        + [
            fixed(shape)
            for shape in (
                vectors.shape,
                attn_latent.shape,
                up_latent.shape,
                down_latent.shape,
                (rows, D),
                (rows, D),
            )
        ],
        out_specs=[window(0, attend_steps, (rows, lanes), 1)] * 2
        + [student_columns(quad)] * 3
        + [
            student_columns(lanes),
            fixed((rows, D)),
            window(2 * attend_steps, tail_steps, (block, D), 0),
            fixed(vectors.shape),
        ]
        + [whole(pl.ANY)] * 4,
        out_shape=[jax.ShapeDtypeStruct((rows, D), BF16)] * 2
        + [jax.ShapeDtypeStruct((rows, 2 * D), BF16)] * 3
        + [
            jax.ShapeDtypeStruct((rows, D), F32),
            jax.ShapeDtypeStruct((rows, D), BF16),
            jax.ShapeDtypeStruct((rows, D), F32),
            jax.ShapeDtypeStruct(vectors.shape, F32),
        ]
        + [
            jax.ShapeDtypeStruct(shape, BF16)
            for shape in (qkv_shape, wo_shape, up_shape, down_shape)
        ],
        scratch_shapes=[
            pltpu.VMEM(shape, BF16)
            for shape in (
                qkv_shape,
                qkv_shape,
                wo_shape,
                up_shape,
                down_shape,
                attn_latent.shape,
                up_latent.shape,
                down_latent.shape,
                (rows, D),
                (3, D, D),
                (D, D),
                (D, down_latent.shape[1]),
            )
        ]
        + [dma]
        + shared_scratch(depth, vectors.shape[0], BF16)
        + gather_scratch(gather_chunks, depth),
        compiler_params=pltpu.CompilerParams(
            collective_id=0, has_side_effects=True, vmem_limit_bytes=vmem_bytes
        ),
        name="gather_attention_and_teacher",
    )(
        own_length,
        clip_scales,
        teacher_attn,
        teacher_up,
        teacher_down,
        vectors,
        attn_latent,
        up_latent,
        down_latent,
        teacher_tokens,
        tokens,
    )
    return list(results[:9]) + gathered(results[9:])


between_stages = {
    0: ((0, 1),),
    1: ((0, 2), (1, 1), (1, 2)),
    2: ((2, 1), (2, 2)),
    4: ((0, 3),),
    6: ((1, 3),),
    7: ((0, 4), (2, 3)),
    8: ((0, 5),),
    9: ((1, 4), (0, 6)),
    10: ((0, 7), (2, 4), (1, 5)),
    11: ((0, 8), (1, 6), (2, 5)),
}
after_query = ((1, 7), (2, 6))
after_key = ((3, 1), (1, 8), (2, 7))
after_value = ((4, 1), (3, 2), (2, 8))


def latent_rows(latent, grad):
    size = latent.shape[-1]
    scale = jnp.mean(jnp.abs(latent), axis=-1, keepdims=True)
    sign = jnp.where(latent > 0, 1.0, jnp.where(latent < 0, -1.0, 0.0))
    return scale * grad + sign * (jnp.sum(grad * latent, axis=-1, keepdims=True) / size)


def finish_kernel(depth, lengths, scalars, clip, *refs):
    pair_refs, refs = refs[:7], refs[7:]
    dw_refs, refs = refs[:3], refs[3:]
    (w_ref, low_ref, tok_ref, res_ref, sums_ref, upsum_ref, attn_ref, up_ref, down_ref), refs = (
        refs[:9],
        refs[9:],
    )
    (input_ref, attn_grad, up_grad, down_grad, line_grad), refs = refs[:5], refs[5:]
    (grad_ref, square_ref, dwq_ref, dwk_ref, dwv_ref), refs = refs[:5], refs[5:]
    shared, scratch = refs[:5], refs[5:]
    place = Place(depth)
    step = pl.program_id(0)
    last = pl.num_programs(0) - 1
    pairs = D // LANES

    def finish(item, lead, total):
        if item == 0:
            down_grad[...] = latent_rows(down_ref[...], total)
        elif item == 1:
            up_grad[...] = latent_rows(up_ref[...], total)
        else:
            slot = 3 if item == 2 else item - 3
            attn_grad[slot] = latent_rows(attn_ref[slot], total)

    def finish_lines(total):
        line_grad[...] = total

    own = (dwq_ref, dwk_ref, dwv_ref)
    stage = scatter_stage(place, tuple(dw_refs) + own, finish, scratch, 6)
    line_stage = shared_stage(place, finish_lines, shared)

    @pl.when(step == 0)
    def _():
        place.barrier()
        for item in range(3):
            stage(item, 0)
        square_ref[...] = jnp.zeros_like(square_ref)

    @pl.when(step < pairs)
    def _():
        def between(odd):
            for at, stages in between_stages.items():
                if at % 2 == odd:

                    @pl.when(step == at // 2)
                    def _():
                        for item, number in stages:
                            stage(item, number)

        grads, squares = attend_back_pair(lengths[0], scalars[0], *pair_refs, between)
        square_ref[...] += squares
        lanes = pl.ds(pl.multiple_of(step * LANES, LANES), LANES)
        for slot in range(3):
            grad_ref[slot, :, lanes] = grads[slot]

    def weight_grad(slot):
        total = outer_rows(grad_ref[slot], low_ref[...]).astype(BF16)
        rows = dwq_ref.shape[-2]
        for owner in range(D // rows):
            where = (owner // 8, owner // 4 % 2, owner // 2 % 2, owner % 2)
            own[slot][where] = total[owner * rows : (owner + 1) * rows]
        stage(3 + slot, 0)

    def run(stages):
        for item, number in stages:
            stage(item, number)

    @pl.when(step == pairs)
    def _():
        weight_grad(0)
        run(after_query)
        weight_grad(1)
        run(after_key)

    @pl.when(step == last)
    def _():
        weight_grad(2)
        held = shared[0]
        held[0] = jnp.zeros_like(held[0])
        for slot in range(3):
            held[0, slot : slot + 1] = jnp.sum(
                grad_ref[slot].astype(F32), axis=0, keepdims=True
            )
        held[0, 3:9] = sums_ref[0:6]
        held[0, 9:13] = upsum_ref[...]
        held[0, 13:14] = sums_ref[6:7] * scalars[1]
        held[0, 13:14, :LANES] += jnp.sum(square_ref[...], axis=0, keepdims=True)
        line_stage(0)
        run(after_value)
        total = dot(grad_ref[0], w_ref[0], 1, 0)
        line_stage(1)
        run(((3, 3), (5, 1), (4, 2)))
        total += dot(grad_ref[1], w_ref[1], 1, 0)
        line_stage(2)
        run(((3, 4), (5, 2), (4, 3)))
        total += dot(grad_ref[2], w_ref[2], 1, 0)
        bent = jnp.tanh(tok_ref[...].astype(F32) / (saturation * clip[0]))
        input_ref[...] = (res_ref[...] + total * (1.0 - bent * bent)).astype(BF16)
        line_stage(3)
        run(((4, 4), (3, 5), (5, 3)))
        line_stage(4)
        run(((3, 6), (4, 5), (5, 4)))
        line_stage(5)
        run(((3, 7), (4, 6), (5, 5)))
        line_stage(6)
        run(((3, 8), (4, 7), (5, 6), (4, 8), (5, 7), (5, 8)))
        line_stage(7)


def finish_backward(
    own_length,
    inverse_pairs,
    inverse_hidden,
    clip_scales,
    pair_arrays,
    weight_grads,
    qkv_w,
    low,
    tokens,
    residual,
    sums,
    up_sums,
    latents,
    narrow,
    wide,
):
    dp, shard = lax.axis_size("dp"), lax.axis_size("shard")
    attn_latent, up_latent, down_latent = latents
    if not tiled_over((dp, shard), narrow):
        grads, squares = attend_back(own_length, inverse_pairs, *pair_arrays)
        input_grad, qkv_weight_grad, qkv_sums = input_grads(
            clip_scales, grads, qkv_w, low, tokens, residual
        )
        local_loss = sums[6:7] * inverse_hidden
        local_loss = local_loss + jnp.pad(
            jnp.sum(squares, axis=0, keepdims=True), ((0, 0), (0, D - LANES))
        )
        lines = jnp.concatenate(
            [qkv_sums[:, 0], sums[:6], up_sums.reshape(-1, D), local_loss], axis=0
        )
        lines = lax.psum(lines, AXES)
        down_total, up_total, attn_total = scatter(
            weight_grads[:2]
            + [jnp.concatenate([qkv_weight_grad, weight_grads[2][None].astype(BF16)], axis=0)]
        )
        attn_grad = latent_grad(attn_latent, attn_total)
        up_grad = latent_grad(up_latent, up_total)
        down_grad = latent_grad(down_latent, down_total)
    else:
        depth = dp // 2
        rows = tokens.shape[0]
        dw = [split_rows(grad, depth) for grad in weight_grads]
        own_shape = (depth, 2, 2, 2, narrow, D)
        shapes = [(1,) + grad.shape[-2:] for grad in dw] + [(1, narrow, D)] * 3
        scalar = whole(pltpu.SMEM)
        pairs = D // LANES

        def pair_columns(width):
            return pl.BlockSpec((rows, width), lambda i: (0, jnp.minimum(i, pairs - 1)))

        input_grad, attn_grad, up_grad, down_grad, lines = pl.pallas_call(
            functools.partial(finish_kernel, depth),
            grid=(pairs + 2,),
            in_specs=[scalar] * 3
            + [pair_columns(2 * LANES)] * 3
            + [pair_columns(LANES)] * 4
            + [whole(pl.ANY)] * 3
            + [
                fixed(array_shape)
                for array_shape in (
                    (3, D, D),
                    (rows, D),
                    (rows, D),
                    (rows, D),
                    sums.shape,
                    (up_sums.size // D, D),
                    attn_latent.shape,
                    up_latent.shape,
                    down_latent.shape,
                )
            ],
            out_specs=[
                fixed(array_shape)
                for array_shape in (
                    (rows, D),
                    attn_latent.shape,
                    up_latent.shape,
                    down_latent.shape,
                    (line_rows, D),
                )
            ],
            out_shape=[
                jax.ShapeDtypeStruct((rows, D), BF16),
                jax.ShapeDtypeStruct(attn_latent.shape, F32),
                jax.ShapeDtypeStruct(up_latent.shape, F32),
                jax.ShapeDtypeStruct(down_latent.shape, F32),
                jax.ShapeDtypeStruct((line_rows, D), F32),
            ],
            scratch_shapes=[
                pltpu.VMEM((3, rows, D), BF16),
                pltpu.VMEM((8, LANES), F32),
                pltpu.VMEM(own_shape, BF16),
                pltpu.VMEM(own_shape, BF16),
                pltpu.VMEM(own_shape, BF16),
            ]
            + shared_scratch(depth, line_rows, F32)
            + scatter_scratch(shapes, [BF16] * 6, depth),
            compiler_params=pltpu.CompilerParams(
                collective_id=1, has_side_effects=True, vmem_limit_bytes=vmem_bytes
            ),
            name="attention_backward_and_sums",
        )(
            own_length,
            jnp.stack([inverse_pairs[0], inverse_hidden]),
            clip_scales,
            *pair_arrays,
            *dw,
            qkv_w,
            low,
            tokens,
            residual,
            sums,
            up_sums.reshape(-1, D),
            attn_latent,
            up_latent,
            down_latent,
        )
    at = lax.axis_index(AXES)
    line_total = lax.dynamic_slice_in_dim(lines[:9], at * narrow, narrow, axis=1)
    up_bias_total = lax.dynamic_slice_in_dim(lines[9:13].reshape(-1), at * wide, wide)
    return (
        jnp.sum(lines[13]),
        input_grad,
        attn_grad,
        up_grad,
        down_grad,
        line_total[:5],
        up_bias_total,
        line_total[5:7],
        line_total[7:9],
    )


def on_device(
    tokens,
    teacher_tokens,
    cotangent,
    lengths,
    clip_scales,
    attn_latent,
    up_latent,
    down_latent,
    biases,
    up_bias,
    norm_gains,
    norm_shifts,
    teacher_attn,
    teacher_up,
    teacher_down,
    teacher_biases,
    teacher_up_bias,
    teacher_gains,
    teacher_shifts,
):
    sizes = (lax.axis_size("dp"), lax.axis_size("shard"))
    narrow, wide = biases.shape[1], up_bias.shape[0]
    at = lax.axis_index(AXES)
    own_length = lax.dynamic_slice_in_dim(lengths, at, 1)
    live_float = lengths.astype(F32)
    token_norm = jnp.sum(live_float)
    pair_norm = HEADS * jnp.sum(live_float * live_float)
    inverse_pairs = (1.0 / pair_norm).reshape(1)
    lines = jnp.concatenate(
        [teacher_biases, teacher_gains, teacher_shifts, biases, norm_gains, norm_shifts], axis=0
    )
    lines = lax.dynamic_update_slice(
        jnp.zeros((lines.shape[0], D), BF16), lines, (0, at * narrow)
    )
    ups = lax.dynamic_update_slice(
        jnp.zeros((2, wide * sizes[0] * sizes[1]), BF16),
        jnp.stack([teacher_up_bias, up_bias]),
        (0, at * wide),
    )
    vectors = jnp.concatenate([lines, ups.reshape(-1, D)], axis=0)
    vectors = jnp.pad(vectors, ((0, -vectors.shape[0] % 16), (0, 0)))
    latents = (attn_latent, up_latent, down_latent)
    if tiled_over(sizes, narrow):
        (
            tq,
            tk,
            query,
            key,
            value,
            context,
            x_low,
            teach_out,
            vec,
            qkv_w,
            out_w,
            up_w,
            down_w,
        ) = forward(
            own_length,
            clip_scales,
            teacher_attn,
            teacher_up,
            teacher_down,
            vectors,
            latents,
            teacher_tokens,
            tokens,
        )
    else:
        vec = lax.psum(vectors.astype(F32), AXES)
        teach_qkv, teach_wo, teach_up, teach_down, qkv_w, out_w, up_w, down_w = gather(
            [
                teacher_attn[:3],
                teacher_attn[3],
                teacher_up,
                teacher_down,
                binarize(attn_latent[:3]),
                binarize(attn_latent[3]),
                binarize(up_latent),
                binarize(down_latent),
            ]
        )
        tq, tk, teach_context = attend(
            False, own_length, clip_scales, teacher_tokens, teach_qkv, vec[:3].reshape(3, 1, D)
        )
        query, key, value, context, x_low = attend(
            True, own_length, clip_scales, tokens, qkv_w, vec[9:12].reshape(3, 1, D)
        )
        teach_out = teacher_tail(
            teacher_tokens, teach_context, teach_wo, teach_up, teach_down, vec[:9], vec[18:22]
        )
    result, grad_context, residual, sums, up_sums, *weight_grads = student_middle(
        own_length,
        clip_scales,
        tokens,
        cotangent,
        teach_out,
        context,
        out_w,
        up_w,
        down_w,
        vec,
    )
    return (result,) + finish_backward(
        own_length,
        inverse_pairs,
        1.0 / (D * token_norm),
        clip_scales,
        (query, key, value, context, grad_context, tq, tk),
        weight_grads,
        qkv_w,
        x_low,
        tokens,
        residual,
        sums,
        up_sums,
        latents,
        narrow,
        wide,
    )


def solution(mesh):
    in_specs = (
        P(("dp", "shard"), None),
        P(("dp", "shard"), None),
        P(("dp", "shard"), None),
        P(),
        P(),
        P(None, ("dp", "shard"), None),
        P(("dp", "shard"), None),
        P(("dp", "shard"), None),
        P(None, ("dp", "shard")),
        P(("dp", "shard")),
        P(None, ("dp", "shard")),
        P(None, ("dp", "shard")),
        P(None, ("dp", "shard"), None),
        P(("dp", "shard"), None),
        P(("dp", "shard"), None),
        P(None, ("dp", "shard")),
        P(("dp", "shard")),
        P(None, ("dp", "shard")),
        P(None, ("dp", "shard")),
    )
    out_specs = (
        P(("dp", "shard"), None),
        P(),
        P(("dp", "shard"), None),
        P(None, ("dp", "shard"), None),
        P(("dp", "shard"), None),
        P(("dp", "shard"), None),
        P(None, ("dp", "shard")),
        P(("dp", "shard")),
        P(None, ("dp", "shard")),
        P(None, ("dp", "shard")),
    )
    return jax.shard_map(
        on_device, mesh=mesh, in_specs=in_specs, out_specs=out_specs, check_vma=False
    )
```

```python
import functools
import math

import jax
import jax.numpy as jnp
from jax import lax
from jax.experimental import pallas as pl
from jax.experimental.pallas import tpu as pltpu
from jax.sharding import PartitionSpec as P

D = 768
HEADS = 12
HEAD_DIM = 64
SEQ_LEN = 1024
AXES = ("dp", "shard")
MESH = pl.DeviceIdType.MESH
F32 = jnp.float32
BF16 = jnp.bfloat16

epsilon = 1e-05
masked_score = -1e30
hidden_weight = 0.25
saturation = 7.5
LANES = 128
log2e = math.log2(math.e)
scaling = HEAD_DIM ** (-0.5)
exponent = scaling * log2e
vmem_bytes = 60 * 1024 * 1024
line_rows = 16
vector_rows = 32


def dot(left, right, left_dim, right_dim):
    return lax.dot_general(
        left, right, (((left_dim,), (right_dim,)), ((), ())), preferred_element_type=F32
    )


def outer_rows(left, right):
    return dot(left, right, 0, 0)


def binarize(latent):
    scale = jnp.mean(jnp.abs(latent), axis=-1, keepdims=True)
    return (scale * jnp.sign(latent)).astype(BF16)


def surrogate(latent):
    return jnp.mean(jnp.abs(latent), axis=-1, keepdims=True) * latent


def latent_grad(latent, grad):
    _, pull = jax.vjp(surrogate, latent)
    return pull(grad)[0]


def normalize(values):
    center = values - jnp.mean(values, axis=-1, keepdims=True)
    inverse = lax.rsqrt(jnp.mean(center * center, axis=-1, keepdims=True) + epsilon)
    return (center * inverse, inverse)


def norm_back(grad_norm, normed, inverse):
    return inverse * (
        grad_norm
        - jnp.mean(grad_norm, axis=-1, keepdims=True)
        - normed * jnp.mean(grad_norm * normed, axis=-1, keepdims=True)
    )


def whole(memory=pltpu.VMEM):
    return pl.BlockSpec(memory_space=memory)


def fixed(shape):
    return pl.BlockSpec(shape, lambda *_: (0,) * len(shape), pipeline_mode=pl.Buffered(1))


def columns(shape):
    return pl.BlockSpec(shape, lambda i: (0,) * (len(shape) - 1) + (i,))


def row_blocks(shape):
    return pl.BlockSpec(shape, lambda i: (i,) + (0,) * (len(shape) - 1))


def own_index():
    return lax.axis_index("dp") * lax.axis_size("shard") + lax.axis_index("shard")


def lanes_of(width, start):
    row = lax.broadcasted_iota(jnp.int32, (width, D), 0)
    lane = lax.broadcasted_iota(jnp.int32, (width, D), 1)
    return jnp.where(lane == row + start, 1.0, 0.0).astype(BF16)


def take_lanes(values, width, start):
    chosen = lanes_of(width, start)
    return sum(dot(part.astype(BF16), chosen, 1, 1) for part in three_parts(values))


class Place:
    def __init__(self, depth):
        self.depth = depth
        dp, shard = lax.axis_index("dp"), lax.axis_index("shard")
        z, y = dp // 2, lax.rem(dp, 2)
        x, core = shard // 2, lax.rem(shard, 2)
        self.z, self.y, self.x, self.core = z, y, x, core

        def device(z_at, y_at, x_at, core_at):
            return (z_at * 2 + y_at, x_at * 2 + core_at)

        self.above = device(jnp.minimum(z + 1, depth - 1), y, x, core)
        self.below = device(jnp.maximum(z - 1, 0), y, x, core)
        one = (lax.rem(y + 1 - core, 2), lax.rem(x + core, 2))
        two = (lax.rem(y + core, 2), lax.rem(x + 1 - core, 2))
        self.pieces = ((y, x), one, two, (1 - y, 1 - x))
        self.first, self.second = device(z, *one, core), device(z, *two, core)
        self.sibling = device(z, y, x, 1 - core)

    def barrier(self):
        semaphore = pltpu.get_barrier_semaphore()
        for partner in (self.first, self.second, self.sibling):
            pl.semaphore_signal(semaphore, inc=1, device_id=partner, device_id_type=MESH)

        @pl.when(self.z < self.depth - 1)
        def _():
            pl.semaphore_signal(semaphore, inc=1, device_id=self.above, device_id_type=MESH)

        @pl.when(self.z > 0)
        def _():
            pl.semaphore_signal(semaphore, inc=1, device_id=self.below, device_id_type=MESH)

        pl.semaphore_wait(
            semaphore, 3 + jnp.minimum(self.z, 1) + jnp.minimum(self.depth - 1 - self.z, 1)
        )


def remote(source, target, send_sem, recv_sem, device):
    return pltpu.make_async_remote_copy(
        src_ref=source,
        dst_ref=target,
        send_sem=send_sem,
        recv_sem=recv_sem,
        device_id=device,
        device_id_type=MESH,
    )


def tiled_over(mesh_sizes, rows):
    return mesh_sizes == (8, 4) and rows % 8 == 0


def gather_scratch(chunks, depth):
    dma = pltpu.SemaphoreType.DMA
    sizes = (len(chunks), max(len(chunk) for chunk in chunks))
    return [
        dma(sizes + (depth - 1, 2)),
        dma(sizes + (depth - 1, 2)),
        dma(sizes + (3 + max(depth, 4),)),
        dma(sizes + (3 + max(depth, 4),)),
        dma(sizes),
    ]


def gather_stage(place, ins, outs, leads, chunks, late, sems):
    line_send, line_recv, pair_send, pair_recv, own_sem = sems
    depth, z, y, x, core = place.depth, place.z, place.y, place.x, place.core

    def slot(item, *index):
        return outs[item].at[((slice(None),) if leads[item] > 1 else ()) + index]

    def group(chunk, item, z_at):
        if chunk in late:
            return slot(item, z_at, slice(None), slice(None), core)
        return slot(item, z_at, y, x, core)

    def line_copy(chunk, at, item, turn, upward):
        if upward:
            owner, target = jnp.maximum(z - (turn - 1), 0), place.above
        else:
            owner, target = jnp.minimum(z + (turn - 1), depth - 1), place.below
        block = group(chunk, item, owner)
        where = (chunk, at, turn - 1, int(upward))
        return remote(block, block, line_send.at[where], line_recv.at[where], target)

    def sends(turn, upward):
        if upward:
            return (z - (turn - 1) >= 0) & (z < depth - 1)
        return (z + (turn - 1) <= depth - 1) & (z > 0)

    def receives(turn, upward):
        return (z - turn >= 0) if upward else (z + turn <= depth - 1)

    def own_copy(chunk, at, item):
        return pltpu.make_async_copy(
            ins[item], slot(item, z, y, x, core), own_sem.at[chunk, at]
        )

    plans = (
        (0, place.first),
        (0, place.second),
        (1, place.second),
        (0, place.sibling),
        (1, place.sibling),
        (2, place.sibling),
        (3, place.sibling),
    )

    def pair_copy(chunk, at, item, plan):
        piece, target = plans[plan]
        z_at = z if chunk in late else slice(None)
        block = slot(item, z_at, *place.pieces[piece], core)
        where = (chunk, at, plan)
        return remote(block, block, pair_send.at[where], pair_recv.at[where], target)

    def each(chunk, action):
        for at, item in enumerate(chunks[chunk]):
            action(at, item)

    def line_start(chunk, turn):
        for upward in (True, False):

            @pl.when(sends(turn, upward))
            def _():
                each(chunk, lambda at, item: line_copy(chunk, at, item, turn, upward).start())

    def line_received(chunk, turn):
        for upward in (True, False):

            @pl.when(receives(turn, upward))
            def _():
                each(chunk, lambda at, item: line_copy(chunk, at, item, turn, upward).wait_recv())

    def line_sent(chunk, turn):
        for upward in (True, False):

            @pl.when(sends(turn, upward))
            def _():
                each(chunk, lambda at, item: line_copy(chunk, at, item, turn, upward).wait_send())

    def start(chunk, *plan_list):
        for plan in plan_list:
            each(chunk, lambda at, item: pair_copy(chunk, at, item, plan).start())

    def received(chunk, *plan_list):
        for plan in plan_list:
            each(chunk, lambda at, item: pair_copy(chunk, at, item, plan).wait_recv())

    def plane_copy(chunk, at, item, z_at):
        block = group(chunk, item, z_at)
        where = (chunk, at, 3 + z_at)
        return remote(block, block, pair_send.at[where], pair_recv.at[where], place.sibling)

    def late_stage(chunk, number):
        if number == 0:
            each(chunk, lambda at, item: own_copy(chunk, at, item).wait())
            start(chunk, 0, 1)
        elif number == 1:
            received(chunk, 0)
            start(chunk, 2)
        elif number == 2:
            received(chunk, 1, 2)
            line_start(chunk, 1)
            each(chunk, lambda at, item: plane_copy(chunk, at, item, z).start())
        elif number < depth + 2:
            turn = number - 2
            line_received(chunk, turn)
            if turn < depth - 1:
                line_start(chunk, turn + 1)
            for upward in (True, False):
                owner = jnp.maximum(z - turn, 0) if upward else jnp.minimum(z + turn, depth - 1)

                @pl.when(receives(turn, upward))
                def _():
                    each(chunk, lambda at, item: plane_copy(chunk, at, item, owner).start())
        elif number == depth + 2:
            for z_at in range(depth):
                each(chunk, lambda at, item: plane_copy(chunk, at, item, z_at).wait_recv())

    def stage(chunk, number):
        if chunk in late:
            late_stage(chunk, number)
        elif number == 0:
            each(chunk, lambda at, item: own_copy(chunk, at, item).wait())
            line_start(chunk, 1)
        elif number < depth:
            line_received(chunk, number)
            if number < depth - 1:
                line_start(chunk, number + 1)
            else:
                start(chunk, 0, 1, 3)
        elif number == depth:
            received(chunk, 0)
            start(chunk, 2, 4)
        elif number == depth + 1:
            received(chunk, 1)
            start(chunk, 5)
        elif number == depth + 2:
            received(chunk, 2)
            start(chunk, 6)
        else:
            received(chunk, 3, 4, 5, 6)

    def sent(chunk):
        for turn in range(1, depth):
            line_sent(chunk, turn)
        for plan in range(3 if chunk in late else 7):
            each(chunk, lambda at, item: pair_copy(chunk, at, item, plan).wait_send())
        if chunk in late:
            for z_at in range(depth):
                each(chunk, lambda at, item: plane_copy(chunk, at, item, z_at).wait_send())

    def begin(begun):
        for chunk in begun:
            each(chunk, lambda at, item: own_copy(chunk, at, item).start())

    return begin, stage, sent


def gathered(results):
    return [
        result.reshape(result.shape[:-6] + (-1, result.shape[-1])) for result in results
    ]


def gather(arrays):
    return [lax.all_gather(array, AXES, axis=array.ndim - 2, tiled=True) for array in arrays]


def scatter_scratch(shapes, dtypes, depth):
    dma = pltpu.SemaphoreType.DMA
    scratch = []
    for shape, dtype in zip(shapes, dtypes):
        lead, rows, cols = shape
        block = (depth, lead, rows, cols)
        scratch += [
            pltpu.VMEM((4,) + block, dtype),
            pltpu.VMEM((4,) + block, dtype),
            pltpu.VMEM((3,) + block, dtype),
            pltpu.VMEM((2,) + block, dtype),
        ]
    count = len(shapes)
    return scratch + [
        dma((count, 4)),
        dma((count, 7)),
        dma((count, 7)),
        dma((count, depth, 2)),
        dma((count, depth, 2)),
    ]


def scatter_stage(place, ins, finish, scratch, count):
    depth, z, core = place.depth, place.z, place.core
    own_sem, pair_send, pair_recv, line_send, line_recv = scratch[4 * count :]

    def buffers(item):
        return scratch[4 * item : 4 * item + 4]

    def source(item, piece, lead, side):
        index = (slice(None),) + place.pieces[piece] + (side,)
        ref = ins[item]
        return ref.at[((lead,) if ref.shape[:-6] else ()) + index]

    def leads(item):
        return range(buffers(item)[0].shape[2])

    def own_copy(item, piece, lead):
        held = buffers(item)[0]
        return pltpu.make_async_copy(
            source(item, piece, lead, core), held.at[piece, :, lead], own_sem.at[item, piece]
        )

    names = (0, 2, 1, 3)

    def core_copy(item, piece, lead):
        arrived = buffers(item)[1]
        name = names[piece]
        return remote(
            source(item, piece, lead, 1 - core),
            arrived.at[name, :, lead],
            pair_send.at[item, piece],
            pair_recv.at[item, name],
            place.sibling,
        )

    def core_wait(item, piece):
        arrived = buffers(item)[1]
        block = arrived.at[piece]
        remote(
            block, block, pair_send.at[item, piece], pair_recv.at[item, piece], place.sibling
        ).wait_recv()

    def chip_copy(item, plan):
        held, _, arrived, _ = buffers(item)
        piece, target = ((2, place.second), (3, place.second), (1, place.first))[plan]
        return remote(
            held.at[piece],
            arrived.at[plan],
            pair_send.at[item, 4 + plan],
            pair_recv.at[item, 4 + plan],
            target,
        )

    def line_copy(item, owner, upward, fresh):
        held, _, _, arrived = buffers(item)
        block = arrived.at[int(upward), owner]
        where = (item, owner, int(upward))
        return remote(
            held.at[0, owner] if fresh else block,
            block,
            line_send.at[where],
            line_recv.at[where],
            place.above if upward else place.below,
        )

    def add(target, *others):
        def one(at):
            if len(others) == 1:
                target[at] = target[at] + others[0][at]
                return
            total = target[at].astype(F32)
            for other in others:
                total = total + other[at].astype(F32)
            target[at] = total.astype(target.dtype)

        for first in range(target.shape[0]):
            for second in range(target.shape[1]):
                one((first, second))

    def add_block(target, other):
        for lead in range(target.shape[0]):
            target[lead] = target[lead] + other[lead]

    def merge(item, piece):
        held, arrived, _, _ = buffers(item)
        block = held.at[piece]
        pltpu.make_async_copy(block, block, own_sem.at[item, piece]).wait()
        core_wait(item, piece)
        add(block, arrived.at[piece])

    def line_turn(item, turn, upward):
        held, _, _, arrived = buffers(item)
        at = turn if upward else depth - 1 - turn
        beyond = range(at + 1, depth) if upward else range(at)

        @pl.when(z == at)
        def _():
            for owner in sorted(beyond, key=lambda owner: -abs(owner - at)):
                if turn:
                    line_copy(item, owner, upward, False).wait_recv()
                    add_block(arrived.at[int(upward), owner], held.at[0, owner])
                line_copy(item, owner, upward, not turn).start()
            if turn:
                line_copy(item, at, upward, False).wait_recv()

    def stage(item, number):
        held, _, arrived, line = buffers(item)
        if number == 0:
            for piece in (3, 1, 2, 0):
                for lead in leads(item):
                    core_copy(item, piece, lead).start()
            for piece in (2, 3, 1, 0):
                for lead in leads(item):
                    own_copy(item, piece, lead).start()
        elif number == 1:
            for piece, plan in ((3, 1), (2, 0)):
                merge(item, piece)
                chip_copy(item, plan).start()
        elif number == 2:
            merge(item, 1)
            merge(item, 0)
        elif number == 3:
            chip_copy(item, 1).wait_recv()
            add(held.at[1], arrived.at[1])
            chip_copy(item, 2).start()
        elif number == 4:
            chip_copy(item, 0).wait_recv()
            chip_copy(item, 2).wait_recv()
            add(held.at[0], arrived.at[0], arrived.at[2])
            for upward in (True, False):
                line_turn(item, 0, upward)
        elif number < 4 + depth:
            for upward in (True, False):
                line_turn(item, number - 4, upward)
        else:
            for lead in leads(item):
                total = held[0, z, lead].astype(F32)
                for upward, near in ((1, z > 0), (0, z < depth - 1)):
                    total = jnp.where(near, total + line[upward, z, lead].astype(F32), total)
                finish(item, lead, total)

            for piece in range(4):
                block = buffers(item)[1].at[piece]
                remote(
                    block, block, pair_send.at[item, piece], pair_recv.at[item, piece], place.sibling
                ).wait_send()
            for plan in range(3):
                chip_copy(item, plan).wait_send()
            for upward in (True, False):
                for owner in range(depth):

                    @pl.when((z < owner) if upward else (z > owner))
                    def _():
                        line_copy(item, owner, upward, False).wait_send()

    return stage


def split_rows(array, depth):
    return array.reshape(array.shape[:-2] + (depth, 2, 2, 2, -1, array.shape[-1]))


def shared_scratch(depth, rows, dtype):
    dma = pltpu.SemaphoreType.DMA
    return [
        pltpu.VMEM((4, rows, D), dtype),
        pltpu.VMEM((5, rows, D), dtype),
        pltpu.VMEM((2, rows, D), dtype),
        dma((5,)),
        dma((5,)),
    ]


def shared_stage(place, finish, scratch):
    held, arrived, line, send_sem, recv_sem = scratch
    depth, z = place.depth, place.z
    partners = (place.sibling, place.second, place.first)

    def pair_copy(at):
        return remote(
            held.at[at], arrived.at[at], send_sem.at[at], recv_sem.at[at], partners[at]
        )

    def line_copy(upward, fresh):
        at = 3 + int(upward)
        return remote(
            held.at[3] if fresh else line.at[int(upward)],
            arrived.at[at],
            send_sem.at[at],
            recv_sem.at[at],
            place.above if upward else place.below,
        )

    def line_turn(turn, upward):
        at = turn if upward else depth - 1 - turn

        @pl.when(z == at)
        def _():
            if turn:
                line_copy(upward, False).wait_recv()
            if turn < depth - 1:
                if turn:
                    line[int(upward)] = held[3] + arrived[3 + int(upward)]
                line_copy(upward, not turn).start()

    def stage(number):
        if number == 0:
            pair_copy(0).start()
        elif number < 4:
            pair_copy(number - 1).wait_recv()
            held[number] = held[number - 1] + arrived[number - 1]
            if number < 3:
                pair_copy(number).start()
            else:
                for upward in (True, False):
                    line_turn(0, upward)
        elif number < 3 + depth:
            for upward in (True, False):
                line_turn(number - 3, upward)
        else:
            total = held[3]
            total = jnp.where(z > 0, total + arrived[4], total)
            finish(jnp.where(z < depth - 1, total + arrived[3], total))
            for at in range(3):
                pair_copy(at).wait_send()
            for upward in (True, False):

                @pl.when((z < depth - 1) if upward else (z > 0))
                def _():
                    line_copy(upward, False).wait_send()

    return stage


def scatter(arrays):
    return [
        lax.psum_scatter(array.astype(F32), AXES, scatter_dimension=array.ndim - 2, tiled=True)
        for array in arrays
    ]


def lane_index(rows):
    return lax.broadcasted_iota(jnp.int32, (rows, LANES), 1)


def halves(lane, odd):
    own = (lane >= HEAD_DIM) if odd else (lane < HEAD_DIM)
    other = lane if odd else lane - HEAD_DIM
    return own, other


def three_parts(values):
    high = values.astype(BF16).astype(F32)
    rest = values - high
    middle = rest.astype(BF16).astype(F32)
    return high, middle, rest - middle


def with_terms(own, other, values, terms):
    result = jnp.zeros_like(values)
    for at, term in enumerate(terms):
        result = jnp.where(other == at, term, result)
    return jnp.where(own, values, result)


def attend_quad(student, length, inputs, weights, biases, targets, between):
    q_ref, k_ref, v_ref, ctx_ref = targets
    rows = inputs.shape[0]
    lane = lane_index(rows)
    position = lax.broadcasted_iota(jnp.int32, (rows, LANES), 0)
    hidden_key = jnp.where(position < length, 0.0, masked_score)
    queries, keys, values = (
        (dot(inputs, weight, 1, 1) + bias).astype(BF16) for weight, bias in zip(weights, biases)
    )
    if not student:
        q_ref[...] = queries
        k_ref[...] = keys
    block = 512
    for pair in range(2):
        lanes = slice(pair * LANES, (pair + 1) * LANES)
        query, key, value = (
            array[:, lanes].astype(F32) for array in (queries, keys, values)
        )
        parts = []
        for odd in range(2):
            own, other = halves(lane, odd)
            place = slice((pair * 2 + odd) * LANES, (pair * 2 + odd + 1) * LANES)
            query_full = with_terms(own, other, query, (0.0, 0.0, 0.0, 1.0)).astype(BF16)
            key_full = with_terms(own, other, key, (1.0, 1.0, 1.0, hidden_key)).astype(BF16)
            value_full = with_terms(own, other, value, (1.0, 1.0, 1.0)).astype(BF16)
            if student:
                k_ref[:, place] = key_full
                v_ref[:, place] = value_full
            found = []
            for start in range(0, rows, block):
                take = slice(start, start + block)
                scores = dot(query_full[take], key_full, 1, 1)
                top = jnp.max(scores, axis=1, keepdims=True)
                expo = jnp.exp2((scores - top) * exponent).astype(BF16)
                mixed = dot(expo, value_full, 1, 0)
                at = 0 if odd else HEAD_DIM
                total = mixed[:, at : at + 1]
                found.append(mixed / total)
                if student:
                    logsum = top + jnp.log(total) / scaling
                    q_ref[take, place] = with_terms(
                        own[take],
                        other[take],
                        query[take],
                        tuple(-part for part in three_parts(logsum)) + (1.0,),
                    ).astype(BF16)
            parts.append(jnp.concatenate(found, axis=0))
            between(pair * 2 + odd)
        context = jnp.where(lane < HEAD_DIM, parts[0], parts[1])
        ctx_ref[:, lanes] = context.astype(ctx_ref.dtype)


def attend_kernel(student, lengths, *refs):
    if student:
        clip, x_ref, w_ref, b_ref, q_ref, k_ref, v_ref, ctx_ref, low_ref = refs

        @pl.when(pl.program_id(0) == 0)
        def _():
            width = saturation * clip[0]
            low_ref[...] = (width * jnp.tanh(x_ref[...].astype(F32) / width)).astype(BF16)

        x_ref = low_ref
        targets = (q_ref, k_ref, v_ref, ctx_ref)
    else:
        x_ref, w_ref, b_ref, q_ref, k_ref, ctx_ref = refs
        targets = (q_ref, k_ref, None, ctx_ref)
    attend_quad(
        student,
        lengths[own_index()],
        x_ref[...],
        [w_ref[slot] for slot in range(3)],
        [b_ref[slot] for slot in range(3)],
        targets,
        lambda head: None,
    )


def attend(student, lengths, clip_scales, inputs, weights, bias):
    rows = inputs.shape[0]
    wide = 4 * LANES
    narrow = 2 * LANES
    scalar = whole(pltpu.SMEM)
    in_specs = [scalar] + ([scalar] if student else [])
    in_specs += [
        fixed((rows, D)),
        pl.BlockSpec((3, narrow, D), lambda i: (0, i, 0)),
        columns((3, 1, narrow)),
    ]
    if student:
        out_shape = [jax.ShapeDtypeStruct((rows, 2 * D), BF16)] * 3 + [
            jax.ShapeDtypeStruct((rows, D), F32),
            jax.ShapeDtypeStruct((rows, D), BF16),
        ]
        out_specs = [columns((rows, wide))] * 3 + [columns((rows, narrow)), fixed((rows, D))]
        args = (lengths, clip_scales, inputs, weights, bias)
    else:
        out_shape = [jax.ShapeDtypeStruct((rows, D), BF16)] * 3
        out_specs = [columns((rows, narrow))] * 3
        args = (lengths, inputs, weights, bias)
    return pl.pallas_call(
        functools.partial(attend_kernel, student),
        grid=(D // narrow,),
        in_specs=in_specs,
        out_specs=out_specs,
        out_shape=out_shape,
        compiler_params=pltpu.CompilerParams(vmem_limit_bytes=vmem_bytes),
        name="student_attention" if student else "teacher_attention",
    )(*args)


def split_dot(left, right):
    high = right.astype(BF16)
    low = (right - high.astype(F32)).astype(BF16)
    return dot(left, high, 1, 0) + dot(left, low, 1, 0)


def attend_back_pair(length, inverse_pairs, q_ref, k_ref, v_ref, ctx_ref, dctx_ref, tq_ref, tk_ref, between):
    rows = ctx_ref.shape[0]
    lane = lane_index(rows)
    position = lax.broadcasted_iota(jnp.int32, (rows, LANES), 0)
    live = position < length
    low_half = lane < HEAD_DIM
    grad_context = dctx_ref[...].astype(F32)
    product = grad_context * ctx_ref[...]
    block = 512
    pieces = []
    for odd in range(2):
        own, other = halves(lane, odd)
        place = slice(odd * LANES, (odd + 1) * LANES)
        query, key, value = q_ref[:, place], k_ref[:, place], v_ref[:, place]
        weighted = jnp.sum(jnp.where(own, product, 0.0), axis=1, keepdims=True)
        grad_full = with_terms(
            own, other, grad_context, tuple(-part for part in three_parts(weighted))
        ).astype(BF16)
        grad_query = None
        key_parts, value_parts = [], []
        for start in range(0, rows, block):
            take = slice(start, start + block)
            probs = jnp.exp2(dot(key[take], query, 1, 1) * exponent)
            grad_scores = (probs * dot(value[take], grad_full, 1, 1)).astype(BF16)
            value_parts.append(dot(probs.astype(BF16), grad_full, 1, 0))
            key_parts.append(dot(grad_scores, query, 1, 0))
            part = dot(grad_scores, key[take], 0, 0)
            grad_query = part if grad_query is None else grad_query + part
        pieces.append(
            (grad_query, jnp.concatenate(key_parts, axis=0), jnp.concatenate(value_parts, axis=0))
        )
        between(odd)
    query_live, key_live = (
        jnp.where(live, jnp.where(low_half, ref[:, :LANES], ref[:, LANES:]), 0.0).astype(BF16)
        for ref in (q_ref, k_ref)
    )
    teach_query, teach_key = (
        jnp.where(live, ref[...], 0.0).astype(BF16) for ref in (tq_ref, tk_ref)
    )
    row = lax.broadcasted_iota(jnp.int32, (LANES, LANES), 0)
    col = lax.broadcasted_iota(jnp.int32, (LANES, LANES), 1)
    same = (row < HEAD_DIM) == (col < HEAD_DIM)

    def gram(left, right):
        return jnp.where(same, outer_rows(left, right), 0.0)

    key_key, teach_key_key = gram(key_live, key_live), gram(teach_key, key_live)
    query_query, teach_query_query = gram(query_live, query_live), gram(teach_query, query_live)
    squares = (
        query_query * key_key
        - 2.0 * teach_query_query * teach_key_key
        + gram(teach_query, teach_query) * gram(teach_key, teach_key)
    )
    squares = jnp.sum(squares.reshape(LANES // 8, 8, LANES), axis=0)

    squares = squares * (scaling * scaling * inverse_pairs)
    factor = 2.0 * scaling * scaling * inverse_pairs
    query_term = split_dot(
        jnp.concatenate([query_live, teach_query], axis=1),
        jnp.concatenate([key_key, -teach_key_key], axis=0),
    )
    key_term = split_dot(
        jnp.concatenate([key_live, teach_key], axis=1),
        jnp.concatenate([query_query, -teach_query_query], axis=0),
    )
    (even_q, even_k, even_v), (odd_q, odd_k, odd_v) = pieces
    return (
        (jnp.where(low_half, even_q, odd_q) * scaling + factor * query_term).astype(BF16),
        (jnp.where(low_half, even_k, odd_k) * scaling + factor * key_term).astype(BF16),
        jnp.where(low_half, even_v, odd_v).astype(BF16),
    ), squares


def attend_back_kernel(
    lengths, inverse_pairs, q_ref, k_ref, v_ref, ctx_ref, dctx_ref, tq_ref, tk_ref, grad_ref, sum_ref
):
    refs = (q_ref, k_ref, v_ref, ctx_ref, dctx_ref, tq_ref, tk_ref)
    grads, squares = attend_back_pair(lengths[own_index()], inverse_pairs[0], *refs, lambda odd: None)

    @pl.when(pl.program_id(0) == 0)
    def _():
        sum_ref[...] = jnp.zeros_like(sum_ref)

    sum_ref[...] += squares
    for slot in range(3):
        grad_ref[slot] = grads[slot]


def attend_back(lengths, inverse_pairs, query, key, value, context, grad_context, tq, tk):
    rows = context.shape[0]
    scalar = whole(pltpu.SMEM)
    return pl.pallas_call(
        attend_back_kernel,
        grid=(D // LANES,),
        in_specs=[scalar, scalar]
        + [columns((rows, 2 * LANES))] * 3
        + [columns((rows, LANES))] * 4,
        out_specs=[columns((3, rows, LANES)), fixed((8, LANES))],
        out_shape=[
            jax.ShapeDtypeStruct((3, rows, D), BF16),
            jax.ShapeDtypeStruct((8, LANES), F32),
        ],
        compiler_params=pltpu.CompilerParams(vmem_limit_bytes=vmem_bytes),
        name="attention_backward",
    )(lengths, inverse_pairs, query, key, value, context, grad_context, tq, tk)


def gelu_parts(upper):
    cumulative = 0.5 * (1.0 + lax.erf(upper * (1.0 / math.sqrt(2.0))))
    return cumulative, upper * cumulative


ff_part = D


def teacher_rows(tokens, context, wo_ref, up_part, w2_ref, vec, up_bias, out_ref, between):
    normed, _ = normalize(tokens.astype(F32) + dot(context, wo_ref[...], 1, 1) + vec[3:4])
    hidden = normed * vec[5:6] + vec[7:8]
    low = hidden.astype(BF16)
    lower = None
    for at in range(w2_ref.shape[1] // ff_part):
        take = slice(at * ff_part, (at + 1) * ff_part)
        _, bent = gelu_parts(dot(low, up_part(at), 1, 1) + up_bias[at : at + 1])
        part = dot(bent.astype(BF16), w2_ref[:, take], 1, 1)
        lower = part if lower is None else lower + part
        between(at)
    final, _ = normalize(hidden + lower + vec[4:5])
    out_ref[...] = final * vec[6:7] + vec[8:9]


def teacher_kernel(tok_ref, ctx_ref, wo_ref, w1_ref, w2_ref, vec_ref, ub_ref, out_ref):
    teacher_rows(
        tok_ref[...],
        ctx_ref[...],
        wo_ref,
        lambda at: w1_ref[at * ff_part : (at + 1) * ff_part],
        w2_ref,
        vec_ref[...],
        ub_ref[...],
        out_ref,
        lambda at: None,
    )


def teacher_tail(tokens, context, wo, w1, w2, vectors, up_bias):
    rows, wide = tokens.shape[0], w1.shape[0]
    block = 256
    return pl.pallas_call(
        teacher_kernel,
        grid=(rows // block,),
        in_specs=[
            row_blocks((block, D)),
            row_blocks((block, D)),
            fixed((D, D)),
            fixed((wide, D)),
            fixed((D, wide)),
            fixed(vectors.shape),
            fixed(up_bias.shape),
        ],
        out_specs=row_blocks((block, D)),
        out_shape=jax.ShapeDtypeStruct((rows, D), F32),
        compiler_params=pltpu.CompilerParams(vmem_limit_bytes=vmem_bytes),
        name="teacher_feed_forward",
    )(tokens, context, wo, w1, w2, vectors, up_bias)


def student_kernel(
    row_steps,
    lengths,
    clip,
    tok_ref,
    cot_ref,
    teach_ref,
    ctx_ref,
    wo_ref,
    w1_ref,
    w2_ref,
    vec_ref,
    out_ref,
    dctx_ref,
    res_ref,
    sums_ref,
    upsum_ref,
    dw2_ref,
    dw1_ref,
    dwo_ref,
    df_all,
    fb_all,
    du_all,
    hb_all,
    dao_all,
    cb_all,
    slope_ref,
):
    step = pl.program_id(0)
    down_steps, up_steps = D // dw2_ref.shape[0], w1_ref.shape[0] // dw1_ref.shape[0]

    @pl.when(step < row_steps)
    def _():
        rows = out_ref.shape[0]
        here = pl.ds(pl.multiple_of(step * rows, rows), rows)
        student_rows(
            step,
            lengths,
            clip,
            tok_ref,
            cot_ref,
            teach_ref,
            ctx_ref,
            wo_ref,
            w1_ref,
            w2_ref,
            vec_ref[9:18],
            vec_ref[22:26],
            out_ref,
            dctx_ref,
            *(ref.at[here] for ref in (dao_all, cb_all, du_all, hb_all, df_all, fb_all)),
            res_ref,
            sums_ref,
            upsum_ref,
            slope_ref,
        )

    def weight_grad(target, left, right, at):
        width = target.shape[0]
        lanes = pl.ds(pl.multiple_of(at * width, width), width)
        target[...] = outer_rows(left[:, lanes], right[...]).astype(BF16)

    @pl.when((step >= row_steps) & (step < row_steps + down_steps))
    def _():
        weight_grad(dw2_ref, df_all, fb_all, step - row_steps)

    @pl.when((step >= row_steps + down_steps) & (step < row_steps + down_steps + up_steps))
    def _():
        weight_grad(dw1_ref, du_all, hb_all, step - row_steps - down_steps)

    @pl.when(step == row_steps + down_steps + up_steps)
    def _():
        dwo_ref[...] = outer_rows(dao_all[...], cb_all[...]).astype(BF16)


def student_rows(
    step,
    lengths,
    clip,
    tok_ref,
    cot_ref,
    teach_ref,
    ctx_ref,
    wo_ref,
    w1_ref,
    w2_ref,
    vec,
    up_bias,
    out_ref,
    dctx_ref,
    dao_ref,
    cb_ref,
    du_ref,
    hb_ref,
    df_ref,
    fb_ref,
    res_ref,
    sums_ref,
    upsum_ref,
    slope_ref,
):
    wide = w1_ref.shape[0]
    ctx_width, hid_width, act_width = (saturation * clip[at] for at in (1, 2, 3))
    ctx_bent = jnp.tanh(ctx_ref[...] / ctx_width)
    ctx_low = (ctx_width * ctx_bent).astype(BF16)
    cb_ref[...] = ctx_low
    first, first_inverse = normalize(
        tok_ref[...].astype(F32) + dot(ctx_low, wo_ref[...], 1, 1) + vec[3:4]
    )
    hidden = first * vec[5:6] + vec[7:8]
    hid_bent = jnp.tanh(hidden / hid_width)
    hid_low = (hid_width * hid_bent).astype(BF16)
    hb_ref[...] = hid_low
    lower = None
    for at in range(wide // ff_part):
        take = slice(at * ff_part, (at + 1) * ff_part)
        upper = dot(hid_low, w1_ref[take], 1, 1) + up_bias[at : at + 1]
        cumulative, bent = gelu_parts(upper)
        act = jnp.tanh(bent / act_width)
        density = jnp.exp(-0.5 * upper * upper) * (1.0 / math.sqrt(2.0 * math.pi))
        slope_ref[:, take] = (1.0 - act * act) * (cumulative + upper * density)
        act_low = (act_width * act).astype(BF16)
        fb_ref[:, take] = act_low
        part = dot(act_low, w2_ref[:, take], 1, 1)
        lower = part if lower is None else lower + part
    second, second_inverse = normalize(hidden + lower + vec[4:5])
    result = second * vec[6:7] + vec[8:9]
    out_ref[...] = result.astype(BF16)
    rows = result.shape[0]
    position = lax.broadcasted_iota(jnp.int32, (rows, D), 0) + step * rows
    gap = jnp.where(position < lengths[own_index()], result - teach_ref[...], 0.0)
    grad_out = cot_ref[...].astype(F32) + gap * (2.0 * hidden_weight)
    grad_second = norm_back(grad_out * vec[6:7], second, second_inverse)
    grad_lower = grad_second.astype(BF16)
    df_ref[...] = grad_lower
    grad_hidden = None
    up_sums = []
    for at in range(wide // ff_part):
        take = slice(at * ff_part, (at + 1) * ff_part)
        grad_upper = (dot(grad_lower, w2_ref[:, take], 1, 0) * slope_ref[:, take]).astype(BF16)
        du_ref[:, take] = grad_upper
        up_sums.append(jnp.sum(grad_upper.astype(F32), axis=0, keepdims=True))
        part = dot(grad_upper, w1_ref[take], 1, 0)
        grad_hidden = part if grad_hidden is None else grad_hidden + part
    grad_hidden = grad_second + grad_hidden * (1.0 - hid_bent * hid_bent)
    grad_first = norm_back(grad_hidden * vec[5:6], first, first_inverse)
    res_ref[...] = grad_first
    grad_attn = grad_first.astype(BF16)
    dao_ref[...] = grad_attn
    dctx_ref[...] = (
        dot(grad_attn, wo_ref[...], 1, 0) * (1.0 - ctx_bent * ctx_bent)
    ).astype(BF16)

    @pl.when(step == 0)
    def _():
        sums_ref[...] = jnp.zeros_like(sums_ref)
        upsum_ref[...] = jnp.zeros_like(upsum_ref)

    for at, term in enumerate(
        (
            grad_attn.astype(F32),
            grad_lower.astype(F32),
            grad_hidden * first,
            grad_out * second,
            grad_hidden,
            grad_out,
            gap * gap,
        )
    ):
        sums_ref[at : at + 1] += jnp.sum(term, axis=0, keepdims=True)
    for at, total in enumerate(up_sums):
        upsum_ref[at : at + 1] += total


def student_middle(
    lengths, clip_scales, tokens, cotangent, teach_out, context, wo, w1, w2, vectors
):
    rows, wide = tokens.shape[0], w1.shape[0]
    block, down_block, up_block = 256, 256, D
    row_steps, down_steps, up_steps = rows // block, D // down_block, wide // up_block
    scalar = whole(pltpu.SMEM)

    def window(first, count, shape):
        return pl.BlockSpec(shape, lambda i: (jnp.clip(i - first, 0, count - 1), 0))

    row_spec = window(0, row_steps, (block, D))
    narrow, broad = pltpu.VMEM((rows, D), BF16), pltpu.VMEM((rows, wide), BF16)
    return pl.pallas_call(
        functools.partial(student_kernel, row_steps),
        grid=(row_steps + down_steps + up_steps + 1,),
        in_specs=[scalar, scalar]
        + [row_spec] * 4
        + [fixed((D, D)), fixed((wide, D)), fixed((D, wide)), fixed(vectors.shape)],
        out_specs=[row_spec] * 3
        + [
            fixed((8, D)),
            fixed((wide // D, D)),
            window(row_steps, down_steps, (down_block, wide)),
            window(row_steps + down_steps, up_steps, (up_block, D)),
            fixed((D, D)),
        ],
        out_shape=[
            jax.ShapeDtypeStruct((rows, D), BF16),
            jax.ShapeDtypeStruct((rows, D), BF16),
            jax.ShapeDtypeStruct((rows, D), F32),
            jax.ShapeDtypeStruct((8, D), F32),
            jax.ShapeDtypeStruct((wide // D, D), F32),
            jax.ShapeDtypeStruct((D, wide), BF16),
            jax.ShapeDtypeStruct((wide, D), BF16),
            jax.ShapeDtypeStruct((D, D), BF16),
        ],
        scratch_shapes=[narrow, broad, broad, narrow, narrow, narrow]
        + [pltpu.VMEM((block, wide), F32)],
        compiler_params=pltpu.CompilerParams(vmem_limit_bytes=vmem_bytes),
        name="student_feed_forward",
    )(lengths, clip_scales, tokens, cotangent, teach_out, context, wo, w1, w2, vectors)


def input_kernel(clip, grad_ref, w_ref, low_ref, tok_ref, res_ref, out_ref, dw_ref, sum_ref, acc_ref):
    slot = pl.program_id(0)
    grad = grad_ref[0]
    part = dot(grad, w_ref[0], 1, 0)
    dw_ref[0] = outer_rows(grad, low_ref[...]).astype(dw_ref.dtype)
    sum_ref[0] = jnp.sum(grad.astype(F32), axis=0, keepdims=True)

    @pl.when(slot == 0)
    def _():
        acc_ref[...] = part

    @pl.when(slot > 0)
    def _():
        acc_ref[...] += part

    @pl.when(slot == pl.num_programs(0) - 1)
    def _():
        bent = jnp.tanh(tok_ref[...].astype(F32) / (saturation * clip[0]))
        out_ref[...] = (res_ref[...] + acc_ref[...] * (1.0 - bent * bent)).astype(BF16)


def input_grads(clip_scales, grads, weights, low, tokens, residual):
    rows = tokens.shape[0]
    slotted = lambda *shape: pl.BlockSpec((1,) + shape, lambda i: (i, 0, 0))
    return pl.pallas_call(
        input_kernel,
        grid=(3,),
        in_specs=[
            whole(pltpu.SMEM),
            slotted(rows, D),
            slotted(D, D),
            fixed((rows, D)),
            fixed((rows, D)),
            fixed((rows, D)),
        ],
        out_specs=[fixed((rows, D)), slotted(D, D), slotted(1, D)],
        out_shape=[
            jax.ShapeDtypeStruct((rows, D), BF16),
            jax.ShapeDtypeStruct((3, D, D), BF16),
            jax.ShapeDtypeStruct((3, 1, D), F32),
        ],
        scratch_shapes=[pltpu.VMEM((rows, D), F32)],
        compiler_params=pltpu.CompilerParams(vmem_limit_bytes=vmem_bytes),
        name="input_gradient",
    )(clip_scales, grads, weights, low, tokens, residual)


gather_chunks = ((0,), (1,), (2,), (3,), (4, 5), (6,), (7, 8), (9,))
gather_leads = (1, 1, 1, 3, 1, 1, 1, 1, 1, 1)
late_chunks = (5,)
ahead_stages = ((0, 0), (1, 0), (2, 0), (0, 1), (1, 1), (2, 1), (0, 2), (1, 2), (3, 0), (2, 2), (4, 0), (0, 3), (1, 3), (3, 1), (0, 4), (2, 3), (0, 5), (1, 4), (4, 1), (1, 5), (5, 0), (0, 6), (3, 2), (2, 4), (0, 7), (6, 0), (2, 5), (4, 2), (1, 6), (5, 1), (3, 3), (1, 7), (2, 6), (6, 1), (5, 2), (2, 7))
opening_stages = {3: (), 6: ()}
gather_between = {(0, 1): ((3, 4), (4, 3), (6, 2)), (0, 3): ((3, 5),), (1, 1): ((3, 6), (7, 0)), (1, 3): ((3, 7), (5, 3)), (2, 1): ((4, 4), (6, 3)), (2, 3): ((7, 1),), (3, 1): ((4, 5),), (3, 3): ((4, 6), (5, 4)), (4, 1): ((4, 7), (7, 2), (6, 4)), (5, 1): ((5, 5), (6, 5)), (5, 3): ((7, 3), (5, 6)), (6, 1): ((6, 6),), (6, 3): ((7, 4),), (7, 1): ((6, 7),), (7, 3): ((7, 5),), (8, 3): ((7, 6),), (9, 1): ((7, 7),)}
closing_stages = ()


def lay_flat(flat, owners):
    rows = owners.shape[-2]
    for owner in range(flat.shape[0] // rows):
        flat[owner * rows : (owner + 1) * rows] = owners[
            owner // 8, owner // 4 % 2, owner // 2 % 2, owner % 2
        ]


def own_lines(target, line_refs, up_bias_refs):
    at = own_index()
    target[...] = jnp.zeros_like(target)
    width = line_refs[0].shape[1]
    place, row = lanes_of(width, at * width), 0
    for ref in line_refs:
        target[row : row + ref.shape[0]] = dot(ref[...], place, 1, 0)
        row += ref.shape[0]
    wide = up_bias_refs[0].shape[1]
    owners = D // wide
    place = lanes_of(wide, lax.rem(at, owners) * wide)
    for ref in up_bias_refs:
        rows = wide * count_of() // D
        where = lax.broadcasted_iota(jnp.int32, (rows, D), 0) == at // owners
        target[row : row + rows] = jnp.where(where, dot(ref[...], place, 1, 0), 0.0)
        row += rows


def count_of():
    return lax.axis_size("dp") * lax.axis_size("shard")


def forward_kernel(depth, tail_steps, lengths, clip, *refs):
    (teach_attn, teach_up, teach_down, attn_ref, up_ref, down_ref, teach_tok, tok), refs = (
        refs[:8],
        refs[8:],
    )
    line_refs, up_bias_refs, refs = refs[:6], refs[6:8], refs[8:]
    (tq_ref, tk_ref, q_ref, k_ref, v_ref, ctx_ref, low_ref, out_ref, vec_ref), refs = (
        refs[:9],
        refs[9:],
    )
    (qkv_out, wo_out, up_out, down_out), refs = refs[:4], refs[4:]
    (teach_qkv, own_qkv, teach_wo, teach_w1, teach_w2, attn_low, up_low, down_low, teach_ctx), refs = (
        refs[:9],
        refs[9:],
    )
    (qkv_flat, wo_flat, w2_flat), refs = refs[:3], refs[3:]
    qkv_sem, shared, sems = refs[0], refs[1:6], refs[6:]
    place = Place(depth)
    step = pl.program_id(0)
    narrow = 2 * LANES
    attend_steps = D // narrow
    last = pl.num_programs(0) - 1

    ins = [teach_attn.at[slot] for slot in range(3)] + [
        attn_low.at[pl.ds(0, 3)],
        teach_attn.at[3],
        teach_up,
        teach_down,
        attn_low.at[3],
        up_low,
        down_low,
    ]
    outs = [teach_qkv.at[slot] for slot in range(3)] + [
        own_qkv,
        teach_wo,
        teach_w1,
        teach_w2,
        wo_out,
        up_out,
        down_out,
    ]
    begin, stage, sent = gather_stage(place, ins, outs, gather_leads, gather_chunks, late_chunks, sems)

    def run(stages):
        for chunk, number in stages:
            stage(chunk, number)

    def finish_lines(total):
        vec_ref[...] = total.astype(F32)

    line_stage = shared_stage(place, finish_lines, shared)
    line_count = depth + 4

    @pl.when(step == 0)
    def _():
        own_lines(vec_ref, line_refs, up_bias_refs)
        shared[0][0] = vec_ref[...].astype(BF16)
        place.barrier()
        begin((0, 1, 2))
        lines = iter(range(line_count))
        for at, (chunk, number) in enumerate(ahead_stages):
            if at == 2:
                for latent, low in ((attn_ref, attn_low), (up_ref, up_low), (down_ref, down_low)):
                    values = latent[...]
                    scale = jnp.mean(jnp.abs(values), axis=-1, keepdims=True)
                    sign = jnp.where(values > 0, 1.0, jnp.where(values < 0, -1.0, 0.0))
                    low[...] = (scale * sign).astype(BF16)
                begin((4, 5, 3, 6, 7))
            stage(chunk, number)
            if at % 2 == 0:
                for line in lines:
                    line_stage(line)
                    break
        for line in lines:
            line_stage(line)

    def slots(first, steps, at):
        for local in range(steps):
            stages = gather_between.get((first + local, at))
            if stages:

                @pl.when(step == first + local)
                def _():
                    run(stages)

    def opening(first):
        if opening_stages[first]:

            @pl.when(step == first)
            def _():
                run(opening_stages[first])

    def qkv_copy():
        return pltpu.make_async_copy(own_qkv, qkv_out, qkv_sem)

    def attend_step(student, first, inputs, weights, line, targets):
        local = step - first
        @pl.when(local == 0)
        def _():
            for slot in range(3):
                lay_flat(qkv_flat.at[slot], weights.at[slot])

        rows = pl.ds(pl.multiple_of(local * narrow, narrow), narrow)
        attend_quad(
            student,
            lengths[own_index()],
            inputs[...],
            [qkv_flat[slot, rows, :] for slot in range(3)],
            [vec_ref[line + slot : line + slot + 1, rows] for slot in range(3)],
            targets,
            lambda head: slots(first, attend_steps, head),
        )

    @pl.when(step < attend_steps)
    def _():
        lanes = pl.ds(pl.multiple_of(step * narrow, narrow), narrow)
        attend_step(
            False, 0, teach_tok, teach_qkv, 0, (tq_ref, tk_ref, None, teach_ctx.at[:, lanes])
        )

    @pl.when((step >= attend_steps) & (step < 2 * attend_steps))
    def _():
        opening(attend_steps)

        @pl.when(step == attend_steps)
        def _():
            qkv_copy().start()
            width = saturation * clip[0]
            low_ref[...] = (width * jnp.tanh(tok[...].astype(F32) / width)).astype(BF16)

        attend_step(True, attend_steps, low_ref, own_qkv, 9, (q_ref, k_ref, v_ref, ctx_ref))

    @pl.when(step >= 2 * attend_steps)
    def _():
        first = 2 * attend_steps
        opening(first)

        @pl.when(step == first)
        def _():
            lay_flat(wo_flat, teach_wo)
            lay_flat(w2_flat, teach_w2)

        block = out_ref.shape[0]
        rows = pl.ds(pl.multiple_of((step - first) * block, block), block)
        teacher_rows(
            teach_tok[rows, :],
            teach_ctx[rows, :],
            wo_flat,
            lambda at: teach_w1[at].reshape(D, D),
            w2_flat,
            vec_ref[0:9],
            vec_ref[18:22],
            out_ref,
            lambda at: slots(first, tail_steps, at),
        )

    @pl.when(step == last)
    def _():
        run(closing_stages)
        qkv_copy().wait()
        for chunk in range(len(gather_chunks)):
            sent(chunk)


def forward(
    lengths,
    clip_scales,
    teacher_attn,
    teacher_up,
    teacher_down,
    lines,
    up_biases,
    latents,
    teacher_tokens,
    tokens,
):
    rows = tokens.shape[0]
    depth = lax.axis_size("dp") // 2
    attn_latent, up_latent, down_latent = latents
    narrow, wide = attn_latent.shape[1], up_latent.shape[0]
    lanes, quad, block = 2 * LANES, 4 * LANES, 256
    attend_steps, tail_steps = D // lanes, rows // block
    dma = pltpu.SemaphoreType.DMA
    owners = (depth, 2, 2, 2)
    qkv_shape, wo_shape = (3,) + owners + (narrow, D), owners + (narrow, D)
    up_shape, down_shape = owners + (wide, D), owners + (narrow, down_latent.shape[1])
    scalar = whole(pltpu.SMEM)

    def window(first, count, shape, along):
        def index(i):
            at = jnp.clip(i - first, 0, count - 1)
            return (at, 0) if along == 0 else (0, at)

        return pl.BlockSpec(shape, index)

    def student_columns(width):
        return window(attend_steps, attend_steps, (rows, width), 1)

    results = pl.pallas_call(
        functools.partial(forward_kernel, depth, tail_steps),
        grid=(2 * attend_steps + tail_steps,),
        in_specs=[scalar] * 2
        + [whole(pl.ANY)] * 3
        + [
            fixed(shape)
            for shape in (
                attn_latent.shape,
                up_latent.shape,
                down_latent.shape,
                (rows, D),
                (rows, D),
                *(line.shape for line in lines),
                *(line.shape for line in up_biases),
            )
        ],
        out_specs=[window(0, attend_steps, (rows, lanes), 1)] * 2
        + [student_columns(quad)] * 3
        + [
            student_columns(lanes),
            fixed((rows, D)),
            window(2 * attend_steps, tail_steps, (block, D), 0),
            fixed((vector_rows, D)),
        ]
        + [whole(pl.ANY)] * 4,
        out_shape=[jax.ShapeDtypeStruct((rows, D), BF16)] * 2
        + [jax.ShapeDtypeStruct((rows, 2 * D), BF16)] * 3
        + [
            jax.ShapeDtypeStruct((rows, D), F32),
            jax.ShapeDtypeStruct((rows, D), BF16),
            jax.ShapeDtypeStruct((rows, D), F32),
            jax.ShapeDtypeStruct((vector_rows, D), F32),
        ]
        + [
            jax.ShapeDtypeStruct(shape, BF16)
            for shape in (qkv_shape, wo_shape, up_shape, down_shape)
        ],
        scratch_shapes=[
            pltpu.VMEM(shape, BF16)
            for shape in (
                qkv_shape,
                qkv_shape,
                wo_shape,
                up_shape,
                down_shape,
                attn_latent.shape,
                up_latent.shape,
                down_latent.shape,
                (rows, D),
                (3, D, D),
                (D, D),
                (D, down_latent.shape[1]),
            )
        ]
        + [dma]
        + shared_scratch(depth, vector_rows, BF16)
        + gather_scratch(gather_chunks, depth),
        compiler_params=pltpu.CompilerParams(
            collective_id=0, has_side_effects=True, vmem_limit_bytes=vmem_bytes
        ),
        name="gather_attention_and_teacher",
    )(
        lengths,
        clip_scales,
        teacher_attn,
        teacher_up,
        teacher_down,
        attn_latent,
        up_latent,
        down_latent,
        teacher_tokens,
        tokens,
        *lines,
        *up_biases,
    )
    return list(results[:9]) + gathered(results[9:])


first_stages = ((0, 0), (1, 0), (2, 0))
between_stages = {1: ((0, 1), (0, 2)), 3: ((1, 1), (1, 2), (0, 3), (2, 1), (2, 2)), 5: ((1, 3),), 9: ((0, 4), (2, 3)), 11: ((1, 4), (2, 4))}
after_weights = (((0, 5),), ((3, 1), (3, 2)), ((4, 1), (4, 2), (3, 3)))
after_inputs = (((1, 5), (4, 3), (0, 6), (5, 1), (5, 2), (2, 5)), ((4, 4), (3, 4), (0, 7), (0, 8), (5, 3)), ((1, 6), (4, 5), (5, 4), (2, 6)))
last_stages = ((3, 5), (4, 6), (5, 5), (1, 7), (1, 8), (3, 6), (2, 7), (2, 8), (4, 7), (4, 8), (5, 6), (3, 7), (3, 8), (5, 7), (5, 8))


def latent_rows(latent, grad):
    size = latent.shape[-1]
    scale = jnp.mean(jnp.abs(latent), axis=-1, keepdims=True)
    sign = jnp.where(latent > 0, 1.0, jnp.where(latent < 0, -1.0, 0.0))
    return scale * grad + sign * (jnp.sum(grad * latent, axis=-1, keepdims=True) / size)


def inverse_norms(lengths, width):
    tokens, pairs = jnp.int32(0), jnp.int32(0)
    for at in range(lengths.shape[0]):
        tokens, pairs = tokens + lengths[at], pairs + lengths[at] * lengths[at]
    return tuple(
        1.0 / (jnp.full((1, width), total.astype(F32)) * factor)
        for total, factor in ((pairs, float(HEADS)), (tokens, float(D)))
    )


def finish_kernel(depth, lengths, clip, *refs):
    pair_refs, refs = refs[:7], refs[7:]
    dw_refs, refs = refs[:3], refs[3:]
    held_refs, refs = refs[:4], refs[4:]
    (sums_ref, upsum_ref, attn_ref, up_ref, down_ref), refs = refs[:5], refs[5:]
    (input_ref, attn_grad, up_grad, down_grad), refs = refs[:4], refs[4:]
    (bias_grad, gain_grad, shift_grad, up_bias_grad, loss_ref), refs = refs[:5], refs[5:]
    (grad_ref, square_ref, dwq_ref, dwk_ref, dwv_ref), refs = refs[:5], refs[5:]
    (low_ref, w_ref, tok_ref, res_ref, load_sem), refs = refs[:5], refs[5:]
    loads = [
        pltpu.make_async_copy(source, target, load_sem.at[at])
        for at, (source, target) in enumerate(zip(held_refs, (low_ref, w_ref, tok_ref, res_ref)))
    ]
    shared, scratch = refs[:5], refs[5:]
    place = Place(depth)
    step = pl.program_id(0)
    last = pl.num_programs(0) - 1
    pairs = D // LANES

    def finish(item, lead, total):
        if item == 0:
            down_grad[...] = latent_rows(down_ref[...], total)
        elif item == 1:
            up_grad[...] = latent_rows(up_ref[...], total)
        else:
            slot = 3 if item == 2 else item - 3
            attn_grad[slot] = latent_rows(attn_ref[slot], total)

    def finish_lines(total):
        at = own_index()
        width, wide = bias_grad.shape[1], up_bias_grad.shape[1]
        taken = take_lanes(total[0:9], width, at * width)
        bias_grad[...] = taken[0:5]
        gain_grad[...] = taken[5:7]
        shift_grad[...] = taken[7:9]
        owners, rows = D // wide, total[9:13]
        where = lax.broadcasted_iota(jnp.int32, rows.shape, 0) == at // owners
        row = jnp.sum(jnp.where(where, rows, 0.0), axis=0, keepdims=True)
        up_bias_grad[...] = take_lanes(row, wide, lax.rem(at, owners) * wide)
        loss_ref[...] = jnp.sum(total[13:14], axis=1, keepdims=True)

    own = (dwq_ref, dwk_ref, dwv_ref)
    stage = scatter_stage(place, tuple(dw_refs) + own, finish, scratch, 6)
    line_stage = shared_stage(place, finish_lines, shared)

    def run(stages):
        for item, number in stages:
            stage(item, number)

    @pl.when(step == 0)
    def _():
        place.barrier()
        run(first_stages)
        for load in loads:
            load.start()
        square_ref[...] = jnp.zeros_like(square_ref)

    @pl.when(step < pairs)
    def _():
        def between(odd):
            for at, stages in between_stages.items():
                if at % 2 == odd:

                    @pl.when(step == at // 2)
                    def _():
                        for item, number in stages:
                            stage(item, number)

        grads, squares = attend_back_pair(
            lengths[own_index()], inverse_norms(lengths, LANES)[0], *pair_refs, between
        )
        square_ref[...] += squares
        lanes = pl.ds(pl.multiple_of(step * LANES, LANES), LANES)
        for slot in range(3):
            grad_ref[slot, :, lanes] = grads[slot]

    def weight_grad(slot):
        total = outer_rows(grad_ref[slot], low_ref[...]).astype(BF16)
        rows = dwq_ref.shape[-2]
        for owner in range(D // rows):
            where = (owner // 8, owner // 4 % 2, owner // 2 % 2, owner % 2)
            own[slot][where] = total[owner * rows : (owner + 1) * rows]
        stage(3 + slot, 0)

    @pl.when(step == pairs)
    def _():
        held = shared[0]
        held[0] = jnp.zeros_like(held[0])
        for slot in range(3):
            held[0, slot : slot + 1] = jnp.sum(
                grad_ref[slot].astype(F32), axis=0, keepdims=True
            )
        held[0, 3:9] = sums_ref[0:6]
        held[0, 9:13] = upsum_ref[...]
        held[0, 13:14] = sums_ref[6:7] * inverse_norms(lengths, D)[1]
        held[0, 13:14, :LANES] += jnp.sum(square_ref[...], axis=0, keepdims=True)
        line_stage(0)
        loads[0].wait()
        weight_grad(0)
        run(after_weights[0])
        weight_grad(1)
        run(after_weights[1])

    @pl.when(step == last)
    def _():
        line_stage(1)
        weight_grad(2)
        run(after_weights[2])
        for load in loads[1:]:
            load.wait()
        total = None
        for slot in range(3):
            line_stage(2 + slot)
            part = dot(grad_ref[slot], w_ref[slot], 1, 0)
            total = part if total is None else total + part
            run(after_inputs[slot])
        bent = jnp.tanh(tok_ref[...].astype(F32) / (saturation * clip[0]))
        input_ref[...] = (res_ref[...] + total * (1.0 - bent * bent)).astype(BF16)
        for at, (item, number) in enumerate(last_stages):
            if at < 3 and 5 + at < depth + 4:
                line_stage(5 + at)
            stage(item, number)


def move_kernel(count, *refs):
    copies = [
        pltpu.make_async_copy(refs[at], refs[count + at], refs[2 * count].at[at])
        for at in range(count)
    ]
    for copy in copies:
        copy.start()
    for copy in copies:
        copy.wait()


def moved(*arrays):
    count = len(arrays)
    return pl.pallas_call(
        functools.partial(move_kernel, count),
        in_specs=[whole()] * count,
        out_specs=[whole(pl.ANY)] * count,
        out_shape=[jax.ShapeDtypeStruct(array.shape, array.dtype) for array in arrays],
        compiler_params=pltpu.CompilerParams(vmem_limit_bytes=vmem_bytes),
        scratch_shapes=[pltpu.SemaphoreType.DMA((count,))],
        name="move_results",
    )(*arrays)


def finish_backward(
    lengths,
    clip_scales,
    pair_arrays,
    weight_grads,
    qkv_w,
    low,
    tokens,
    residual,
    sums,
    up_sums,
    latents,
    narrow,
    wide,
):
    dp, shard = lax.axis_size("dp"), lax.axis_size("shard")
    attn_latent, up_latent, down_latent = latents
    if not tiled_over((dp, shard), narrow):
        live_float = lengths.astype(F32)
        inverse_pairs = (1.0 / (HEADS * jnp.sum(live_float * live_float))).reshape(1)
        inverse_hidden = 1.0 / (D * jnp.sum(live_float))
        grads, squares = attend_back(lengths, inverse_pairs, *pair_arrays)
        input_grad, qkv_weight_grad, qkv_sums = input_grads(
            clip_scales, grads, qkv_w, low, tokens, residual
        )
        local_loss = sums[6:7] * inverse_hidden
        local_loss = local_loss + jnp.pad(
            jnp.sum(squares, axis=0, keepdims=True), ((0, 0), (0, D - LANES))
        )
        lines = jnp.concatenate(
            [qkv_sums[:, 0], sums[:6], up_sums, local_loss], axis=0
        )
        lines = lax.psum(lines, AXES)
        down_total, up_total, attn_total = scatter(
            weight_grads[:2]
            + [jnp.concatenate([qkv_weight_grad, weight_grads[2][None].astype(BF16)], axis=0)]
        )
        attn_grad = latent_grad(attn_latent, attn_total)
        up_grad = latent_grad(up_latent, up_total)
        down_grad = latent_grad(down_latent, down_total)
        at = lax.axis_index(AXES)
        own = lax.dynamic_slice_in_dim(lines[:9], at * narrow, narrow, axis=1)
        bias_grad, gain_grad, shift_grad = own[:5], own[5:7], own[7:9]
        up_bias_grad = lax.dynamic_slice_in_dim(lines[9:13].reshape(-1), at * wide, wide)
        loss = jnp.sum(lines[13])
    else:
        depth = dp // 2
        rows = tokens.shape[0]
        dw = [split_rows(grad, depth) for grad in weight_grads]
        own_shape = (depth, 2, 2, 2, narrow, D)
        shapes = [(1,) + grad.shape[-2:] for grad in dw] + [(1, narrow, D)] * 3
        scalar = whole(pltpu.SMEM)
        pairs = D // LANES

        def pair_columns(width):
            return pl.BlockSpec((rows, width), lambda i: (0, jnp.minimum(i, pairs - 1)))

        small_shapes = ((5, narrow), (2, narrow), (2, narrow), (1, wide), (1, 1))
        (
            input_grad,
            attn_grad,
            up_grad,
            down_grad,
            bias_grad,
            gain_grad,
            shift_grad,
            up_bias_grad,
            loss,
        ) = pl.pallas_call(
            functools.partial(finish_kernel, depth),
            grid=(pairs + 2,),
            in_specs=[scalar] * 2
            + [pair_columns(2 * LANES)] * 3
            + [pair_columns(LANES)] * 4
            + [whole(pl.ANY)] * 7
            + [
                fixed(array_shape)
                for array_shape in (
                    sums.shape,
                    up_sums.shape,
                    attn_latent.shape,
                    up_latent.shape,
                    down_latent.shape,
                )
            ],
            out_specs=[
                fixed(array_shape)
                for array_shape in (
                    (rows, D),
                    attn_latent.shape,
                    up_latent.shape,
                    down_latent.shape,
                    *small_shapes,
                )
            ],
            out_shape=[
                jax.ShapeDtypeStruct((rows, D), BF16),
                jax.ShapeDtypeStruct(attn_latent.shape, F32),
                jax.ShapeDtypeStruct(up_latent.shape, F32),
                jax.ShapeDtypeStruct(down_latent.shape, F32),
            ]
            + [jax.ShapeDtypeStruct(shape, F32) for shape in small_shapes],
            scratch_shapes=[
                pltpu.VMEM((3, rows, D), BF16),
                pltpu.VMEM((8, LANES), F32),
                pltpu.VMEM(own_shape, BF16),
                pltpu.VMEM(own_shape, BF16),
                pltpu.VMEM(own_shape, BF16),
                pltpu.VMEM((rows, D), BF16),
                pltpu.VMEM((3, D, D), BF16),
                pltpu.VMEM((rows, D), BF16),
                pltpu.VMEM((rows, D), F32),
                pltpu.SemaphoreType.DMA((4,)),
            ]
            + shared_scratch(depth, line_rows, F32)
            + scatter_scratch(shapes, [BF16] * 6, depth),
            compiler_params=pltpu.CompilerParams(
                collective_id=1, has_side_effects=True, vmem_limit_bytes=vmem_bytes
            ),
            name="attention_backward_and_sums",
        )(
            lengths,
            clip_scales,
            *pair_arrays,
            *dw,
            low,
            qkv_w,
            tokens,
            residual,
            sums,
            up_sums,
            attn_latent,
            up_latent,
            down_latent,
        )
        (
            input_grad,
            attn_grad,
            up_grad,
            down_grad,
            bias_grad,
            gain_grad,
            shift_grad,
            up_bias_grad,
            loss,
        ) = moved(
            input_grad,
            attn_grad,
            up_grad,
            down_grad,
            bias_grad,
            gain_grad,
            shift_grad,
            up_bias_grad,
            loss,
        )
    return (
        loss.reshape(()),
        input_grad,
        attn_grad,
        up_grad,
        down_grad,
        bias_grad,
        up_bias_grad.reshape(-1),
        gain_grad,
        shift_grad,
    )


def on_device(
    tokens,
    teacher_tokens,
    cotangent,
    lengths,
    clip_scales,
    attn_latent,
    up_latent,
    down_latent,
    biases,
    up_bias,
    norm_gains,
    norm_shifts,
    teacher_attn,
    teacher_up,
    teacher_down,
    teacher_biases,
    teacher_up_bias,
    teacher_gains,
    teacher_shifts,
):
    sizes = (lax.axis_size("dp"), lax.axis_size("shard"))
    narrow, wide = biases.shape[1], up_bias.shape[0]
    lines = (teacher_biases, teacher_gains, teacher_shifts, biases, norm_gains, norm_shifts)
    latents = (attn_latent, up_latent, down_latent)
    if tiled_over(sizes, narrow):
        (
            tq,
            tk,
            query,
            key,
            value,
            context,
            x_low,
            teach_out,
            vec,
            qkv_w,
            out_w,
            up_w,
            down_w,
        ) = forward(
            lengths,
            clip_scales,
            teacher_attn,
            teacher_up,
            teacher_down,
            lines,
            (teacher_up_bias.reshape(1, -1), up_bias.reshape(1, -1)),
            latents,
            teacher_tokens,
            tokens,
        )
    else:
        vec = jnp.concatenate(
            [
                lax.all_gather(jnp.concatenate(lines, axis=0), AXES, axis=1, tiled=True),
                *(
                    lax.all_gather(line, AXES, tiled=True).reshape(-1, D)
                    for line in (teacher_up_bias, up_bias)
                ),
            ],
            axis=0,
        ).astype(F32)
        vec = jnp.pad(vec, ((0, vector_rows - vec.shape[0]), (0, 0)))
        teach_qkv, teach_wo, teach_up, teach_down, qkv_w, out_w, up_w, down_w = gather(
            [
                teacher_attn[:3],
                teacher_attn[3],
                teacher_up,
                teacher_down,
                binarize(attn_latent[:3]),
                binarize(attn_latent[3]),
                binarize(up_latent),
                binarize(down_latent),
            ]
        )
        tq, tk, teach_context = attend(
            False, lengths, clip_scales, teacher_tokens, teach_qkv, vec[:3].reshape(3, 1, D)
        )
        query, key, value, context, x_low = attend(
            True, lengths, clip_scales, tokens, qkv_w, vec[9:12].reshape(3, 1, D)
        )
        teach_out = teacher_tail(
            teacher_tokens, teach_context, teach_wo, teach_up, teach_down, vec[:9], vec[18:22]
        )
    result, grad_context, residual, sums, up_sums, *weight_grads = student_middle(
        lengths,
        clip_scales,
        tokens,
        cotangent,
        teach_out,
        context,
        out_w,
        up_w,
        down_w,
        vec,
    )
    return (result,) + finish_backward(
        lengths,
        clip_scales,
        (query, key, value, context, grad_context, tq, tk),
        weight_grads,
        qkv_w,
        x_low,
        tokens,
        residual,
        sums,
        up_sums,
        latents,
        narrow,
        wide,
    )


def solution(mesh):
    in_specs = (
        P(("dp", "shard"), None),
        P(("dp", "shard"), None),
        P(("dp", "shard"), None),
        P(),
        P(),
        P(None, ("dp", "shard"), None),
        P(("dp", "shard"), None),
        P(("dp", "shard"), None),
        P(None, ("dp", "shard")),
        P(("dp", "shard")),
        P(None, ("dp", "shard")),
        P(None, ("dp", "shard")),
        P(None, ("dp", "shard"), None),
        P(("dp", "shard"), None),
        P(("dp", "shard"), None),
        P(None, ("dp", "shard")),
        P(("dp", "shard")),
        P(None, ("dp", "shard")),
        P(None, ("dp", "shard")),
    )
    out_specs = (
        P(("dp", "shard"), None),
        P(),
        P(("dp", "shard"), None),
        P(None, ("dp", "shard"), None),
        P(("dp", "shard"), None),
        P(("dp", "shard"), None),
        P(None, ("dp", "shard")),
        P(("dp", "shard")),
        P(None, ("dp", "shard")),
        P(None, ("dp", "shard")),
    )
    return jax.shard_map(
        on_device, mesh=mesh, in_specs=in_specs, out_specs=out_specs, check_vma=False
    )
```

```python
import functools
import math

import jax
import jax.numpy as jnp
from jax import lax
from jax.experimental import pallas as pl
from jax.experimental.pallas import tpu as pltpu
from jax.sharding import PartitionSpec as P

D = 768
HEADS = 12
HEAD_DIM = 64
SEQ_LEN = 1024
AXES = ("dp", "shard")
MESH = pl.DeviceIdType.MESH
F32 = jnp.float32
BF16 = jnp.bfloat16

epsilon = 1e-05
masked_score = -1e30
hidden_weight = 0.25
saturation = 7.5
LANES = 128
log2e = math.log2(math.e)
scaling = HEAD_DIM ** (-0.5)
exponent = scaling * log2e
vmem_bytes = 60 * 1024 * 1024
line_rows = 16
vector_rows = 32


def dot(left, right, left_dim, right_dim):
    return lax.dot_general(
        left, right, (((left_dim,), (right_dim,)), ((), ())), preferred_element_type=F32
    )


def outer_rows(left, right):
    return dot(left, right, 0, 0)


def binarize(latent):
    scale = jnp.mean(jnp.abs(latent), axis=-1, keepdims=True)
    return (scale * jnp.sign(latent)).astype(BF16)


def surrogate(latent):
    return jnp.mean(jnp.abs(latent), axis=-1, keepdims=True) * latent


def latent_grad(latent, grad):
    _, pull = jax.vjp(surrogate, latent)
    return pull(grad)[0]


def normalize(values):
    center = values - jnp.mean(values, axis=-1, keepdims=True)
    inverse = lax.rsqrt(jnp.mean(center * center, axis=-1, keepdims=True) + epsilon)
    return (center * inverse, inverse)


def norm_back(grad_norm, normed, inverse):
    return inverse * (
        grad_norm
        - jnp.mean(grad_norm, axis=-1, keepdims=True)
        - normed * jnp.mean(grad_norm * normed, axis=-1, keepdims=True)
    )


def whole(memory=pltpu.VMEM):
    return pl.BlockSpec(memory_space=memory)


def fixed(shape):
    return pl.BlockSpec(shape, lambda *_: (0,) * len(shape), pipeline_mode=pl.Buffered(1))


def columns(shape):
    return pl.BlockSpec(shape, lambda i: (0,) * (len(shape) - 1) + (i,))


def row_blocks(shape):
    return pl.BlockSpec(shape, lambda i: (i,) + (0,) * (len(shape) - 1))


def own_index():
    return lax.axis_index("dp") * lax.axis_size("shard") + lax.axis_index("shard")


def lanes_of(width, start):
    row = lax.broadcasted_iota(jnp.int32, (width, D), 0)
    lane = lax.broadcasted_iota(jnp.int32, (width, D), 1)
    return jnp.where(lane == row + start, 1.0, 0.0).astype(BF16)


def take_lanes(values, width, start):
    chosen = lanes_of(width, start)
    return sum(dot(part.astype(BF16), chosen, 1, 1) for part in three_parts(values))


class Place:
    def __init__(self, depth):
        self.depth = depth
        dp, shard = lax.axis_index("dp"), lax.axis_index("shard")
        z, y = dp // 2, lax.rem(dp, 2)
        x, core = shard // 2, lax.rem(shard, 2)
        self.z, self.y, self.x, self.core = z, y, x, core

        def device(z_at, y_at, x_at, core_at):
            return (z_at * 2 + y_at, x_at * 2 + core_at)

        self.above = device(jnp.minimum(z + 1, depth - 1), y, x, core)
        self.below = device(jnp.maximum(z - 1, 0), y, x, core)
        one = (lax.rem(y + 1 - core, 2), lax.rem(x + core, 2))
        two = (lax.rem(y + core, 2), lax.rem(x + 1 - core, 2))
        self.pieces = ((y, x), one, two, (1 - y, 1 - x))
        self.first, self.second = device(z, *one, core), device(z, *two, core)
        self.sibling = device(z, y, x, 1 - core)

    def barrier(self):
        semaphore = pltpu.get_barrier_semaphore()
        for partner in (self.first, self.second, self.sibling):
            pl.semaphore_signal(semaphore, inc=1, device_id=partner, device_id_type=MESH)

        @pl.when(self.z < self.depth - 1)
        def _():
            pl.semaphore_signal(semaphore, inc=1, device_id=self.above, device_id_type=MESH)

        @pl.when(self.z > 0)
        def _():
            pl.semaphore_signal(semaphore, inc=1, device_id=self.below, device_id_type=MESH)

        pl.semaphore_wait(
            semaphore, 3 + jnp.minimum(self.z, 1) + jnp.minimum(self.depth - 1 - self.z, 1)
        )


def remote(source, target, send_sem, recv_sem, device):
    return pltpu.make_async_remote_copy(
        src_ref=source,
        dst_ref=target,
        send_sem=send_sem,
        recv_sem=recv_sem,
        device_id=device,
        device_id_type=MESH,
    )


def tiled_over(mesh_sizes, rows):
    return mesh_sizes == (8, 4) and rows % 8 == 0


def gather_scratch(chunks, depth):
    dma = pltpu.SemaphoreType.DMA
    sizes = (len(chunks), max(len(chunk) for chunk in chunks))
    return [
        dma(sizes + (depth - 1, 2)),
        dma(sizes + (depth - 1, 2)),
        dma(sizes + (3 + max(depth, 4),)),
        dma(sizes + (3 + max(depth, 4),)),
        dma(sizes),
    ]


def gather_stage(place, ins, outs, leads, chunks, late, sems):
    line_send, line_recv, pair_send, pair_recv, own_sem = sems
    depth, z, y, x, core = place.depth, place.z, place.y, place.x, place.core

    def slot(item, *index):
        return outs[item].at[((slice(None),) if leads[item] > 1 else ()) + index]

    def group(chunk, item, z_at):
        if chunk in late:
            return slot(item, z_at, slice(None), slice(None), core)
        return slot(item, z_at, y, x, core)

    def line_copy(chunk, at, item, turn, upward):
        if upward:
            owner, target = jnp.maximum(z - (turn - 1), 0), place.above
        else:
            owner, target = jnp.minimum(z + (turn - 1), depth - 1), place.below
        block = group(chunk, item, owner)
        where = (chunk, at, turn - 1, int(upward))
        return remote(block, block, line_send.at[where], line_recv.at[where], target)

    def sends(turn, upward):
        if upward:
            return (z - (turn - 1) >= 0) & (z < depth - 1)
        return (z + (turn - 1) <= depth - 1) & (z > 0)

    def receives(turn, upward):
        return (z - turn >= 0) if upward else (z + turn <= depth - 1)

    def own_copy(chunk, at, item):
        return pltpu.make_async_copy(
            ins[item], slot(item, z, y, x, core), own_sem.at[chunk, at]
        )

    plans = (
        (0, place.first),
        (0, place.second),
        (1, place.second),
        (0, place.sibling),
        (1, place.sibling),
        (2, place.sibling),
        (3, place.sibling),
    )

    def pair_copy(chunk, at, item, plan):
        piece, target = plans[plan]
        z_at = z if chunk in late else slice(None)
        block = slot(item, z_at, *place.pieces[piece], core)
        where = (chunk, at, plan)
        return remote(block, block, pair_send.at[where], pair_recv.at[where], target)

    def each(chunk, action):
        for at, item in enumerate(chunks[chunk]):
            action(at, item)

    def line_start(chunk, turn):
        for upward in (True, False):

            @pl.when(sends(turn, upward))
            def _():
                each(chunk, lambda at, item: line_copy(chunk, at, item, turn, upward).start())

    def line_received(chunk, turn):
        for upward in (True, False):

            @pl.when(receives(turn, upward))
            def _():
                each(chunk, lambda at, item: line_copy(chunk, at, item, turn, upward).wait_recv())

    def line_sent(chunk, turn):
        for upward in (True, False):

            @pl.when(sends(turn, upward))
            def _():
                each(chunk, lambda at, item: line_copy(chunk, at, item, turn, upward).wait_send())

    def start(chunk, *plan_list):
        for plan in plan_list:
            each(chunk, lambda at, item: pair_copy(chunk, at, item, plan).start())

    def received(chunk, *plan_list):
        for plan in plan_list:
            each(chunk, lambda at, item: pair_copy(chunk, at, item, plan).wait_recv())

    def plane_copy(chunk, at, item, z_at):
        block = group(chunk, item, z_at)
        where = (chunk, at, 3 + z_at)
        return remote(block, block, pair_send.at[where], pair_recv.at[where], place.sibling)

    def late_stage(chunk, number):
        if number == 0:
            each(chunk, lambda at, item: own_copy(chunk, at, item).wait())
            start(chunk, 0, 1)
        elif number == 1:
            received(chunk, 0)
            start(chunk, 2)
        elif number == 2:
            received(chunk, 1, 2)
            line_start(chunk, 1)
            each(chunk, lambda at, item: plane_copy(chunk, at, item, z).start())
        elif number < depth + 2:
            turn = number - 2
            line_received(chunk, turn)
            if turn < depth - 1:
                line_start(chunk, turn + 1)
            for upward in (True, False):
                owner = jnp.maximum(z - turn, 0) if upward else jnp.minimum(z + turn, depth - 1)

                @pl.when(receives(turn, upward))
                def _():
                    each(chunk, lambda at, item: plane_copy(chunk, at, item, owner).start())
        elif number == depth + 2:
            for z_at in range(depth):
                each(chunk, lambda at, item: plane_copy(chunk, at, item, z_at).wait_recv())

    def stage(chunk, number):
        if chunk in late:
            late_stage(chunk, number)
        elif number == 0:
            each(chunk, lambda at, item: own_copy(chunk, at, item).wait())
            line_start(chunk, 1)
        elif number < depth:
            line_received(chunk, number)
            if number < depth - 1:
                line_start(chunk, number + 1)
            else:
                start(chunk, 0, 1, 3)
        elif number == depth:
            received(chunk, 0)
            start(chunk, 2, 4)
        elif number == depth + 1:
            received(chunk, 1)
            start(chunk, 5)
        elif number == depth + 2:
            received(chunk, 2)
            start(chunk, 6)
        else:
            received(chunk, 3, 4, 5, 6)

    def sent(chunk):
        for turn in range(1, depth):
            line_sent(chunk, turn)
        for plan in range(3 if chunk in late else 7):
            each(chunk, lambda at, item: pair_copy(chunk, at, item, plan).wait_send())
        if chunk in late:
            for z_at in range(depth):
                each(chunk, lambda at, item: plane_copy(chunk, at, item, z_at).wait_send())

    def begin(begun):
        for chunk in begun:
            each(chunk, lambda at, item: own_copy(chunk, at, item).start())

    return begin, stage, sent


def gathered(results):
    return [
        result.reshape(result.shape[:-6] + (-1, result.shape[-1])) for result in results
    ]


def gather(arrays):
    return [lax.all_gather(array, AXES, axis=array.ndim - 2, tiled=True) for array in arrays]


def scatter_scratch(shapes, dtypes, depth):
    dma = pltpu.SemaphoreType.DMA
    scratch = []
    for shape, dtype in zip(shapes, dtypes):
        lead, rows, cols = shape
        block = (depth, lead, rows, cols)
        scratch += [
            pltpu.VMEM((4,) + block, dtype),
            pltpu.VMEM((4,) + block, dtype),
            pltpu.VMEM((3,) + block, dtype),
            pltpu.VMEM((2,) + block, dtype),
        ]
    count = len(shapes)
    return scratch + [
        dma((count, 4)),
        dma((count, 7)),
        dma((count, 7)),
        dma((count, depth, 2)),
        dma((count, depth, 2)),
    ]


def scatter_stage(place, ins, finish, scratch, count):
    depth, z, core = place.depth, place.z, place.core
    own_sem, pair_send, pair_recv, line_send, line_recv = scratch[4 * count :]

    def buffers(item):
        return scratch[4 * item : 4 * item + 4]

    def source(item, piece, lead, side):
        index = (slice(None),) + place.pieces[piece] + (side,)
        ref = ins[item]
        return ref.at[((lead,) if ref.shape[:-6] else ()) + index]

    def leads(item):
        return range(buffers(item)[0].shape[2])

    def own_copy(item, piece, lead):
        held = buffers(item)[0]
        return pltpu.make_async_copy(
            source(item, piece, lead, core), held.at[piece, :, lead], own_sem.at[item, piece]
        )

    names = (0, 2, 1, 3)

    def core_copy(item, piece, lead):
        arrived = buffers(item)[1]
        name = names[piece]
        return remote(
            source(item, piece, lead, 1 - core),
            arrived.at[name, :, lead],
            pair_send.at[item, piece],
            pair_recv.at[item, name],
            place.sibling,
        )

    def core_wait(item, piece):
        arrived = buffers(item)[1]
        block = arrived.at[piece]
        remote(
            block, block, pair_send.at[item, piece], pair_recv.at[item, piece], place.sibling
        ).wait_recv()

    def chip_copy(item, plan):
        held, _, arrived, _ = buffers(item)
        piece, target = ((2, place.second), (3, place.second), (1, place.first))[plan]
        return remote(
            held.at[piece],
            arrived.at[plan],
            pair_send.at[item, 4 + plan],
            pair_recv.at[item, 4 + plan],
            target,
        )

    def line_copy(item, owner, upward, fresh):
        held, _, _, arrived = buffers(item)
        block = arrived.at[int(upward), owner]
        where = (item, owner, int(upward))
        return remote(
            held.at[0, owner] if fresh else block,
            block,
            line_send.at[where],
            line_recv.at[where],
            place.above if upward else place.below,
        )

    def add(target, *others):
        def one(at):
            if len(others) == 1:
                target[at] = target[at] + others[0][at]
                return
            total = target[at].astype(F32)
            for other in others:
                total = total + other[at].astype(F32)
            target[at] = total.astype(target.dtype)

        for first in range(target.shape[0]):
            for second in range(target.shape[1]):
                one((first, second))

    def add_block(target, other):
        for lead in range(target.shape[0]):
            target[lead] = target[lead] + other[lead]

    def merge(item, piece):
        held, arrived, _, _ = buffers(item)
        block = held.at[piece]
        pltpu.make_async_copy(block, block, own_sem.at[item, piece]).wait()
        core_wait(item, piece)
        add(block, arrived.at[piece])

    def line_turn(item, turn, upward):
        held, _, _, arrived = buffers(item)
        at = turn if upward else depth - 1 - turn
        beyond = range(at + 1, depth) if upward else range(at)

        @pl.when(z == at)
        def _():
            for owner in sorted(beyond, key=lambda owner: -abs(owner - at)):
                if turn:
                    line_copy(item, owner, upward, False).wait_recv()
                    add_block(arrived.at[int(upward), owner], held.at[0, owner])
                line_copy(item, owner, upward, not turn).start()
            if turn:
                line_copy(item, at, upward, False).wait_recv()

    def stage(item, number):
        held, _, arrived, line = buffers(item)
        if number == 0:
            for piece in (3, 1, 2, 0):
                for lead in leads(item):
                    core_copy(item, piece, lead).start()
            for piece in (2, 3, 1, 0):
                for lead in leads(item):
                    own_copy(item, piece, lead).start()
        elif number == 1:
            for piece, plan in ((3, 1), (2, 0)):
                merge(item, piece)
                chip_copy(item, plan).start()
        elif number == 2:
            merge(item, 1)
            merge(item, 0)
        elif number == 3:
            chip_copy(item, 1).wait_recv()
            add(held.at[1], arrived.at[1])
            chip_copy(item, 2).start()
        elif number == 4:
            chip_copy(item, 0).wait_recv()
            chip_copy(item, 2).wait_recv()
            add(held.at[0], arrived.at[0], arrived.at[2])
            for upward in (True, False):
                line_turn(item, 0, upward)
        elif number < 4 + depth:
            for upward in (True, False):
                line_turn(item, number - 4, upward)
        else:
            for lead in leads(item):
                total = held[0, z, lead].astype(F32)
                for upward, near in ((1, z > 0), (0, z < depth - 1)):
                    total = jnp.where(near, total + line[upward, z, lead].astype(F32), total)
                finish(item, lead, total)

            for piece in range(4):
                block = buffers(item)[1].at[piece]
                remote(
                    block, block, pair_send.at[item, piece], pair_recv.at[item, piece], place.sibling
                ).wait_send()
            for plan in range(3):
                chip_copy(item, plan).wait_send()
            for upward in (True, False):
                for owner in range(depth):

                    @pl.when((z < owner) if upward else (z > owner))
                    def _():
                        line_copy(item, owner, upward, False).wait_send()

    return stage


def split_rows(array, depth):
    return array.reshape(array.shape[:-2] + (depth, 2, 2, 2, -1, array.shape[-1]))


def shared_scratch(depth, rows, dtype):
    dma = pltpu.SemaphoreType.DMA
    return [
        pltpu.VMEM((4, rows, D), dtype),
        pltpu.VMEM((5, rows, D), dtype),
        pltpu.VMEM((2, rows, D), dtype),
        dma((5,)),
        dma((5,)),
    ]


def shared_stage(place, finish, scratch):
    held, arrived, line, send_sem, recv_sem = scratch
    depth, z = place.depth, place.z
    partners = (place.sibling, place.second, place.first)

    def pair_copy(at):
        return remote(
            held.at[at], arrived.at[at], send_sem.at[at], recv_sem.at[at], partners[at]
        )

    def line_copy(upward, fresh):
        at = 3 + int(upward)
        return remote(
            held.at[3] if fresh else line.at[int(upward)],
            arrived.at[at],
            send_sem.at[at],
            recv_sem.at[at],
            place.above if upward else place.below,
        )

    def line_turn(turn, upward):
        at = turn if upward else depth - 1 - turn

        @pl.when(z == at)
        def _():
            if turn:
                line_copy(upward, False).wait_recv()
            if turn < depth - 1:
                if turn:
                    line[int(upward)] = held[3] + arrived[3 + int(upward)]
                line_copy(upward, not turn).start()

    def stage(number):
        if number == 0:
            pair_copy(0).start()
        elif number < 4:
            pair_copy(number - 1).wait_recv()
            held[number] = held[number - 1] + arrived[number - 1]
            if number < 3:
                pair_copy(number).start()
            else:
                for upward in (True, False):
                    line_turn(0, upward)
        elif number < 3 + depth:
            for upward in (True, False):
                line_turn(number - 3, upward)
        else:
            total = held[3]
            total = jnp.where(z > 0, total + arrived[4], total)
            finish(jnp.where(z < depth - 1, total + arrived[3], total))
            for at in range(3):
                pair_copy(at).wait_send()
            for upward in (True, False):

                @pl.when((z < depth - 1) if upward else (z > 0))
                def _():
                    line_copy(upward, False).wait_send()

    return stage


def scatter(arrays):
    return [
        lax.psum_scatter(array.astype(F32), AXES, scatter_dimension=array.ndim - 2, tiled=True)
        for array in arrays
    ]


def lane_index(rows):
    return lax.broadcasted_iota(jnp.int32, (rows, LANES), 1)


def halves(lane, odd):
    own = (lane >= HEAD_DIM) if odd else (lane < HEAD_DIM)
    other = lane if odd else lane - HEAD_DIM
    return own, other


def three_parts(values):
    high = values.astype(BF16).astype(F32)
    rest = values - high
    middle = rest.astype(BF16).astype(F32)
    return high, middle, rest - middle


def with_terms(own, other, values, terms):
    result = jnp.zeros_like(values)
    for at, term in enumerate(terms):
        result = jnp.where(other == at, term, result)
    return jnp.where(own, values, result)


def attend_quad(student, length, inputs, weights, biases, targets, between):
    q_ref, k_ref, v_ref, ctx_ref = targets
    rows = inputs.shape[0]
    lane = lane_index(rows)
    position = lax.broadcasted_iota(jnp.int32, (rows, LANES), 0)
    hidden_key = jnp.where(position < length, 0.0, masked_score)
    queries, keys, values = (
        (dot(inputs, weight, 1, 1) + bias).astype(BF16) for weight, bias in zip(weights, biases)
    )
    if not student:
        q_ref[...] = queries
        k_ref[...] = keys
    block = 512
    for pair in range(2):
        lanes = slice(pair * LANES, (pair + 1) * LANES)
        query, key, value = (
            array[:, lanes].astype(F32) for array in (queries, keys, values)
        )
        parts = []
        for odd in range(2):
            own, other = halves(lane, odd)
            place = slice((pair * 2 + odd) * LANES, (pair * 2 + odd + 1) * LANES)
            query_full = with_terms(own, other, query, (0.0, 0.0, 0.0, 1.0)).astype(BF16)
            key_full = with_terms(own, other, key, (1.0, 1.0, 1.0, hidden_key)).astype(BF16)
            value_full = with_terms(own, other, value, (1.0, 1.0, 1.0)).astype(BF16)
            if student:
                k_ref[:, place] = key_full
                v_ref[:, place] = value_full
            found = []
            for start in range(0, rows, block):
                take = slice(start, start + block)
                scores = dot(query_full[take], key_full, 1, 1)
                top = jnp.max(scores, axis=1, keepdims=True)
                expo = jnp.exp2((scores - top) * exponent).astype(BF16)
                mixed = dot(expo, value_full, 1, 0)
                at = 0 if odd else HEAD_DIM
                total = mixed[:, at : at + 1]
                found.append(mixed / total)
                if student:
                    logsum = top + jnp.log(total) / scaling
                    q_ref[take, place] = with_terms(
                        own[take],
                        other[take],
                        query[take],
                        tuple(-part for part in three_parts(logsum)) + (1.0,),
                    ).astype(BF16)
            parts.append(jnp.concatenate(found, axis=0))
            between(pair * 2 + odd)
        context = jnp.where(lane < HEAD_DIM, parts[0], parts[1])
        ctx_ref[:, lanes] = context.astype(ctx_ref.dtype)


def attend_kernel(student, lengths, *refs):
    if student:
        clip, x_ref, w_ref, b_ref, q_ref, k_ref, v_ref, ctx_ref, low_ref = refs

        @pl.when(pl.program_id(0) == 0)
        def _():
            width = saturation * clip[0]
            low_ref[...] = (width * jnp.tanh(x_ref[...].astype(F32) / width)).astype(BF16)

        x_ref = low_ref
        targets = (q_ref, k_ref, v_ref, ctx_ref)
    else:
        x_ref, w_ref, b_ref, q_ref, k_ref, ctx_ref = refs
        targets = (q_ref, k_ref, None, ctx_ref)
    attend_quad(
        student,
        lengths[own_index()],
        x_ref[...],
        [w_ref[slot] for slot in range(3)],
        [b_ref[slot] for slot in range(3)],
        targets,
        lambda head: None,
    )


def attend(student, lengths, clip_scales, inputs, weights, bias):
    rows = inputs.shape[0]
    wide = 4 * LANES
    narrow = 2 * LANES
    scalar = whole(pltpu.SMEM)
    in_specs = [scalar] + ([scalar] if student else [])
    in_specs += [
        fixed((rows, D)),
        pl.BlockSpec((3, narrow, D), lambda i: (0, i, 0)),
        columns((3, 1, narrow)),
    ]
    if student:
        out_shape = [jax.ShapeDtypeStruct((rows, 2 * D), BF16)] * 3 + [
            jax.ShapeDtypeStruct((rows, D), F32),
            jax.ShapeDtypeStruct((rows, D), BF16),
        ]
        out_specs = [columns((rows, wide))] * 3 + [columns((rows, narrow)), fixed((rows, D))]
        args = (lengths, clip_scales, inputs, weights, bias)
    else:
        out_shape = [jax.ShapeDtypeStruct((rows, D), BF16)] * 3
        out_specs = [columns((rows, narrow))] * 3
        args = (lengths, inputs, weights, bias)
    return pl.pallas_call(
        functools.partial(attend_kernel, student),
        grid=(D // narrow,),
        in_specs=in_specs,
        out_specs=out_specs,
        out_shape=out_shape,
        compiler_params=pltpu.CompilerParams(vmem_limit_bytes=vmem_bytes),
        name="student_attention" if student else "teacher_attention",
    )(*args)


def split_dot(left, right):
    high = right.astype(BF16)
    low = (right - high.astype(F32)).astype(BF16)
    return dot(left, high, 1, 0) + dot(left, low, 1, 0)


def attend_back_pair(length, inverse_pairs, q_ref, k_ref, v_ref, ctx_ref, dctx_ref, tq_ref, tk_ref, between):
    rows = ctx_ref.shape[0]
    lane = lane_index(rows)
    position = lax.broadcasted_iota(jnp.int32, (rows, LANES), 0)
    live = position < length
    low_half = lane < HEAD_DIM
    grad_context = dctx_ref[...].astype(F32)
    product = grad_context * ctx_ref[...]
    block = 512
    pieces = []
    for odd in range(2):
        own, other = halves(lane, odd)
        place = slice(odd * LANES, (odd + 1) * LANES)
        query, key, value = q_ref[:, place], k_ref[:, place], v_ref[:, place]
        weighted = jnp.sum(jnp.where(own, product, 0.0), axis=1, keepdims=True)
        grad_full = with_terms(
            own, other, grad_context, tuple(-part for part in three_parts(weighted))
        ).astype(BF16)
        grad_query = None
        key_parts, value_parts = [], []
        for start in range(0, rows, block):
            take = slice(start, start + block)
            probs = jnp.exp2(dot(key[take], query, 1, 1) * exponent)
            grad_scores = (probs * dot(value[take], grad_full, 1, 1)).astype(BF16)
            value_parts.append(dot(probs.astype(BF16), grad_full, 1, 0))
            key_parts.append(dot(grad_scores, query, 1, 0))
            part = dot(grad_scores, key[take], 0, 0)
            grad_query = part if grad_query is None else grad_query + part
        pieces.append(
            (grad_query, jnp.concatenate(key_parts, axis=0), jnp.concatenate(value_parts, axis=0))
        )
        between(odd)
    query_live, key_live = (
        jnp.where(live, jnp.where(low_half, ref[:, :LANES], ref[:, LANES:]), 0.0).astype(BF16)
        for ref in (q_ref, k_ref)
    )
    teach_query, teach_key = (
        jnp.where(live, ref[...], 0.0).astype(BF16) for ref in (tq_ref, tk_ref)
    )
    row = lax.broadcasted_iota(jnp.int32, (LANES, LANES), 0)
    col = lax.broadcasted_iota(jnp.int32, (LANES, LANES), 1)
    same = (row < HEAD_DIM) == (col < HEAD_DIM)

    def gram(left, right):
        return jnp.where(same, outer_rows(left, right), 0.0)

    key_key, teach_key_key = gram(key_live, key_live), gram(teach_key, key_live)
    query_query, teach_query_query = gram(query_live, query_live), gram(teach_query, query_live)
    squares = (
        query_query * key_key
        - 2.0 * teach_query_query * teach_key_key
        + gram(teach_query, teach_query) * gram(teach_key, teach_key)
    )
    squares = jnp.sum(squares.reshape(LANES // 8, 8, LANES), axis=0)

    squares = squares * (scaling * scaling * inverse_pairs)
    factor = 2.0 * scaling * scaling * inverse_pairs
    query_term = split_dot(
        jnp.concatenate([query_live, teach_query], axis=1),
        jnp.concatenate([key_key, -teach_key_key], axis=0),
    )
    key_term = split_dot(
        jnp.concatenate([key_live, teach_key], axis=1),
        jnp.concatenate([query_query, -teach_query_query], axis=0),
    )
    (even_q, even_k, even_v), (odd_q, odd_k, odd_v) = pieces
    return (
        (jnp.where(low_half, even_q, odd_q) * scaling + factor * query_term).astype(BF16),
        (jnp.where(low_half, even_k, odd_k) * scaling + factor * key_term).astype(BF16),
        jnp.where(low_half, even_v, odd_v).astype(BF16),
    ), squares


def attend_back_kernel(
    lengths, inverse_pairs, q_ref, k_ref, v_ref, ctx_ref, dctx_ref, tq_ref, tk_ref, grad_ref, sum_ref
):
    refs = (q_ref, k_ref, v_ref, ctx_ref, dctx_ref, tq_ref, tk_ref)
    grads, squares = attend_back_pair(lengths[own_index()], inverse_pairs[0], *refs, lambda odd: None)

    @pl.when(pl.program_id(0) == 0)
    def _():
        sum_ref[...] = jnp.zeros_like(sum_ref)

    sum_ref[...] += squares
    for slot in range(3):
        grad_ref[slot] = grads[slot]


def attend_back(lengths, inverse_pairs, query, key, value, context, grad_context, tq, tk):
    rows = context.shape[0]
    scalar = whole(pltpu.SMEM)
    return pl.pallas_call(
        attend_back_kernel,
        grid=(D // LANES,),
        in_specs=[scalar, scalar]
        + [columns((rows, 2 * LANES))] * 3
        + [columns((rows, LANES))] * 4,
        out_specs=[columns((3, rows, LANES)), fixed((8, LANES))],
        out_shape=[
            jax.ShapeDtypeStruct((3, rows, D), BF16),
            jax.ShapeDtypeStruct((8, LANES), F32),
        ],
        compiler_params=pltpu.CompilerParams(vmem_limit_bytes=vmem_bytes),
        name="attention_backward",
    )(lengths, inverse_pairs, query, key, value, context, grad_context, tq, tk)


def gelu_parts(upper):
    cumulative = 0.5 * (1.0 + lax.erf(upper * (1.0 / math.sqrt(2.0))))
    return cumulative, upper * cumulative


ff_part = D


def teacher_rows(tokens, context, wo_ref, up_part, w2_ref, vec, up_bias, out_ref, between):
    normed, _ = normalize(tokens.astype(F32) + dot(context, wo_ref[...], 1, 1) + vec[3:4])
    hidden = normed * vec[5:6] + vec[7:8]
    low = hidden.astype(BF16)
    lower = None
    for at in range(w2_ref.shape[1] // ff_part):
        take = slice(at * ff_part, (at + 1) * ff_part)
        _, bent = gelu_parts(dot(low, up_part(at), 1, 1) + up_bias[at : at + 1])
        part = dot(bent.astype(BF16), w2_ref[:, take], 1, 1)
        lower = part if lower is None else lower + part
        between(at)
    final, _ = normalize(hidden + lower + vec[4:5])
    out_ref[...] = final * vec[6:7] + vec[8:9]


def teacher_kernel(tok_ref, ctx_ref, wo_ref, w1_ref, w2_ref, vec_ref, ub_ref, out_ref):
    teacher_rows(
        tok_ref[...],
        ctx_ref[...],
        wo_ref,
        lambda at: w1_ref[at * ff_part : (at + 1) * ff_part],
        w2_ref,
        vec_ref[...],
        ub_ref[...],
        out_ref,
        lambda at: None,
    )


def teacher_tail(tokens, context, wo, w1, w2, vectors, up_bias):
    rows, wide = tokens.shape[0], w1.shape[0]
    block = 256
    return pl.pallas_call(
        teacher_kernel,
        grid=(rows // block,),
        in_specs=[
            row_blocks((block, D)),
            row_blocks((block, D)),
            fixed((D, D)),
            fixed((wide, D)),
            fixed((D, wide)),
            fixed(vectors.shape),
            fixed(up_bias.shape),
        ],
        out_specs=row_blocks((block, D)),
        out_shape=jax.ShapeDtypeStruct((rows, D), F32),
        compiler_params=pltpu.CompilerParams(vmem_limit_bytes=vmem_bytes),
        name="teacher_feed_forward",
    )(tokens, context, wo, w1, w2, vectors, up_bias)


def student_kernel(
    row_steps,
    lengths,
    clip,
    tok_ref,
    cot_ref,
    teach_ref,
    ctx_ref,
    wo_ref,
    w1_ref,
    w2_ref,
    vec_ref,
    out_ref,
    dctx_ref,
    res_ref,
    sums_ref,
    upsum_ref,
    dw2_ref,
    dw1_ref,
    dwo_ref,
    df_all,
    fb_all,
    du_all,
    hb_all,
    dao_all,
    cb_all,
    slope_ref,
):
    step = pl.program_id(0)
    down_steps, up_steps = D // dw2_ref.shape[0], w1_ref.shape[0] // dw1_ref.shape[0]

    @pl.when(step < row_steps)
    def _():
        rows = out_ref.shape[0]
        here = pl.ds(pl.multiple_of(step * rows, rows), rows)
        student_rows(
            step,
            lengths,
            clip,
            tok_ref,
            cot_ref,
            teach_ref,
            ctx_ref,
            wo_ref,
            w1_ref,
            w2_ref,
            vec_ref[9:18],
            vec_ref[22:26],
            out_ref,
            dctx_ref,
            *(ref.at[here] for ref in (dao_all, cb_all, du_all, hb_all, df_all, fb_all)),
            res_ref,
            sums_ref,
            upsum_ref,
            slope_ref,
        )

    def weight_grad(target, left, right, at):
        width = target.shape[0]
        lanes = pl.ds(pl.multiple_of(at * width, width), width)
        target[...] = outer_rows(left[:, lanes], right[...]).astype(BF16)

    @pl.when((step >= row_steps) & (step < row_steps + down_steps))
    def _():
        weight_grad(dw2_ref, df_all, fb_all, step - row_steps)

    @pl.when((step >= row_steps + down_steps) & (step < row_steps + down_steps + up_steps))
    def _():
        weight_grad(dw1_ref, du_all, hb_all, step - row_steps - down_steps)

    @pl.when(step == row_steps + down_steps + up_steps)
    def _():
        dwo_ref[...] = outer_rows(dao_all[...], cb_all[...]).astype(BF16)


def student_rows(
    step,
    lengths,
    clip,
    tok_ref,
    cot_ref,
    teach_ref,
    ctx_ref,
    wo_ref,
    w1_ref,
    w2_ref,
    vec,
    up_bias,
    out_ref,
    dctx_ref,
    dao_ref,
    cb_ref,
    du_ref,
    hb_ref,
    df_ref,
    fb_ref,
    res_ref,
    sums_ref,
    upsum_ref,
    slope_ref,
):
    wide = w1_ref.shape[0]
    ctx_width, hid_width, act_width = (saturation * clip[at] for at in (1, 2, 3))
    ctx_bent = jnp.tanh(ctx_ref[...] / ctx_width)
    ctx_low = (ctx_width * ctx_bent).astype(BF16)
    cb_ref[...] = ctx_low
    first, first_inverse = normalize(
        tok_ref[...].astype(F32) + dot(ctx_low, wo_ref[...], 1, 1) + vec[3:4]
    )
    hidden = first * vec[5:6] + vec[7:8]
    hid_bent = jnp.tanh(hidden / hid_width)
    hid_low = (hid_width * hid_bent).astype(BF16)
    hb_ref[...] = hid_low
    lower = None
    for at in range(wide // ff_part):
        take = slice(at * ff_part, (at + 1) * ff_part)
        upper = dot(hid_low, w1_ref[take], 1, 1) + up_bias[at : at + 1]
        cumulative, bent = gelu_parts(upper)
        act = jnp.tanh(bent / act_width)
        density = jnp.exp(-0.5 * upper * upper) * (1.0 / math.sqrt(2.0 * math.pi))
        slope_ref[:, take] = (1.0 - act * act) * (cumulative + upper * density)
        act_low = (act_width * act).astype(BF16)
        fb_ref[:, take] = act_low
        part = dot(act_low, w2_ref[:, take], 1, 1)
        lower = part if lower is None else lower + part
    second, second_inverse = normalize(hidden + lower + vec[4:5])
    result = second * vec[6:7] + vec[8:9]
    out_ref[...] = result.astype(BF16)
    rows = result.shape[0]
    position = lax.broadcasted_iota(jnp.int32, (rows, D), 0) + step * rows
    gap = jnp.where(position < lengths[own_index()], result - teach_ref[...], 0.0)
    grad_out = cot_ref[...].astype(F32) + gap * (2.0 * hidden_weight)
    grad_second = norm_back(grad_out * vec[6:7], second, second_inverse)
    grad_lower = grad_second.astype(BF16)
    df_ref[...] = grad_lower
    grad_hidden = None
    up_sums = []
    for at in range(wide // ff_part):
        take = slice(at * ff_part, (at + 1) * ff_part)
        grad_upper = (dot(grad_lower, w2_ref[:, take], 1, 0) * slope_ref[:, take]).astype(BF16)
        du_ref[:, take] = grad_upper
        up_sums.append(jnp.sum(grad_upper.astype(F32), axis=0, keepdims=True))
        part = dot(grad_upper, w1_ref[take], 1, 0)
        grad_hidden = part if grad_hidden is None else grad_hidden + part
    grad_hidden = grad_second + grad_hidden * (1.0 - hid_bent * hid_bent)
    grad_first = norm_back(grad_hidden * vec[5:6], first, first_inverse)
    res_ref[...] = grad_first
    grad_attn = grad_first.astype(BF16)
    dao_ref[...] = grad_attn
    dctx_ref[...] = (
        dot(grad_attn, wo_ref[...], 1, 0) * (1.0 - ctx_bent * ctx_bent)
    ).astype(BF16)

    @pl.when(step == 0)
    def _():
        sums_ref[...] = jnp.zeros_like(sums_ref)
        upsum_ref[...] = jnp.zeros_like(upsum_ref)

    for at, term in enumerate(
        (
            grad_attn.astype(F32),
            grad_lower.astype(F32),
            grad_hidden * first,
            grad_out * second,
            grad_hidden,
            grad_out,
            gap * gap,
        )
    ):
        sums_ref[at : at + 1] += jnp.sum(term, axis=0, keepdims=True)
    for at, total in enumerate(up_sums):
        upsum_ref[at : at + 1] += total


def student_middle(
    lengths, clip_scales, tokens, cotangent, teach_out, context, wo, w1, w2, vectors
):
    rows, wide = tokens.shape[0], w1.shape[0]
    block, down_block, up_block = 256, 256, D
    row_steps, down_steps, up_steps = rows // block, D // down_block, wide // up_block
    scalar = whole(pltpu.SMEM)

    def window(first, count, shape):
        return pl.BlockSpec(shape, lambda i: (jnp.clip(i - first, 0, count - 1), 0))

    row_spec = window(0, row_steps, (block, D))
    narrow, broad = pltpu.VMEM((rows, D), BF16), pltpu.VMEM((rows, wide), BF16)
    return pl.pallas_call(
        functools.partial(student_kernel, row_steps),
        grid=(row_steps + down_steps + up_steps + 1,),
        in_specs=[scalar, scalar]
        + [row_spec] * 4
        + [fixed((D, D)), fixed((wide, D)), fixed((D, wide)), fixed(vectors.shape)],
        out_specs=[row_spec] * 3
        + [
            fixed((8, D)),
            fixed((wide // D, D)),
            window(row_steps, down_steps, (down_block, wide)),
            window(row_steps + down_steps, up_steps, (up_block, D)),
            fixed((D, D)),
        ],
        out_shape=[
            jax.ShapeDtypeStruct((rows, D), BF16),
            jax.ShapeDtypeStruct((rows, D), BF16),
            jax.ShapeDtypeStruct((rows, D), F32),
            jax.ShapeDtypeStruct((8, D), F32),
            jax.ShapeDtypeStruct((wide // D, D), F32),
            jax.ShapeDtypeStruct((D, wide), BF16),
            jax.ShapeDtypeStruct((wide, D), BF16),
            jax.ShapeDtypeStruct((D, D), BF16),
        ],
        scratch_shapes=[narrow, broad, broad, narrow, narrow, narrow]
        + [pltpu.VMEM((block, wide), F32)],
        compiler_params=pltpu.CompilerParams(vmem_limit_bytes=vmem_bytes),
        name="student_feed_forward",
    )(lengths, clip_scales, tokens, cotangent, teach_out, context, wo, w1, w2, vectors)


def input_kernel(clip, grad_ref, w_ref, low_ref, tok_ref, res_ref, out_ref, dw_ref, sum_ref, acc_ref):
    slot = pl.program_id(0)
    grad = grad_ref[0]
    part = dot(grad, w_ref[0], 1, 0)
    dw_ref[0] = outer_rows(grad, low_ref[...]).astype(dw_ref.dtype)
    sum_ref[0] = jnp.sum(grad.astype(F32), axis=0, keepdims=True)

    @pl.when(slot == 0)
    def _():
        acc_ref[...] = part

    @pl.when(slot > 0)
    def _():
        acc_ref[...] += part

    @pl.when(slot == pl.num_programs(0) - 1)
    def _():
        bent = jnp.tanh(tok_ref[...].astype(F32) / (saturation * clip[0]))
        out_ref[...] = (res_ref[...] + acc_ref[...] * (1.0 - bent * bent)).astype(BF16)


def input_grads(clip_scales, grads, weights, low, tokens, residual):
    rows = tokens.shape[0]
    slotted = lambda *shape: pl.BlockSpec((1,) + shape, lambda i: (i, 0, 0))
    return pl.pallas_call(
        input_kernel,
        grid=(3,),
        in_specs=[
            whole(pltpu.SMEM),
            slotted(rows, D),
            slotted(D, D),
            fixed((rows, D)),
            fixed((rows, D)),
            fixed((rows, D)),
        ],
        out_specs=[fixed((rows, D)), slotted(D, D), slotted(1, D)],
        out_shape=[
            jax.ShapeDtypeStruct((rows, D), BF16),
            jax.ShapeDtypeStruct((3, D, D), BF16),
            jax.ShapeDtypeStruct((3, 1, D), F32),
        ],
        scratch_shapes=[pltpu.VMEM((rows, D), F32)],
        compiler_params=pltpu.CompilerParams(vmem_limit_bytes=vmem_bytes),
        name="input_gradient",
    )(clip_scales, grads, weights, low, tokens, residual)


gather_chunks = ((0,), (1,), (2,), (3,), (4, 5), (6,), (7, 8), (9,))
gather_leads = (1, 1, 1, 3, 1, 1, 1, 1, 1, 1)
late_chunks = (6,)
ahead_stages = ((0, 0), (1, 0), (2, 0), (0, 1), (1, 1), (2, 1), (0, 2), (1, 2), (2, 2), (0, 3), (1, 3), (3, 0), (2, 3), (0, 4), (5, 0), (0, 5), (3, 1), (1, 4), (1, 5), (5, 1), (2, 4), (3, 2), (4, 0), (6, 0), (2, 5), (0, 6), (5, 2), (7, 0), (1, 6), (0, 7), (2, 6), (3, 3), (1, 7), (6, 1), (2, 7))
opening_stages = {3: (), 6: ((4, 6), (5, 7), (6, 4), (4, 7))}
gather_between = {(0, 3): ((4, 1), (3, 4), (7, 1), (5, 3)), (1, 3): ((4, 2), (3, 5), (3, 6), (6, 2)), (2, 3): ((4, 3), (3, 7), (7, 2), (5, 4)), (3, 3): ((5, 5),), (4, 3): ((4, 4), (6, 3), (7, 3), (4, 5)), (5, 3): ((5, 6),), (6, 3): ((7, 4),), (7, 3): ((7, 5),), (8, 3): ((6, 5), (7, 6)), (9, 3): ((6, 6),)}
closing_stages = ((7, 7),)


def lay_flat(flat, owners):
    rows = owners.shape[-2]
    for owner in range(flat.shape[0] // rows):
        flat[owner * rows : (owner + 1) * rows] = owners[
            owner // 8, owner // 4 % 2, owner // 2 % 2, owner % 2
        ]


def own_lines(target, line_refs, up_bias_refs):
    at = own_index()
    target[...] = jnp.zeros_like(target)
    width = line_refs[0].shape[1]
    place, row = lanes_of(width, at * width), 0
    for ref in line_refs:
        target[row : row + ref.shape[0]] = dot(ref[...], place, 1, 0)
        row += ref.shape[0]
    wide = up_bias_refs[0].shape[1]
    owners = D // wide
    place = lanes_of(wide, lax.rem(at, owners) * wide)
    for ref in up_bias_refs:
        rows = wide * count_of() // D
        where = lax.broadcasted_iota(jnp.int32, (rows, D), 0) == at // owners
        target[row : row + rows] = jnp.where(where, dot(ref[...], place, 1, 0), 0.0)
        row += rows


def count_of():
    return lax.axis_size("dp") * lax.axis_size("shard")


def forward_kernel(depth, tail_steps, lengths, clip, *refs):
    (teach_attn, teach_up, teach_down, attn_ref, up_ref, down_ref, teach_tok, tok), refs = (
        refs[:8],
        refs[8:],
    )
    line_refs, up_bias_refs, refs = refs[:6], refs[6:8], refs[8:]
    (tq_ref, tk_ref, q_ref, k_ref, v_ref, ctx_ref, low_ref, out_ref, vec_ref), refs = (
        refs[:9],
        refs[9:],
    )
    (qkv_out, wo_out, up_out, down_out), refs = refs[:4], refs[4:]
    (teach_qkv, own_qkv, teach_wo, teach_w1, teach_w2, attn_low, up_low, down_low, teach_ctx), refs = (
        refs[:9],
        refs[9:],
    )
    (qkv_flat, wo_flat, w2_flat), refs = refs[:3], refs[3:]
    qkv_sem, shared, sems = refs[0], refs[1:6], refs[6:]
    place = Place(depth)
    step = pl.program_id(0)
    narrow = 2 * LANES
    attend_steps = D // narrow
    last = pl.num_programs(0) - 1

    ins = [teach_attn.at[slot] for slot in range(3)] + [
        attn_low.at[pl.ds(0, 3)],
        teach_attn.at[3],
        teach_up,
        teach_down,
        attn_low.at[3],
        up_low,
        down_low,
    ]
    outs = [teach_qkv.at[slot] for slot in range(3)] + [
        own_qkv,
        teach_wo,
        teach_w1,
        teach_w2,
        wo_out,
        up_out,
        down_out,
    ]
    begin, stage, sent = gather_stage(place, ins, outs, gather_leads, gather_chunks, late_chunks, sems)

    def run(stages):
        for chunk, number in stages:
            stage(chunk, number)

    def finish_lines(total):
        vec_ref[...] = total.astype(F32)

    line_stage = shared_stage(place, finish_lines, shared)
    line_count = depth + 4

    @pl.when(step == 0)
    def _():
        own_lines(vec_ref, line_refs, up_bias_refs)
        shared[0][0] = vec_ref[...].astype(BF16)
        place.barrier()
        begin((0, 1, 2))
        lines = iter(range(line_count))
        for at, (chunk, number) in enumerate(ahead_stages):
            if at == 2:
                for latent, low in ((attn_ref, attn_low), (up_ref, up_low), (down_ref, down_low)):
                    values = latent[...]
                    scale = jnp.mean(jnp.abs(values), axis=-1, keepdims=True)
                    sign = jnp.where(values > 0, 1.0, jnp.where(values < 0, -1.0, 0.0))
                    low[...] = (scale * sign).astype(BF16)
                begin((4, 5, 3, 6, 7))
            stage(chunk, number)
            if at % 2 == 0:
                for line in lines:
                    line_stage(line)
                    break
        for line in lines:
            line_stage(line)

    def slots(first, steps, at):
        for local in range(steps):
            stages = gather_between.get((first + local, at))
            if stages:

                @pl.when(step == first + local)
                def _():
                    run(stages)

    def opening(first):
        if opening_stages[first]:

            @pl.when(step == first)
            def _():
                run(opening_stages[first])

    def qkv_copy():
        return pltpu.make_async_copy(own_qkv, qkv_out, qkv_sem)

    def attend_step(student, first, inputs, weights, line, targets):
        local = step - first
        @pl.when(local == 0)
        def _():
            for slot in range(3):
                lay_flat(qkv_flat.at[slot], weights.at[slot])

        rows = pl.ds(pl.multiple_of(local * narrow, narrow), narrow)
        attend_quad(
            student,
            lengths[own_index()],
            inputs[...],
            [qkv_flat[slot, rows, :] for slot in range(3)],
            [vec_ref[line + slot : line + slot + 1, rows] for slot in range(3)],
            targets,
            lambda head: None,
        )
        slots(first, attend_steps, 3)

    @pl.when(step < attend_steps)
    def _():
        lanes = pl.ds(pl.multiple_of(step * narrow, narrow), narrow)
        attend_step(
            False, 0, teach_tok, teach_qkv, 0, (tq_ref, tk_ref, None, teach_ctx.at[:, lanes])
        )

    @pl.when((step >= attend_steps) & (step < 2 * attend_steps))
    def _():
        opening(attend_steps)

        @pl.when(step == attend_steps)
        def _():
            qkv_copy().start()
            width = saturation * clip[0]
            low_ref[...] = (width * jnp.tanh(tok[...].astype(F32) / width)).astype(BF16)

        attend_step(True, attend_steps, low_ref, own_qkv, 9, (q_ref, k_ref, v_ref, ctx_ref))

    @pl.when(step >= 2 * attend_steps)
    def _():
        first = 2 * attend_steps
        opening(first)

        @pl.when(step == first)
        def _():
            lay_flat(wo_flat, teach_wo)
            lay_flat(w2_flat, teach_w2)

        block = out_ref.shape[0]
        rows = pl.ds(pl.multiple_of((step - first) * block, block), block)
        teacher_rows(
            teach_tok[rows, :],
            teach_ctx[rows, :],
            wo_flat,
            lambda at: teach_w1[at].reshape(D, D),
            w2_flat,
            vec_ref[0:9],
            vec_ref[18:22],
            out_ref,
            lambda at: None,
        )
        slots(first, tail_steps, 3)

    @pl.when(step == last)
    def _():
        run(closing_stages)
        qkv_copy().wait()
        for chunk in range(len(gather_chunks)):
            sent(chunk)


def forward(
    lengths,
    clip_scales,
    teacher_attn,
    teacher_up,
    teacher_down,
    lines,
    up_biases,
    latents,
    teacher_tokens,
    tokens,
):
    rows = tokens.shape[0]
    depth = lax.axis_size("dp") // 2
    attn_latent, up_latent, down_latent = latents
    narrow, wide = attn_latent.shape[1], up_latent.shape[0]
    lanes, quad, block = 2 * LANES, 4 * LANES, 256
    attend_steps, tail_steps = D // lanes, rows // block
    dma = pltpu.SemaphoreType.DMA
    owners = (depth, 2, 2, 2)
    qkv_shape, wo_shape = (3,) + owners + (narrow, D), owners + (narrow, D)
    up_shape, down_shape = owners + (wide, D), owners + (narrow, down_latent.shape[1])
    scalar = whole(pltpu.SMEM)

    def window(first, count, shape, along):
        def index(i):
            at = jnp.clip(i - first, 0, count - 1)
            return (at, 0) if along == 0 else (0, at)

        return pl.BlockSpec(shape, index)

    def student_columns(width):
        return window(attend_steps, attend_steps, (rows, width), 1)

    results = pl.pallas_call(
        functools.partial(forward_kernel, depth, tail_steps),
        grid=(2 * attend_steps + tail_steps,),
        in_specs=[scalar] * 2
        + [whole(pl.ANY)] * 3
        + [
            fixed(shape)
            for shape in (
                attn_latent.shape,
                up_latent.shape,
                down_latent.shape,
                (rows, D),
                (rows, D),
                *(line.shape for line in lines),
                *(line.shape for line in up_biases),
            )
        ],
        out_specs=[window(0, attend_steps, (rows, lanes), 1)] * 2
        + [student_columns(quad)] * 3
        + [
            student_columns(lanes),
            fixed((rows, D)),
            window(2 * attend_steps, tail_steps, (block, D), 0),
            fixed((vector_rows, D)),
        ]
        + [whole(pl.ANY)] * 4,
        out_shape=[jax.ShapeDtypeStruct((rows, D), BF16)] * 2
        + [jax.ShapeDtypeStruct((rows, 2 * D), BF16)] * 3
        + [
            jax.ShapeDtypeStruct((rows, D), F32),
            jax.ShapeDtypeStruct((rows, D), BF16),
            jax.ShapeDtypeStruct((rows, D), F32),
            jax.ShapeDtypeStruct((vector_rows, D), F32),
        ]
        + [
            jax.ShapeDtypeStruct(shape, BF16)
            for shape in (qkv_shape, wo_shape, up_shape, down_shape)
        ],
        scratch_shapes=[
            pltpu.VMEM(shape, BF16)
            for shape in (
                qkv_shape,
                qkv_shape,
                wo_shape,
                up_shape,
                down_shape,
                attn_latent.shape,
                up_latent.shape,
                down_latent.shape,
                (rows, D),
                (3, D, D),
                (D, D),
                (D, down_latent.shape[1]),
            )
        ]
        + [dma]
        + shared_scratch(depth, vector_rows, BF16)
        + gather_scratch(gather_chunks, depth),
        compiler_params=pltpu.CompilerParams(
            collective_id=0, has_side_effects=True, vmem_limit_bytes=vmem_bytes
        ),
        name="gather_attention_and_teacher",
    )(
        lengths,
        clip_scales,
        teacher_attn,
        teacher_up,
        teacher_down,
        attn_latent,
        up_latent,
        down_latent,
        teacher_tokens,
        tokens,
        *lines,
        *up_biases,
    )
    return list(results[:9]) + gathered(results[9:])


first_stages = ((0, 0), (2, 0), (1, 0))
between_stages = {1: ((0, 1), (0, 2)), 2: ((1, 1), (1, 2), (0, 3)), 4: ((1, 3),), 5: ((0, 4), (2, 1), (2, 2)), 6: ((1, 4), (2, 3))}
after_weights = (((0, 5), (2, 4)), ((3, 1), (3, 2)), ((4, 1), (4, 2), (3, 3)))
after_inputs = (((1, 5), (4, 3), (0, 6), (5, 1), (5, 2), (2, 5)), ((4, 4), (3, 4), (0, 7), (0, 8), (5, 3)), ((1, 6), (4, 5), (5, 4), (2, 6)))
last_stages = ((3, 5), (4, 6), (5, 5), (1, 7), (1, 8), (3, 6), (2, 7), (2, 8), (4, 7), (4, 8), (5, 6), (3, 7), (3, 8), (5, 7), (5, 8))


def latent_rows(latent, grad):
    size = latent.shape[-1]
    scale = jnp.mean(jnp.abs(latent), axis=-1, keepdims=True)
    sign = jnp.where(latent > 0, 1.0, jnp.where(latent < 0, -1.0, 0.0))
    return scale * grad + sign * (jnp.sum(grad * latent, axis=-1, keepdims=True) / size)


def inverse_norms(lengths, width):
    tokens, pairs = jnp.int32(0), jnp.int32(0)
    for at in range(lengths.shape[0]):
        tokens, pairs = tokens + lengths[at], pairs + lengths[at] * lengths[at]
    return tuple(
        1.0 / (jnp.full((1, width), total.astype(F32)) * factor)
        for total, factor in ((pairs, float(HEADS)), (tokens, float(D)))
    )


def finish_kernel(depth, lengths, clip, *refs):
    pair_refs, refs = refs[:7], refs[7:]
    dw_refs, refs = refs[:3], refs[3:]
    held_refs, refs = refs[:4], refs[4:]
    (sums_ref, upsum_ref, attn_ref, up_ref, down_ref), refs = refs[:5], refs[5:]
    (input_ref, attn_grad, up_grad, down_grad), refs = refs[:4], refs[4:]
    (bias_grad, gain_grad, shift_grad, up_bias_grad, loss_ref), refs = refs[:5], refs[5:]
    (grad_ref, square_ref, dwq_ref, dwk_ref, dwv_ref), refs = refs[:5], refs[5:]
    (low_ref, w_ref, tok_ref, res_ref, load_sem), refs = refs[:5], refs[5:]
    loads = [
        pltpu.make_async_copy(source, target, load_sem.at[at])
        for at, (source, target) in enumerate(zip(held_refs, (low_ref, w_ref, tok_ref, res_ref)))
    ]
    shared, scratch = refs[:5], refs[5:]
    place = Place(depth)
    step = pl.program_id(0)
    last = pl.num_programs(0) - 1
    pairs = D // LANES

    def finish(item, lead, total):
        if item == 0:
            down_grad[...] = latent_rows(down_ref[...], total)
        elif item == 1:
            up_grad[...] = latent_rows(up_ref[...], total)
        else:
            slot = 3 if item == 2 else item - 3
            attn_grad[slot] = latent_rows(attn_ref[slot], total)

    def finish_lines(total):
        at = own_index()
        width, wide = bias_grad.shape[1], up_bias_grad.shape[1]
        taken = take_lanes(total[0:9], width, at * width)
        bias_grad[...] = taken[0:5]
        gain_grad[...] = taken[5:7]
        shift_grad[...] = taken[7:9]
        owners, rows = D // wide, total[9:13]
        where = lax.broadcasted_iota(jnp.int32, rows.shape, 0) == at // owners
        row = jnp.sum(jnp.where(where, rows, 0.0), axis=0, keepdims=True)
        up_bias_grad[...] = take_lanes(row, wide, lax.rem(at, owners) * wide)
        loss_ref[...] = jnp.sum(total[13:14], axis=1, keepdims=True)

    own = (dwq_ref, dwk_ref, dwv_ref)
    stage = scatter_stage(place, tuple(dw_refs) + own, finish, scratch, 6)
    line_stage = shared_stage(place, finish_lines, shared)

    def run(stages):
        for item, number in stages:
            stage(item, number)

    @pl.when(step == 0)
    def _():
        place.barrier()
        run(first_stages)
        for load in loads:
            load.start()
        square_ref[...] = jnp.zeros_like(square_ref)

    @pl.when(step < pairs)
    def _():
        for before, stages in between_stages.items():

            @pl.when(step == before)
            def _():
                run(stages)

        grads, squares = attend_back_pair(
            lengths[own_index()], inverse_norms(lengths, LANES)[0], *pair_refs, lambda odd: None
        )
        square_ref[...] += squares
        lanes = pl.ds(pl.multiple_of(step * LANES, LANES), LANES)
        for slot in range(3):
            grad_ref[slot, :, lanes] = grads[slot]

    def weight_grad(slot):
        total = outer_rows(grad_ref[slot], low_ref[...]).astype(BF16)
        rows = dwq_ref.shape[-2]
        for owner in range(D // rows):
            where = (owner // 8, owner // 4 % 2, owner // 2 % 2, owner % 2)
            own[slot][where] = total[owner * rows : (owner + 1) * rows]
        stage(3 + slot, 0)

    @pl.when(step == pairs)
    def _():
        run(between_stages.get(pairs, ()))
        held = shared[0]
        held[0] = jnp.zeros_like(held[0])
        for slot in range(3):
            held[0, slot : slot + 1] = jnp.sum(
                grad_ref[slot].astype(F32), axis=0, keepdims=True
            )
        held[0, 3:9] = sums_ref[0:6]
        held[0, 9:13] = upsum_ref[...]
        held[0, 13:14] = sums_ref[6:7] * inverse_norms(lengths, D)[1]
        held[0, 13:14, :LANES] += jnp.sum(square_ref[...], axis=0, keepdims=True)
        line_stage(0)
        loads[0].wait()
        weight_grad(0)
        run(after_weights[0])
        weight_grad(1)
        run(after_weights[1])

    @pl.when(step == last)
    def _():
        line_stage(1)
        weight_grad(2)
        run(after_weights[2])
        for load in loads[1:]:
            load.wait()
        total = None
        for slot in range(3):
            line_stage(2 + slot)
            part = dot(grad_ref[slot], w_ref[slot], 1, 0)
            total = part if total is None else total + part
            run(after_inputs[slot])
        bent = jnp.tanh(tok_ref[...].astype(F32) / (saturation * clip[0]))
        input_ref[...] = (res_ref[...] + total * (1.0 - bent * bent)).astype(BF16)
        for at, (item, number) in enumerate(last_stages):
            if at < 3 and 5 + at < depth + 4:
                line_stage(5 + at)
            stage(item, number)


def move_kernel(count, *refs):
    copies = [
        pltpu.make_async_copy(refs[at], refs[count + at], refs[2 * count].at[at])
        for at in range(count)
    ]
    for copy in copies:
        copy.start()
    for copy in copies:
        copy.wait()


def moved(*arrays):
    count = len(arrays)
    return pl.pallas_call(
        functools.partial(move_kernel, count),
        in_specs=[whole()] * count,
        out_specs=[whole(pl.ANY)] * count,
        out_shape=[jax.ShapeDtypeStruct(array.shape, array.dtype) for array in arrays],
        compiler_params=pltpu.CompilerParams(vmem_limit_bytes=vmem_bytes),
        scratch_shapes=[pltpu.SemaphoreType.DMA((count,))],
        name="move_results",
    )(*arrays)


def finish_backward(
    lengths,
    clip_scales,
    pair_arrays,
    weight_grads,
    qkv_w,
    low,
    tokens,
    residual,
    sums,
    up_sums,
    latents,
    narrow,
    wide,
):
    dp, shard = lax.axis_size("dp"), lax.axis_size("shard")
    attn_latent, up_latent, down_latent = latents
    if not tiled_over((dp, shard), narrow):
        live_float = lengths.astype(F32)
        inverse_pairs = (1.0 / (HEADS * jnp.sum(live_float * live_float))).reshape(1)
        inverse_hidden = 1.0 / (D * jnp.sum(live_float))
        grads, squares = attend_back(lengths, inverse_pairs, *pair_arrays)
        input_grad, qkv_weight_grad, qkv_sums = input_grads(
            clip_scales, grads, qkv_w, low, tokens, residual
        )
        local_loss = sums[6:7] * inverse_hidden
        local_loss = local_loss + jnp.pad(
            jnp.sum(squares, axis=0, keepdims=True), ((0, 0), (0, D - LANES))
        )
        lines = jnp.concatenate(
            [qkv_sums[:, 0], sums[:6], up_sums, local_loss], axis=0
        )
        lines = lax.psum(lines, AXES)
        down_total, up_total, attn_total = scatter(
            weight_grads[:2]
            + [jnp.concatenate([qkv_weight_grad, weight_grads[2][None].astype(BF16)], axis=0)]
        )
        attn_grad = latent_grad(attn_latent, attn_total)
        up_grad = latent_grad(up_latent, up_total)
        down_grad = latent_grad(down_latent, down_total)
        at = lax.axis_index(AXES)
        own = lax.dynamic_slice_in_dim(lines[:9], at * narrow, narrow, axis=1)
        bias_grad, gain_grad, shift_grad = own[:5], own[5:7], own[7:9]
        up_bias_grad = lax.dynamic_slice_in_dim(lines[9:13].reshape(-1), at * wide, wide)
        loss = jnp.sum(lines[13])
    else:
        depth = dp // 2
        rows = tokens.shape[0]
        dw = [split_rows(grad, depth) for grad in weight_grads]
        own_shape = (depth, 2, 2, 2, narrow, D)
        shapes = [(1,) + grad.shape[-2:] for grad in dw] + [(1, narrow, D)] * 3
        scalar = whole(pltpu.SMEM)
        pairs = D // LANES

        def pair_columns(width):
            return pl.BlockSpec((rows, width), lambda i: (0, jnp.minimum(i, pairs - 1)))

        small_shapes = ((5, narrow), (2, narrow), (2, narrow), (1, wide), (1, 1))
        (
            input_grad,
            attn_grad,
            up_grad,
            down_grad,
            bias_grad,
            gain_grad,
            shift_grad,
            up_bias_grad,
            loss,
        ) = pl.pallas_call(
            functools.partial(finish_kernel, depth),
            grid=(pairs + 2,),
            in_specs=[scalar] * 2
            + [pair_columns(2 * LANES)] * 3
            + [pair_columns(LANES)] * 4
            + [whole(pl.ANY)] * 7
            + [
                fixed(array_shape)
                for array_shape in (
                    sums.shape,
                    up_sums.shape,
                    attn_latent.shape,
                    up_latent.shape,
                    down_latent.shape,
                )
            ],
            out_specs=[
                fixed(array_shape)
                for array_shape in (
                    (rows, D),
                    attn_latent.shape,
                    up_latent.shape,
                    down_latent.shape,
                    *small_shapes,
                )
            ],
            out_shape=[
                jax.ShapeDtypeStruct((rows, D), BF16),
                jax.ShapeDtypeStruct(attn_latent.shape, F32),
                jax.ShapeDtypeStruct(up_latent.shape, F32),
                jax.ShapeDtypeStruct(down_latent.shape, F32),
            ]
            + [jax.ShapeDtypeStruct(shape, F32) for shape in small_shapes],
            scratch_shapes=[
                pltpu.VMEM((3, rows, D), BF16),
                pltpu.VMEM((8, LANES), F32),
                pltpu.VMEM(own_shape, BF16),
                pltpu.VMEM(own_shape, BF16),
                pltpu.VMEM(own_shape, BF16),
                pltpu.VMEM((rows, D), BF16),
                pltpu.VMEM((3, D, D), BF16),
                pltpu.VMEM((rows, D), BF16),
                pltpu.VMEM((rows, D), F32),
                pltpu.SemaphoreType.DMA((4,)),
            ]
            + shared_scratch(depth, line_rows, F32)
            + scatter_scratch(shapes, [BF16] * 6, depth),
            compiler_params=pltpu.CompilerParams(
                collective_id=1, has_side_effects=True, vmem_limit_bytes=vmem_bytes
            ),
            name="attention_backward_and_sums",
        )(
            lengths,
            clip_scales,
            *pair_arrays,
            *dw,
            low,
            qkv_w,
            tokens,
            residual,
            sums,
            up_sums,
            attn_latent,
            up_latent,
            down_latent,
        )
        (
            input_grad,
            attn_grad,
            up_grad,
            down_grad,
            bias_grad,
            gain_grad,
            shift_grad,
            up_bias_grad,
            loss,
        ) = moved(
            input_grad,
            attn_grad,
            up_grad,
            down_grad,
            bias_grad,
            gain_grad,
            shift_grad,
            up_bias_grad,
            loss,
        )
    return (
        loss.reshape(()),
        input_grad,
        attn_grad,
        up_grad,
        down_grad,
        bias_grad,
        up_bias_grad.reshape(-1),
        gain_grad,
        shift_grad,
    )


def on_device(
    tokens,
    teacher_tokens,
    cotangent,
    lengths,
    clip_scales,
    attn_latent,
    up_latent,
    down_latent,
    biases,
    up_bias,
    norm_gains,
    norm_shifts,
    teacher_attn,
    teacher_up,
    teacher_down,
    teacher_biases,
    teacher_up_bias,
    teacher_gains,
    teacher_shifts,
):
    sizes = (lax.axis_size("dp"), lax.axis_size("shard"))
    narrow, wide = biases.shape[1], up_bias.shape[0]
    lines = (teacher_biases, teacher_gains, teacher_shifts, biases, norm_gains, norm_shifts)
    latents = (attn_latent, up_latent, down_latent)
    if tiled_over(sizes, narrow):
        (
            tq,
            tk,
            query,
            key,
            value,
            context,
            x_low,
            teach_out,
            vec,
            qkv_w,
            out_w,
            up_w,
            down_w,
        ) = forward(
            lengths,
            clip_scales,
            teacher_attn,
            teacher_up,
            teacher_down,
            lines,
            (teacher_up_bias.reshape(1, -1), up_bias.reshape(1, -1)),
            latents,
            teacher_tokens,
            tokens,
        )
    else:
        vec = jnp.concatenate(
            [
                lax.all_gather(jnp.concatenate(lines, axis=0), AXES, axis=1, tiled=True),
                *(
                    lax.all_gather(line, AXES, tiled=True).reshape(-1, D)
                    for line in (teacher_up_bias, up_bias)
                ),
            ],
            axis=0,
        ).astype(F32)
        vec = jnp.pad(vec, ((0, vector_rows - vec.shape[0]), (0, 0)))
        teach_qkv, teach_wo, teach_up, teach_down, qkv_w, out_w, up_w, down_w = gather(
            [
                teacher_attn[:3],
                teacher_attn[3],
                teacher_up,
                teacher_down,
                binarize(attn_latent[:3]),
                binarize(attn_latent[3]),
                binarize(up_latent),
                binarize(down_latent),
            ]
        )
        tq, tk, teach_context = attend(
            False, lengths, clip_scales, teacher_tokens, teach_qkv, vec[:3].reshape(3, 1, D)
        )
        query, key, value, context, x_low = attend(
            True, lengths, clip_scales, tokens, qkv_w, vec[9:12].reshape(3, 1, D)
        )
        teach_out = teacher_tail(
            teacher_tokens, teach_context, teach_wo, teach_up, teach_down, vec[:9], vec[18:22]
        )
    result, grad_context, residual, sums, up_sums, *weight_grads = student_middle(
        lengths,
        clip_scales,
        tokens,
        cotangent,
        teach_out,
        context,
        out_w,
        up_w,
        down_w,
        vec,
    )
    return (result,) + finish_backward(
        lengths,
        clip_scales,
        (query, key, value, context, grad_context, tq, tk),
        weight_grads,
        qkv_w,
        x_low,
        tokens,
        residual,
        sums,
        up_sums,
        latents,
        narrow,
        wide,
    )


def solution(mesh):
    in_specs = (
        P(("dp", "shard"), None),
        P(("dp", "shard"), None),
        P(("dp", "shard"), None),
        P(),
        P(),
        P(None, ("dp", "shard"), None),
        P(("dp", "shard"), None),
        P(("dp", "shard"), None),
        P(None, ("dp", "shard")),
        P(("dp", "shard")),
        P(None, ("dp", "shard")),
        P(None, ("dp", "shard")),
        P(None, ("dp", "shard"), None),
        P(("dp", "shard"), None),
        P(("dp", "shard"), None),
        P(None, ("dp", "shard")),
        P(("dp", "shard")),
        P(None, ("dp", "shard")),
        P(None, ("dp", "shard")),
    )
    out_specs = (
        P(("dp", "shard"), None),
        P(),
        P(("dp", "shard"), None),
        P(None, ("dp", "shard"), None),
        P(("dp", "shard"), None),
        P(("dp", "shard"), None),
        P(None, ("dp", "shard")),
        P(("dp", "shard")),
        P(None, ("dp", "shard")),
        P(None, ("dp", "shard")),
    )
    return jax.shard_map(
        on_device, mesh=mesh, in_specs=in_specs, out_specs=out_specs, check_vma=False
    )
```

```python
import functools
import math

import jax
import jax.numpy as jnp
from jax import lax
from jax.experimental import pallas as pl
from jax.experimental.pallas import tpu as pltpu
from jax.sharding import PartitionSpec as P

D = 768
HEADS = 12
HEAD_DIM = 64
SEQ_LEN = 1024
AXES = ("dp", "shard")
MESH = pl.DeviceIdType.MESH
F32 = jnp.float32
BF16 = jnp.bfloat16

epsilon = 1e-05
masked_score = -1e30
hidden_weight = 0.25
saturation = 7.5
LANES = 128
log2e = math.log2(math.e)
scaling = HEAD_DIM ** (-0.5)
exponent = scaling * log2e
vmem_bytes = 60 * 1024 * 1024
line_rows = 16
vector_rows = 32


def dot(left, right, left_dim, right_dim):
    return lax.dot_general(
        left, right, (((left_dim,), (right_dim,)), ((), ())), preferred_element_type=F32
    )


def outer_rows(left, right):
    return dot(left, right, 0, 0)


def binarize(latent):
    scale = jnp.mean(jnp.abs(latent), axis=-1, keepdims=True)
    return (scale * jnp.sign(latent)).astype(BF16)


def surrogate(latent):
    return jnp.mean(jnp.abs(latent), axis=-1, keepdims=True) * latent


def latent_grad(latent, grad):
    _, pull = jax.vjp(surrogate, latent)
    return pull(grad)[0]


def normalize(values):
    center = values - jnp.mean(values, axis=-1, keepdims=True)
    inverse = lax.rsqrt(jnp.mean(center * center, axis=-1, keepdims=True) + epsilon)
    return (center * inverse, inverse)


def norm_back(grad_norm, normed, inverse):
    return inverse * (
        grad_norm
        - jnp.mean(grad_norm, axis=-1, keepdims=True)
        - normed * jnp.mean(grad_norm * normed, axis=-1, keepdims=True)
    )


def whole(memory=pltpu.VMEM):
    return pl.BlockSpec(memory_space=memory)


def fixed(shape):
    return pl.BlockSpec(shape, lambda *_: (0,) * len(shape), pipeline_mode=pl.Buffered(1))


def columns(shape):
    return pl.BlockSpec(shape, lambda i: (0,) * (len(shape) - 1) + (i,))


def row_blocks(shape):
    return pl.BlockSpec(shape, lambda i: (i,) + (0,) * (len(shape) - 1))


def own_index():
    return lax.axis_index("dp") * lax.axis_size("shard") + lax.axis_index("shard")


def lanes_of(width, start):
    row = lax.broadcasted_iota(jnp.int32, (width, D), 0)
    lane = lax.broadcasted_iota(jnp.int32, (width, D), 1)
    return jnp.where(lane == row + start, 1.0, 0.0).astype(BF16)


def take_lanes(values, width, start):
    chosen = lanes_of(width, start)
    return sum(dot(part.astype(BF16), chosen, 1, 1) for part in three_parts(values))


class Place:
    def __init__(self, depth):
        self.depth = depth
        dp, shard = lax.axis_index("dp"), lax.axis_index("shard")
        z, y = dp // 2, lax.rem(dp, 2)
        x, core = shard // 2, lax.rem(shard, 2)
        self.z, self.y, self.x, self.core = z, y, x, core

        def device(z_at, y_at, x_at, core_at):
            return (z_at * 2 + y_at, x_at * 2 + core_at)

        self.above = device(jnp.minimum(z + 1, depth - 1), y, x, core)
        self.below = device(jnp.maximum(z - 1, 0), y, x, core)
        one = (lax.rem(y + 1 - core, 2), lax.rem(x + core, 2))
        two = (lax.rem(y + core, 2), lax.rem(x + 1 - core, 2))
        self.pieces = ((y, x), one, two, (1 - y, 1 - x))
        self.first, self.second = device(z, *one, core), device(z, *two, core)
        self.sibling = device(z, y, x, 1 - core)

    def barrier(self):
        semaphore = pltpu.get_barrier_semaphore()
        for partner in (self.first, self.second, self.sibling):
            pl.semaphore_signal(semaphore, inc=1, device_id=partner, device_id_type=MESH)

        @pl.when(self.z < self.depth - 1)
        def _():
            pl.semaphore_signal(semaphore, inc=1, device_id=self.above, device_id_type=MESH)

        @pl.when(self.z > 0)
        def _():
            pl.semaphore_signal(semaphore, inc=1, device_id=self.below, device_id_type=MESH)

        pl.semaphore_wait(
            semaphore, 3 + jnp.minimum(self.z, 1) + jnp.minimum(self.depth - 1 - self.z, 1)
        )


def remote(source, target, send_sem, recv_sem, device):
    return pltpu.make_async_remote_copy(
        src_ref=source,
        dst_ref=target,
        send_sem=send_sem,
        recv_sem=recv_sem,
        device_id=device,
        device_id_type=MESH,
    )


def tiled_over(mesh_sizes, rows):
    return mesh_sizes == (8, 4) and rows % 8 == 0


def gather_scratch(chunks, depth):
    dma = pltpu.SemaphoreType.DMA
    sizes = (len(chunks), max(len(chunk) for chunk in chunks))
    return [
        dma(sizes + (depth - 1, 2)),
        dma(sizes + (depth - 1, 2)),
        dma(sizes + (3 + max(depth, 4),)),
        dma(sizes + (3 + max(depth, 4),)),
        dma(sizes),
    ]


def gather_stage(place, ins, outs, leads, chunks, late, sems):
    line_send, line_recv, pair_send, pair_recv, own_sem = sems
    depth, z, y, x, core = place.depth, place.z, place.y, place.x, place.core

    def slot(item, *index):
        return outs[item].at[((slice(None),) if leads[item] > 1 else ()) + index]

    def group(chunk, item, z_at):
        if chunk in late:
            return slot(item, z_at, slice(None), slice(None), core)
        return slot(item, z_at, y, x, core)

    def line_copy(chunk, at, item, turn, upward):
        if upward:
            owner, target = jnp.maximum(z - (turn - 1), 0), place.above
        else:
            owner, target = jnp.minimum(z + (turn - 1), depth - 1), place.below
        block = group(chunk, item, owner)
        where = (chunk, at, turn - 1, int(upward))
        return remote(block, block, line_send.at[where], line_recv.at[where], target)

    def sends(turn, upward):
        if upward:
            return (z - (turn - 1) >= 0) & (z < depth - 1)
        return (z + (turn - 1) <= depth - 1) & (z > 0)

    def receives(turn, upward):
        return (z - turn >= 0) if upward else (z + turn <= depth - 1)

    def own_copy(chunk, at, item):
        return pltpu.make_async_copy(
            ins[item], slot(item, z, y, x, core), own_sem.at[chunk, at]
        )

    plans = (
        (0, place.first),
        (0, place.second),
        (1, place.second),
        (0, place.sibling),
        (1, place.sibling),
        (2, place.sibling),
        (3, place.sibling),
    )

    def pair_copy(chunk, at, item, plan):
        piece, target = plans[plan]
        z_at = z if chunk in late else slice(None)
        block = slot(item, z_at, *place.pieces[piece], core)
        where = (chunk, at, plan)
        return remote(block, block, pair_send.at[where], pair_recv.at[where], target)

    def each(chunk, action):
        for at, item in enumerate(chunks[chunk]):
            action(at, item)

    def line_start(chunk, turn):
        for upward in (True, False):

            @pl.when(sends(turn, upward))
            def _():
                each(chunk, lambda at, item: line_copy(chunk, at, item, turn, upward).start())

    def line_received(chunk, turn):
        for upward in (True, False):

            @pl.when(receives(turn, upward))
            def _():
                each(chunk, lambda at, item: line_copy(chunk, at, item, turn, upward).wait_recv())

    def line_sent(chunk, turn):
        for upward in (True, False):

            @pl.when(sends(turn, upward))
            def _():
                each(chunk, lambda at, item: line_copy(chunk, at, item, turn, upward).wait_send())

    def start(chunk, *plan_list):
        for plan in plan_list:
            each(chunk, lambda at, item: pair_copy(chunk, at, item, plan).start())

    def received(chunk, *plan_list):
        for plan in plan_list:
            each(chunk, lambda at, item: pair_copy(chunk, at, item, plan).wait_recv())

    def plane_copy(chunk, at, item, z_at):
        block = group(chunk, item, z_at)
        where = (chunk, at, 3 + z_at)
        return remote(block, block, pair_send.at[where], pair_recv.at[where], place.sibling)

    def late_stage(chunk, number):
        if number == 0:
            each(chunk, lambda at, item: own_copy(chunk, at, item).wait())
            start(chunk, 0, 1)
        elif number == 1:
            received(chunk, 0)
            start(chunk, 2)
        elif number == 2:
            received(chunk, 1, 2)
            line_start(chunk, 1)
            each(chunk, lambda at, item: plane_copy(chunk, at, item, z).start())
        elif number < depth + 2:
            turn = number - 2
            line_received(chunk, turn)
            if turn < depth - 1:
                line_start(chunk, turn + 1)
            for upward in (True, False):
                owner = jnp.maximum(z - turn, 0) if upward else jnp.minimum(z + turn, depth - 1)

                @pl.when(receives(turn, upward))
                def _():
                    each(chunk, lambda at, item: plane_copy(chunk, at, item, owner).start())
        elif number == depth + 2:
            for z_at in range(depth):
                each(chunk, lambda at, item: plane_copy(chunk, at, item, z_at).wait_recv())

    def stage(chunk, number):
        if chunk in late:
            late_stage(chunk, number)
        elif number == 0:
            each(chunk, lambda at, item: own_copy(chunk, at, item).wait())
            line_start(chunk, 1)
        elif number < depth:
            line_received(chunk, number)
            if number < depth - 1:
                line_start(chunk, number + 1)
            else:
                start(chunk, 0, 1, 3)
        elif number == depth:
            received(chunk, 0)
            start(chunk, 2, 4)
        elif number == depth + 1:
            received(chunk, 1)
            start(chunk, 5)
        elif number == depth + 2:
            received(chunk, 2)
            start(chunk, 6)
        else:
            received(chunk, 3, 4, 5, 6)

    def sent(chunk):
        for turn in range(1, depth):
            line_sent(chunk, turn)
        for plan in range(3 if chunk in late else 7):
            each(chunk, lambda at, item: pair_copy(chunk, at, item, plan).wait_send())
        if chunk in late:
            for z_at in range(depth):
                each(chunk, lambda at, item: plane_copy(chunk, at, item, z_at).wait_send())

    def begin(begun):
        for chunk in begun:
            each(chunk, lambda at, item: own_copy(chunk, at, item).start())

    return begin, stage, sent


def gathered(results):
    return [
        result.reshape(result.shape[:-6] + (-1, result.shape[-1])) for result in results
    ]


def gather(arrays):
    return [lax.all_gather(array, AXES, axis=array.ndim - 2, tiled=True) for array in arrays]


def scatter_scratch(shapes, dtypes, depth):
    dma = pltpu.SemaphoreType.DMA
    scratch = []
    for shape, dtype in zip(shapes, dtypes):
        lead, rows, cols = shape
        block = (depth, lead, rows, cols)
        scratch += [
            pltpu.VMEM((4,) + block, dtype),
            pltpu.VMEM((4,) + block, dtype),
            pltpu.VMEM((3,) + block, dtype),
            pltpu.VMEM((2,) + block, dtype),
        ]
    count = len(shapes)
    return scratch + [
        dma((count, 4)),
        dma((count, 7)),
        dma((count, 7)),
        dma((count, depth, 2)),
        dma((count, depth, 2)),
    ]


def scatter_stage(place, ins, finish, scratch, count):
    depth, z, core = place.depth, place.z, place.core
    own_sem, pair_send, pair_recv, line_send, line_recv = scratch[4 * count :]

    def buffers(item):
        return scratch[4 * item : 4 * item + 4]

    def source(item, piece, lead, side):
        index = (slice(None),) + place.pieces[piece] + (side,)
        ref = ins[item]
        return ref.at[((lead,) if ref.shape[:-6] else ()) + index]

    def leads(item):
        return range(buffers(item)[0].shape[2])

    def own_copy(item, piece, lead):
        held = buffers(item)[0]
        return pltpu.make_async_copy(
            source(item, piece, lead, core), held.at[piece, :, lead], own_sem.at[item, piece]
        )

    names = (0, 2, 1, 3)

    def core_copy(item, piece, lead):
        arrived = buffers(item)[1]
        name = names[piece]
        return remote(
            source(item, piece, lead, 1 - core),
            arrived.at[name, :, lead],
            pair_send.at[item, piece],
            pair_recv.at[item, name],
            place.sibling,
        )

    def core_wait(item, piece):
        arrived = buffers(item)[1]
        block = arrived.at[piece]
        remote(
            block, block, pair_send.at[item, piece], pair_recv.at[item, piece], place.sibling
        ).wait_recv()

    def chip_copy(item, plan):
        held, _, arrived, _ = buffers(item)
        piece, target = ((2, place.second), (3, place.second), (1, place.first))[plan]
        return remote(
            held.at[piece],
            arrived.at[plan],
            pair_send.at[item, 4 + plan],
            pair_recv.at[item, 4 + plan],
            target,
        )

    def line_copy(item, owner, upward, fresh):
        held, _, _, arrived = buffers(item)
        block = arrived.at[int(upward), owner]
        where = (item, owner, int(upward))
        return remote(
            held.at[0, owner] if fresh else block,
            block,
            line_send.at[where],
            line_recv.at[where],
            place.above if upward else place.below,
        )

    def add(target, *others):
        def one(at):
            if len(others) == 1:
                target[at] = target[at] + others[0][at]
                return
            total = target[at].astype(F32)
            for other in others:
                total = total + other[at].astype(F32)
            target[at] = total.astype(target.dtype)

        for first in range(target.shape[0]):
            for second in range(target.shape[1]):
                one((first, second))

    def add_block(target, other):
        for lead in range(target.shape[0]):
            target[lead] = target[lead] + other[lead]

    def merge(item, piece):
        held, arrived, _, _ = buffers(item)
        block = held.at[piece]
        pltpu.make_async_copy(block, block, own_sem.at[item, piece]).wait()
        core_wait(item, piece)
        add(block, arrived.at[piece])

    def line_turn(item, turn, upward):
        held, _, _, arrived = buffers(item)
        at = turn if upward else depth - 1 - turn
        beyond = range(at + 1, depth) if upward else range(at)

        @pl.when(z == at)
        def _():
            for owner in sorted(beyond, key=lambda owner: -abs(owner - at)):
                if turn:
                    line_copy(item, owner, upward, False).wait_recv()
                    add_block(arrived.at[int(upward), owner], held.at[0, owner])
                line_copy(item, owner, upward, not turn).start()
            if turn:
                line_copy(item, at, upward, False).wait_recv()

    def stage(item, number):
        held, _, arrived, line = buffers(item)
        if number == 0:
            for piece in (3, 1, 2, 0):
                for lead in leads(item):
                    core_copy(item, piece, lead).start()
            for piece in (2, 3, 1, 0):
                for lead in leads(item):
                    own_copy(item, piece, lead).start()
        elif number == 1:
            for piece, plan in ((3, 1), (2, 0)):
                merge(item, piece)
                chip_copy(item, plan).start()
        elif number == 2:
            merge(item, 1)
            merge(item, 0)
        elif number == 3:
            chip_copy(item, 1).wait_recv()
            add(held.at[1], arrived.at[1])
            chip_copy(item, 2).start()
        elif number == 4:
            chip_copy(item, 0).wait_recv()
            chip_copy(item, 2).wait_recv()
            add(held.at[0], arrived.at[0], arrived.at[2])
            for upward in (True, False):
                line_turn(item, 0, upward)
        elif number < 4 + depth:
            for upward in (True, False):
                line_turn(item, number - 4, upward)
        else:
            for lead in leads(item):
                total = held[0, z, lead].astype(F32)
                for upward, near in ((1, z > 0), (0, z < depth - 1)):
                    total = jnp.where(near, total + line[upward, z, lead].astype(F32), total)
                finish(item, lead, total)

            for piece in range(4):
                block = buffers(item)[1].at[piece]
                remote(
                    block, block, pair_send.at[item, piece], pair_recv.at[item, piece], place.sibling
                ).wait_send()
            for plan in range(3):
                chip_copy(item, plan).wait_send()
            for upward in (True, False):
                for owner in range(depth):

                    @pl.when((z < owner) if upward else (z > owner))
                    def _():
                        line_copy(item, owner, upward, False).wait_send()

    return stage


def split_rows(array, depth):
    return array.reshape(array.shape[:-2] + (depth, 2, 2, 2, -1, array.shape[-1]))


def shared_scratch(depth, rows, dtype):
    dma = pltpu.SemaphoreType.DMA
    return [
        pltpu.VMEM((4, rows, D), dtype),
        pltpu.VMEM((5, rows, D), dtype),
        pltpu.VMEM((2, rows, D), dtype),
        dma((5,)),
        dma((5,)),
    ]


def shared_stage(place, finish, scratch):
    held, arrived, line, send_sem, recv_sem = scratch
    depth, z = place.depth, place.z
    partners = (place.sibling, place.second, place.first)

    def pair_copy(at):
        return remote(
            held.at[at], arrived.at[at], send_sem.at[at], recv_sem.at[at], partners[at]
        )

    def line_copy(upward, fresh):
        at = 3 + int(upward)
        return remote(
            held.at[3] if fresh else line.at[int(upward)],
            arrived.at[at],
            send_sem.at[at],
            recv_sem.at[at],
            place.above if upward else place.below,
        )

    def line_turn(turn, upward):
        at = turn if upward else depth - 1 - turn

        @pl.when(z == at)
        def _():
            if turn:
                line_copy(upward, False).wait_recv()
            if turn < depth - 1:
                if turn:
                    line[int(upward)] = held[3] + arrived[3 + int(upward)]
                line_copy(upward, not turn).start()

    def stage(number):
        if number == 0:
            pair_copy(0).start()
        elif number < 4:
            pair_copy(number - 1).wait_recv()
            held[number] = held[number - 1] + arrived[number - 1]
            if number < 3:
                pair_copy(number).start()
            else:
                for upward in (True, False):
                    line_turn(0, upward)
        elif number < 3 + depth:
            for upward in (True, False):
                line_turn(number - 3, upward)
        else:
            total = held[3]
            total = jnp.where(z > 0, total + arrived[4], total)
            finish(jnp.where(z < depth - 1, total + arrived[3], total))
            for at in range(3):
                pair_copy(at).wait_send()
            for upward in (True, False):

                @pl.when((z < depth - 1) if upward else (z > 0))
                def _():
                    line_copy(upward, False).wait_send()

    return stage


def scatter(arrays):
    return [
        lax.psum_scatter(array.astype(F32), AXES, scatter_dimension=array.ndim - 2, tiled=True)
        for array in arrays
    ]


def lane_index(rows):
    return lax.broadcasted_iota(jnp.int32, (rows, LANES), 1)


def halves(lane, odd):
    own = (lane >= HEAD_DIM) if odd else (lane < HEAD_DIM)
    other = lane if odd else lane - HEAD_DIM
    return own, other


def three_parts(values):
    high = values.astype(BF16).astype(F32)
    rest = values - high
    middle = rest.astype(BF16).astype(F32)
    return high, middle, rest - middle


def with_terms(own, other, values, terms):
    result = jnp.zeros_like(values)
    for at, term in enumerate(terms):
        result = jnp.where(other == at, term, result)
    return jnp.where(own, values, result)


def attend_quad(student, length, inputs, weights, biases, targets, between):
    q_ref, k_ref, v_ref, ctx_ref = targets
    rows = inputs.shape[0]
    lane = lane_index(rows)
    position = lax.broadcasted_iota(jnp.int32, (rows, LANES), 0)
    hidden_key = jnp.where(position < length, 0.0, masked_score)
    queries, keys, values = (
        (dot(inputs, weight, 1, 1) + bias).astype(BF16) for weight, bias in zip(weights, biases)
    )
    if not student:
        q_ref[...] = queries
        k_ref[...] = keys
    block = 512
    for pair in range(2):
        lanes = slice(pair * LANES, (pair + 1) * LANES)
        query, key, value = (
            array[:, lanes].astype(F32) for array in (queries, keys, values)
        )
        parts = []
        for odd in range(2):
            own, other = halves(lane, odd)
            place = slice((pair * 2 + odd) * LANES, (pair * 2 + odd + 1) * LANES)
            query_full = with_terms(own, other, query, (0.0, 0.0, 0.0, 1.0)).astype(BF16)
            key_full = with_terms(own, other, key, (1.0, 1.0, 1.0, hidden_key)).astype(BF16)
            value_full = with_terms(own, other, value, (1.0, 1.0, 1.0)).astype(BF16)
            if student:
                k_ref[:, place] = key_full
                v_ref[:, place] = value_full
            found = []
            for start in range(0, rows, block):
                take = slice(start, start + block)
                scores = dot(query_full[take], key_full, 1, 1)
                top = jnp.max(scores, axis=1, keepdims=True)
                expo = jnp.exp2((scores - top) * exponent).astype(BF16)
                mixed = dot(expo, value_full, 1, 0)
                at = 0 if odd else HEAD_DIM
                total = mixed[:, at : at + 1]
                found.append(mixed / total)
                if student:
                    logsum = top + jnp.log(total) / scaling
                    q_ref[take, place] = with_terms(
                        own[take],
                        other[take],
                        query[take],
                        tuple(-part for part in three_parts(logsum)) + (1.0,),
                    ).astype(BF16)
            parts.append(jnp.concatenate(found, axis=0))
            between(pair * 2 + odd)
        context = jnp.where(lane < HEAD_DIM, parts[0], parts[1])
        ctx_ref[:, lanes] = context.astype(ctx_ref.dtype)


def attend_kernel(student, lengths, *refs):
    if student:
        clip, x_ref, w_ref, b_ref, q_ref, k_ref, v_ref, ctx_ref, low_ref = refs

        @pl.when(pl.program_id(0) == 0)
        def _():
            width = saturation * clip[0]
            low_ref[...] = (width * jnp.tanh(x_ref[...].astype(F32) / width)).astype(BF16)

        x_ref = low_ref
        targets = (q_ref, k_ref, v_ref, ctx_ref)
    else:
        x_ref, w_ref, b_ref, q_ref, k_ref, ctx_ref = refs
        targets = (q_ref, k_ref, None, ctx_ref)
    attend_quad(
        student,
        lengths[own_index()],
        x_ref[...],
        [w_ref[slot] for slot in range(3)],
        [b_ref[slot] for slot in range(3)],
        targets,
        lambda head: None,
    )


def attend(student, lengths, clip_scales, inputs, weights, bias):
    rows = inputs.shape[0]
    wide = 4 * LANES
    narrow = 2 * LANES
    scalar = whole(pltpu.SMEM)
    in_specs = [scalar] + ([scalar] if student else [])
    in_specs += [
        fixed((rows, D)),
        pl.BlockSpec((3, narrow, D), lambda i: (0, i, 0)),
        columns((3, 1, narrow)),
    ]
    if student:
        out_shape = [jax.ShapeDtypeStruct((rows, 2 * D), BF16)] * 3 + [
            jax.ShapeDtypeStruct((rows, D), F32),
            jax.ShapeDtypeStruct((rows, D), BF16),
        ]
        out_specs = [columns((rows, wide))] * 3 + [columns((rows, narrow)), fixed((rows, D))]
        args = (lengths, clip_scales, inputs, weights, bias)
    else:
        out_shape = [jax.ShapeDtypeStruct((rows, D), BF16)] * 3
        out_specs = [columns((rows, narrow))] * 3
        args = (lengths, inputs, weights, bias)
    return pl.pallas_call(
        functools.partial(attend_kernel, student),
        grid=(D // narrow,),
        in_specs=in_specs,
        out_specs=out_specs,
        out_shape=out_shape,
        compiler_params=pltpu.CompilerParams(vmem_limit_bytes=vmem_bytes),
        name="student_attention" if student else "teacher_attention",
    )(*args)


def split_dot(left, right):
    high = right.astype(BF16)
    low = (right - high.astype(F32)).astype(BF16)
    return dot(left, high, 1, 0) + dot(left, low, 1, 0)


def attend_back_pair(length, inverse_pairs, q_ref, k_ref, v_ref, ctx_ref, dctx_ref, tq_ref, tk_ref, between):
    rows = ctx_ref.shape[0]
    lane = lane_index(rows)
    position = lax.broadcasted_iota(jnp.int32, (rows, LANES), 0)
    live = position < length
    low_half = lane < HEAD_DIM
    grad_context = dctx_ref[...].astype(F32)
    product = grad_context * ctx_ref[...]
    block = 512
    pieces = []
    for odd in range(2):
        own, other = halves(lane, odd)
        place = slice(odd * LANES, (odd + 1) * LANES)
        query, key, value = q_ref[:, place], k_ref[:, place], v_ref[:, place]
        weighted = jnp.sum(jnp.where(own, product, 0.0), axis=1, keepdims=True)
        grad_full = with_terms(
            own, other, grad_context, tuple(-part for part in three_parts(weighted))
        ).astype(BF16)
        grad_query = None
        key_parts, value_parts = [], []
        for start in range(0, rows, block):
            take = slice(start, start + block)
            probs = jnp.exp2(dot(key[take], query, 1, 1) * exponent)
            grad_scores = (probs * dot(value[take], grad_full, 1, 1)).astype(BF16)
            value_parts.append(dot(probs.astype(BF16), grad_full, 1, 0))
            key_parts.append(dot(grad_scores, query, 1, 0))
            part = dot(grad_scores, key[take], 0, 0)
            grad_query = part if grad_query is None else grad_query + part
        pieces.append(
            (grad_query, jnp.concatenate(key_parts, axis=0), jnp.concatenate(value_parts, axis=0))
        )
        between(odd)
    query_live, key_live = (
        jnp.where(live, jnp.where(low_half, ref[:, :LANES], ref[:, LANES:]), 0.0).astype(BF16)
        for ref in (q_ref, k_ref)
    )
    teach_query, teach_key = (
        jnp.where(live, ref[...], 0.0).astype(BF16) for ref in (tq_ref, tk_ref)
    )
    row = lax.broadcasted_iota(jnp.int32, (LANES, LANES), 0)
    col = lax.broadcasted_iota(jnp.int32, (LANES, LANES), 1)
    same = (row < HEAD_DIM) == (col < HEAD_DIM)

    def gram(left, right):
        return jnp.where(same, outer_rows(left, right), 0.0)

    key_key, teach_key_key = gram(key_live, key_live), gram(teach_key, key_live)
    query_query, teach_query_query = gram(query_live, query_live), gram(teach_query, query_live)
    squares = (
        query_query * key_key
        - 2.0 * teach_query_query * teach_key_key
        + gram(teach_query, teach_query) * gram(teach_key, teach_key)
    )
    squares = jnp.sum(squares.reshape(LANES // 8, 8, LANES), axis=0)

    squares = squares * (scaling * scaling * inverse_pairs)
    factor = 2.0 * scaling * scaling * inverse_pairs
    query_term = split_dot(
        jnp.concatenate([query_live, teach_query], axis=1),
        jnp.concatenate([key_key, -teach_key_key], axis=0),
    )
    key_term = split_dot(
        jnp.concatenate([key_live, teach_key], axis=1),
        jnp.concatenate([query_query, -teach_query_query], axis=0),
    )
    (even_q, even_k, even_v), (odd_q, odd_k, odd_v) = pieces
    return (
        (jnp.where(low_half, even_q, odd_q) * scaling + factor * query_term).astype(BF16),
        (jnp.where(low_half, even_k, odd_k) * scaling + factor * key_term).astype(BF16),
        jnp.where(low_half, even_v, odd_v).astype(BF16),
    ), squares


def attend_back_kernel(
    lengths, inverse_pairs, q_ref, k_ref, v_ref, ctx_ref, dctx_ref, tq_ref, tk_ref, grad_ref, sum_ref
):
    refs = (q_ref, k_ref, v_ref, ctx_ref, dctx_ref, tq_ref, tk_ref)
    grads, squares = attend_back_pair(lengths[own_index()], inverse_pairs[0], *refs, lambda odd: None)

    @pl.when(pl.program_id(0) == 0)
    def _():
        sum_ref[...] = jnp.zeros_like(sum_ref)

    sum_ref[...] += squares
    for slot in range(3):
        grad_ref[slot] = grads[slot]


def attend_back(lengths, inverse_pairs, query, key, value, context, grad_context, tq, tk):
    rows = context.shape[0]
    scalar = whole(pltpu.SMEM)
    return pl.pallas_call(
        attend_back_kernel,
        grid=(D // LANES,),
        in_specs=[scalar, scalar]
        + [columns((rows, 2 * LANES))] * 3
        + [columns((rows, LANES))] * 4,
        out_specs=[columns((3, rows, LANES)), fixed((8, LANES))],
        out_shape=[
            jax.ShapeDtypeStruct((3, rows, D), BF16),
            jax.ShapeDtypeStruct((8, LANES), F32),
        ],
        compiler_params=pltpu.CompilerParams(vmem_limit_bytes=vmem_bytes),
        name="attention_backward",
    )(lengths, inverse_pairs, query, key, value, context, grad_context, tq, tk)


def gelu_parts(upper):
    cumulative = 0.5 * (1.0 + lax.erf(upper * (1.0 / math.sqrt(2.0))))
    return cumulative, upper * cumulative


ff_part = D


def teacher_rows(tokens, context, wo_ref, up_part, w2_ref, vec, up_bias, out_ref, between):
    normed, _ = normalize(tokens.astype(F32) + dot(context, wo_ref[...], 1, 1) + vec[3:4])
    hidden = normed * vec[5:6] + vec[7:8]
    low = hidden.astype(BF16)
    lower = None
    for at in range(w2_ref.shape[1] // ff_part):
        take = slice(at * ff_part, (at + 1) * ff_part)
        _, bent = gelu_parts(dot(low, up_part(at), 1, 1) + up_bias[at : at + 1])
        part = dot(bent.astype(BF16), w2_ref[:, take], 1, 1)
        lower = part if lower is None else lower + part
        between(at)
    final, _ = normalize(hidden + lower + vec[4:5])
    out_ref[...] = final * vec[6:7] + vec[8:9]


def teacher_kernel(tok_ref, ctx_ref, wo_ref, w1_ref, w2_ref, vec_ref, ub_ref, out_ref):
    teacher_rows(
        tok_ref[...],
        ctx_ref[...],
        wo_ref,
        lambda at: w1_ref[at * ff_part : (at + 1) * ff_part],
        w2_ref,
        vec_ref[...],
        ub_ref[...],
        out_ref,
        lambda at: None,
    )


def teacher_tail(tokens, context, wo, w1, w2, vectors, up_bias):
    rows, wide = tokens.shape[0], w1.shape[0]
    block = 256
    return pl.pallas_call(
        teacher_kernel,
        grid=(rows // block,),
        in_specs=[
            row_blocks((block, D)),
            row_blocks((block, D)),
            fixed((D, D)),
            fixed((wide, D)),
            fixed((D, wide)),
            fixed(vectors.shape),
            fixed(up_bias.shape),
        ],
        out_specs=row_blocks((block, D)),
        out_shape=jax.ShapeDtypeStruct((rows, D), F32),
        compiler_params=pltpu.CompilerParams(vmem_limit_bytes=vmem_bytes),
        name="teacher_feed_forward",
    )(tokens, context, wo, w1, w2, vectors, up_bias)


def student_kernel(
    row_steps,
    lengths,
    clip,
    tok_ref,
    cot_ref,
    teach_ref,
    ctx_ref,
    wo_ref,
    w1_ref,
    w2_ref,
    vec_ref,
    out_ref,
    dctx_ref,
    res_ref,
    sums_ref,
    upsum_ref,
    dw2_ref,
    dw1_ref,
    dwo_ref,
    df_all,
    fb_all,
    du_all,
    hb_all,
    dao_all,
    cb_all,
    slope_ref,
):
    step = pl.program_id(0)
    down_steps, up_steps = D // dw2_ref.shape[0], w1_ref.shape[0] // dw1_ref.shape[0]

    @pl.when(step < row_steps)
    def _():
        rows = out_ref.shape[0]
        here = pl.ds(pl.multiple_of(step * rows, rows), rows)
        student_rows(
            step,
            lengths,
            clip,
            tok_ref,
            cot_ref,
            teach_ref,
            ctx_ref,
            wo_ref,
            w1_ref,
            w2_ref,
            vec_ref[9:18],
            vec_ref[22:26],
            out_ref,
            dctx_ref,
            *(ref.at[here] for ref in (dao_all, cb_all, du_all, hb_all, df_all, fb_all)),
            res_ref,
            sums_ref,
            upsum_ref,
            slope_ref,
        )

    def weight_grad(target, left, right, at):
        width = target.shape[0]
        lanes = pl.ds(pl.multiple_of(at * width, width), width)
        target[...] = outer_rows(left[:, lanes], right[...]).astype(BF16)

    @pl.when((step >= row_steps) & (step < row_steps + down_steps))
    def _():
        weight_grad(dw2_ref, df_all, fb_all, step - row_steps)

    @pl.when((step >= row_steps + down_steps) & (step < row_steps + down_steps + up_steps))
    def _():
        weight_grad(dw1_ref, du_all, hb_all, step - row_steps - down_steps)

    @pl.when(step == row_steps + down_steps + up_steps)
    def _():
        dwo_ref[...] = outer_rows(dao_all[...], cb_all[...]).astype(BF16)


def student_rows(
    step,
    lengths,
    clip,
    tok_ref,
    cot_ref,
    teach_ref,
    ctx_ref,
    wo_ref,
    w1_ref,
    w2_ref,
    vec,
    up_bias,
    out_ref,
    dctx_ref,
    dao_ref,
    cb_ref,
    du_ref,
    hb_ref,
    df_ref,
    fb_ref,
    res_ref,
    sums_ref,
    upsum_ref,
    slope_ref,
):
    wide = w1_ref.shape[0]
    ctx_width, hid_width, act_width = (saturation * clip[at] for at in (1, 2, 3))
    ctx_bent = jnp.tanh(ctx_ref[...] / ctx_width)
    ctx_low = (ctx_width * ctx_bent).astype(BF16)
    cb_ref[...] = ctx_low
    first, first_inverse = normalize(
        tok_ref[...].astype(F32) + dot(ctx_low, wo_ref[...], 1, 1) + vec[3:4]
    )
    hidden = first * vec[5:6] + vec[7:8]
    hid_bent = jnp.tanh(hidden / hid_width)
    hid_low = (hid_width * hid_bent).astype(BF16)
    hb_ref[...] = hid_low
    lower = None
    for at in range(wide // ff_part):
        take = slice(at * ff_part, (at + 1) * ff_part)
        upper = dot(hid_low, w1_ref[take], 1, 1) + up_bias[at : at + 1]
        cumulative, bent = gelu_parts(upper)
        act = jnp.tanh(bent / act_width)
        density = jnp.exp(-0.5 * upper * upper) * (1.0 / math.sqrt(2.0 * math.pi))
        slope_ref[:, take] = (1.0 - act * act) * (cumulative + upper * density)
        act_low = (act_width * act).astype(BF16)
        fb_ref[:, take] = act_low
        part = dot(act_low, w2_ref[:, take], 1, 1)
        lower = part if lower is None else lower + part
    second, second_inverse = normalize(hidden + lower + vec[4:5])
    result = second * vec[6:7] + vec[8:9]
    out_ref[...] = result.astype(BF16)
    rows = result.shape[0]
    position = lax.broadcasted_iota(jnp.int32, (rows, D), 0) + step * rows
    gap = jnp.where(position < lengths[own_index()], result - teach_ref[...], 0.0)
    grad_out = cot_ref[...].astype(F32) + gap * (2.0 * hidden_weight)
    grad_second = norm_back(grad_out * vec[6:7], second, second_inverse)
    grad_lower = grad_second.astype(BF16)
    df_ref[...] = grad_lower
    grad_hidden = None
    up_sums = []
    for at in range(wide // ff_part):
        take = slice(at * ff_part, (at + 1) * ff_part)
        grad_upper = (dot(grad_lower, w2_ref[:, take], 1, 0) * slope_ref[:, take]).astype(BF16)
        du_ref[:, take] = grad_upper
        up_sums.append(jnp.sum(grad_upper.astype(F32), axis=0, keepdims=True))
        part = dot(grad_upper, w1_ref[take], 1, 0)
        grad_hidden = part if grad_hidden is None else grad_hidden + part
    grad_hidden = grad_second + grad_hidden * (1.0 - hid_bent * hid_bent)
    grad_first = norm_back(grad_hidden * vec[5:6], first, first_inverse)
    res_ref[...] = grad_first
    grad_attn = grad_first.astype(BF16)
    dao_ref[...] = grad_attn
    dctx_ref[...] = (
        dot(grad_attn, wo_ref[...], 1, 0) * (1.0 - ctx_bent * ctx_bent)
    ).astype(BF16)

    @pl.when(step == 0)
    def _():
        sums_ref[...] = jnp.zeros_like(sums_ref)
        upsum_ref[...] = jnp.zeros_like(upsum_ref)

    for at, term in enumerate(
        (
            grad_attn.astype(F32),
            grad_lower.astype(F32),
            grad_hidden * first,
            grad_out * second,
            grad_hidden,
            grad_out,
            gap * gap,
        )
    ):
        sums_ref[at : at + 1] += jnp.sum(term, axis=0, keepdims=True)
    for at, total in enumerate(up_sums):
        upsum_ref[at : at + 1] += total


def student_middle(
    lengths, clip_scales, tokens, cotangent, teach_out, context, wo, w1, w2, vectors
):
    rows, wide = tokens.shape[0], w1.shape[0]
    block, down_block, up_block = 256, 256, D
    row_steps, down_steps, up_steps = rows // block, D // down_block, wide // up_block
    scalar = whole(pltpu.SMEM)

    def window(first, count, shape):
        return pl.BlockSpec(shape, lambda i: (jnp.clip(i - first, 0, count - 1), 0))

    row_spec = window(0, row_steps, (block, D))
    narrow, broad = pltpu.VMEM((rows, D), BF16), pltpu.VMEM((rows, wide), BF16)
    return pl.pallas_call(
        functools.partial(student_kernel, row_steps),
        grid=(row_steps + down_steps + up_steps + 1,),
        in_specs=[scalar, scalar]
        + [row_spec] * 4
        + [fixed((D, D)), fixed((wide, D)), fixed((D, wide)), fixed(vectors.shape)],
        out_specs=[row_spec] * 3
        + [
            fixed((8, D)),
            fixed((wide // D, D)),
            window(row_steps, down_steps, (down_block, wide)),
            window(row_steps + down_steps, up_steps, (up_block, D)),
            fixed((D, D)),
        ],
        out_shape=[
            jax.ShapeDtypeStruct((rows, D), BF16),
            jax.ShapeDtypeStruct((rows, D), BF16),
            jax.ShapeDtypeStruct((rows, D), F32),
            jax.ShapeDtypeStruct((8, D), F32),
            jax.ShapeDtypeStruct((wide // D, D), F32),
            jax.ShapeDtypeStruct((D, wide), BF16),
            jax.ShapeDtypeStruct((wide, D), BF16),
            jax.ShapeDtypeStruct((D, D), BF16),
        ],
        scratch_shapes=[narrow, broad, broad, narrow, narrow, narrow]
        + [pltpu.VMEM((block, wide), F32)],
        compiler_params=pltpu.CompilerParams(vmem_limit_bytes=vmem_bytes),
        name="student_feed_forward",
    )(lengths, clip_scales, tokens, cotangent, teach_out, context, wo, w1, w2, vectors)


def input_kernel(clip, grad_ref, w_ref, low_ref, tok_ref, res_ref, out_ref, dw_ref, sum_ref, acc_ref):
    slot = pl.program_id(0)
    grad = grad_ref[0]
    part = dot(grad, w_ref[0], 1, 0)
    dw_ref[0] = outer_rows(grad, low_ref[...]).astype(dw_ref.dtype)
    sum_ref[0] = jnp.sum(grad.astype(F32), axis=0, keepdims=True)

    @pl.when(slot == 0)
    def _():
        acc_ref[...] = part

    @pl.when(slot > 0)
    def _():
        acc_ref[...] += part

    @pl.when(slot == pl.num_programs(0) - 1)
    def _():
        bent = jnp.tanh(tok_ref[...].astype(F32) / (saturation * clip[0]))
        out_ref[...] = (res_ref[...] + acc_ref[...] * (1.0 - bent * bent)).astype(BF16)


def input_grads(clip_scales, grads, weights, low, tokens, residual):
    rows = tokens.shape[0]
    slotted = lambda *shape: pl.BlockSpec((1,) + shape, lambda i: (i, 0, 0))
    return pl.pallas_call(
        input_kernel,
        grid=(3,),
        in_specs=[
            whole(pltpu.SMEM),
            slotted(rows, D),
            slotted(D, D),
            fixed((rows, D)),
            fixed((rows, D)),
            fixed((rows, D)),
        ],
        out_specs=[fixed((rows, D)), slotted(D, D), slotted(1, D)],
        out_shape=[
            jax.ShapeDtypeStruct((rows, D), BF16),
            jax.ShapeDtypeStruct((3, D, D), BF16),
            jax.ShapeDtypeStruct((3, 1, D), F32),
        ],
        scratch_shapes=[pltpu.VMEM((rows, D), F32)],
        compiler_params=pltpu.CompilerParams(vmem_limit_bytes=vmem_bytes),
        name="input_gradient",
    )(clip_scales, grads, weights, low, tokens, residual)


gather_chunks = ((0,), (1,), (2,), (3,), (4, 5), (6,), (7, 8), (9,))
gather_leads = (1, 1, 1, 3, 1, 1, 1, 1, 1, 1)
late_chunks = (6,)
ahead_stages = ((0, 0), (1, 0), (2, 0), (0, 1), (1, 1), (2, 1), (0, 2), (1, 2), (2, 2), (0, 3), (1, 3), (3, 0), (2, 3), (0, 4), (5, 0), (0, 5), (3, 1), (1, 4), (1, 5), (5, 1), (2, 4), (3, 2), (4, 0), (6, 0), (2, 5), (0, 6), (5, 2), (7, 0), (1, 6), (0, 7), (2, 6), (3, 3), (1, 7), (6, 1), (2, 7))
opening_stages = {3: (), 6: ((4, 6), (5, 7), (6, 4), (4, 7))}
gather_between = {(0, 3): ((4, 1), (3, 4), (7, 1), (5, 3)), (1, 3): ((4, 2), (3, 5), (3, 6), (6, 2)), (2, 3): ((4, 3), (3, 7), (7, 2), (5, 4)), (3, 3): ((5, 5),), (4, 3): ((4, 4), (6, 3), (7, 3), (4, 5)), (5, 3): ((5, 6),), (6, 3): ((7, 4),), (7, 3): ((7, 5),), (8, 3): ((6, 5), (7, 6)), (9, 3): ((6, 6),)}
closing_stages = ((7, 7),)


def lay_flat(flat, owners):
    rows = owners.shape[-2]
    for owner in range(flat.shape[0] // rows):
        flat[owner * rows : (owner + 1) * rows] = owners[
            owner // 8, owner // 4 % 2, owner // 2 % 2, owner % 2
        ]


def own_lines(target, line_refs, up_bias_refs):
    at = own_index()
    target[...] = jnp.zeros_like(target)
    width = line_refs[0].shape[1]
    place, row = lanes_of(width, at * width), 0
    for ref in line_refs:
        target[row : row + ref.shape[0]] = dot(ref[...], place, 1, 0)
        row += ref.shape[0]
    wide = up_bias_refs[0].shape[1]
    owners = D // wide
    place = lanes_of(wide, lax.rem(at, owners) * wide)
    for ref in up_bias_refs:
        rows = wide * count_of() // D
        where = lax.broadcasted_iota(jnp.int32, (rows, D), 0) == at // owners
        target[row : row + rows] = jnp.where(where, dot(ref[...], place, 1, 0), 0.0)
        row += rows


def count_of():
    return lax.axis_size("dp") * lax.axis_size("shard")


def forward_kernel(depth, tail_steps, lengths, clip, *refs):
    (teach_attn, teach_up, teach_down, attn_ref, up_ref, down_ref, teach_tok, tok), refs = (
        refs[:8],
        refs[8:],
    )
    line_refs, up_bias_refs, refs = refs[:6], refs[6:8], refs[8:]
    (tq_ref, tk_ref, q_ref, k_ref, v_ref, ctx_ref, low_ref, out_ref, vec_ref), refs = (
        refs[:9],
        refs[9:],
    )
    (qkv_out, wo_out, up_out, down_out), refs = refs[:4], refs[4:]
    (teach_qkv, own_qkv, teach_wo, teach_w1, teach_w2, attn_low, up_low, down_low, teach_ctx), refs = (
        refs[:9],
        refs[9:],
    )
    (qkv_flat, wo_flat, w2_flat), refs = refs[:3], refs[3:]
    qkv_sem, shared, sems = refs[0], refs[1:6], refs[6:]
    place = Place(depth)
    step = pl.program_id(0)
    narrow = 2 * LANES
    attend_steps = D // narrow
    last = pl.num_programs(0) - 1

    ins = [teach_attn.at[slot] for slot in range(3)] + [
        attn_low.at[pl.ds(0, 3)],
        teach_attn.at[3],
        teach_up,
        teach_down,
        attn_low.at[3],
        up_low,
        down_low,
    ]
    outs = [teach_qkv.at[slot] for slot in range(3)] + [
        own_qkv,
        teach_wo,
        teach_w1,
        teach_w2,
        wo_out,
        up_out,
        down_out,
    ]
    begin, stage, sent = gather_stage(place, ins, outs, gather_leads, gather_chunks, late_chunks, sems)

    def run(stages):
        for chunk, number in stages:
            stage(chunk, number)

    def finish_lines(total):
        vec_ref[...] = total.astype(F32)

    line_stage = shared_stage(place, finish_lines, shared)
    line_count = depth + 4

    @pl.when(step == 0)
    def _():
        own_lines(vec_ref, line_refs, up_bias_refs)
        shared[0][0] = vec_ref[...].astype(BF16)
        place.barrier()
        begin((0, 1, 2))
        lines = iter(range(line_count))
        for at, (chunk, number) in enumerate(ahead_stages):
            if at == 2:
                for latent, low in ((attn_ref, attn_low), (up_ref, up_low), (down_ref, down_low)):
                    values = latent[...]
                    scale = jnp.mean(jnp.abs(values), axis=-1, keepdims=True)
                    sign = jnp.where(values > 0, 1.0, jnp.where(values < 0, -1.0, 0.0))
                    low[...] = (scale * sign).astype(BF16)
                begin((4, 5, 3, 6, 7))
            stage(chunk, number)
            if at % 2 == 0:
                for line in lines:
                    line_stage(line)
                    break
        for line in lines:
            line_stage(line)

    def slots(first, steps, at):
        for local in range(steps):
            stages = gather_between.get((first + local, at))
            if stages:

                @pl.when(step == first + local)
                def _():
                    run(stages)

    def opening(first):
        if opening_stages[first]:

            @pl.when(step == first)
            def _():
                run(opening_stages[first])

    def qkv_copy():
        return pltpu.make_async_copy(own_qkv, qkv_out, qkv_sem)

    def attend_step(student, first, inputs, weights, line, targets):
        local = step - first
        @pl.when(local == 0)
        def _():
            for slot in range(3):
                lay_flat(qkv_flat.at[slot], weights.at[slot])

        rows = pl.ds(pl.multiple_of(local * narrow, narrow), narrow)
        attend_quad(
            student,
            lengths[own_index()],
            inputs[...],
            [qkv_flat[slot, rows, :] for slot in range(3)],
            [vec_ref[line + slot : line + slot + 1, rows] for slot in range(3)],
            targets,
            lambda head: None,
        )
        slots(first, attend_steps, 3)

    @pl.when(step < attend_steps)
    def _():
        lanes = pl.ds(pl.multiple_of(step * narrow, narrow), narrow)
        attend_step(
            False, 0, teach_tok, teach_qkv, 0, (tq_ref, tk_ref, None, teach_ctx.at[:, lanes])
        )

    @pl.when((step >= attend_steps) & (step < 2 * attend_steps))
    def _():
        opening(attend_steps)

        @pl.when(step == attend_steps)
        def _():
            qkv_copy().start()
            width = saturation * clip[0]
            low_ref[...] = (width * jnp.tanh(tok[...].astype(F32) / width)).astype(BF16)

        attend_step(True, attend_steps, low_ref, own_qkv, 9, (q_ref, k_ref, v_ref, ctx_ref))

    @pl.when(step >= 2 * attend_steps)
    def _():
        first = 2 * attend_steps
        opening(first)

        @pl.when(step == first)
        def _():
            lay_flat(wo_flat, teach_wo)
            lay_flat(w2_flat, teach_w2)

        block = out_ref.shape[0]
        rows = pl.ds(pl.multiple_of((step - first) * block, block), block)
        teacher_rows(
            teach_tok[rows, :],
            teach_ctx[rows, :],
            wo_flat,
            lambda at: teach_w1[at].reshape(D, D),
            w2_flat,
            vec_ref[0:9],
            vec_ref[18:22],
            out_ref,
            lambda at: None,
        )
        slots(first, tail_steps, 3)

    @pl.when(step == last)
    def _():
        run(closing_stages)
        qkv_copy().wait()
        for chunk in range(len(gather_chunks)):
            sent(chunk)


def forward(
    lengths,
    clip_scales,
    teacher_attn,
    teacher_up,
    teacher_down,
    lines,
    up_biases,
    latents,
    teacher_tokens,
    tokens,
):
    rows = tokens.shape[0]
    depth = lax.axis_size("dp") // 2
    attn_latent, up_latent, down_latent = latents
    narrow, wide = attn_latent.shape[1], up_latent.shape[0]
    lanes, quad, block = 2 * LANES, 4 * LANES, 256
    attend_steps, tail_steps = D // lanes, rows // block
    dma = pltpu.SemaphoreType.DMA
    owners = (depth, 2, 2, 2)
    qkv_shape, wo_shape = (3,) + owners + (narrow, D), owners + (narrow, D)
    up_shape, down_shape = owners + (wide, D), owners + (narrow, down_latent.shape[1])
    scalar = whole(pltpu.SMEM)

    def window(first, count, shape, along):
        def index(i):
            at = jnp.clip(i - first, 0, count - 1)
            return (at, 0) if along == 0 else (0, at)

        return pl.BlockSpec(shape, index)

    def student_columns(width):
        return window(attend_steps, attend_steps, (rows, width), 1)

    results = pl.pallas_call(
        functools.partial(forward_kernel, depth, tail_steps),
        grid=(2 * attend_steps + tail_steps,),
        in_specs=[scalar] * 2
        + [whole(pl.ANY)] * 3
        + [
            fixed(shape)
            for shape in (
                attn_latent.shape,
                up_latent.shape,
                down_latent.shape,
                (rows, D),
                (rows, D),
                *(line.shape for line in lines),
                *(line.shape for line in up_biases),
            )
        ],
        out_specs=[window(0, attend_steps, (rows, lanes), 1)] * 2
        + [student_columns(quad)] * 3
        + [
            student_columns(lanes),
            fixed((rows, D)),
            window(2 * attend_steps, tail_steps, (block, D), 0),
            fixed((vector_rows, D)),
        ]
        + [whole(pl.ANY)] * 4,
        out_shape=[jax.ShapeDtypeStruct((rows, D), BF16)] * 2
        + [jax.ShapeDtypeStruct((rows, 2 * D), BF16)] * 3
        + [
            jax.ShapeDtypeStruct((rows, D), F32),
            jax.ShapeDtypeStruct((rows, D), BF16),
            jax.ShapeDtypeStruct((rows, D), F32),
            jax.ShapeDtypeStruct((vector_rows, D), F32),
        ]
        + [
            jax.ShapeDtypeStruct(shape, BF16)
            for shape in (qkv_shape, wo_shape, up_shape, down_shape)
        ],
        scratch_shapes=[
            pltpu.VMEM(shape, BF16)
            for shape in (
                qkv_shape,
                qkv_shape,
                wo_shape,
                up_shape,
                down_shape,
                attn_latent.shape,
                up_latent.shape,
                down_latent.shape,
                (rows, D),
                (3, D, D),
                (D, D),
                (D, down_latent.shape[1]),
            )
        ]
        + [dma]
        + shared_scratch(depth, vector_rows, BF16)
        + gather_scratch(gather_chunks, depth),
        compiler_params=pltpu.CompilerParams(
            collective_id=0, has_side_effects=True, vmem_limit_bytes=vmem_bytes
        ),
        name="gather_attention_and_teacher",
    )(
        lengths,
        clip_scales,
        teacher_attn,
        teacher_up,
        teacher_down,
        attn_latent,
        up_latent,
        down_latent,
        teacher_tokens,
        tokens,
        *lines,
        *up_biases,
    )
    return list(results[:9]) + gathered(results[9:])


first_stages = ((0, 0), (2, 0), (1, 0))
between_stages = {1: ((0, 1), (0, 2)), 2: ((1, 1), (1, 2), (0, 3)), 4: ((1, 3),), 5: ((0, 4), (2, 1), (2, 2)), 6: ((1, 4), (2, 3))}
after_weights = (((0, 5), (2, 4)), ((3, 1), (3, 2)), ((4, 1), (4, 2), (3, 3)))
after_inputs = (((1, 5), (4, 3), (0, 6), (5, 1), (5, 2), (2, 5)), ((4, 4), (3, 4), (0, 7), (0, 8), (5, 3)), ((1, 6), (4, 5), (5, 4), (2, 6)))
last_stages = ((3, 5), (4, 6), (5, 5), (1, 7), (1, 8), (3, 6), (2, 7), (2, 8), (4, 7), (4, 8), (5, 6), (3, 7), (3, 8), (5, 7), (5, 8))


def latent_rows(latent, grad):
    size = latent.shape[-1]
    scale = jnp.mean(jnp.abs(latent), axis=-1, keepdims=True)
    sign = jnp.where(latent > 0, 1.0, jnp.where(latent < 0, -1.0, 0.0))
    return scale * grad + sign * (jnp.sum(grad * latent, axis=-1, keepdims=True) / size)


def inverse_norms(lengths, width):
    tokens, pairs = jnp.int32(0), jnp.int32(0)
    for at in range(lengths.shape[0]):
        tokens, pairs = tokens + lengths[at], pairs + lengths[at] * lengths[at]
    return tuple(
        1.0 / (jnp.full((1, width), total.astype(F32)) * factor)
        for total, factor in ((pairs, float(HEADS)), (tokens, float(D)))
    )


def finish_kernel(depth, lengths, clip, *refs):
    pair_refs, refs = refs[:7], refs[7:]
    dw_refs, refs = refs[:3], refs[3:]
    held_refs, refs = refs[:4], refs[4:]
    (sums_ref, upsum_ref, attn_ref, up_ref, down_ref), refs = refs[:5], refs[5:]
    (input_ref, attn_grad, up_grad, down_grad), refs = refs[:4], refs[4:]
    (bias_grad, gain_grad, shift_grad, up_bias_grad, loss_ref), refs = refs[:5], refs[5:]
    (grad_ref, square_ref, dwq_ref, dwk_ref, dwv_ref), refs = refs[:5], refs[5:]
    (low_ref, w_ref, tok_ref, res_ref, load_sem), refs = refs[:5], refs[5:]
    loads = [
        pltpu.make_async_copy(source, target, load_sem.at[at])
        for at, (source, target) in enumerate(zip(held_refs, (low_ref, w_ref, tok_ref, res_ref)))
    ]
    shared, scratch = refs[:5], refs[5:]
    place = Place(depth)
    step = pl.program_id(0)
    last = pl.num_programs(0) - 1
    pairs = D // LANES

    def finish(item, lead, total):
        if item == 0:
            down_grad[...] = latent_rows(down_ref[...], total)
        elif item == 1:
            up_grad[...] = latent_rows(up_ref[...], total)
        else:
            slot = 3 if item == 2 else item - 3
            attn_grad[slot] = latent_rows(attn_ref[slot], total)

    def finish_lines(total):
        at = own_index()
        width, wide = bias_grad.shape[1], up_bias_grad.shape[1]
        taken = take_lanes(total[0:9], width, at * width)
        bias_grad[...] = taken[0:5]
        gain_grad[...] = taken[5:7]
        shift_grad[...] = taken[7:9]
        owners, rows = D // wide, total[9:13]
        where = lax.broadcasted_iota(jnp.int32, rows.shape, 0) == at // owners
        row = jnp.sum(jnp.where(where, rows, 0.0), axis=0, keepdims=True)
        up_bias_grad[...] = take_lanes(row, wide, lax.rem(at, owners) * wide)
        loss_ref[...] = jnp.sum(total[13:14], axis=1, keepdims=True)

    own = (dwq_ref, dwk_ref, dwv_ref)
    stage = scatter_stage(place, tuple(dw_refs) + own, finish, scratch, 6)
    line_stage = shared_stage(place, finish_lines, shared)

    def run(stages):
        for item, number in stages:
            stage(item, number)

    @pl.when(step == 0)
    def _():
        place.barrier()
        run(first_stages)
        for load in loads:
            load.start()
        square_ref[...] = jnp.zeros_like(square_ref)

    @pl.when(step < pairs)
    def _():
        for before, stages in between_stages.items():

            @pl.when(step == before)
            def _():
                run(stages)

        grads, squares = attend_back_pair(
            lengths[own_index()], inverse_norms(lengths, LANES)[0], *pair_refs, lambda odd: None
        )
        square_ref[...] += squares
        lanes = pl.ds(pl.multiple_of(step * LANES, LANES), LANES)
        for slot in range(3):
            grad_ref[slot, :, lanes] = grads[slot]

    def weight_grad(slot):
        total = outer_rows(grad_ref[slot], low_ref[...]).astype(BF16)
        rows = dwq_ref.shape[-2]
        for owner in range(D // rows):
            where = (owner // 8, owner // 4 % 2, owner // 2 % 2, owner % 2)
            own[slot][where] = total[owner * rows : (owner + 1) * rows]
        stage(3 + slot, 0)

    @pl.when(step == pairs)
    def _():
        run(between_stages.get(pairs, ()))
        held = shared[0]
        held[0] = jnp.zeros_like(held[0])
        for slot in range(3):
            held[0, slot : slot + 1] = jnp.sum(
                grad_ref[slot].astype(F32), axis=0, keepdims=True
            )
        held[0, 3:9] = sums_ref[0:6]
        held[0, 9:13] = upsum_ref[...]
        held[0, 13:14] = sums_ref[6:7] * inverse_norms(lengths, D)[1]
        held[0, 13:14, :LANES] += jnp.sum(square_ref[...], axis=0, keepdims=True)
        line_stage(0)
        loads[0].wait()
        weight_grad(0)
        run(after_weights[0])
        weight_grad(1)
        run(after_weights[1])

    @pl.when(step == last)
    def _():
        line_stage(1)
        weight_grad(2)
        run(after_weights[2])
        for load in loads[1:]:
            load.wait()
        total = None
        for slot in range(3):
            line_stage(2 + slot)
            part = dot(grad_ref[slot], w_ref[slot], 1, 0)
            total = part if total is None else total + part
            run(after_inputs[slot])
        bent = jnp.tanh(tok_ref[...].astype(F32) / (saturation * clip[0]))
        input_ref[...] = (res_ref[...] + total * (1.0 - bent * bent)).astype(BF16)
        for at, (item, number) in enumerate(last_stages):
            if at < 3 and 5 + at < depth + 4:
                line_stage(5 + at)
            stage(item, number)


def move_kernel(count, *refs):
    sources, targets, held = refs[:count], refs[count : 2 * count], refs[2 * count : 3 * count]
    in_sem, out_sem = refs[3 * count :]
    loads = [
        pltpu.make_async_copy(sources[at], held[at], in_sem.at[at]) for at in range(count)
    ]
    stores = [
        pltpu.make_async_copy(held[at], targets[at], out_sem.at[at]) for at in range(count)
    ]
    for load in loads:
        load.start()
    for at in range(count):
        loads[at].wait()
        stores[at].start()
    for store in stores:
        store.wait()


def moved(*arrays):
    count = len(arrays)
    dma = pltpu.SemaphoreType.DMA
    return pl.pallas_call(
        functools.partial(move_kernel, count),
        in_specs=[whole(pl.ANY)] * count,
        out_specs=[whole(pl.ANY)] * count,
        out_shape=[jax.ShapeDtypeStruct(array.shape, array.dtype) for array in arrays],
        scratch_shapes=[pltpu.VMEM(array.shape, array.dtype) for array in arrays]
        + [dma((count,)), dma((count,))],
        compiler_params=pltpu.CompilerParams(vmem_limit_bytes=vmem_bytes),
        name="move_results",
    )(*arrays)


def finish_backward(
    lengths,
    clip_scales,
    pair_arrays,
    weight_grads,
    qkv_w,
    low,
    tokens,
    residual,
    sums,
    up_sums,
    latents,
    narrow,
    wide,
):
    dp, shard = lax.axis_size("dp"), lax.axis_size("shard")
    attn_latent, up_latent, down_latent = latents
    if not tiled_over((dp, shard), narrow):
        live_float = lengths.astype(F32)
        inverse_pairs = (1.0 / (HEADS * jnp.sum(live_float * live_float))).reshape(1)
        inverse_hidden = 1.0 / (D * jnp.sum(live_float))
        grads, squares = attend_back(lengths, inverse_pairs, *pair_arrays)
        input_grad, qkv_weight_grad, qkv_sums = input_grads(
            clip_scales, grads, qkv_w, low, tokens, residual
        )
        local_loss = sums[6:7] * inverse_hidden
        local_loss = local_loss + jnp.pad(
            jnp.sum(squares, axis=0, keepdims=True), ((0, 0), (0, D - LANES))
        )
        lines = jnp.concatenate(
            [qkv_sums[:, 0], sums[:6], up_sums, local_loss], axis=0
        )
        lines = lax.psum(lines, AXES)
        down_total, up_total, attn_total = scatter(
            weight_grads[:2]
            + [jnp.concatenate([qkv_weight_grad, weight_grads[2][None].astype(BF16)], axis=0)]
        )
        attn_grad = latent_grad(attn_latent, attn_total)
        up_grad = latent_grad(up_latent, up_total)
        down_grad = latent_grad(down_latent, down_total)
        at = lax.axis_index(AXES)
        own = lax.dynamic_slice_in_dim(lines[:9], at * narrow, narrow, axis=1)
        bias_grad, gain_grad, shift_grad = own[:5], own[5:7], own[7:9]
        up_bias_grad = lax.dynamic_slice_in_dim(lines[9:13].reshape(-1), at * wide, wide)
        loss = jnp.sum(lines[13])
    else:
        depth = dp // 2
        rows = tokens.shape[0]
        dw = [split_rows(grad, depth) for grad in weight_grads]
        own_shape = (depth, 2, 2, 2, narrow, D)
        shapes = [(1,) + grad.shape[-2:] for grad in dw] + [(1, narrow, D)] * 3
        scalar = whole(pltpu.SMEM)
        pairs = D // LANES

        def pair_columns(width):
            return pl.BlockSpec((rows, width), lambda i: (0, jnp.minimum(i, pairs - 1)))

        small_shapes = ((5, narrow), (2, narrow), (2, narrow), (1, wide), (1, 1))
        (
            input_grad,
            attn_grad,
            up_grad,
            down_grad,
            bias_grad,
            gain_grad,
            shift_grad,
            up_bias_grad,
            loss,
        ) = pl.pallas_call(
            functools.partial(finish_kernel, depth),
            grid=(pairs + 2,),
            in_specs=[scalar] * 2
            + [pair_columns(2 * LANES)] * 3
            + [pair_columns(LANES)] * 4
            + [whole(pl.ANY)] * 7
            + [
                fixed(array_shape)
                for array_shape in (
                    sums.shape,
                    up_sums.shape,
                    attn_latent.shape,
                    up_latent.shape,
                    down_latent.shape,
                )
            ],
            out_specs=[
                fixed(array_shape)
                for array_shape in (
                    (rows, D),
                    attn_latent.shape,
                    up_latent.shape,
                    down_latent.shape,
                    *small_shapes,
                )
            ],
            out_shape=[
                jax.ShapeDtypeStruct((rows, D), BF16),
                jax.ShapeDtypeStruct(attn_latent.shape, F32),
                jax.ShapeDtypeStruct(up_latent.shape, F32),
                jax.ShapeDtypeStruct(down_latent.shape, F32),
            ]
            + [jax.ShapeDtypeStruct(shape, F32) for shape in small_shapes],
            scratch_shapes=[
                pltpu.VMEM((3, rows, D), BF16),
                pltpu.VMEM((8, LANES), F32),
                pltpu.VMEM(own_shape, BF16),
                pltpu.VMEM(own_shape, BF16),
                pltpu.VMEM(own_shape, BF16),
                pltpu.VMEM((rows, D), BF16),
                pltpu.VMEM((3, D, D), BF16),
                pltpu.VMEM((rows, D), BF16),
                pltpu.VMEM((rows, D), F32),
                pltpu.SemaphoreType.DMA((4,)),
            ]
            + shared_scratch(depth, line_rows, F32)
            + scatter_scratch(shapes, [BF16] * 6, depth),
            compiler_params=pltpu.CompilerParams(
                collective_id=1, has_side_effects=True, vmem_limit_bytes=vmem_bytes
            ),
            name="attention_backward_and_sums",
        )(
            lengths,
            clip_scales,
            *pair_arrays,
            *dw,
            low,
            qkv_w,
            tokens,
            residual,
            sums,
            up_sums,
            attn_latent,
            up_latent,
            down_latent,
        )
        (
            input_grad,
            attn_grad,
            up_grad,
            down_grad,
            bias_grad,
            gain_grad,
            shift_grad,
            up_bias_grad,
            loss,
        ) = moved(
            input_grad,
            attn_grad,
            up_grad,
            down_grad,
            bias_grad,
            gain_grad,
            shift_grad,
            up_bias_grad,
            loss,
        )
    return (
        loss.reshape(()),
        input_grad,
        attn_grad,
        up_grad,
        down_grad,
        bias_grad,
        up_bias_grad.reshape(-1),
        gain_grad,
        shift_grad,
    )


def on_device(
    tokens,
    teacher_tokens,
    cotangent,
    lengths,
    clip_scales,
    attn_latent,
    up_latent,
    down_latent,
    biases,
    up_bias,
    norm_gains,
    norm_shifts,
    teacher_attn,
    teacher_up,
    teacher_down,
    teacher_biases,
    teacher_up_bias,
    teacher_gains,
    teacher_shifts,
):
    sizes = (lax.axis_size("dp"), lax.axis_size("shard"))
    narrow, wide = biases.shape[1], up_bias.shape[0]
    lines = (teacher_biases, teacher_gains, teacher_shifts, biases, norm_gains, norm_shifts)
    latents = (attn_latent, up_latent, down_latent)
    if tiled_over(sizes, narrow):
        (
            tq,
            tk,
            query,
            key,
            value,
            context,
            x_low,
            teach_out,
            vec,
            qkv_w,
            out_w,
            up_w,
            down_w,
        ) = forward(
            lengths,
            clip_scales,
            teacher_attn,
            teacher_up,
            teacher_down,
            lines,
            (teacher_up_bias.reshape(1, -1), up_bias.reshape(1, -1)),
            latents,
            teacher_tokens,
            tokens,
        )
    else:
        vec = jnp.concatenate(
            [
                lax.all_gather(jnp.concatenate(lines, axis=0), AXES, axis=1, tiled=True),
                *(
                    lax.all_gather(line, AXES, tiled=True).reshape(-1, D)
                    for line in (teacher_up_bias, up_bias)
                ),
            ],
            axis=0,
        ).astype(F32)
        vec = jnp.pad(vec, ((0, vector_rows - vec.shape[0]), (0, 0)))
        teach_qkv, teach_wo, teach_up, teach_down, qkv_w, out_w, up_w, down_w = gather(
            [
                teacher_attn[:3],
                teacher_attn[3],
                teacher_up,
                teacher_down,
                binarize(attn_latent[:3]),
                binarize(attn_latent[3]),
                binarize(up_latent),
                binarize(down_latent),
            ]
        )
        tq, tk, teach_context = attend(
            False, lengths, clip_scales, teacher_tokens, teach_qkv, vec[:3].reshape(3, 1, D)
        )
        query, key, value, context, x_low = attend(
            True, lengths, clip_scales, tokens, qkv_w, vec[9:12].reshape(3, 1, D)
        )
        teach_out = teacher_tail(
            teacher_tokens, teach_context, teach_wo, teach_up, teach_down, vec[:9], vec[18:22]
        )
    result, grad_context, residual, sums, up_sums, *weight_grads = student_middle(
        lengths,
        clip_scales,
        tokens,
        cotangent,
        teach_out,
        context,
        out_w,
        up_w,
        down_w,
        vec,
    )
    return (result,) + finish_backward(
        lengths,
        clip_scales,
        (query, key, value, context, grad_context, tq, tk),
        weight_grads,
        qkv_w,
        x_low,
        tokens,
        residual,
        sums,
        up_sums,
        latents,
        narrow,
        wide,
    )


def solution(mesh):
    in_specs = (
        P(("dp", "shard"), None),
        P(("dp", "shard"), None),
        P(("dp", "shard"), None),
        P(),
        P(),
        P(None, ("dp", "shard"), None),
        P(("dp", "shard"), None),
        P(("dp", "shard"), None),
        P(None, ("dp", "shard")),
        P(("dp", "shard")),
        P(None, ("dp", "shard")),
        P(None, ("dp", "shard")),
        P(None, ("dp", "shard"), None),
        P(("dp", "shard"), None),
        P(("dp", "shard"), None),
        P(None, ("dp", "shard")),
        P(("dp", "shard")),
        P(None, ("dp", "shard")),
        P(None, ("dp", "shard")),
    )
    out_specs = (
        P(("dp", "shard"), None),
        P(),
        P(("dp", "shard"), None),
        P(None, ("dp", "shard"), None),
        P(("dp", "shard"), None),
        P(("dp", "shard"), None),
        P(None, ("dp", "shard")),
        P(("dp", "shard")),
        P(None, ("dp", "shard")),
        P(None, ("dp", "shard")),
    )
    return jax.shard_map(
        on_device, mesh=mesh, in_specs=in_specs, out_specs=out_specs, check_vma=False
    )
```
